32 devices in a mesh: seq: 2 (over x), dp: 16 (over z, y, core).
Axes of the slice: x: 2, y: 2, z: 4, core: 2. Of those that a mesh axis runs over, the one named last changes fastest.
Arguments:
- tokens: bfloat16 [16384, 1536], P(('seq', 'dp')), may hold values from -6 to 6
- cotangent: bfloat16 [16384, 1536], P(('seq', 'dp')), may hold values from -6 to 6
- positions: int32 [16, 1024], P('dp'), may hold values from 0 to 1023, each once within a row
- lengths: int32 [16, 3], P('dp'), may hold values from 1 to 512, 1024 in all within a row
- routes: int32 [16384, 8], P(('seq', 'dp')), may hold values from 0 to 15, all different within a row; in each aligned block of 512 rows (0 to 511, 512 to 1023, ...) at most 320 rows name the same one
- logits: float32 [16384, 8], P(('seq', 'dp')), may hold values from -3 to 3
- w_query: bfloat16 [1536, 1536], P(('seq', 'dp')), may hold values from -0.59765625 to 0.59765625
- w_key: bfloat16 [1536, 512], P(('seq', 'dp')), may hold values from -0.59765625 to 0.59765625
- w_value: bfloat16 [1536, 512], P(('seq', 'dp')), may hold values from -0.15625 to 0.15625
- w_output: bfloat16 [1536, 1536], P(('seq', 'dp')), may hold values from -4 to 4
- gain_attn: bfloat16 [1536], P(('seq', 'dp')), may hold values from 0.5 to 1.5
- gain_ffn: bfloat16 [1536], P(('seq', 'dp')), may hold values from 0.5 to 1.5
- w_in: bfloat16 [16, 1536, 1024], P('dp', None, 'seq'), may hold values from -0.15625 to 0.15625
- w_out: bfloat16 [16, 512, 1536], P('dp', 'seq'), may hold values from -6 to 6
Outputs:
- output: bfloat16 [16384, 1536], P(('seq', 'dp'))
- grad_tokens: float32 [16384, 1536], P(('seq', 'dp'))
- grad_w_query: float32 [1536, 1536], P(('seq', 'dp'))
- grad_w_key: float32 [1536, 512], P(('seq', 'dp'))
- grad_w_value: float32 [1536, 512], P(('seq', 'dp'))
- grad_w_output: float32 [1536, 1536], P(('seq', 'dp'))
- grad_gain_attn: float32 [1536], P(('seq', 'dp'))
- grad_gain_ffn: float32 [1536], P(('seq', 'dp'))
- grad_w_in: float32 [16, 1536, 1024], P('dp', None, 'seq')
- grad_w_out: float32 [16, 512, 1536], P('dp', 'seq')
The draws below stay inside these ranges and needn't reach their ends.
Inputs may be any that keep to these rules, and one draw needn't show every extreme that they name: `positions`: each row is a permutation of 0 to 1023. `lengths`: each row sums to 1024 and its largest entry is 512. `routes`: each row names 8 different experts. Among the rows of one device no expert is named more than 320 times, and in every draw some expert is named exactly 320 times by the rows of some device.
All inputs are finite; a program needn't handle non-finite values.
Results may differ from the reference program's by a relative error of at most 0.015.
The reference program's roundings to bfloat16 on the way count: a program that leaves them out, or rounds other values in their place, can miss the bound.
Values may be sent and summed in bfloat16 or wider, within the bound.
No kernel may reach another device: no remote copies, remote signals or barrier semaphores. Data moves between devices by JAX's collectives and lax.ppermute only.
A program may use at most 256 MiB of HBM per device.

```python
import math
import jax
import jax.numpy as jnp
import numpy as np
from jax import lax

D = 1536
QHEADS = 24
KVHEADS = 8
HDIM = 64
FF = 512
TOP = 8
NSEG = 3
TOK_DEV = 512
EXPERTS = 16
GROUP = 1024
SEQ_MAX = 512
CAP = 320
TOKENS = 16384
N_SEQ = 2
N_DP = 16


def level_of(own_key, shape, shards, least, largest):
    def one(position, blocks):
        steps = jax.random.uniform(jax.random.fold_in(jax.random.fold_in(own_key, 6), position), (blocks,), jnp.float32, least / len(shards), largest / len(shards))
        return jnp.repeat(jnp.exp(steps), shape[position] // blocks).reshape((-1,) + (1,) * (len(shape) - position - 1))

    level = one(*shards[0])
    for cut in shards[1:]:
        level = level * one(*cut)
    return level


def length_profile(count, total, most, slope):
    loads = [(1 << 20) // math.isqrt(standing ** slope) + 1 for standing in range(2, count + 1)]
    spare, counts = total - most - (count - 1), [1] * (count - 1)
    while spare > 0:
        free = [i for i in range(count - 1) if counts[i] < most]
        mass, remaining = sum([loads[i] for i in free]), spare
        for i in free:
            more = min(most - counts[i], max(1, remaining * loads[i] // mass), spare)
            counts[i] = counts[i] + more
            spare = spare - more
    return np.array([most] + counts)


def uneven(rng, amount, total, reach, lean):
    if amount == 2:
        one = jax.random.randint(rng, (), max(1, total - reach), min(reach, total - 1) + 1)
        return jnp.stack([one, total - one])
    tallies = jnp.asarray(length_profile(amount, total, reach, lean), jnp.int32)
    pairs = (amount - 1) // 2
    donor, sink = tallies[1:1 + 2 * pairs:2], tallies[2:2 + 2 * pairs:2]
    slack = jnp.minimum(donor - 1, reach - sink)
    moved = jax.random.randint(jax.random.fold_in(rng, 1), (pairs,), 0, 1 << 20) % (slack + 1)
    tallies = tallies.at[1:1 + 2 * pairs:2].set(donor - moved).at[2:2 + 2 * pairs:2].set(sink + moved)
    return tallies[jax.random.permutation(jax.random.fold_in(rng, 2), amount)]


def assign_block(rng, own, number, rows, amount, top, most, lean):
    order = jax.random.permutation(rng, amount)
    packed, usual = portions_of(amount, rows * top, most, lean, True), portions_of(amount, rows * top, most, lean, False)
    places = jnp.arange(amount)

    def named(tallies, offset_by):
        used = int((tallies > 0).sum())
        fixed = max(1, used // 4)
        passed = fixed + (places - fixed + offset_by * (used - fixed)) % max(1, amount - fixed)
        return jnp.zeros((amount,), jnp.int32).at[order[jnp.where(places < fixed, places, passed)]].set(jnp.asarray(tallies, jnp.int32))

    tallies = jnp.where(number % 4 == 0, named(packed, number // 4), named(usual, number - number // 4 - 1))
    mixed = jax.random.permutation(jax.random.fold_in(own, 3), amount)
    source_of, taker = mixed[0:amount // 2 * 2:2], mixed[1:amount // 2 * 2:2]
    margin = jnp.minimum(tallies[source_of] - 1, most - tallies[taker]) // 2
    margin = jnp.where((source_of == order[0]) | (taker == order[0]) | (tallies[taker] == 0), 0, jnp.maximum(margin, 0))
    passed = jax.random.randint(jax.random.fold_in(own, 4), (amount // 2,), 0, 1 << 20) % (margin + 1)
    tallies = tallies.at[source_of].add(-passed).at[taker].add(passed)
    members = jnp.searchsorted(jnp.cumsum(tallies), jnp.arange(rows * top), side="right").astype(jnp.int32)
    grid = members.reshape(top, rows).T
    grid = grid[jax.random.permutation(jax.random.fold_in(own, 1), rows)]
    offset_by = jax.random.randint(jax.random.fold_in(own, 2), (rows, 1), 0, top)
    return jnp.take_along_axis(grid, (jnp.arange(top)[None, :] + offset_by) % top, axis=1)


def portions_of(count, total, most, slope, full):
    weights = [(1 << 20) // math.isqrt(grade ** slope) + 1 for grade in range(1, count + 1)]
    largest = most if full else min(most, max(-(-total // count), total * weights[0] // sum(weights)))
    least = 1 if total - largest >= count - 1 else 0
    holding, surplus = [largest] + [least] * (count - 1), total - largest - least * (count - 1)
    while surplus > 0:
        free = [i for i in range(1, count) if holding[i] < largest] or [i for i in range(1, count) if holding[i] < most]
        mass, remaining = sum([weights[i] for i in free]), surplus
        for i in free:
            more = min(most - holding[i], max(1, remaining * weights[i] // mass), surplus)
            holding[i] = holding[i] + more
            surplus = surplus - more
    return np.array(holding)


def bell_draw(key, dims, scale, most, cuts=(), held_as=jnp.bfloat16):
    array = jax.random.normal(key, dims, jnp.float32) * scale
    if len(cuts) > 0:
        array = level_of(key, dims, cuts, -0.22, 0.18) * array
    return jnp.clip(array, min=-most, max=most).astype(held_as)


def setup_inputs(seed: int = 0) -> dict:
    key_of = jax.random.split(jax.random.key(seed), 15)
    tokens = bell_draw(key_of[0], (TOKENS, D), 1.0, 6.0, ((0, 32),))
    cotangent = bell_draw(key_of[1], (TOKENS, D), 1.0, 6.0, ((0, 32),))
    positions = jax.vmap(lambda own: jax.random.permutation(own, GROUP))(jax.random.split(key_of[2], N_DP)).reshape((N_DP, GROUP)).astype(jnp.int32)
    lengths = jax.vmap(lambda own: uneven(own, NSEG, GROUP, SEQ_MAX, 1))(jax.random.split(key_of[3], N_DP)).reshape((N_DP, NSEG)).astype(jnp.int32)
    routes_keys = jax.random.split(jax.random.fold_in(key_of[4], 1), TOKENS // TOK_DEV)
    routes_turns = jax.random.permutation(jax.random.fold_in(key_of[4], 3), TOKENS // TOK_DEV)
    routes = jax.vmap(lambda own, number: assign_block(jax.random.fold_in(key_of[4], 2), own, number, TOK_DEV, EXPERTS, TOP, CAP, 1))(routes_keys, routes_turns).reshape((TOKENS, TOP))
    logits = bell_draw(key_of[5], (TOKENS, TOP), 0.5, 3.0, ((0, 32),), jnp.float32)
    w_query = bell_draw(key_of[6], (D, QHEADS * HDIM), 0.1, 0.59765625, ((0, 32),))
    w_key = bell_draw(key_of[7], (D, KVHEADS * HDIM), 0.1, 0.59765625, ((0, 32),))
    w_value = bell_draw(key_of[8], (D, KVHEADS * HDIM), D ** -0.5, 0.15625, ((0, 32),))
    w_output = bell_draw(key_of[9], (QHEADS * HDIM, D), 2 ** -0.5, 4.0, ((0, 32),))
    gain_attn = jnp.clip(1.0 + 0.1 * jax.random.normal(key_of[10], (D,), jnp.float32), 0.5, 1.5).astype(jnp.bfloat16)
    gain_ffn = jnp.clip(1.0 + 0.1 * jax.random.normal(key_of[11], (D,), jnp.float32), 0.5, 1.5).astype(jnp.bfloat16)
    w_in = bell_draw(key_of[12], (EXPERTS, D, 2 * FF), D ** -0.5, 0.15625, ((0, 16), (2, 2)))
    w_out = bell_draw(key_of[13], (EXPERTS, FF, D), 1 ** -0.5, 6.0, ((0, 16), (1, 2)))
    return {"tokens": tokens, "cotangent": cotangent, "positions": positions, "lengths": lengths, "routes": routes, "logits": logits, "w_query": w_query, "w_key": w_key, "w_value": w_value, "w_output": w_output, "gain_attn": gain_attn, "gain_ffn": gain_ffn, "w_in": w_in, "w_out": w_out}


EPSILON = 1e-06
BRANCH_SCALE = 0.22
SCORE_SCALE = 1.0 / 64.0
THETA = 10000.0
HIGHEST = lax.Precision.HIGHEST

@jax.custom_vjp
def low(v):
    return lax.optimization_barrier(v.astype(jnp.bfloat16)).astype(jnp.float32)

@jax.custom_vjp
def low_back(v):
    return v

def low_keep(v):
    return (low(v), None)

def low_pass(kept, grad):
    return (grad,)

def back_keep(v):
    return (v, None)

def back_low(kept, grad):
    return (low(grad),)
low.defvjp(low_keep, low_pass)
low_back.defvjp(back_keep, back_low)

def wire_round(value):
    return low(low_back(value))

def rms_norm(value, gain):
    return value * lax.rsqrt(lax.optimization_barrier(jnp.mean(value * value, axis=-1, keepdims=True)) + EPSILON) * gain

def product(left, right):
    return jnp.dot(left, right, precision=HIGHEST, preferred_element_type=jnp.float32)

def local_places(placing, seq_lengths):
    placing = placing.astype(jnp.int32)
    seq_lengths = seq_lengths.astype(jnp.int32)
    ends = jnp.cumsum(seq_lengths).astype(jnp.int32)
    segment = lax.optimization_barrier(jnp.sum((placing[:, None] >= ends[None, :]).astype(jnp.int32), axis=1)).astype(jnp.int32)
    starts = (ends - seq_lengths).astype(jnp.int32)
    member = segment[:, None] == jnp.arange(seq_lengths.shape[0], dtype=jnp.int32)[None, :]
    start_of = lax.optimization_barrier(jnp.sum(jnp.where(member, starts[None, :], 0), axis=1)).astype(jnp.int32)
    return (segment, (placing - start_of).astype(jnp.int32))

def rotate(values, place, direction):
    half = values.shape[-1] // 2
    freqs = jnp.power(THETA, -jnp.arange(half, dtype=jnp.float32) * 2.0 / values.shape[-1])
    angles = place.astype(jnp.float32)[:, None] * freqs[None, :]
    cosine = jnp.cos(angles)[:, None, :]
    sine = direction * jnp.sin(angles)[:, None, :]
    first = values[..., :half]
    second = values[..., half:]
    return jnp.concatenate([first * cosine - second * sine, second * cosine + first * sine], axis=-1)

def to_groups(values):
    shaped = values.reshape((N_SEQ, N_DP, TOK_DEV) + values.shape[1:])
    return jnp.swapaxes(shaped, 0, 1).reshape((N_DP, N_SEQ * TOK_DEV) + values.shape[1:])

def from_groups(values):
    shaped = values.reshape((N_DP, N_SEQ, TOK_DEV) + values.shape[2:])
    return jnp.swapaxes(shaped, 0, 1).reshape((N_SEQ * N_DP * TOK_DEV,) + values.shape[2:])

def attend_block(query, keys, values, seg_query, place_query, seg_keys, place_keys):
    length = query.shape[0]
    ratio = QHEADS // KVHEADS
    grouped = query.reshape(length, KVHEADS, ratio, HDIM)
    scores = jnp.einsum('qgrd,kgd->grqk', grouped, keys, precision=HIGHEST) * SCORE_SCALE
    scores = low_back(scores)
    allowed = (seg_query[:, None] == seg_keys[None, :]) & (place_keys[None, :] <= place_query[:, None])
    scores = jnp.where(allowed[None, None], scores, -1e+30)
    weights = low(jax.nn.softmax(scores, axis=-1))
    mixed = jnp.einsum('grqk,kgd->qgrd', weights, values, precision=HIGHEST)
    return wire_round(mixed.reshape(length, QHEADS * HDIM))

def attend_group(arguments):
    query, keys, values, segment, place = arguments
    length = min(512, GROUP)
    count = GROUP // length

    def one_block(pieces):
        query_block, seg_block, place_block = pieces
        return attend_block(query_block, keys, values, seg_block, place_block, segment, place)
    mixed = lax.map(jax.checkpoint(one_block), (query.reshape(count, length, QHEADS, HDIM), segment.reshape(count, length), place.reshape(count, length)))
    return mixed.reshape(GROUP, QHEADS * HDIM)

def dispatch_tables(routes, gates):
    blocks = TOKENS // TOK_DEV
    chosen = routes.astype(jnp.int32).reshape(blocks, TOK_DEV * TOP)
    onehot = (chosen[:, :, None] == jnp.arange(EXPERTS, dtype=jnp.int32)[None, None, :]).astype(jnp.int32)
    ranking = (lax.optimization_barrier(jnp.sum(jnp.cumsum(onehot, axis=1) * onehot, axis=2)) - 1).astype(jnp.int32)
    block_of = jnp.arange(blocks, dtype=jnp.int32)[:, None]
    target = (chosen * (blocks * CAP) + block_of * CAP + ranking).astype(jnp.int32).reshape(-1)
    token_of = (jnp.arange(TOKENS * TOP, dtype=jnp.int32) // TOP).astype(jnp.int32)
    source = jnp.full((EXPERTS * blocks * CAP,), TOKENS, jnp.int32).at[target].set(token_of)
    slot_gate = jnp.zeros((EXPERTS * blocks * CAP,), jnp.float32).at[target].set(gates.reshape(-1))
    return (source.reshape(EXPERTS, blocks * CAP), slot_gate.reshape(EXPERTS, blocks * CAP))

def forward(inputs, w_query, w_key, w_value, w_output, gain_attn, gain_ffn, w_in, w_out, segment, place, place_tokens, source, slot_gate):
    normed = low(rms_norm(inputs, gain_attn))
    query = low_back(product(normed, w_query)).reshape(TOKENS, QHEADS, HDIM)
    keys = low_back(product(normed, w_key)).reshape(TOKENS, KVHEADS, HDIM)
    values = wire_round(product(normed, w_value)).reshape(TOKENS, KVHEADS, HDIM)
    query = wire_round(rotate(query, place_tokens, 1.0))
    keys = wire_round(rotate(keys, place_tokens, 1.0))
    mixed = lax.map(jax.checkpoint(attend_group), (to_groups(query), to_groups(keys), to_groups(values), segment, place))
    mixed = from_groups(mixed)
    attn = low_back(product(mixed, w_output))
    middle = inputs + BRANCH_SCALE * attn
    normed_ffn = low(rms_norm(middle, gain_ffn))
    padded = jnp.concatenate([normed_ffn, jnp.zeros((1, D), jnp.float32)], axis=0)

    def expert(total, pieces):
        slot_source, gate_slot, weight_in, weight_out = pieces
        expert_rows = low_back(padded[slot_source])
        both = low_back(product(expert_rows, weight_in))
        hidden = low(jax.nn.silu(both[:, :FF]) * both[:, FF:])
        result = wire_round(product(hidden, weight_out))
        return (total.at[slot_source].add(gate_slot[:, None] * result), None)
    total, ignored = lax.scan(jax.checkpoint(expert), jnp.zeros((TOKENS + 1, D), jnp.float32), (source, slot_gate, w_in, w_out))
    return middle + BRANCH_SCALE * total[:TOKENS]

def reference(tokens, cotangent, positions, lengths, routes, logits, w_query, w_key, w_value, w_output, gain_attn, gain_ffn, w_in, w_out):
    segment, place = jax.vmap(local_places)(positions, lengths)
    place_tokens = from_groups(place)
    gates = jax.nn.softmax(logits.astype(jnp.float32), axis=-1)
    source, slot_gate = dispatch_tables(routes, gates)

    def layer(inputs, wq, wk, wv, wo, ga, gf, wi, wu):
        return forward(inputs, wq, wk, wv, wo, ga, gf, wi, wu, segment, place, place_tokens, source, slot_gate)
    floats = [value.astype(jnp.float32) for value in (tokens, w_query, w_key, w_value, w_output, gain_attn, gain_ffn, w_in, w_out)]
    result, pullback = jax.vjp(layer, *floats)
    grads = pullback(cotangent.astype(jnp.float32))
    return (result.astype(jnp.bfloat16), grads[0], grads[1], grads[2], grads[3], grads[4], grads[5], grads[6], grads[7], grads[8])
```

```python
import jax
import jax.numpy as jnp
from jax import lax
from jax.experimental import pallas as pl
from jax.experimental.pallas import tpu as pltpu
from jax.sharding import PartitionSpec as P

QHEADS = 24
KVHEADS = 8
HDIM = 64
FF = 512
TOP = 8


EPSILON = 1e-06
BRANCH_SCALE = 0.22
SCORE_SCALE = 1.0 / 64.0
THETA = 10000.0


def rms_norm(value, gain):
    return value * lax.rsqrt(jnp.mean(value * value, axis=-1, keepdims=True) + EPSILON) * gain


def local_places(placing, seq_lengths):
    ends = jnp.cumsum(seq_lengths)
    segment = jnp.sum((placing[:, None] >= ends[None, :]).astype(jnp.int32), axis=1)
    starts = ends - seq_lengths
    member = segment[:, None] == jnp.arange(seq_lengths.shape[0], dtype=jnp.int32)[None, :]
    start_of = jnp.sum(jnp.where(member, starts[None, :], 0), axis=1)
    return (segment, placing - start_of)


def rotate(values, place, direction):
    half = values.shape[-1] // 2
    freqs = jnp.power(THETA, -jnp.arange(half, dtype=jnp.float32) * 2.0 / values.shape[-1])
    angles = place.astype(jnp.float32)[:, None] * freqs[None, :]
    cosine = jnp.cos(angles)[:, None, :]
    sine = direction * jnp.sin(angles)[:, None, :]
    first = values[..., :half]
    second = values[..., half:]
    return jnp.concatenate(
        [first * cosine - second * sine, second * cosine + first * sine], axis=-1
    )


def shards_general(
    tokens,
    cotangent,
    positions,
    lengths,
    routes,
    logits,
    w_query,
    w_key,
    w_value,
    w_output,
    gain_attn,
    gain_ffn,
    w_in,
    w_out,
):
    seq_count = lax.axis_size("seq")
    data_count = lax.axis_size("dp")
    tok_count = tokens.shape[0]
    group_len = positions.shape[1]
    local_experts = w_in.shape[0]
    experts_all = local_experts * data_count
    capacity = min(tok_count, 5 * tok_count * TOP // (4 * experts_all))
    heads_local = QHEADS // seq_count
    kv_local = KVHEADS // seq_count
    ratio = QHEADS // KVHEADS
    width = tokens.shape[1]
    query_full, key_full, value_full, output_full, gain_one, gain_two = (
        lax.all_gather(w_query, ("seq", "dp"), axis=0, tiled=True),
        lax.all_gather(w_key, ("seq", "dp"), axis=0, tiled=True),
        lax.all_gather(w_value, ("seq", "dp"), axis=0, tiled=True),
        lax.all_gather(w_output, ("seq", "dp"), axis=0, tiled=True),
        lax.all_gather(gain_attn, ("seq", "dp"), axis=0, tiled=True),
        lax.all_gather(gain_ffn, ("seq", "dp"), axis=0, tiled=True),
    )
    in_full, out_full = (
        lax.all_gather(w_in, "seq", axis=2, tiled=True),
        lax.all_gather(w_out, "seq", axis=1, tiled=True),
    )
    gain_one = gain_one.astype(jnp.float32)
    gain_two = gain_two.astype(jnp.float32)
    segment, place = local_places(positions[0], lengths[0])
    my_start = lax.axis_index("seq") * tok_count
    my_place = lax.dynamic_slice_in_dim(place, my_start, tok_count)
    inputs = tokens.astype(jnp.float32)
    normed = rms_norm(inputs, gain_one).astype(jnp.bfloat16)
    query_pre = jnp.dot(normed, query_full, preferred_element_type=jnp.float32)
    key_pre = jnp.dot(normed, key_full, preferred_element_type=jnp.float32)
    query_rot = (
        rotate(query_pre.reshape(tok_count, QHEADS, HDIM), my_place, 1.0)
        .reshape(tok_count, QHEADS * HDIM)
        .astype(jnp.bfloat16)
    )
    key_rot = (
        rotate(key_pre.reshape(tok_count, KVHEADS, HDIM), my_place, 1.0)
        .reshape(tok_count, KVHEADS * HDIM)
        .astype(jnp.bfloat16)
    )
    value_low = jnp.dot(normed, value_full, preferred_element_type=jnp.float32).astype(jnp.bfloat16)
    query_heads, key_heads, value_heads = (
        lax.all_to_all(query_rot, "seq", split_axis=1, concat_axis=0, tiled=True),
        lax.all_to_all(key_rot, "seq", split_axis=1, concat_axis=0, tiled=True),
        lax.all_to_all(value_low, "seq", split_axis=1, concat_axis=0, tiled=True),
    )
    keys_three = key_heads.reshape(group_len, kv_local, HDIM)
    values_three = value_heads.reshape(group_len, kv_local, HDIM)
    length = min(512, group_len)
    count = group_len // length

    def scores_of(query_block, seg_block, place_block):
        grouped = query_block.reshape(length, kv_local, ratio, HDIM)
        raw_scores = (
            jnp.einsum("qgrd,kgd->grqk", grouped, keys_three, preferred_element_type=jnp.float32)
            * SCORE_SCALE
        )
        allowed = (seg_block[:, None] == segment[None, :]) & (
            place[None, :] <= place_block[:, None]
        )
        return jnp.where(allowed[None, None], raw_scores, -1e30)

    def forward_block(pieces):
        query_block, seg_block, place_block = pieces
        scores = scores_of(query_block, seg_block, place_block)
        highest = jnp.max(scores, axis=-1, keepdims=True)
        expon = jnp.exp(scores - highest)
        totals = jnp.sum(expon, axis=-1, keepdims=True)
        probs = expon / totals
        mixed = jnp.einsum(
            "grqk,kgd->qgrd",
            probs.astype(jnp.bfloat16),
            values_three,
            preferred_element_type=jnp.float32,
        )
        return (
            mixed.reshape(length, heads_local * HDIM).astype(jnp.bfloat16),
            highest + jnp.log(totals),
            probs,
        )

    query_blocks = query_heads.reshape(count, length, heads_local * HDIM)
    seg_blocks = segment.reshape(count, length)
    place_blocks = place.reshape(count, length)
    block_args = (query_blocks, seg_blocks, place_blocks)

    def forward_light(pieces):
        mixed, lse_part, unused_probs = forward_block(pieces)
        return (mixed, lse_part)

    mixed_blocks, lse_blocks = lax.map(forward_light, block_args)
    mixed_heads = mixed_blocks.reshape(group_len, heads_local * HDIM)
    mixed_tokens = lax.all_to_all(mixed_heads, "seq", split_axis=0, concat_axis=1, tiled=True)
    attn = jnp.dot(mixed_tokens, output_full, preferred_element_type=jnp.float32)
    middle = inputs + BRANCH_SCALE * attn
    normed_ffn = rms_norm(middle, gain_two).astype(jnp.bfloat16)
    chosen = routes.reshape(-1)
    onehot = (chosen[:, None] == jnp.arange(experts_all, dtype=jnp.int32)[None, :]).astype(
        jnp.int32
    )
    ranking = jnp.sum(jnp.cumsum(onehot, axis=0) * onehot, axis=1) - 1
    target = chosen * capacity + ranking
    token_of = jnp.arange(tok_count * TOP, dtype=jnp.int32) // TOP
    gates = jax.nn.softmax(logits, axis=-1)
    source = jnp.full((experts_all * capacity,), tok_count, jnp.int32).at[target].set(token_of)
    slot_gate = jnp.zeros((experts_all * capacity,), jnp.float32).at[target].set(gates.reshape(-1))
    padded = jnp.concatenate([normed_ffn, jnp.zeros((1, width), jnp.bfloat16)], axis=0)
    outgoing = padded[source].reshape(data_count, local_experts * capacity, width)

    def expert_layout(arrived):
        return jnp.swapaxes(
            arrived.reshape(data_count, local_experts, capacity, width), 0, 1
        ).reshape(local_experts, data_count * capacity, width)

    def home_layout(values):
        return jnp.swapaxes(
            values.reshape(local_experts, data_count, capacity, width), 0, 1
        ).reshape(data_count, local_experts * capacity, width)

    def expert_forward(expert_rows):
        both = jnp.einsum("erd,edf->erf", expert_rows, in_full, preferred_element_type=jnp.float32)
        hidden = (jax.nn.silu(both[..., :FF]) * both[..., FF:]).astype(jnp.bfloat16)
        return (both, hidden)

    expert_rows = expert_layout(
        lax.all_to_all(outgoing, "dp", split_axis=0, concat_axis=0, tiled=True)
    )
    both, hidden = expert_forward(expert_rows)
    result = jnp.einsum(
        "erf,efd->erd", hidden, out_full, preferred_element_type=jnp.float32
    ).astype(jnp.bfloat16)
    returned = lax.all_to_all(
        home_layout(result), "dp", split_axis=0, concat_axis=0, tiled=True
    ).reshape(experts_all * capacity, width)
    picked = returned[target].reshape(tok_count, TOP, width).astype(jnp.float32)
    ffn = jnp.sum(picked * gates[:, :, None], axis=1)
    final = middle + BRANCH_SCALE * ffn
    output = final.astype(jnp.bfloat16)
    grad_final = cotangent.astype(jnp.float32)
    padded_grad = jnp.concatenate(
        [BRANCH_SCALE * grad_final, jnp.zeros((1, width), jnp.float32)], axis=0
    )
    grad_slots = (slot_gate[:, None] * padded_grad[source]).astype(jnp.bfloat16)
    grad_result = expert_layout(
        lax.all_to_all(
            grad_slots.reshape(data_count, local_experts * capacity, width),
            "dp",
            split_axis=0,
            concat_axis=0,
            tiled=True,
        )
    )
    rows_back = expert_layout(
        lax.all_to_all(outgoing, "dp", split_axis=0, concat_axis=0, tiled=True)
    )
    both_back, hidden_back = expert_forward(rows_back)
    grad_hidden = jnp.einsum(
        "erd,efd->erf", grad_result, out_full, preferred_element_type=jnp.float32
    )
    gate_part = both_back[..., :FF]
    up_part = both_back[..., FF:]
    sigma = jax.nn.sigmoid(gate_part)
    grad_gate = grad_hidden * up_part * sigma * (1.0 + gate_part * (1.0 - sigma))
    grad_up = grad_hidden * gate_part * sigma
    grad_both = jnp.concatenate([grad_gate, grad_up], axis=-1).astype(jnp.bfloat16)
    grad_out_local = jnp.einsum(
        "erf,erd->efd", hidden_back, grad_result, preferred_element_type=jnp.float32
    )
    grad_in_local = jnp.einsum(
        "erd,erf->edf", rows_back, grad_both, preferred_element_type=jnp.float32
    )
    grad_rows = jnp.einsum(
        "erf,edf->erd", grad_both, in_full, preferred_element_type=jnp.float32
    ).astype(jnp.bfloat16)
    grad_home = lax.all_to_all(
        home_layout(grad_rows), "dp", split_axis=0, concat_axis=0, tiled=True
    ).reshape(experts_all * capacity, width)
    grad_normed_ffn = jnp.sum(
        grad_home[target].reshape(tok_count, TOP, width).astype(jnp.float32), axis=1
    )
    grad_w_in, grad_w_out = (
        lax.psum_scatter(
            grad_in_local.astype(jnp.bfloat16), "seq", scatter_dimension=2, tiled=True
        ).astype(jnp.float32),
        lax.psum_scatter(
            grad_out_local.astype(jnp.bfloat16), "seq", scatter_dimension=1, tiled=True
        ).astype(jnp.float32),
    )
    unused_norm, norm_pull = jax.vjp(rms_norm, middle, gain_two)
    grad_middle_norm, grad_gain_two = norm_pull(grad_normed_ffn)
    grad_middle = grad_final + grad_middle_norm
    grad_attn = (BRANCH_SCALE * grad_middle).astype(jnp.bfloat16)
    grad_w_output = jnp.einsum(
        "te,td->ed", mixed_tokens, grad_attn, preferred_element_type=jnp.float32
    )
    grad_mixed = jnp.einsum(
        "td,ed->te", grad_attn, output_full, preferred_element_type=jnp.float32
    ).astype(jnp.bfloat16)
    grad_mixed_heads = lax.all_to_all(grad_mixed, "seq", split_axis=1, concat_axis=0, tiled=True)
    grad_blocks = grad_mixed_heads.reshape(count, length, heads_local * HDIM)
    back_args = (query_blocks, seg_blocks, place_blocks, lse_blocks, grad_blocks)

    def backward_block(carry, pieces):
        grad_keys, grad_values = carry
        query_block, seg_block, place_block, lse_block, grad_block = pieces[:5]
        probs = jnp.exp(scores_of(query_block, seg_block, place_block) - lse_block)
        grad_out = grad_block.reshape(length, kv_local, ratio, HDIM)
        grad_probs = jnp.einsum(
            "qgrd,kgd->grqk", grad_out, values_three, preferred_element_type=jnp.float32
        )
        grad_scores = (
            probs * (grad_probs - jnp.sum(probs * grad_probs, axis=-1, keepdims=True))
        ).astype(jnp.bfloat16)
        grad_query = SCORE_SCALE * jnp.einsum(
            "grqk,kgd->qgrd", grad_scores, keys_three, preferred_element_type=jnp.float32
        )
        grouped = query_block.reshape(length, kv_local, ratio, HDIM)
        grad_keys = grad_keys + SCORE_SCALE * jnp.einsum(
            "grqk,qgrd->kgd", grad_scores, grouped, preferred_element_type=jnp.float32
        )
        grad_values = grad_values + jnp.einsum(
            "grqk,qgrd->kgd",
            probs.astype(jnp.bfloat16),
            grad_out,
            preferred_element_type=jnp.float32,
        )
        return (
            (grad_keys, grad_values),
            grad_query.reshape(length, heads_local * HDIM).astype(jnp.bfloat16),
        )

    empty_keys = jnp.zeros((group_len, kv_local, HDIM), jnp.float32)
    (grad_keys, grad_values), grad_query_blocks = lax.scan(
        backward_block, (empty_keys, empty_keys), back_args
    )
    grad_query_heads = grad_query_blocks.reshape(group_len, heads_local * HDIM)
    grad_key_heads = grad_keys.reshape(group_len, kv_local * HDIM).astype(jnp.bfloat16)
    grad_value_heads = grad_values.reshape(group_len, kv_local * HDIM).astype(jnp.bfloat16)
    grad_query_tok, grad_key_tok, grad_value_tok = (
        lax.all_to_all(grad_query_heads, "seq", split_axis=0, concat_axis=1, tiled=True),
        lax.all_to_all(grad_key_heads, "seq", split_axis=0, concat_axis=1, tiled=True),
        lax.all_to_all(grad_value_heads, "seq", split_axis=0, concat_axis=1, tiled=True),
    )
    grad_query_pre = (
        rotate(grad_query_tok.astype(jnp.float32).reshape(tok_count, QHEADS, HDIM), my_place, -1.0)
        .reshape(tok_count, QHEADS * HDIM)
        .astype(jnp.bfloat16)
    )
    grad_key_pre = (
        rotate(grad_key_tok.astype(jnp.float32).reshape(tok_count, KVHEADS, HDIM), my_place, -1.0)
        .reshape(tok_count, KVHEADS * HDIM)
        .astype(jnp.bfloat16)
    )
    grad_w_query = jnp.einsum(
        "td,te->de", normed, grad_query_pre, preferred_element_type=jnp.float32
    )
    grad_w_key = jnp.einsum("td,te->de", normed, grad_key_pre, preferred_element_type=jnp.float32)
    grad_w_value = jnp.einsum(
        "td,te->de", normed, grad_value_tok, preferred_element_type=jnp.float32
    )
    grad_normed = jnp.einsum(
        "te,de->td", grad_query_pre, query_full, preferred_element_type=jnp.float32
    )
    grad_normed = grad_normed + jnp.einsum(
        "te,de->td", grad_key_pre, key_full, preferred_element_type=jnp.float32
    )
    grad_normed = grad_normed + jnp.einsum(
        "te,de->td", grad_value_tok, value_full, preferred_element_type=jnp.float32
    )
    unused_first, first_pull = jax.vjp(rms_norm, inputs, gain_one)
    grad_inputs_norm, grad_gain_one = first_pull(grad_normed)
    grad_tokens = grad_middle + grad_inputs_norm
    summed = (
        lax.psum_scatter(grad_w_query, ("seq", "dp"), scatter_dimension=0, tiled=True),
        lax.psum_scatter(grad_w_key, ("seq", "dp"), scatter_dimension=0, tiled=True),
        lax.psum_scatter(grad_w_value, ("seq", "dp"), scatter_dimension=0, tiled=True),
        lax.psum_scatter(grad_w_output, ("seq", "dp"), scatter_dimension=0, tiled=True),
        lax.psum_scatter(grad_gain_one, ("seq", "dp"), scatter_dimension=0, tiled=True),
        lax.psum_scatter(grad_gain_two, ("seq", "dp"), scatter_dimension=0, tiled=True),
    )
    return (
        output,
        grad_tokens,
        summed[0],
        summed[1],
        summed[2],
        summed[3],
        summed[4],
        summed[5],
        grad_w_in,
        grad_w_out,
    )


BF16 = jnp.bfloat16
F32 = jnp.float32
LINE = 4
VMEM_BYTES = 60 * 1024 * 1024


def in_planes(mesh):
    return mesh.shape["seq"] == 2 and mesh.shape["dp"] == 4 * LINE


def swap_seq(value):
    return lax.ppermute(value, "seq", [(0, 1), (1, 0)])


def swap_dp(value, mask):
    return lax.ppermute(value, "dp", [(i, i ^ mask) for i in range(4 * LINE)])


def swap_core(value):
    return swap_dp(value, 1)


def swap_y(value):
    return swap_dp(value, 2)


def line_up(value):
    return lax.ppermute(value, "dp", [(i, i + 4) for i in range(4 * LINE - 4)])


def line_down(value):
    return lax.ppermute(value, "dp", [(i, i - 4) for i in range(4, 4 * LINE)])


def sum_everywhere(value):
    for mask in (1, 2, 4, 8):
        value = value + swap_dp(value, mask)
    return value + swap_seq(value)


def line_gather(own):
    ups, downs = [own], [own]
    for _ in range(LINE - 1):
        ups.append(line_up(ups[-1]))
        downs.append(line_down(downs[-1]))
    return ups[:0:-1] + [own] + downs[1:]


def line_scatter(take, place):
    up = down = None
    for step in range(LINE - 1):
        far = jnp.minimum(LINE - 1 - step + place, LINE - 1)
        near = jnp.maximum(step - LINE + 1 + place, 0)
        right, left = take(far), take(near)
        if up is not None:
            right = right + up.astype(F32)
            left = left + down.astype(F32)
        up = line_up(right.astype(BF16))
        down = line_down(left.astype(BF16))
    return take(place) + up.astype(F32) + down.astype(F32)


def plane_gather(value, axis):
    half = value.shape[axis] // 2
    first = lax.slice_in_dim(value, 0, half, axis=axis)
    second = lax.slice_in_dim(value, half, 2 * half, axis=axis)

    def join(*pieces):
        return lax.concatenate(pieces, axis)

    first_near = swap_seq(first)
    second_near = swap_y(second)
    near = join(first_near, second_near)
    far = join(
        swap_y(first), swap_y(first_near), swap_seq(second), swap_seq(second_near)
    )
    return [
        join(value, swap_core(value)),
        join(near, swap_core(near)),
        join(far, swap_core(far)),
    ]


def plane_scatter(pieces):
    def over_cores(piece):
        half = piece.shape[0] // 2
        return piece[:half].astype(F32) + swap_core(piece[half:]).astype(F32)

    far = over_cores(pieces[2]).astype(BF16)
    near = over_cores(pieces[1])
    own = over_cores(pieces[0])
    half = own.shape[0] // 2
    own_first = own[:half] + swap_y(far[:half]).astype(F32)
    near_first = near[:half] + swap_y(far[half : 2 * half]).astype(F32)
    own_second = own[half:] + swap_seq(far[2 * half : 3 * half]).astype(F32)
    near_second = near[half:] + swap_seq(far[3 * half :]).astype(F32)
    own_first = own_first + swap_seq(near_first.astype(BF16)).astype(F32)
    own_second = own_second + swap_y(near_second.astype(BF16)).astype(F32)
    return jnp.concatenate([own_first, own_second], axis=0)


def turned(values, cos, sin, direction):
    lanes = values.shape[1]
    place = lax.broadcasted_iota(jnp.int32, values.shape, 1) % HDIM
    swapped = jnp.where(
        place < HDIM // 2,
        pltpu.roll(values, lanes - HDIM // 2, 1),
        pltpu.roll(values, HDIM // 2, 1),
    )
    times = lanes // cos.shape[1]
    cos = jnp.concatenate([cos] * times, axis=1)
    sin = jnp.concatenate([sin] * times, axis=1)
    if direction > 0:
        return values * cos + swapped * sin
    return values * cos - swapped * sin


def qkv_kernel(x_ref, gain_ref, w_ref, cos_ref, sin_ref, h_ref, q_ref, k_ref, v_ref):
    value = x_ref[...].astype(F32)
    scale = lax.rsqrt(jnp.mean(value * value, axis=-1, keepdims=True) + EPSILON)
    normed = (value * scale * gain_ref[...]).astype(BF16)
    h_ref[...] = normed
    both = jnp.dot(normed, w_ref[...], preferred_element_type=F32)
    q_width, kv_heads = q_ref.shape[1], k_ref.shape[0]
    kv_width = kv_heads * HDIM
    spun = turned(both[:, : q_width + kv_width], cos_ref[...], sin_ref[...], 1)
    q_ref[...] = (spun[:, :q_width] * SCORE_SCALE).astype(BF16)
    for head in range(kv_heads):
        low = q_width + head * HDIM
        k_ref[head] = spun[:, low : low + HDIM].astype(BF16)
        low = low + kv_width
        v_ref[head] = both[:, low : low + HDIM].astype(BF16)


def project(x_sorted, gain, weights, cos, sin, q_width, kv_heads):
    rows, width = x_sorted.shape
    tile = 256
    columns = weights.shape[1]

    def row_block(lanes):
        return pl.BlockSpec((tile, lanes), lambda i: (i, 0))

    heads = pl.BlockSpec((kv_heads, tile, HDIM), lambda i: (0, i, 0))
    return pl.pallas_call(
        qkv_kernel,
        grid=(rows // tile,),
        in_specs=[
            row_block(width),
            pl.BlockSpec((1, width), lambda i: (0, 0)),
            pl.BlockSpec((width, columns), lambda i: (0, 0)),
            row_block(cos.shape[1]),
            row_block(cos.shape[1]),
        ],
        out_specs=[row_block(width), row_block(q_width), heads, heads],
        out_shape=[
            jax.ShapeDtypeStruct((rows, width), BF16),
            jax.ShapeDtypeStruct((rows, q_width), BF16),
            jax.ShapeDtypeStruct((kv_heads, rows, HDIM), BF16),
            jax.ShapeDtypeStruct((kv_heads, rows, HDIM), BF16),
        ],
        compiler_params=pltpu.CompilerParams(vmem_limit_bytes=VMEM_BYTES),
        cost_estimate=pl.CostEstimate(
            flops=2 * rows * width * columns,
            bytes_accessed=2 * (2 * rows * width + width * columns + rows * columns),
            transcendentals=rows,
        ),
        name="project",
    )(x_sorted, gain, weights, cos, sin)


Q_TILE = 256


def windows(rows):
    longest = rows // 2
    for start in range(0, rows, Q_TILE):
        low = max(0, start - longest + 1) // Q_TILE * Q_TILE
        yield start, low, start + Q_TILE


def allowed_keys(start_ref, row, low, high):
    shape = (Q_TILE, high - low)
    rows = lax.broadcasted_iota(jnp.int32, shape, 0) + row
    keys = lax.broadcasted_iota(jnp.int32, shape, 1) + low
    return (keys <= rows) & (keys >= start_ref[row : row + Q_TILE, :])


def contract(left, right, left_dim, right_dim):
    return lax.dot_general(
        left, right, (((left_dim,), (right_dim,)), ((), ())), preferred_element_type=F32
    )


def probabilities(query, keys, allowed):
    scores = jnp.where(allowed, contract(query, keys, 1, 1), -1e30)
    expon = jnp.exp(scores - jnp.max(scores, axis=-1, keepdims=True))
    return expon * (1.0 / jnp.sum(expon, axis=-1, keepdims=True))


def attend_kernel(q_ref, k_ref, v_ref, start_ref, o_ref):
    pair = pl.program_id(0)
    ratio = QHEADS // KVHEADS
    for row, low, high in windows(q_ref.shape[0]):
        allowed = allowed_keys(start_ref, row, low, high)
        for side in range(2):
            head = (2 * pair + side) // ratio
            lanes = slice(side * HDIM, (side + 1) * HDIM)
            probs = probabilities(
                q_ref[row : row + Q_TILE, lanes], k_ref[head, low:high, :], allowed
            )
            mixed = contract(probs.astype(BF16), v_ref[head, low:high, :], 1, 0)
            o_ref[row : row + Q_TILE, lanes] = mixed.astype(BF16)


def attention_cost(rows, heads, products):
    area = sum(Q_TILE * (high - low) for _, low, high in windows(rows))
    return pl.CostEstimate(
        flops=2 * products * heads * area * 128,
        bytes_accessed=8 * rows * heads * HDIM,
        transcendentals=heads * area,
    )


def attend(query, keys, values, starts):
    rows, lanes = query.shape
    pairs = lanes // (2 * HDIM)
    pair_block = pl.BlockSpec((rows, 2 * HDIM), lambda j: (0, j))
    whole = pl.BlockSpec(keys.shape, lambda j: (0, 0, 0))
    return pl.pallas_call(
        attend_kernel,
        grid=(pairs,),
        in_specs=[pair_block, whole, whole, pl.BlockSpec((rows, 1), lambda j: (0, 0))],
        out_specs=pair_block,
        out_shape=jax.ShapeDtypeStruct(query.shape, BF16),
        compiler_params=pltpu.CompilerParams(vmem_limit_bytes=VMEM_BYTES),
        cost_estimate=attention_cost(rows, 2 * pairs, 2),
        name="attend",
    )(query, keys, values, starts)


def attend_back_kernel(
    q_ref, k_ref, v_ref, d_ref, start_ref, cos_ref, sin_ref,
    dq_ref, dk_ref, dv_ref, dk_sum, dv_sum,
):
    pair = pl.program_id(0)
    ratio = QHEADS // KVHEADS

    @pl.when(pair == 0)
    def _():
        dk_sum[...] = jnp.zeros_like(dk_sum)
        dv_sum[...] = jnp.zeros_like(dv_sum)

    for row, low, high in windows(q_ref.shape[0]):
        allowed = allowed_keys(start_ref, row, low, high)
        grads = []
        for side in range(2):
            head = (2 * pair + side) // ratio
            lanes = slice(side * HDIM, (side + 1) * HDIM)
            query = q_ref[row : row + Q_TILE, lanes]
            keys = k_ref[head, low:high, :]
            probs = probabilities(query, keys, allowed)
            grad_out = d_ref[row : row + Q_TILE, lanes]
            grad_probs = contract(grad_out, v_ref[head, low:high, :], 1, 1)
            inner = jnp.sum(probs * grad_probs, axis=-1, keepdims=True)
            grad_scores = (probs * (grad_probs - inner)).astype(BF16)
            grads.append(contract(grad_scores, keys, 1, 0) * SCORE_SCALE)
            dk_sum[head, low:high, :] += contract(grad_scores, query, 0, 0)
            dv_sum[head, low:high, :] += contract(probs.astype(BF16), grad_out, 0, 0)
        grad_query = jnp.concatenate(grads, axis=1).astype(BF16).astype(F32)
        dq_ref[row : row + Q_TILE, :] = turned(
            grad_query,
            cos_ref[row : row + Q_TILE, :],
            sin_ref[row : row + Q_TILE, :],
            -1,
        ).astype(BF16)

    @pl.when(pair == pl.num_programs(0) - 1)
    def _():
        heads = range(dk_sum.shape[0])
        grad_keys = jnp.concatenate([dk_sum[head] for head in heads], axis=1)
        grad_keys = grad_keys.astype(BF16).astype(F32)
        dk_ref[...] = turned(grad_keys, cos_ref[...], sin_ref[...], -1).astype(BF16)
        dv_ref[...] = jnp.concatenate([dv_sum[head] for head in heads], axis=1).astype(BF16)


def attend_back(query, keys, values, grad_out, starts, cos, sin):
    rows, lanes = query.shape
    pairs = lanes // (2 * HDIM)
    kv_heads = keys.shape[0]
    pair_block = pl.BlockSpec((rows, 2 * HDIM), lambda j: (0, j))
    whole = pl.BlockSpec(keys.shape, lambda j: (0, 0, 0))

    def fixed(lanes_of):
        return pl.BlockSpec((rows, lanes_of), lambda j: (0, 0))

    flat = kv_heads * HDIM
    return pl.pallas_call(
        attend_back_kernel,
        grid=(pairs,),
        in_specs=[
            pair_block, whole, whole, pair_block, fixed(1), fixed(2 * HDIM), fixed(2 * HDIM),
        ],
        out_specs=[pair_block, fixed(flat), fixed(flat)],
        out_shape=[
            jax.ShapeDtypeStruct(query.shape, BF16),
            jax.ShapeDtypeStruct((rows, flat), BF16),
            jax.ShapeDtypeStruct((rows, flat), BF16),
        ],
        scratch_shapes=[pltpu.VMEM(keys.shape, F32), pltpu.VMEM(keys.shape, F32)],
        compiler_params=pltpu.CompilerParams(vmem_limit_bytes=VMEM_BYTES),
        cost_estimate=attention_cost(rows, 2 * pairs, 5),
        name="attend_back",
    )(query, keys, values, grad_out, starts, cos, sin)


SLOTS = 2 * LINE - 1
MOE_TILE = 512


def experts_kernel(place_ref, *refs):
    h_ref, g_ref, gate_ref = refs[:3]
    in_slots, out_slots = refs[3 : 3 + SLOTS], refs[3 + SLOTS : 3 + 2 * SLOTS]
    (
        f_ref, dh_ref, hidden_ref, du_ref, hcopy_ref, gcopy_ref, w_in, w_out, sems,
    ) = refs[-9:]
    part = in_slots[0].shape[1]
    half = part // 2

    def copies(expert, slot):
        return (
            pltpu.make_async_copy(
                in_slots[slot],
                w_in.at[:, expert * part : (expert + 1) * part],
                sems.at[0, expert],
            ),
            pltpu.make_async_copy(
                out_slots[slot],
                w_out.at[expert * half : (expert + 1) * half, :],
                sems.at[1, expert],
            ),
        )

    @pl.when(pl.program_id(0) == 0)
    def _():
        for expert in range(LINE):
            for slot in range(expert, expert + LINE):

                @pl.when(slot == LINE - 1 + expert - place_ref[0])
                def _():
                    for copy in copies(expert, slot):
                        copy.start()

        for expert in range(LINE):
            for copy in copies(expert, LINE - 1):
                copy.wait()

    rows = h_ref[...]
    grads = g_ref[...]
    hcopy_ref[...] = rows
    gcopy_ref[...] = grads
    for expert in range(LINE):
        both = jnp.dot(
            rows, w_in[:, expert * part : (expert + 1) * part], preferred_element_type=F32
        )
        back = contract(grads, w_out[expert * half : (expert + 1) * half, :], 1, 1)
        gate = gate_ref[:, expert : expert + 1]
        first, second = both[:, :half], both[:, half:]
        sigma = jax.nn.sigmoid(first)
        silu = first * sigma
        hidden_ref[:, expert * half : (expert + 1) * half] = (gate * (silu * second)).astype(BF16)
        back = back * (BRANCH_SCALE * gate)
        d_first = back * second * (sigma * (1.0 + first * (1.0 - sigma)))
        d_second = back * silu
        du_ref[:, expert * part : expert * part + half] = d_first.astype(BF16)
        du_ref[:, expert * part + half : (expert + 1) * part] = d_second.astype(BF16)
    f_ref[...] = jnp.dot(hidden_ref[...], w_out[...], preferred_element_type=F32).astype(BF16)
    dh_ref[...] = contract(du_ref[...], w_in[...], 1, 1).astype(BF16)


def run_experts(place, rows, grads, gates, in_slots, out_slots, total, offset, kept):
    count, width = rows.shape
    part, half = in_slots[0].shape[1], out_slots[0].shape[0]
    tile = MOE_TILE
    base = offset // tile

    def block(lanes):
        return pl.BlockSpec((tile, lanes), lambda i, p: (i, 0))

    def late(lanes):
        return pl.BlockSpec((tile, lanes), lambda i, p: (i + base, 0))

    anywhere = pl.BlockSpec(memory_space=pl.ANY)
    kept = list(kept)
    lead = 4 + 2 * SLOTS
    return pl.pallas_call(
        experts_kernel,
        grid_spec=pltpu.PrefetchScalarGridSpec(
            num_scalar_prefetch=1,
            grid=(count // tile,),
            in_specs=[block(width), block(width), block(LINE)]
            + [anywhere] * (2 * SLOTS + len(kept)),
            out_specs=[
                block(width), block(width),
                late(LINE * half), late(LINE * part), late(width), late(width),
            ],
            scratch_shapes=[
                pltpu.VMEM((width, LINE * part), BF16),
                pltpu.VMEM((LINE * half, width), BF16),
                pltpu.SemaphoreType.DMA((2, LINE)),
            ],
        ),
        out_shape=[
            jax.ShapeDtypeStruct((count, width), BF16),
            jax.ShapeDtypeStruct((count, width), BF16),
            jax.ShapeDtypeStruct((total, LINE * half), BF16),
            jax.ShapeDtypeStruct((total, LINE * part), BF16),
            jax.ShapeDtypeStruct((total, width), BF16),
            jax.ShapeDtypeStruct((total, width), BF16),
        ],
        input_output_aliases={lead + i: 2 + i for i in range(len(kept))},
        compiler_params=pltpu.CompilerParams(vmem_limit_bytes=VMEM_BYTES),
        cost_estimate=pl.CostEstimate(
            flops=2 * count * width * LINE * (2 * part + 2 * half),
            bytes_accessed=2 * count * (6 * width + LINE * (part + half)),
            transcendentals=count * LINE * half,
        ),
        name="experts",
    )(place, rows, grads, gates, *in_slots, *out_slots, *kept)


def norm_back(value, gain, grad):
    scale = lax.rsqrt(jnp.mean(value * value, axis=-1, keepdims=True) + EPSILON)
    unit = value * scale
    grad_gain = jnp.sum(grad * unit, axis=0)
    scaled = grad * gain
    inner = jnp.mean(scaled * unit, axis=-1, keepdims=True)
    return scale * (scaled - unit * inner), grad_gain


def shards_plane(
    tokens,
    cotangent,
    positions,
    lengths,
    routes,
    logits,
    w_query,
    w_key,
    w_value,
    w_output,
    gain_attn,
    gain_ffn,
    w_in,
    w_out,
):
    seq = lax.axis_index("seq")
    data = lax.axis_index("dp")
    line, row_of, core = data // 4, (data // 2) % 2, data % 2
    tok_count, width = tokens.shape
    group_len = positions.shape[1]
    shard = w_query.shape[0]
    q_width = w_query.shape[1] // 2
    kv_width = w_key.shape[1] // 2
    kv_heads = kv_width // HDIM
    first_seq = seq == 0

    def ordered(mine, theirs, axis):
        low = jnp.where(first_seq, mine, theirs)
        high = jnp.where(first_seq, theirs, mine)
        return jnp.concatenate([low, high], axis=axis)

    def half_of(weights, which):
        half = weights.shape[1] // 2
        return lax.dynamic_slice_in_dim(weights, which * half, half, axis=1)

    other_tokens = swap_seq(tokens)
    projections = (w_query, w_key, w_value)
    mine = jnp.concatenate([half_of(w, seq) for w in projections], axis=1)
    theirs = jnp.concatenate([half_of(w, 1 - seq) for w in projections], axis=1)
    theirs = swap_seq(theirs)
    pair = jnp.stack([jnp.where(first_seq, mine, theirs), jnp.where(first_seq, theirs, mine)])
    w_qkv = lax.all_gather(pair, "dp", axis=1, tiled=True).reshape(width, q_width + 2 * kv_width)
    output_full = lax.all_gather(w_output, ("seq", "dp"), axis=0, tiled=True)

    gains = jnp.stack([gain_attn, gain_ffn]).astype(F32)
    index = seq * (4 * LINE) + data
    gains = lax.dynamic_update_slice(jnp.zeros((2, width), F32), gains, (0, index * shard))
    gains = sum_everywhere(gains)
    gain_one, gain_two = gains[0], gains[1]

    def both_axes(value, pairs):
        return lax.ppermute(value, ("seq", "dp"), pairs)

    def device(s, d):
        return s * 4 * LINE + d

    straight, crossed = [], []
    for s in range(2):
        for d in range(4 * LINE):
            c = d % 2
            straight.append((device(s, d), device(c, d - c + s)))
            crossed.append((device(s, d), device(c, d - c + 1 - s)))
    crossed_back = [(there, here) for here, there in crossed]
    in_own = w_in[0]
    half = in_own.shape[1] // 2
    same = both_axes(lax.dynamic_slice_in_dim(in_own, seq * half, half, axis=1), straight)
    cross = both_axes(lax.dynamic_slice_in_dim(in_own, (1 - seq) * half, half, axis=1), crossed)
    first_core = core == 0
    in_part = jnp.concatenate(
        [jnp.where(first_core, same, cross), jnp.where(first_core, cross, same)], axis=1
    )
    out_part = both_axes(w_out[0], straight)
    in_slots = line_gather(in_part)
    out_slots = line_gather(out_part)

    grad_pieces = plane_gather(cotangent, 0)
    experts_all = 4 * LINE
    gates = jax.nn.softmax(logits, axis=-1)
    named = routes[None, :, :] == jnp.arange(experts_all, dtype=jnp.int32)[:, None, None]
    gate_table = jnp.sum(jnp.where(named, gates[None], 0.0), axis=2)
    gate_pieces = [
        lax.dynamic_index_in_dim(
            piece.reshape(LINE, 4, piece.shape[1]), 2 * row_of + seq, axis=1, keepdims=False
        ).T
        for piece in plane_gather(gate_table, 1)
    ]

    places = positions[0]
    ends = jnp.cumsum(lengths[0])
    ranks = jnp.arange(group_len, dtype=jnp.int32)
    reached = ranks[:, None] >= ends[None, :]
    starts = jnp.max(jnp.where(reached, ends[None, :], 0), axis=1)
    local = (ranks - starts).astype(F32)
    freqs = jnp.power(THETA, -jnp.arange(HDIM // 2, dtype=F32) * 2.0 / HDIM)
    angles = local[:, None] * freqs[None, :]
    cos, sin = jnp.cos(angles), jnp.sin(angles)
    cos = jnp.concatenate([cos, cos, cos, cos], axis=1)
    sin = jnp.concatenate([-sin, sin, -sin, sin], axis=1)
    start_column = starts[:, None]
    own_places = lax.dynamic_slice_in_dim(places, seq * tok_count, tok_count)
    other_places = lax.dynamic_slice_in_dim(places, (1 - seq) * tok_count, tok_count)
    sort_own = (ranks[:, None] == own_places[None, :]).astype(BF16)
    sort_other = (ranks[:, None] == other_places[None, :]).astype(BF16)

    def to_order(own, other):
        return (
            contract(sort_own, own, 1, 0) + contract(sort_other, other, 1, 0)
        ).astype(BF16)

    def from_order(sort, values):
        return contract(sort, values, 0, 0).astype(BF16)

    x_sorted = to_order(tokens, other_tokens)
    normed, query, keys, values = project(
        x_sorted, gain_one[None, :], w_qkv, cos, sin, q_width, kv_heads
    )
    mixed_sorted = attend(query, keys, values, start_column)
    mixed_other = swap_seq(from_order(sort_other, mixed_sorted))
    mixed = ordered(from_order(sort_own, mixed_sorted), mixed_other, 1)
    inputs = tokens.astype(F32)
    attn = jnp.dot(mixed, output_full, preferred_element_type=F32)
    middle = inputs + BRANCH_SCALE * attn
    normed_ffn = rms_norm(middle, gain_two).astype(BF16)

    row_pieces = plane_gather(normed_ffn, 0)
    total = 8 * tok_count
    place = line.astype(jnp.int32)[None]
    ffn_pieces, back_pieces, kept, offset = [], [], (), 0
    for rows, grads, gate in zip(row_pieces, grad_pieces, gate_pieces):
        result = run_experts(
            place, rows, grads, gate, in_slots, out_slots, total, offset, kept
        )
        ffn_pieces.append(result[0])
        back_pieces.append(result[1])
        kept = tuple(result[2:])
        offset = offset + rows.shape[0]
    hidden, grad_both, all_rows, all_grads = kept

    grad_normed_ffn = plane_scatter(back_pieces)
    grad_in_all = contract(all_rows, grad_both, 0, 0)
    grad_out_all = contract(hidden, all_grads, 0, 0) * BRANCH_SCALE
    ffn = plane_scatter(ffn_pieces)
    output = (middle + BRANCH_SCALE * ffn).astype(BF16)

    grad_final = cotangent.astype(F32)
    grad_norm, grad_gain_two = norm_back(middle, gain_two, grad_normed_ffn)
    grad_middle = grad_final + grad_norm
    grad_attn = (BRANCH_SCALE * grad_middle).astype(BF16)
    grad_mixed = contract(grad_attn, output_full, 1, 1).astype(BF16)
    grad_w_output = contract(mixed, grad_attn, 0, 0)
    grad_other = swap_seq(half_of(grad_mixed, 1 - seq))
    grad_sorted = to_order(half_of(grad_mixed, seq), grad_other)
    grad_query, grad_keys, grad_values = attend_back(
        query, keys, values, grad_sorted, start_column, cos, sin
    )
    grad_qkv = jnp.concatenate([grad_query, grad_keys, grad_values], axis=1)
    grad_w_qkv = contract(normed, grad_qkv, 0, 0)
    grad_normed = contract(grad_qkv, w_qkv, 1, 1).astype(BF16)
    sent_normed = swap_seq(from_order(sort_other, grad_normed))
    grad_normed = from_order(sort_own, grad_normed).astype(F32) + sent_normed.astype(F32)
    grad_first, grad_gain_one = norm_back(inputs, gain_one, grad_normed)
    grad_tokens = grad_middle + grad_first

    def expert_part(grads, size, axis):
        return lambda which: lax.dynamic_slice_in_dim(grads, which * size, size, axis=axis)

    grad_in_part = line_scatter(expert_part(grad_in_all, 2 * half, 1), line).astype(BF16)
    grad_out_part = line_scatter(expert_part(grad_out_all, half, 0), line).astype(BF16)
    grad_w_out = both_axes(grad_out_part, straight)
    same = jnp.where(first_core, grad_in_part[:, :half], grad_in_part[:, half:])
    cross = jnp.where(first_core, grad_in_part[:, half:], grad_in_part[:, :half])
    grad_w_in = ordered(both_axes(same, straight), both_axes(cross, crossed_back), 1)

    summed_output = lax.psum_scatter(
        grad_w_output.astype(BF16), ("seq", "dp"), scatter_dimension=0, tiled=True
    )
    summed_qkv = lax.psum_scatter(
        grad_w_qkv.astype(BF16).reshape(2, width // 2, q_width + 2 * kv_width),
        "dp",
        scatter_dimension=1,
        tiled=True,
    )
    kept_rows = lax.dynamic_index_in_dim(summed_qkv, seq, axis=0, keepdims=False)
    sent_rows = swap_seq(lax.dynamic_index_in_dim(summed_qkv, 1 - seq, axis=0, keepdims=False))
    cuts = (q_width, q_width + kv_width)
    grad_projections = [
        ordered(a, b, 1).astype(F32)
        for a, b in zip(jnp.split(kept_rows, cuts, axis=1), jnp.split(sent_rows, cuts, axis=1))
    ]
    grad_gains = sum_everywhere(jnp.stack([grad_gain_one, grad_gain_two]))
    grad_gains = lax.dynamic_slice_in_dim(grad_gains, index * shard, shard, axis=1)
    return (
        output,
        grad_tokens,
        grad_projections[0],
        grad_projections[1],
        grad_projections[2],
        summed_output.astype(F32),
        grad_gains[0],
        grad_gains[1],
        grad_w_in.astype(F32)[None],
        grad_w_out.astype(F32)[None],
    )


def solution(mesh):
    placed = (
        P(("seq", "dp"), None),
        P(("seq", "dp"), None),
        P("dp", None),
        P("dp", None),
        P(("seq", "dp"), None),
        P(("seq", "dp"), None),
        P(("seq", "dp"), None),
        P(("seq", "dp"), None),
        P(("seq", "dp"), None),
        P(("seq", "dp"), None),
        P(("seq", "dp")),
        P(("seq", "dp")),
        P("dp", None, "seq"),
        P("dp", "seq", None),
    )
    return jax.shard_map(
        shards_plane if in_planes(mesh) else shards_general,
        mesh=mesh,
        in_specs=placed,
        out_specs=(
            P(("seq", "dp"), None),
            P(("seq", "dp"), None),
            P(("seq", "dp"), None),
            P(("seq", "dp"), None),
            P(("seq", "dp"), None),
            P(("seq", "dp"), None),
            P(("seq", "dp")),
            P(("seq", "dp")),
            P("dp", None, "seq"),
            P("dp", "seq", None),
        ),
        check_vma=False,
    )
```

```python
import functools

import jax
import jax.numpy as jnp
from jax import lax
from jax.experimental import pallas as pl
from jax.experimental.pallas import tpu as pltpu
from jax.sharding import PartitionSpec as P

QHEADS = 24
KVHEADS = 8
HDIM = 64
FF = 512
TOP = 8


EPSILON = 1e-06
BRANCH_SCALE = 0.22
SCORE_SCALE = 1.0 / 64.0
THETA = 10000.0


def rms_norm(value, gain):
    return value * lax.rsqrt(jnp.mean(value * value, axis=-1, keepdims=True) + EPSILON) * gain


def local_places(placing, seq_lengths):
    ends = jnp.cumsum(seq_lengths)
    segment = jnp.sum((placing[:, None] >= ends[None, :]).astype(jnp.int32), axis=1)
    starts = ends - seq_lengths
    member = segment[:, None] == jnp.arange(seq_lengths.shape[0], dtype=jnp.int32)[None, :]
    start_of = jnp.sum(jnp.where(member, starts[None, :], 0), axis=1)
    return (segment, placing - start_of)


def rotate(values, place, direction):
    half = values.shape[-1] // 2
    freqs = jnp.power(THETA, -jnp.arange(half, dtype=jnp.float32) * 2.0 / values.shape[-1])
    angles = place.astype(jnp.float32)[:, None] * freqs[None, :]
    cosine = jnp.cos(angles)[:, None, :]
    sine = direction * jnp.sin(angles)[:, None, :]
    first = values[..., :half]
    second = values[..., half:]
    return jnp.concatenate(
        [first * cosine - second * sine, second * cosine + first * sine], axis=-1
    )


def shards_general(
    tokens,
    cotangent,
    positions,
    lengths,
    routes,
    logits,
    w_query,
    w_key,
    w_value,
    w_output,
    gain_attn,
    gain_ffn,
    w_in,
    w_out,
):
    seq_count = lax.axis_size("seq")
    data_count = lax.axis_size("dp")
    tok_count = tokens.shape[0]
    group_len = positions.shape[1]
    local_experts = w_in.shape[0]
    experts_all = local_experts * data_count
    capacity = min(tok_count, 5 * tok_count * TOP // (4 * experts_all))
    heads_local = QHEADS // seq_count
    kv_local = KVHEADS // seq_count
    ratio = QHEADS // KVHEADS
    width = tokens.shape[1]
    query_full, key_full, value_full, output_full, gain_one, gain_two = (
        lax.all_gather(w_query, ("seq", "dp"), axis=0, tiled=True),
        lax.all_gather(w_key, ("seq", "dp"), axis=0, tiled=True),
        lax.all_gather(w_value, ("seq", "dp"), axis=0, tiled=True),
        lax.all_gather(w_output, ("seq", "dp"), axis=0, tiled=True),
        lax.all_gather(gain_attn, ("seq", "dp"), axis=0, tiled=True),
        lax.all_gather(gain_ffn, ("seq", "dp"), axis=0, tiled=True),
    )
    in_full, out_full = (
        lax.all_gather(w_in, "seq", axis=2, tiled=True),
        lax.all_gather(w_out, "seq", axis=1, tiled=True),
    )
    gain_one = gain_one.astype(jnp.float32)
    gain_two = gain_two.astype(jnp.float32)
    segment, place = local_places(positions[0], lengths[0])
    my_start = lax.axis_index("seq") * tok_count
    my_place = lax.dynamic_slice_in_dim(place, my_start, tok_count)
    inputs = tokens.astype(jnp.float32)
    normed = rms_norm(inputs, gain_one).astype(jnp.bfloat16)
    query_pre = jnp.dot(normed, query_full, preferred_element_type=jnp.float32)
    key_pre = jnp.dot(normed, key_full, preferred_element_type=jnp.float32)
    query_rot = (
        rotate(query_pre.reshape(tok_count, QHEADS, HDIM), my_place, 1.0)
        .reshape(tok_count, QHEADS * HDIM)
        .astype(jnp.bfloat16)
    )
    key_rot = (
        rotate(key_pre.reshape(tok_count, KVHEADS, HDIM), my_place, 1.0)
        .reshape(tok_count, KVHEADS * HDIM)
        .astype(jnp.bfloat16)
    )
    value_low = jnp.dot(normed, value_full, preferred_element_type=jnp.float32).astype(jnp.bfloat16)
    query_heads, key_heads, value_heads = (
        lax.all_to_all(query_rot, "seq", split_axis=1, concat_axis=0, tiled=True),
        lax.all_to_all(key_rot, "seq", split_axis=1, concat_axis=0, tiled=True),
        lax.all_to_all(value_low, "seq", split_axis=1, concat_axis=0, tiled=True),
    )
    keys_three = key_heads.reshape(group_len, kv_local, HDIM)
    values_three = value_heads.reshape(group_len, kv_local, HDIM)
    length = min(512, group_len)
    count = group_len // length

    def scores_of(query_block, seg_block, place_block):
        grouped = query_block.reshape(length, kv_local, ratio, HDIM)
        raw_scores = (
            jnp.einsum("qgrd,kgd->grqk", grouped, keys_three, preferred_element_type=jnp.float32)
            * SCORE_SCALE
        )
        allowed = (seg_block[:, None] == segment[None, :]) & (
            place[None, :] <= place_block[:, None]
        )
        return jnp.where(allowed[None, None], raw_scores, -1e30)

    def forward_block(pieces):
        query_block, seg_block, place_block = pieces
        scores = scores_of(query_block, seg_block, place_block)
        highest = jnp.max(scores, axis=-1, keepdims=True)
        expon = jnp.exp(scores - highest)
        totals = jnp.sum(expon, axis=-1, keepdims=True)
        probs = expon / totals
        mixed = jnp.einsum(
            "grqk,kgd->qgrd",
            probs.astype(jnp.bfloat16),
            values_three,
            preferred_element_type=jnp.float32,
        )
        return (
            mixed.reshape(length, heads_local * HDIM).astype(jnp.bfloat16),
            highest + jnp.log(totals),
            probs,
        )

    query_blocks = query_heads.reshape(count, length, heads_local * HDIM)
    seg_blocks = segment.reshape(count, length)
    place_blocks = place.reshape(count, length)
    block_args = (query_blocks, seg_blocks, place_blocks)

    def forward_light(pieces):
        mixed, lse_part, unused_probs = forward_block(pieces)
        return (mixed, lse_part)

    mixed_blocks, lse_blocks = lax.map(forward_light, block_args)
    mixed_heads = mixed_blocks.reshape(group_len, heads_local * HDIM)
    mixed_tokens = lax.all_to_all(mixed_heads, "seq", split_axis=0, concat_axis=1, tiled=True)
    attn = jnp.dot(mixed_tokens, output_full, preferred_element_type=jnp.float32)
    middle = inputs + BRANCH_SCALE * attn
    normed_ffn = rms_norm(middle, gain_two).astype(jnp.bfloat16)
    chosen = routes.reshape(-1)
    onehot = (chosen[:, None] == jnp.arange(experts_all, dtype=jnp.int32)[None, :]).astype(
        jnp.int32
    )
    ranking = jnp.sum(jnp.cumsum(onehot, axis=0) * onehot, axis=1) - 1
    target = chosen * capacity + ranking
    token_of = jnp.arange(tok_count * TOP, dtype=jnp.int32) // TOP
    gates = jax.nn.softmax(logits, axis=-1)
    source = jnp.full((experts_all * capacity,), tok_count, jnp.int32).at[target].set(token_of)
    slot_gate = jnp.zeros((experts_all * capacity,), jnp.float32).at[target].set(gates.reshape(-1))
    padded = jnp.concatenate([normed_ffn, jnp.zeros((1, width), jnp.bfloat16)], axis=0)
    outgoing = padded[source].reshape(data_count, local_experts * capacity, width)

    def expert_layout(arrived):
        return jnp.swapaxes(
            arrived.reshape(data_count, local_experts, capacity, width), 0, 1
        ).reshape(local_experts, data_count * capacity, width)

    def home_layout(values):
        return jnp.swapaxes(
            values.reshape(local_experts, data_count, capacity, width), 0, 1
        ).reshape(data_count, local_experts * capacity, width)

    def expert_forward(expert_rows):
        both = jnp.einsum("erd,edf->erf", expert_rows, in_full, preferred_element_type=jnp.float32)
        hidden = (jax.nn.silu(both[..., :FF]) * both[..., FF:]).astype(jnp.bfloat16)
        return (both, hidden)

    expert_rows = expert_layout(
        lax.all_to_all(outgoing, "dp", split_axis=0, concat_axis=0, tiled=True)
    )
    both, hidden = expert_forward(expert_rows)
    result = jnp.einsum(
        "erf,efd->erd", hidden, out_full, preferred_element_type=jnp.float32
    ).astype(jnp.bfloat16)
    returned = lax.all_to_all(
        home_layout(result), "dp", split_axis=0, concat_axis=0, tiled=True
    ).reshape(experts_all * capacity, width)
    picked = returned[target].reshape(tok_count, TOP, width).astype(jnp.float32)
    ffn = jnp.sum(picked * gates[:, :, None], axis=1)
    final = middle + BRANCH_SCALE * ffn
    output = final.astype(jnp.bfloat16)
    grad_final = cotangent.astype(jnp.float32)
    padded_grad = jnp.concatenate(
        [BRANCH_SCALE * grad_final, jnp.zeros((1, width), jnp.float32)], axis=0
    )
    grad_slots = (slot_gate[:, None] * padded_grad[source]).astype(jnp.bfloat16)
    grad_result = expert_layout(
        lax.all_to_all(
            grad_slots.reshape(data_count, local_experts * capacity, width),
            "dp",
            split_axis=0,
            concat_axis=0,
            tiled=True,
        )
    )
    rows_back = expert_layout(
        lax.all_to_all(outgoing, "dp", split_axis=0, concat_axis=0, tiled=True)
    )
    both_back, hidden_back = expert_forward(rows_back)
    grad_hidden = jnp.einsum(
        "erd,efd->erf", grad_result, out_full, preferred_element_type=jnp.float32
    )
    gate_part = both_back[..., :FF]
    up_part = both_back[..., FF:]
    sigma = jax.nn.sigmoid(gate_part)
    grad_gate = grad_hidden * up_part * sigma * (1.0 + gate_part * (1.0 - sigma))
    grad_up = grad_hidden * gate_part * sigma
    grad_both = jnp.concatenate([grad_gate, grad_up], axis=-1).astype(jnp.bfloat16)
    grad_out_local = jnp.einsum(
        "erf,erd->efd", hidden_back, grad_result, preferred_element_type=jnp.float32
    )
    grad_in_local = jnp.einsum(
        "erd,erf->edf", rows_back, grad_both, preferred_element_type=jnp.float32
    )
    grad_rows = jnp.einsum(
        "erf,edf->erd", grad_both, in_full, preferred_element_type=jnp.float32
    ).astype(jnp.bfloat16)
    grad_home = lax.all_to_all(
        home_layout(grad_rows), "dp", split_axis=0, concat_axis=0, tiled=True
    ).reshape(experts_all * capacity, width)
    grad_normed_ffn = jnp.sum(
        grad_home[target].reshape(tok_count, TOP, width).astype(jnp.float32), axis=1
    )
    grad_w_in, grad_w_out = (
        lax.psum_scatter(
            grad_in_local.astype(jnp.bfloat16), "seq", scatter_dimension=2, tiled=True
        ).astype(jnp.float32),
        lax.psum_scatter(
            grad_out_local.astype(jnp.bfloat16), "seq", scatter_dimension=1, tiled=True
        ).astype(jnp.float32),
    )
    unused_norm, norm_pull = jax.vjp(rms_norm, middle, gain_two)
    grad_middle_norm, grad_gain_two = norm_pull(grad_normed_ffn)
    grad_middle = grad_final + grad_middle_norm
    grad_attn = (BRANCH_SCALE * grad_middle).astype(jnp.bfloat16)
    grad_w_output = jnp.einsum(
        "te,td->ed", mixed_tokens, grad_attn, preferred_element_type=jnp.float32
    )
    grad_mixed = jnp.einsum(
        "td,ed->te", grad_attn, output_full, preferred_element_type=jnp.float32
    ).astype(jnp.bfloat16)
    grad_mixed_heads = lax.all_to_all(grad_mixed, "seq", split_axis=1, concat_axis=0, tiled=True)
    grad_blocks = grad_mixed_heads.reshape(count, length, heads_local * HDIM)
    back_args = (query_blocks, seg_blocks, place_blocks, lse_blocks, grad_blocks)

    def backward_block(carry, pieces):
        grad_keys, grad_values = carry
        query_block, seg_block, place_block, lse_block, grad_block = pieces[:5]
        probs = jnp.exp(scores_of(query_block, seg_block, place_block) - lse_block)
        grad_out = grad_block.reshape(length, kv_local, ratio, HDIM)
        grad_probs = jnp.einsum(
            "qgrd,kgd->grqk", grad_out, values_three, preferred_element_type=jnp.float32
        )
        grad_scores = (
            probs * (grad_probs - jnp.sum(probs * grad_probs, axis=-1, keepdims=True))
        ).astype(jnp.bfloat16)
        grad_query = SCORE_SCALE * jnp.einsum(
            "grqk,kgd->qgrd", grad_scores, keys_three, preferred_element_type=jnp.float32
        )
        grouped = query_block.reshape(length, kv_local, ratio, HDIM)
        grad_keys = grad_keys + SCORE_SCALE * jnp.einsum(
            "grqk,qgrd->kgd", grad_scores, grouped, preferred_element_type=jnp.float32
        )
        grad_values = grad_values + jnp.einsum(
            "grqk,qgrd->kgd",
            probs.astype(jnp.bfloat16),
            grad_out,
            preferred_element_type=jnp.float32,
        )
        return (
            (grad_keys, grad_values),
            grad_query.reshape(length, heads_local * HDIM).astype(jnp.bfloat16),
        )

    empty_keys = jnp.zeros((group_len, kv_local, HDIM), jnp.float32)
    (grad_keys, grad_values), grad_query_blocks = lax.scan(
        backward_block, (empty_keys, empty_keys), back_args
    )
    grad_query_heads = grad_query_blocks.reshape(group_len, heads_local * HDIM)
    grad_key_heads = grad_keys.reshape(group_len, kv_local * HDIM).astype(jnp.bfloat16)
    grad_value_heads = grad_values.reshape(group_len, kv_local * HDIM).astype(jnp.bfloat16)
    grad_query_tok, grad_key_tok, grad_value_tok = (
        lax.all_to_all(grad_query_heads, "seq", split_axis=0, concat_axis=1, tiled=True),
        lax.all_to_all(grad_key_heads, "seq", split_axis=0, concat_axis=1, tiled=True),
        lax.all_to_all(grad_value_heads, "seq", split_axis=0, concat_axis=1, tiled=True),
    )
    grad_query_pre = (
        rotate(grad_query_tok.astype(jnp.float32).reshape(tok_count, QHEADS, HDIM), my_place, -1.0)
        .reshape(tok_count, QHEADS * HDIM)
        .astype(jnp.bfloat16)
    )
    grad_key_pre = (
        rotate(grad_key_tok.astype(jnp.float32).reshape(tok_count, KVHEADS, HDIM), my_place, -1.0)
        .reshape(tok_count, KVHEADS * HDIM)
        .astype(jnp.bfloat16)
    )
    grad_w_query = jnp.einsum(
        "td,te->de", normed, grad_query_pre, preferred_element_type=jnp.float32
    )
    grad_w_key = jnp.einsum("td,te->de", normed, grad_key_pre, preferred_element_type=jnp.float32)
    grad_w_value = jnp.einsum(
        "td,te->de", normed, grad_value_tok, preferred_element_type=jnp.float32
    )
    grad_normed = jnp.einsum(
        "te,de->td", grad_query_pre, query_full, preferred_element_type=jnp.float32
    )
    grad_normed = grad_normed + jnp.einsum(
        "te,de->td", grad_key_pre, key_full, preferred_element_type=jnp.float32
    )
    grad_normed = grad_normed + jnp.einsum(
        "te,de->td", grad_value_tok, value_full, preferred_element_type=jnp.float32
    )
    unused_first, first_pull = jax.vjp(rms_norm, inputs, gain_one)
    grad_inputs_norm, grad_gain_one = first_pull(grad_normed)
    grad_tokens = grad_middle + grad_inputs_norm
    summed = (
        lax.psum_scatter(grad_w_query, ("seq", "dp"), scatter_dimension=0, tiled=True),
        lax.psum_scatter(grad_w_key, ("seq", "dp"), scatter_dimension=0, tiled=True),
        lax.psum_scatter(grad_w_value, ("seq", "dp"), scatter_dimension=0, tiled=True),
        lax.psum_scatter(grad_w_output, ("seq", "dp"), scatter_dimension=0, tiled=True),
        lax.psum_scatter(grad_gain_one, ("seq", "dp"), scatter_dimension=0, tiled=True),
        lax.psum_scatter(grad_gain_two, ("seq", "dp"), scatter_dimension=0, tiled=True),
    )
    return (
        output,
        grad_tokens,
        summed[0],
        summed[1],
        summed[2],
        summed[3],
        summed[4],
        summed[5],
        grad_w_in,
        grad_w_out,
    )


BF16 = jnp.bfloat16
F32 = jnp.float32
LINE = 4
PAD = 128
VMEM_BYTES = 60 * 1024 * 1024


def in_planes(mesh):
    return mesh.shape["seq"] == 2 and mesh.shape["dp"] == 4 * LINE


def swap_seq(value):
    return lax.ppermute(value, "seq", [(0, 1), (1, 0)])


def swap_dp(value, mask):
    return lax.ppermute(value, "dp", [(i, i ^ mask) for i in range(4 * LINE)])


def swap_core(value):
    return swap_dp(value, 1)


def swap_y(value):
    return swap_dp(value, 2)


def line_up(value):
    return lax.ppermute(value, "dp", [(i, i + 4) for i in range(4 * LINE - 4)])


def line_down(value):
    return lax.ppermute(value, "dp", [(i, i - 4) for i in range(4, 4 * LINE)])


def after(value, *others):
    return lax.optimization_barrier((value,) + others)[0]


def line_scatter(take, place):
    up = down = None
    for step in range(LINE - 1):
        far = jnp.minimum(LINE - 1 - step + place, LINE - 1)
        near = jnp.maximum(step - LINE + 1 + place, 0)
        right, left = take(far), take(near)
        if up is not None:
            right = right + up.astype(F32)
            left = left + down.astype(F32)
        up = line_up(right.astype(BF16))
        down = line_down(left.astype(BF16))
    return take(place) + up.astype(F32) + down.astype(F32)


def near_pieces(own, own_x):
    return swap_seq(own_x), swap_y(own)


def far_pieces(near_x, near_y):
    half = near_x.shape[0] // 2
    return swap_y(near_x[:half]), swap_seq(near_y[half:])


def with_cores(*pieces):
    return pieces + tuple(swap_core(piece) for piece in pieces)


def over_cores(mine, others):
    return mine.astype(F32) + swap_core(others).astype(F32)


def far_links(far):
    half = far.shape[0] // 2
    return swap_y(far[:half]), swap_seq(far[half:])


def near_links(near, from_y, from_x):
    half = from_y.shape[0] // 2
    first = (near[:half] + from_y[half:].astype(F32)).astype(BF16)
    second = (near[half : 2 * half] + from_x[half:].astype(F32)).astype(BF16)
    return first, second


def own_sum(near, from_y, from_x, first, second):
    half = from_y.shape[0] // 2
    low = near[2 * half : 3 * half] + from_y[:half].astype(F32) + first.astype(F32)
    high = near[3 * half :] + from_x[:half].astype(F32) + second.astype(F32)
    return jnp.concatenate([low, high], axis=0)


def turned(values, cos, sin, direction):
    lanes = values.shape[1]
    place = lax.broadcasted_iota(jnp.int32, values.shape, 1) % HDIM
    swapped = jnp.where(
        place < HDIM // 2,
        pltpu.roll(values, lanes - HDIM // 2, 1),
        pltpu.roll(values, HDIM // 2, 1),
    )
    times = lanes // cos.shape[1]
    cos = jnp.concatenate([cos] * times, axis=1)
    sin = jnp.concatenate([sin] * times, axis=1)
    if direction > 0:
        return values * cos + swapped * sin
    return values * cos - swapped * sin


def qkv_kernel(x_ref, gain_ref, w_ref, cos_ref, sin_ref, h_ref, q_ref, k_ref, v_ref):
    value = x_ref[...].astype(F32)
    scale = lax.rsqrt(jnp.mean(value * value, axis=-1, keepdims=True) + EPSILON)
    normed = (value * scale * gain_ref[...]).astype(BF16)
    h_ref[...] = normed
    both = jnp.dot(normed, w_ref[...], preferred_element_type=F32)
    q_width, kv_heads = q_ref.shape[1], k_ref.shape[0]
    kv_width = kv_heads * HDIM
    spun = turned(both[:, : q_width + kv_width], cos_ref[...], sin_ref[...], 1)
    q_ref[...] = (spun[:, :q_width] * SCORE_SCALE).astype(BF16)
    for head in range(kv_heads):
        low = q_width + head * HDIM
        k_ref[head] = spun[:, low : low + HDIM].astype(BF16)
        low = low + kv_width
        v_ref[head] = both[:, low : low + HDIM].astype(BF16)


def project(x_sorted, gain, weights, cos, sin, q_width, kv_heads):
    rows, width = x_sorted.shape
    tile = 256
    columns = q_width + 2 * kv_heads * HDIM

    def row_block(lanes):
        return pl.BlockSpec((tile, lanes), lambda i: (i, 0))

    heads = pl.BlockSpec((kv_heads, tile, HDIM), lambda i: (0, i, 0))
    return pl.pallas_call(
        qkv_kernel,
        grid=(rows // tile,),
        in_specs=[
            row_block(width),
            pl.BlockSpec((1, width), lambda i: (0, 0)),
            pl.BlockSpec((width, columns), lambda i: (0, 0)),
            row_block(cos.shape[1]),
            row_block(cos.shape[1]),
        ],
        out_specs=[row_block(width), row_block(q_width), heads, heads],
        out_shape=[
            jax.ShapeDtypeStruct((rows, width), BF16),
            jax.ShapeDtypeStruct((rows, q_width), BF16),
            jax.ShapeDtypeStruct((kv_heads, rows, HDIM), BF16),
            jax.ShapeDtypeStruct((kv_heads, rows, HDIM), BF16),
        ],
        compiler_params=pltpu.CompilerParams(vmem_limit_bytes=VMEM_BYTES),
        cost_estimate=pl.CostEstimate(
            flops=2 * rows * width * columns,
            bytes_accessed=2 * (2 * rows * width + width * columns + rows * columns),
            transcendentals=rows,
        ),
        name="project",
    )(x_sorted, gain, weights, cos, sin)


Q_TILE = 256


def windows(rows):
    longest = rows // 2
    for start in range(0, rows, Q_TILE):
        low = max(0, start - longest + 1) // Q_TILE * Q_TILE
        yield start, low, start + Q_TILE


def allowed_keys(start_ref, row, low, high):
    shape = (Q_TILE, high - low)
    rows = lax.broadcasted_iota(jnp.int32, shape, 0) + row
    keys = lax.broadcasted_iota(jnp.int32, shape, 1) + low
    return (keys <= rows) & (keys >= start_ref[row : row + Q_TILE, :])


def contract(left, right, left_dim, right_dim):
    return lax.dot_general(
        left, right, (((left_dim,), (right_dim,)), ((), ())), preferred_element_type=F32
    )


def probabilities(query, keys, allowed):
    scores = jnp.where(allowed, contract(query, keys, 1, 1), -1e30)
    expon = jnp.exp(scores - jnp.max(scores, axis=-1, keepdims=True))
    return expon * (1.0 / jnp.sum(expon, axis=-1, keepdims=True))


def attend_kernel(base, q_ref, k_ref, v_ref, start_ref, o_ref):
    pair = pl.program_id(0) + base
    ratio = QHEADS // KVHEADS
    for row, low, high in windows(q_ref.shape[0]):
        allowed = allowed_keys(start_ref, row, low, high)
        for side in range(2):
            head = (2 * pair + side) // ratio
            lanes = slice(side * HDIM, (side + 1) * HDIM)
            probs = probabilities(
                q_ref[row : row + Q_TILE, lanes], k_ref[head, low:high, :], allowed
            )
            mixed = contract(probs.astype(BF16), v_ref[head, low:high, :], 1, 0)
            o_ref[row : row + Q_TILE, lanes] = mixed.astype(BF16)


def attention_cost(rows, heads, products):
    area = sum(Q_TILE * (high - low) for _, low, high in windows(rows))
    return pl.CostEstimate(
        flops=products * heads * area * 16,
        bytes_accessed=8 * rows * heads * HDIM,
        transcendentals=heads * area,
    )


def attend(query, keys, values, starts, base, pairs):
    rows = query.shape[0]
    pair_block = pl.BlockSpec((rows, 2 * HDIM), lambda j: (0, j + base))
    whole = pl.BlockSpec(keys.shape, lambda j: (0, 0, 0))
    return pl.pallas_call(
        functools.partial(attend_kernel, base),
        grid=(pairs,),
        in_specs=[pair_block, whole, whole, pl.BlockSpec((rows, 1), lambda j: (0, 0))],
        out_specs=pl.BlockSpec((rows, 2 * HDIM), lambda j: (0, j)),
        out_shape=jax.ShapeDtypeStruct((rows, pairs * 2 * HDIM), BF16),
        compiler_params=pltpu.CompilerParams(vmem_limit_bytes=VMEM_BYTES),
        cost_estimate=attention_cost(rows, 2 * pairs, 2),
        name="attend",
    )(query, keys, values, starts)


def attend_back_kernel(
    q_ref, k_ref, v_ref, d_ref, start_ref, cos_ref, sin_ref,
    dq_ref, dk_ref, dv_ref, dk_sum, dv_sum,
):
    pair = pl.program_id(0)
    ratio = QHEADS // KVHEADS

    @pl.when(pair == 0)
    def _():
        dk_sum[...] = jnp.zeros_like(dk_sum)
        dv_sum[...] = jnp.zeros_like(dv_sum)

    for row, low, high in windows(q_ref.shape[0]):
        allowed = allowed_keys(start_ref, row, low, high)
        grads = []
        for side in range(2):
            head = (2 * pair + side) // ratio
            lanes = slice(side * HDIM, (side + 1) * HDIM)
            query = q_ref[row : row + Q_TILE, lanes]
            keys = k_ref[head, low:high, :]
            probs = probabilities(query, keys, allowed)
            grad_out = d_ref[row : row + Q_TILE, lanes]
            grad_probs = contract(grad_out, v_ref[head, low:high, :], 1, 1)
            inner = jnp.sum(probs * grad_probs, axis=-1, keepdims=True)
            grad_scores = (probs * (grad_probs - inner)).astype(BF16)
            grads.append(contract(grad_scores, keys, 1, 0) * SCORE_SCALE)
            dk_sum[head, low:high, :] += contract(grad_scores, query, 0, 0)
            dv_sum[head, low:high, :] += contract(probs.astype(BF16), grad_out, 0, 0)
        grad_query = jnp.concatenate(grads, axis=1).astype(BF16).astype(F32)
        dq_ref[row : row + Q_TILE, :] = turned(
            grad_query,
            cos_ref[row : row + Q_TILE, :],
            sin_ref[row : row + Q_TILE, :],
            -1,
        ).astype(BF16)

    @pl.when(pair == pl.num_programs(0) - 1)
    def _():
        heads = range(dk_sum.shape[0])
        grad_keys = jnp.concatenate([dk_sum[head] for head in heads], axis=1)
        grad_keys = grad_keys.astype(BF16).astype(F32)
        dk_ref[...] = turned(grad_keys, cos_ref[...], sin_ref[...], -1).astype(BF16)
        dv_ref[...] = jnp.concatenate([dv_sum[head] for head in heads], axis=1).astype(BF16)


def attend_back(query, keys, values, grad_out, starts, cos, sin):
    rows, lanes = query.shape
    pairs = lanes // (2 * HDIM)
    kv_heads = keys.shape[0]
    pair_block = pl.BlockSpec((rows, 2 * HDIM), lambda j: (0, j))
    whole = pl.BlockSpec(keys.shape, lambda j: (0, 0, 0))

    def fixed(lanes_of):
        return pl.BlockSpec((rows, lanes_of), lambda j: (0, 0))

    flat = kv_heads * HDIM
    return pl.pallas_call(
        attend_back_kernel,
        grid=(pairs,),
        in_specs=[
            pair_block, whole, whole, pair_block, fixed(1), fixed(2 * HDIM), fixed(2 * HDIM),
        ],
        out_specs=[pair_block, fixed(flat), fixed(flat)],
        out_shape=[
            jax.ShapeDtypeStruct(query.shape, BF16),
            jax.ShapeDtypeStruct((rows, flat), BF16),
            jax.ShapeDtypeStruct((rows, flat), BF16),
        ],
        scratch_shapes=[pltpu.VMEM(keys.shape, F32), pltpu.VMEM(keys.shape, F32)],
        compiler_params=pltpu.CompilerParams(vmem_limit_bytes=VMEM_BYTES),
        cost_estimate=attention_cost(rows, 2 * pairs, 5),
        name="attend_back",
    )(query, keys, values, grad_out, starts, cos, sin)


SLOTS = 2 * LINE - 1
SLOT_ORDER = (0, 3, 1, 2)
OWN, NEAR_X, NEAR_Y, FAR_Y, FAR_X = range(5)
FAR_TILES = (((NEAR_Y, 0), (FAR_Y, 0)), ((NEAR_X, 1), (FAR_X, 0)))
NEAR_TILES = (((NEAR_X, 0), (NEAR_Y, 1)), ((OWN, 0), (OWN, 1)))


def used_pieces(tiles):
    return sorted({piece for tile in tiles for piece, _ in tile})


def experts_kernel(tiles, half_rows, place_ref, *refs):
    used = used_pieces(tiles)
    sides = 2 * len(used)
    h_pieces, g_pieces, slots = refs[:sides], refs[sides : 2 * sides], refs[2 * sides : 2 * sides + SLOTS]
    select_ref = refs[2 * sides + SLOTS]
    (
        f_mine, f_other, d_mine, d_other, hid_a, hid_b, du_a, du_b, hcopy_ref, gcopy_ref,
        w_in, w_out, h_buf, g_buf, hidden, du_all, weight_sems, row_sems,
    ) = refs[-18:]
    width = h_buf.shape[2]
    half = slots[0].shape[1] // 3
    part = 2 * half
    step = pl.program_id(0)
    steps = 2 * len(tiles)

    def weight_copies(spot, slot):
        return (
            pltpu.make_async_copy(
                slots[slot].at[:, :part],
                w_in.at[:, spot * part : (spot + 1) * part],
                weight_sems.at[0, spot],
            ),
            pltpu.make_async_copy(
                slots[slot].at[:, part:],
                w_out.at[:, spot * half : (spot + 1) * half],
                weight_sems.at[1, spot],
            ),
        )

    def row_copies(number, buffer):
        side, tile = divmod(number, len(tiles))
        copies = []
        for spot, (piece, part_of) in enumerate(tiles[tile]):
            index = side * len(used) + used.index(piece)
            for kind, (pieces, held) in enumerate(((h_pieces, h_buf), (g_pieces, g_buf))):
                copies.append(
                    pltpu.make_async_copy(
                        pieces[index].at[pl.ds(part_of * half_rows, half_rows), :],
                        held.at[buffer, pl.ds(spot * half_rows, half_rows), :],
                        row_sems.at[buffer, 2 * kind + spot],
                    )
                )
        return copies

    def fetch(wanted, buffer):
        for number in range(steps):

            @pl.when(wanted == number)
            def _():
                for copy in row_copies(number, buffer):
                    copy.start()

    buffer = step % 2

    @pl.when(step == 0)
    def _():
        fetch(step, 0)
        for spot, expert in enumerate(SLOT_ORDER):
            for slot in range(expert, expert + LINE):

                @pl.when(slot == LINE - 1 + expert - place_ref[0])
                def _():
                    for copy in weight_copies(spot, slot):
                        copy.start()

    @pl.when(step + 1 < steps)
    def _():
        fetch(step + 1, 1 - buffer)

    for copy in row_copies(0, buffer):
        copy.wait()

    rows = h_buf[buffer]
    grads = g_buf[buffer, :, :width]
    hcopy_ref[...] = rows
    gcopy_ref[...] = grads
    gates = jnp.dot(g_buf[buffer, :, width:], select_ref[...], preferred_element_type=F32)
    for spot in range(LINE):
        units = slice(spot * half, (spot + 1) * half)

        @pl.when(step == 0)
        def _():
            for copy in weight_copies(spot, LINE - 1):
                copy.wait()

        both = jnp.dot(
            rows, w_in[:, spot * part : (spot + 1) * part], preferred_element_type=F32
        )
        back = jnp.dot(grads, w_out[:, units], preferred_element_type=F32)
        gate = gates[:, units]
        first, second = both[:, :half], both[:, half:]
        sigma = jax.nn.sigmoid(first)
        silu = first * sigma
        hidden[:, units] = (gate * (silu * second)).astype(BF16)
        back = back * (BRANCH_SCALE * gate)
        d_first = back * second * (sigma * (1.0 + first * (1.0 - sigma)))
        d_second = back * silu
        du_all[:, spot * part : spot * part + half] = d_first.astype(BF16)
        du_all[:, spot * part + half : (spot + 1) * part] = d_second.astype(BF16)
    hid_a[...] = hidden[:, : 2 * half]
    hid_b[...] = hidden[:, 2 * half :]
    du_a[...] = du_all[:, : 2 * part]
    du_b[...] = du_all[:, 2 * part :]
    ffn = contract(hidden[...], w_out[...], 1, 1).astype(BF16)
    back_rows = contract(du_all[...], w_in[...], 1, 1).astype(BF16)

    @pl.when(step < len(tiles))
    def _():
        f_mine[...] = ffn
        d_mine[...] = back_rows

    @pl.when(step >= len(tiles))
    def _():
        f_other[...] = ffn
        d_other[...] = back_rows


def run_experts(tiles, place, row_pieces, grad_pieces, slots, select, base, kept):
    used = used_pieces(tiles)
    sides = len(row_pieces) // 2
    wanted = used + [sides + piece for piece in used]
    rows = [row_pieces[piece] for piece in wanted]
    grads = [grad_pieces[piece] for piece in wanted]
    tile, width = row_pieces[OWN].shape
    wide = grad_pieces[OWN].shape[1]
    half = slots[0].shape[1] // 3
    part = 2 * half
    count = len(tiles)
    steps = 2 * count
    total = 8 * tile

    def late(lanes):
        return pl.BlockSpec((tile, lanes), lambda i, p: (i + base, 0))

    mine = pl.BlockSpec((tile, width), lambda i, p: (jnp.minimum(i, count - 1), 0))
    others = pl.BlockSpec((tile, width), lambda i, p: (jnp.maximum(i - count, 0), 0))
    anywhere = pl.BlockSpec(memory_space=pl.ANY)
    kept = list(kept)
    lead = 1 + 2 * len(wanted) + SLOTS + 1
    partial = jax.ShapeDtypeStruct((count * tile, width), BF16)
    lanes = [2 * half, 2 * half, 2 * part, 2 * part, width, width]
    return pl.pallas_call(
        functools.partial(experts_kernel, tiles, tile // 2),
        grid_spec=pltpu.PrefetchScalarGridSpec(
            num_scalar_prefetch=1,
            grid=(steps,),
            in_specs=[anywhere] * (2 * len(wanted) + SLOTS)
            + [pl.BlockSpec(select.shape, lambda i, p: (0, 0))]
            + [anywhere] * len(kept),
            out_specs=[mine, others, mine, others] + [late(n) for n in lanes],
            scratch_shapes=[
                pltpu.VMEM((width, LINE * part), BF16),
                pltpu.VMEM((width, LINE * half), BF16),
                pltpu.VMEM((2, tile, width), BF16),
                pltpu.VMEM((2, tile, wide), BF16),
                pltpu.VMEM((tile, LINE * half), BF16),
                pltpu.VMEM((tile, LINE * part), BF16),
                pltpu.SemaphoreType.DMA((2, LINE)),
                pltpu.SemaphoreType.DMA((2, 4)),
            ],
        ),
        out_shape=[partial] * 4 + [jax.ShapeDtypeStruct((total, n), BF16) for n in lanes],
        input_output_aliases={lead + i: 4 + i for i in range(len(kept))},
        compiler_params=pltpu.CompilerParams(vmem_limit_bytes=VMEM_BYTES),
        cost_estimate=pl.CostEstimate(
            flops=steps * tile * width * LINE * (part + half) // 4,
            bytes_accessed=2 * steps * tile * (6 * width + LINE * (part + half)),
            transcendentals=steps * tile * LINE * half,
        ),
        name="experts",
    )(place, *rows, *grads, *slots, select, *kept)


def qkv_grad_kernel(h_ref, d_ref, gain_ref, o_ref):
    shard = o_ref.shape[-2]
    columns = d_ref.shape[1]
    product = contract(h_ref[...], d_ref[...], 0, 0).astype(BF16)
    gains = jnp.broadcast_to(gain_ref[...], (PAD, gain_ref.shape[1])).T.astype(BF16)
    for block in range(h_ref.shape[1] // shard):
        rows = slice(block * shard, (block + 1) * shard)
        place = (block % 2, block // 2 % 2, 0, block // 4)
        o_ref[place + (slice(None), slice(0, columns))] = product[rows]
        o_ref[place + (slice(None), slice(columns, columns + PAD))] = gains[rows]


def qkv_grad(normed, grads, gain_row, shard):
    rows, width = normed.shape
    columns = grads.shape[1]
    tile = width // 4
    planes = tile // (4 * shard)
    return pl.pallas_call(
        qkv_grad_kernel,
        grid=(4,),
        in_specs=[
            pl.BlockSpec((rows, tile), lambda i: (0, i)),
            pl.BlockSpec((rows, columns), lambda i: (0, 0)),
            pl.BlockSpec((1, tile), lambda i: (0, i)),
        ],
        out_specs=pl.BlockSpec(
            (2, 2, 1, planes, shard, columns + PAD), lambda i: (0, 0, i // 2, i % 2, 0, 0)
        ),
        out_shape=jax.ShapeDtypeStruct((2, 2, 2, LINE, shard, columns + PAD), BF16),
        compiler_params=pltpu.CompilerParams(vmem_limit_bytes=VMEM_BYTES),
        cost_estimate=pl.CostEstimate(
            flops=rows * width * columns // 4,
            bytes_accessed=2 * rows * (width + columns) + 2 * width * columns,
            transcendentals=0,
        ),
        name="qkv_grad",
    )(normed, grads, gain_row)


def norm_back(value, gain, grad):
    scale = lax.rsqrt(jnp.mean(value * value, axis=-1, keepdims=True) + EPSILON)
    unit = value * scale
    grad_gain = jnp.sum(grad * unit, axis=0)
    scaled = grad * gain
    inner = jnp.mean(scaled * unit, axis=-1, keepdims=True)
    return scale * (scaled - unit * inner), grad_gain


def shards_plane(
    tokens,
    cotangent,
    positions,
    lengths,
    routes,
    logits,
    w_query,
    w_key,
    w_value,
    w_output,
    gain_attn,
    gain_ffn,
    w_in,
    w_out,
):
    seq = lax.axis_index("seq")
    data = lax.axis_index("dp")
    line, row_of, core = data // 4, (data // 2) % 2, data % 2
    tok_count, width = tokens.shape
    group_len = positions.shape[1]
    shard = w_query.shape[0]
    q_width = w_query.shape[1] // 2
    kv_width = w_key.shape[1] // 2
    kv_heads = kv_width // HDIM
    first_seq = seq == 0

    def ordered(mine, theirs, axis):
        low = jnp.where(first_seq, mine, theirs)
        high = jnp.where(first_seq, theirs, mine)
        return jnp.concatenate([low, high], axis=axis)

    def half_of(weights, which):
        half = weights.shape[1] // 2
        return lax.dynamic_slice_in_dim(weights, which * half, half, axis=1)

    def both_axes(value, pairs):
        return lax.ppermute(value, ("seq", "dp"), pairs)

    def device(s, d):
        return s * 4 * LINE + d

    straight, crossed = [], []
    for s in range(2):
        for d in range(4 * LINE):
            c = d % 2
            straight.append((device(s, d), device(c, d - c + s)))
            crossed.append((device(s, d), device(c, d - c + 1 - s)))
    crossed_back = [(there, here) for here, there in crossed]
    first_core = core == 0

    projections = (w_query, w_key, w_value)
    gain_columns = jnp.pad(jnp.stack([gain_attn, gain_ffn], axis=1), ((0, 0), (0, PAD - 2)))
    mine = jnp.concatenate([half_of(w, seq) for w in projections] + [gain_columns], axis=1)
    theirs = jnp.concatenate([half_of(w, 1 - seq) for w in projections] + [gain_columns], axis=1)
    theirs = swap_seq(theirs)
    pair = jnp.stack([jnp.where(first_seq, mine, theirs), jnp.where(first_seq, theirs, mine)])
    qkv_width = q_width + 2 * kv_width
    w_qkv = lax.all_gather(pair, "dp", axis=1, tiled=True).reshape(width, qkv_width + PAD)
    output_full = lax.all_gather(w_output, ("seq", "dp"), axis=0, tiled=True)

    in_own = w_in[0]
    half = in_own.shape[1] // 2
    sent = jnp.concatenate(
        [lax.dynamic_slice_in_dim(in_own, seq * half, half, axis=1), w_out[0].T], axis=1
    )
    same = both_axes(sent, straight)
    cross = both_axes(lax.dynamic_slice_in_dim(in_own, (1 - seq) * half, half, axis=1), crossed)
    own_part = jnp.concatenate(
        [
            jnp.where(first_core, same[:, :half], cross),
            jnp.where(first_core, cross, same[:, :half]),
            same[:, half:],
        ],
        axis=1,
    )
    other_tokens = swap_seq(after(tokens, own_part))
    up_one, down_one = line_up(own_part), line_down(own_part)

    experts_all = 4 * LINE
    gates = jax.nn.softmax(logits, axis=-1)
    named = routes[:, :, None] == jnp.arange(experts_all, dtype=jnp.int32)[None, None, :]
    gate_table = jnp.sum(jnp.where(named, gates[:, :, None], 0.0), axis=1)
    gate_high = lax.reduce_precision(gate_table, 8, 7)
    grad_rows = jnp.concatenate(
        [
            cotangent,
            gate_high.astype(BF16),
            (gate_table - gate_high).astype(BF16),
            jnp.zeros((tok_count, PAD - 2 * experts_all), BF16),
        ],
        axis=1,
    )
    grad_near = near_pieces(grad_rows, after(grad_rows, other_tokens))
    lane = jnp.arange(PAD, dtype=jnp.int32)[:, None]
    hosted = jnp.repeat(
        jnp.array(SLOT_ORDER, jnp.int32) * 4 + 2 * row_of + seq, half, total_repeat_length=LINE * half
    )
    select = ((lane % experts_all == hosted[None, :]) & (lane < 2 * experts_all)).astype(BF16)

    places = positions[0]
    ends = jnp.cumsum(lengths[0])
    ranks = jnp.arange(group_len, dtype=jnp.int32)
    reached = ranks[:, None] >= ends[None, :]
    starts = jnp.max(jnp.where(reached, ends[None, :], 0), axis=1)
    local = (ranks - starts).astype(F32)
    freqs = jnp.power(THETA, -jnp.arange(HDIM // 2, dtype=F32) * 2.0 / HDIM)
    angles = local[:, None] * freqs[None, :]
    cos, sin = jnp.cos(angles), jnp.sin(angles)
    cos = jnp.concatenate([cos, cos, cos, cos], axis=1)
    sin = jnp.concatenate([-sin, sin, -sin, sin], axis=1)
    start_column = starts[:, None]
    own_places = lax.dynamic_slice_in_dim(places, seq * tok_count, tok_count)
    other_places = lax.dynamic_slice_in_dim(places, (1 - seq) * tok_count, tok_count)
    sort_own = (ranks[:, None] == own_places[None, :]).astype(BF16)
    sort_other = (ranks[:, None] == other_places[None, :]).astype(BF16)

    def to_order(own, other):
        return (
            contract(sort_own, own, 1, 0) + contract(sort_other, other, 1, 0)
        ).astype(BF16)

    def from_order(sort, values):
        return contract(sort, values, 0, 0).astype(BF16)

    x_sorted = to_order(tokens, other_tokens)
    gains = w_qkv[:, qkv_width : qkv_width + 2].astype(F32).T
    gain_one, gain_two = gains[0], gains[1]
    x_sorted, up_one, down_one = lax.optimization_barrier((x_sorted, up_one, down_one))
    up_two, down_two = line_up(up_one), line_down(down_one)
    normed, query, keys, values = project(
        x_sorted, gain_one[None, :], w_qkv, cos, sin, q_width, kv_heads
    )
    pairs = q_width // (2 * HDIM)
    first_pairs = (pairs + 1) // 2
    mixed_one = attend(query, keys, values, start_column, 0, first_pairs)
    sent_one = swap_seq(from_order(sort_other, mixed_one))
    query_two, grad_near_x, grad_near_y = after((query, *grad_near), mixed_one)
    grad_near = (grad_near_x, grad_near_y)
    grad_far = far_pieces(*grad_near)
    mixed_two = attend(
        query_two, keys, values, start_column, first_pairs, pairs - first_pairs
    )
    sent_two = swap_seq(from_order(sort_other, mixed_two))
    mixed_mine = [from_order(sort_own, mixed_one), from_order(sort_own, mixed_two)]
    mixed = ordered(
        jnp.concatenate(mixed_mine, axis=1), jnp.concatenate([sent_one, sent_two], axis=1), 1
    )
    mixed, up_two, down_two = lax.optimization_barrier((mixed, up_two, down_two))
    up_three, down_three = line_up(up_two), line_down(down_two)
    inputs = tokens.astype(F32)
    attn = jnp.dot(mixed, output_full, preferred_element_type=F32)
    middle = inputs + BRANCH_SCALE * attn
    normed_ffn = rms_norm(middle, gain_two).astype(BF16)

    normed_ffn = after(normed_ffn, *grad_far)
    row_near = near_pieces(normed_ffn, normed_ffn)
    row_far = far_pieces(*row_near)
    slots = [up_three, up_two, up_one, own_part, down_one, down_two, down_three]
    row_pieces = with_cores(normed_ffn, *row_near, *row_far)
    grad_pieces = with_cores(*after((grad_rows, *grad_near, *grad_far), row_near[0]))
    place = line.astype(jnp.int32)[None]
    far = run_experts(FAR_TILES, place, row_pieces, grad_pieces, slots, select, 0, ())
    far_back = over_cores(far[2], far[3]).astype(BF16)
    back_y, back_x = far_links(far_back)
    near = run_experts(
        NEAR_TILES, after(place, far_back), row_pieces, grad_pieces, slots, select, 4, far[4:]
    )
    hid_a, hid_b, du_a, du_b, all_rows, all_grads = near[4:]

    def weight_grads(rows, grads, grad_both, hidden):
        inner = contract(rows, grad_both, 0, 0)
        outer = contract(grads, hidden, 0, 0) * BRANCH_SCALE
        return [
            jnp.concatenate(
                [inner[:, 2 * half * i : 2 * half * (i + 1)], outer[:, half * i : half * (i + 1)]],
                axis=1,
            ).astype(BF16)
            for i in range(2)
        ]

    rows_early, grads_early, back_y, back_x = lax.optimization_barrier(
        (all_rows, all_grads, back_y, back_x)
    )
    outer_grads = weight_grads(rows_early, grads_early, du_a, hid_a)
    grads_of = dict(zip(SLOT_ORDER[:2], outer_grads))
    far_line = (line_up(outer_grads[1]), line_down(outer_grads[0]))
    near_back = over_cores(after(near[2], *outer_grads), near[3])
    first, second = near_links(near_back, back_y, back_x)
    rows_late, grads_late = after((all_rows, all_grads), first, second)
    inner_grads = weight_grads(rows_late, grads_late, du_b, hid_b)
    grads_of.update(zip(SLOT_ORDER[2:], inner_grads))
    first, second = swap_seq(first), swap_y(second)
    near_back = after(near_back, *inner_grads)
    grad_normed_ffn = own_sum(near_back, back_y, back_x, first, second)

    def line_partial(first, *rest):
        value = grads_of[first]
        for where, expert in enumerate(rest):
            value = jnp.where(line > where, grads_of[expert], value)
        return value.astype(F32)

    def line_step(step, arrived):
        up, down = arrived
        last = LINE - 1
        right = line_partial(*range(last - step, LINE)) + up.astype(F32)
        left = grads_of[step]
        for where in range(step):
            left = jnp.where(line < last - where, grads_of[step - 1 - where], left)
        left = left.astype(F32) + down.astype(F32)
        return right.astype(BF16), left.astype(BF16)

    grad_final = cotangent.astype(F32)
    grad_norm, grad_gain_two = norm_back(middle, gain_two, grad_normed_ffn)
    grad_middle = grad_final + grad_norm
    grad_attn = (BRANCH_SCALE * grad_middle).astype(BF16)
    grad_mixed = contract(grad_attn, output_full, 1, 1).astype(BF16)
    grad_w_output = contract(mixed, grad_attn, 0, 0)
    grad_other = swap_seq(half_of(grad_mixed, 1 - seq))
    far_f, far_f_other, near_f, near_f_other = after(
        (far[0], far[1], near[0], near[1]), grad_mixed
    )
    far_ffn = over_cores(far_f, far_f_other).astype(BF16)
    ffn_y, ffn_x = far_links(far_ffn)
    near_ffn = over_cores(near_f, near_f_other)
    right, left = line_step(1, far_line)
    grad_other = after(grad_other, right, left, far_ffn)
    grad_sorted = to_order(half_of(grad_mixed, seq), grad_other)
    mid_line = (line_up(right), line_down(left))
    grad_query, grad_keys, grad_values = attend_back(
        query, keys, values, grad_sorted, start_column, cos, sin
    )
    (grad_query, grad_keys, grad_values), mid_line, ffn_y, ffn_x = lax.optimization_barrier(
        ((grad_query, grad_keys, grad_values), mid_line, ffn_y, ffn_x)
    )
    right, left = line_step(2, mid_line)
    last_line = (line_up(right), line_down(left))
    first_ffn, second_ffn = near_links(near_ffn, ffn_y, ffn_x)
    first_ffn, second_ffn = swap_seq(first_ffn), swap_y(second_ffn)
    ffn = own_sum(near_ffn, ffn_y, ffn_x, first_ffn, second_ffn)
    output = (middle + BRANCH_SCALE * ffn).astype(BF16)
    grad_qkv = jnp.concatenate([grad_query, grad_keys, grad_values], axis=1)
    grad_qkv = after(grad_qkv, right, left)
    wide = qkv_grad(normed, grad_qkv, grad_gain_two[None, :], shard)
    grad_normed = contract(grad_qkv, w_qkv[:, :qkv_width], 1, 1).astype(BF16)
    sent_normed = swap_seq(from_order(sort_other, grad_normed))
    grad_normed = from_order(sort_own, grad_normed).astype(F32) + sent_normed.astype(F32)
    scale = lax.rsqrt(jnp.mean(inputs * inputs, axis=-1, keepdims=True) + EPSILON)
    unit = inputs * scale
    scaled = grad_normed * gain_one
    inner = jnp.mean(scaled * unit, axis=-1, keepdims=True)
    grad_tokens = grad_middle + scale * (scaled - unit * inner)

    summed_output = lax.psum_scatter(
        grad_w_output.astype(BF16), ("seq", "dp"), scatter_dimension=0, tiled=True
    )

    def chosen(value, which, axis):
        return lax.dynamic_index_in_dim(value, which, axis=axis, keepdims=False)

    kept = chosen(wide, core, 0).astype(F32)
    kept = kept + swap_core(chosen(wide, 1 - core, 0)).astype(F32)
    next_kept = chosen(kept, row_of, 0)
    next_kept = next_kept + swap_y(chosen(kept, 1 - row_of, 0).astype(BF16)).astype(F32)
    next_kept, last_line = lax.optimization_barrier((next_kept, last_line))
    summed = line_scatter(lambda which: chosen(next_kept, which, 1), line)
    part_grads = (
        line_partial(*range(LINE)) + last_line[0].astype(F32) + last_line[1].astype(F32)
    ).astype(BF16)
    same_grads = jnp.where(first_core, part_grads[:, :half], part_grads[:, half : 2 * half])
    cross_grads = jnp.where(first_core, part_grads[:, half : 2 * half], part_grads[:, :half])
    same = both_axes(jnp.concatenate([same_grads, part_grads[:, 2 * half :]], axis=1), straight)
    cross = both_axes(cross_grads, crossed_back)
    grad_w_in = ordered(same[:, :half], cross, 1)
    grad_w_out = same[:, half:].T

    kept_rows = chosen(summed, seq, 0)
    sent_rows = swap_seq(chosen(summed, 1 - seq, 0).astype(BF16)).astype(F32)
    cuts = (q_width, q_width + kv_width, qkv_width)
    pieces = [
        (a, b) for a, b in zip(jnp.split(kept_rows, cuts, axis=1), jnp.split(sent_rows, cuts, axis=1))
    ]
    grad_projections = [ordered(a, b, 1) for a, b in pieces[:3]]
    grad_gain_ffn = (pieces[3][0] + pieces[3][1])[:, 0]
    grad_gain_attn = sum(
        jnp.sum(grad * weight.astype(F32), axis=1)
        for grad, weight in zip(grad_projections, projections)
    ) / gain_attn.astype(F32)
    return (
        output,
        grad_tokens,
        grad_projections[0],
        grad_projections[1],
        grad_projections[2],
        summed_output.astype(F32),
        grad_gain_attn,
        grad_gain_ffn,
        grad_w_in.astype(F32)[None],
        grad_w_out.astype(F32)[None],
    )


def solution(mesh):
    placed = (
        P(("seq", "dp"), None),
        P(("seq", "dp"), None),
        P("dp", None),
        P("dp", None),
        P(("seq", "dp"), None),
        P(("seq", "dp"), None),
        P(("seq", "dp"), None),
        P(("seq", "dp"), None),
        P(("seq", "dp"), None),
        P(("seq", "dp"), None),
        P(("seq", "dp")),
        P(("seq", "dp")),
        P("dp", None, "seq"),
        P("dp", "seq", None),
    )
    return jax.shard_map(
        shards_plane if in_planes(mesh) else shards_general,
        mesh=mesh,
        in_specs=placed,
        out_specs=(
            P(("seq", "dp"), None),
            P(("seq", "dp"), None),
            P(("seq", "dp"), None),
            P(("seq", "dp"), None),
            P(("seq", "dp"), None),
            P(("seq", "dp"), None),
            P(("seq", "dp")),
            P(("seq", "dp")),
            P("dp", None, "seq"),
            P("dp", "seq", None),
        ),
        check_vma=False,
    )
```

```python
import functools

import jax
import jax.numpy as jnp
from jax import lax
from jax.experimental import pallas as pl
from jax.experimental.pallas import tpu as pltpu
from jax.sharding import PartitionSpec as P

QHEADS = 24
KVHEADS = 8
HDIM = 64
FF = 512
TOP = 8


EPSILON = 1e-06
BRANCH_SCALE = 0.22
SCORE_SCALE = 1.0 / 64.0
THETA = 10000.0


def rms_norm(value, gain):
    return value * lax.rsqrt(jnp.mean(value * value, axis=-1, keepdims=True) + EPSILON) * gain


def local_places(placing, seq_lengths):
    ends = jnp.cumsum(seq_lengths)
    segment = jnp.sum((placing[:, None] >= ends[None, :]).astype(jnp.int32), axis=1)
    starts = ends - seq_lengths
    member = segment[:, None] == jnp.arange(seq_lengths.shape[0], dtype=jnp.int32)[None, :]
    start_of = jnp.sum(jnp.where(member, starts[None, :], 0), axis=1)
    return (segment, placing - start_of)


def rotate(values, place, direction):
    half = values.shape[-1] // 2
    freqs = jnp.power(THETA, -jnp.arange(half, dtype=jnp.float32) * 2.0 / values.shape[-1])
    angles = place.astype(jnp.float32)[:, None] * freqs[None, :]
    cosine = jnp.cos(angles)[:, None, :]
    sine = direction * jnp.sin(angles)[:, None, :]
    first = values[..., :half]
    second = values[..., half:]
    return jnp.concatenate(
        [first * cosine - second * sine, second * cosine + first * sine], axis=-1
    )


def shards_general(
    tokens,
    cotangent,
    positions,
    lengths,
    routes,
    logits,
    w_query,
    w_key,
    w_value,
    w_output,
    gain_attn,
    gain_ffn,
    w_in,
    w_out,
):
    seq_count = lax.axis_size("seq")
    data_count = lax.axis_size("dp")
    tok_count = tokens.shape[0]
    group_len = positions.shape[1]
    local_experts = w_in.shape[0]
    experts_all = local_experts * data_count
    capacity = min(tok_count, 5 * tok_count * TOP // (4 * experts_all))
    heads_local = QHEADS // seq_count
    kv_local = KVHEADS // seq_count
    ratio = QHEADS // KVHEADS
    width = tokens.shape[1]
    query_full, key_full, value_full, output_full, gain_one, gain_two = (
        lax.all_gather(w_query, ("seq", "dp"), axis=0, tiled=True),
        lax.all_gather(w_key, ("seq", "dp"), axis=0, tiled=True),
        lax.all_gather(w_value, ("seq", "dp"), axis=0, tiled=True),
        lax.all_gather(w_output, ("seq", "dp"), axis=0, tiled=True),
        lax.all_gather(gain_attn, ("seq", "dp"), axis=0, tiled=True),
        lax.all_gather(gain_ffn, ("seq", "dp"), axis=0, tiled=True),
    )
    in_full, out_full = (
        lax.all_gather(w_in, "seq", axis=2, tiled=True),
        lax.all_gather(w_out, "seq", axis=1, tiled=True),
    )
    gain_one = gain_one.astype(jnp.float32)
    gain_two = gain_two.astype(jnp.float32)
    segment, place = local_places(positions[0], lengths[0])
    my_start = lax.axis_index("seq") * tok_count
    my_place = lax.dynamic_slice_in_dim(place, my_start, tok_count)
    inputs = tokens.astype(jnp.float32)
    normed = rms_norm(inputs, gain_one).astype(jnp.bfloat16)
    query_pre = jnp.dot(normed, query_full, preferred_element_type=jnp.float32)
    key_pre = jnp.dot(normed, key_full, preferred_element_type=jnp.float32)
    query_rot = (
        rotate(query_pre.reshape(tok_count, QHEADS, HDIM), my_place, 1.0)
        .reshape(tok_count, QHEADS * HDIM)
        .astype(jnp.bfloat16)
    )
    key_rot = (
        rotate(key_pre.reshape(tok_count, KVHEADS, HDIM), my_place, 1.0)
        .reshape(tok_count, KVHEADS * HDIM)
        .astype(jnp.bfloat16)
    )
    value_low = jnp.dot(normed, value_full, preferred_element_type=jnp.float32).astype(jnp.bfloat16)
    query_heads, key_heads, value_heads = (
        lax.all_to_all(query_rot, "seq", split_axis=1, concat_axis=0, tiled=True),
        lax.all_to_all(key_rot, "seq", split_axis=1, concat_axis=0, tiled=True),
        lax.all_to_all(value_low, "seq", split_axis=1, concat_axis=0, tiled=True),
    )
    keys_three = key_heads.reshape(group_len, kv_local, HDIM)
    values_three = value_heads.reshape(group_len, kv_local, HDIM)
    length = min(512, group_len)
    count = group_len // length

    def scores_of(query_block, seg_block, place_block):
        grouped = query_block.reshape(length, kv_local, ratio, HDIM)
        raw_scores = (
            jnp.einsum("qgrd,kgd->grqk", grouped, keys_three, preferred_element_type=jnp.float32)
            * SCORE_SCALE
        )
        allowed = (seg_block[:, None] == segment[None, :]) & (
            place[None, :] <= place_block[:, None]
        )
        return jnp.where(allowed[None, None], raw_scores, -1e30)

    def forward_block(pieces):
        query_block, seg_block, place_block = pieces
        scores = scores_of(query_block, seg_block, place_block)
        highest = jnp.max(scores, axis=-1, keepdims=True)
        expon = jnp.exp(scores - highest)
        totals = jnp.sum(expon, axis=-1, keepdims=True)
        probs = expon / totals
        mixed = jnp.einsum(
            "grqk,kgd->qgrd",
            probs.astype(jnp.bfloat16),
            values_three,
            preferred_element_type=jnp.float32,
        )
        return (
            mixed.reshape(length, heads_local * HDIM).astype(jnp.bfloat16),
            highest + jnp.log(totals),
            probs,
        )

    query_blocks = query_heads.reshape(count, length, heads_local * HDIM)
    seg_blocks = segment.reshape(count, length)
    place_blocks = place.reshape(count, length)
    block_args = (query_blocks, seg_blocks, place_blocks)

    def forward_light(pieces):
        mixed, lse_part, unused_probs = forward_block(pieces)
        return (mixed, lse_part)

    mixed_blocks, lse_blocks = lax.map(forward_light, block_args)
    mixed_heads = mixed_blocks.reshape(group_len, heads_local * HDIM)
    mixed_tokens = lax.all_to_all(mixed_heads, "seq", split_axis=0, concat_axis=1, tiled=True)
    attn = jnp.dot(mixed_tokens, output_full, preferred_element_type=jnp.float32)
    middle = inputs + BRANCH_SCALE * attn
    normed_ffn = rms_norm(middle, gain_two).astype(jnp.bfloat16)
    chosen = routes.reshape(-1)
    onehot = (chosen[:, None] == jnp.arange(experts_all, dtype=jnp.int32)[None, :]).astype(
        jnp.int32
    )
    ranking = jnp.sum(jnp.cumsum(onehot, axis=0) * onehot, axis=1) - 1
    target = chosen * capacity + ranking
    token_of = jnp.arange(tok_count * TOP, dtype=jnp.int32) // TOP
    gates = jax.nn.softmax(logits, axis=-1)
    source = jnp.full((experts_all * capacity,), tok_count, jnp.int32).at[target].set(token_of)
    slot_gate = jnp.zeros((experts_all * capacity,), jnp.float32).at[target].set(gates.reshape(-1))
    padded = jnp.concatenate([normed_ffn, jnp.zeros((1, width), jnp.bfloat16)], axis=0)
    outgoing = padded[source].reshape(data_count, local_experts * capacity, width)

    def expert_layout(arrived):
        return jnp.swapaxes(
            arrived.reshape(data_count, local_experts, capacity, width), 0, 1
        ).reshape(local_experts, data_count * capacity, width)

    def home_layout(values):
        return jnp.swapaxes(
            values.reshape(local_experts, data_count, capacity, width), 0, 1
        ).reshape(data_count, local_experts * capacity, width)

    def expert_forward(expert_rows):
        both = jnp.einsum("erd,edf->erf", expert_rows, in_full, preferred_element_type=jnp.float32)
        hidden = (jax.nn.silu(both[..., :FF]) * both[..., FF:]).astype(jnp.bfloat16)
        return (both, hidden)

    expert_rows = expert_layout(
        lax.all_to_all(outgoing, "dp", split_axis=0, concat_axis=0, tiled=True)
    )
    both, hidden = expert_forward(expert_rows)
    result = jnp.einsum(
        "erf,efd->erd", hidden, out_full, preferred_element_type=jnp.float32
    ).astype(jnp.bfloat16)
    returned = lax.all_to_all(
        home_layout(result), "dp", split_axis=0, concat_axis=0, tiled=True
    ).reshape(experts_all * capacity, width)
    picked = returned[target].reshape(tok_count, TOP, width).astype(jnp.float32)
    ffn = jnp.sum(picked * gates[:, :, None], axis=1)
    final = middle + BRANCH_SCALE * ffn
    output = final.astype(jnp.bfloat16)
    grad_final = cotangent.astype(jnp.float32)
    padded_grad = jnp.concatenate(
        [BRANCH_SCALE * grad_final, jnp.zeros((1, width), jnp.float32)], axis=0
    )
    grad_slots = (slot_gate[:, None] * padded_grad[source]).astype(jnp.bfloat16)
    grad_result = expert_layout(
        lax.all_to_all(
            grad_slots.reshape(data_count, local_experts * capacity, width),
            "dp",
            split_axis=0,
            concat_axis=0,
            tiled=True,
        )
    )
    rows_back = expert_layout(
        lax.all_to_all(outgoing, "dp", split_axis=0, concat_axis=0, tiled=True)
    )
    both_back, hidden_back = expert_forward(rows_back)
    grad_hidden = jnp.einsum(
        "erd,efd->erf", grad_result, out_full, preferred_element_type=jnp.float32
    )
    gate_part = both_back[..., :FF]
    up_part = both_back[..., FF:]
    sigma = jax.nn.sigmoid(gate_part)
    grad_gate = grad_hidden * up_part * sigma * (1.0 + gate_part * (1.0 - sigma))
    grad_up = grad_hidden * gate_part * sigma
    grad_both = jnp.concatenate([grad_gate, grad_up], axis=-1).astype(jnp.bfloat16)
    grad_out_local = jnp.einsum(
        "erf,erd->efd", hidden_back, grad_result, preferred_element_type=jnp.float32
    )
    grad_in_local = jnp.einsum(
        "erd,erf->edf", rows_back, grad_both, preferred_element_type=jnp.float32
    )
    grad_rows = jnp.einsum(
        "erf,edf->erd", grad_both, in_full, preferred_element_type=jnp.float32
    ).astype(jnp.bfloat16)
    grad_home = lax.all_to_all(
        home_layout(grad_rows), "dp", split_axis=0, concat_axis=0, tiled=True
    ).reshape(experts_all * capacity, width)
    grad_normed_ffn = jnp.sum(
        grad_home[target].reshape(tok_count, TOP, width).astype(jnp.float32), axis=1
    )
    grad_w_in, grad_w_out = (
        lax.psum_scatter(
            grad_in_local.astype(jnp.bfloat16), "seq", scatter_dimension=2, tiled=True
        ).astype(jnp.float32),
        lax.psum_scatter(
            grad_out_local.astype(jnp.bfloat16), "seq", scatter_dimension=1, tiled=True
        ).astype(jnp.float32),
    )
    unused_norm, norm_pull = jax.vjp(rms_norm, middle, gain_two)
    grad_middle_norm, grad_gain_two = norm_pull(grad_normed_ffn)
    grad_middle = grad_final + grad_middle_norm
    grad_attn = (BRANCH_SCALE * grad_middle).astype(jnp.bfloat16)
    grad_w_output = jnp.einsum(
        "te,td->ed", mixed_tokens, grad_attn, preferred_element_type=jnp.float32
    )
    grad_mixed = jnp.einsum(
        "td,ed->te", grad_attn, output_full, preferred_element_type=jnp.float32
    ).astype(jnp.bfloat16)
    grad_mixed_heads = lax.all_to_all(grad_mixed, "seq", split_axis=1, concat_axis=0, tiled=True)
    grad_blocks = grad_mixed_heads.reshape(count, length, heads_local * HDIM)
    back_args = (query_blocks, seg_blocks, place_blocks, lse_blocks, grad_blocks)

    def backward_block(carry, pieces):
        grad_keys, grad_values = carry
        query_block, seg_block, place_block, lse_block, grad_block = pieces[:5]
        probs = jnp.exp(scores_of(query_block, seg_block, place_block) - lse_block)
        grad_out = grad_block.reshape(length, kv_local, ratio, HDIM)
        grad_probs = jnp.einsum(
            "qgrd,kgd->grqk", grad_out, values_three, preferred_element_type=jnp.float32
        )
        grad_scores = (
            probs * (grad_probs - jnp.sum(probs * grad_probs, axis=-1, keepdims=True))
        ).astype(jnp.bfloat16)
        grad_query = SCORE_SCALE * jnp.einsum(
            "grqk,kgd->qgrd", grad_scores, keys_three, preferred_element_type=jnp.float32
        )
        grouped = query_block.reshape(length, kv_local, ratio, HDIM)
        grad_keys = grad_keys + SCORE_SCALE * jnp.einsum(
            "grqk,qgrd->kgd", grad_scores, grouped, preferred_element_type=jnp.float32
        )
        grad_values = grad_values + jnp.einsum(
            "grqk,qgrd->kgd",
            probs.astype(jnp.bfloat16),
            grad_out,
            preferred_element_type=jnp.float32,
        )
        return (
            (grad_keys, grad_values),
            grad_query.reshape(length, heads_local * HDIM).astype(jnp.bfloat16),
        )

    empty_keys = jnp.zeros((group_len, kv_local, HDIM), jnp.float32)
    (grad_keys, grad_values), grad_query_blocks = lax.scan(
        backward_block, (empty_keys, empty_keys), back_args
    )
    grad_query_heads = grad_query_blocks.reshape(group_len, heads_local * HDIM)
    grad_key_heads = grad_keys.reshape(group_len, kv_local * HDIM).astype(jnp.bfloat16)
    grad_value_heads = grad_values.reshape(group_len, kv_local * HDIM).astype(jnp.bfloat16)
    grad_query_tok, grad_key_tok, grad_value_tok = (
        lax.all_to_all(grad_query_heads, "seq", split_axis=0, concat_axis=1, tiled=True),
        lax.all_to_all(grad_key_heads, "seq", split_axis=0, concat_axis=1, tiled=True),
        lax.all_to_all(grad_value_heads, "seq", split_axis=0, concat_axis=1, tiled=True),
    )
    grad_query_pre = (
        rotate(grad_query_tok.astype(jnp.float32).reshape(tok_count, QHEADS, HDIM), my_place, -1.0)
        .reshape(tok_count, QHEADS * HDIM)
        .astype(jnp.bfloat16)
    )
    grad_key_pre = (
        rotate(grad_key_tok.astype(jnp.float32).reshape(tok_count, KVHEADS, HDIM), my_place, -1.0)
        .reshape(tok_count, KVHEADS * HDIM)
        .astype(jnp.bfloat16)
    )
    grad_w_query = jnp.einsum(
        "td,te->de", normed, grad_query_pre, preferred_element_type=jnp.float32
    )
    grad_w_key = jnp.einsum("td,te->de", normed, grad_key_pre, preferred_element_type=jnp.float32)
    grad_w_value = jnp.einsum(
        "td,te->de", normed, grad_value_tok, preferred_element_type=jnp.float32
    )
    grad_normed = jnp.einsum(
        "te,de->td", grad_query_pre, query_full, preferred_element_type=jnp.float32
    )
    grad_normed = grad_normed + jnp.einsum(
        "te,de->td", grad_key_pre, key_full, preferred_element_type=jnp.float32
    )
    grad_normed = grad_normed + jnp.einsum(
        "te,de->td", grad_value_tok, value_full, preferred_element_type=jnp.float32
    )
    unused_first, first_pull = jax.vjp(rms_norm, inputs, gain_one)
    grad_inputs_norm, grad_gain_one = first_pull(grad_normed)
    grad_tokens = grad_middle + grad_inputs_norm
    summed = (
        lax.psum_scatter(grad_w_query, ("seq", "dp"), scatter_dimension=0, tiled=True),
        lax.psum_scatter(grad_w_key, ("seq", "dp"), scatter_dimension=0, tiled=True),
        lax.psum_scatter(grad_w_value, ("seq", "dp"), scatter_dimension=0, tiled=True),
        lax.psum_scatter(grad_w_output, ("seq", "dp"), scatter_dimension=0, tiled=True),
        lax.psum_scatter(grad_gain_one, ("seq", "dp"), scatter_dimension=0, tiled=True),
        lax.psum_scatter(grad_gain_two, ("seq", "dp"), scatter_dimension=0, tiled=True),
    )
    return (
        output,
        grad_tokens,
        summed[0],
        summed[1],
        summed[2],
        summed[3],
        summed[4],
        summed[5],
        grad_w_in,
        grad_w_out,
    )


BF16 = jnp.bfloat16
F32 = jnp.float32
LINE = 4
PAD = 128
VMEM_BYTES = 60 * 1024 * 1024


def in_planes(mesh):
    return mesh.shape["seq"] == 2 and mesh.shape["dp"] == 4 * LINE


def swap_seq(value):
    return lax.ppermute(value, "seq", [(0, 1), (1, 0)])


def swap_dp(value, mask):
    return lax.ppermute(value, "dp", [(i, i ^ mask) for i in range(4 * LINE)])


def swap_core(value):
    return swap_dp(value, 1)


def swap_y(value):
    return swap_dp(value, 2)


def line_up(value):
    return lax.ppermute(value, "dp", [(i, i + 4) for i in range(4 * LINE - 4)])


def line_down(value):
    return lax.ppermute(value, "dp", [(i, i - 4) for i in range(4, 4 * LINE)])


def after(value, *others):
    return lax.optimization_barrier((value,) + others)[0]


def line_scatter(take, place):
    up = down = None
    for step in range(LINE - 1):
        far = jnp.minimum(LINE - 1 - step + place, LINE - 1)
        near = jnp.maximum(step - LINE + 1 + place, 0)
        right, left = take(far), take(near)
        if up is not None:
            right = right + up.astype(F32)
            left = left + down.astype(F32)
        up = line_up(right.astype(BF16))
        down = line_down(left.astype(BF16))
    return take(place) + up.astype(F32) + down.astype(F32)


def near_pieces(own, own_x):
    return swap_seq(own_x), swap_y(own)


def far_pieces(near_x, near_y):
    half = near_x.shape[0] // 2
    return swap_y(near_x[:half]), swap_seq(near_y[half:])


def with_cores(*pieces):
    return pieces + tuple(swap_core(piece) for piece in pieces)


def over_cores(mine, others):
    return mine.astype(F32) + swap_core(others).astype(F32)


def far_links(far):
    half = far.shape[0] // 2
    return swap_y(far[:half]), swap_seq(far[half:])


def near_links(near, from_y, from_x):
    half = from_y.shape[0] // 2
    first = (near[:half] + from_y[half:].astype(F32)).astype(BF16)
    second = (near[half : 2 * half] + from_x[half:].astype(F32)).astype(BF16)
    return first, second


def own_sum(near, from_y, from_x, first, second):
    half = from_y.shape[0] // 2
    low = near[2 * half : 3 * half] + from_y[:half].astype(F32) + first.astype(F32)
    high = near[3 * half :] + from_x[:half].astype(F32) + second.astype(F32)
    return jnp.concatenate([low, high], axis=0)


def turned(values, cos, sin, direction):
    lanes = values.shape[1]
    place = lax.broadcasted_iota(jnp.int32, values.shape, 1) % HDIM
    swapped = jnp.where(
        place < HDIM // 2,
        pltpu.roll(values, lanes - HDIM // 2, 1),
        pltpu.roll(values, HDIM // 2, 1),
    )
    times = lanes // cos.shape[1]
    cos = jnp.concatenate([cos] * times, axis=1)
    sin = jnp.concatenate([sin] * times, axis=1)
    if direction > 0:
        return values * cos + swapped * sin
    return values * cos - swapped * sin


def place_shards(place_ref, own_ref, other_ref, shard, store):
    for core in range(2):
        source = other_ref if core else own_ref
        for row in range(2):
            for line in range(LINE):
                index = (place_ref[0] ^ line) * 4 + (place_ref[1] ^ row) * 2 + (place_ref[2] ^ core)
                store(source, (row * LINE + line) * shard, pl.multiple_of(index * shard, shard))


def qkv_kernel(x_ref, gain_ref, w_ref, cos_ref, sin_ref, h_ref, q_ref, k_ref, v_ref):
    value = x_ref[...].astype(F32)
    scale = lax.rsqrt(jnp.mean(value * value, axis=-1, keepdims=True) + EPSILON)
    normed = (value * scale * gain_ref[...]).astype(BF16)
    h_ref[...] = normed
    both = jnp.dot(normed, w_ref[...], preferred_element_type=F32)
    q_width, kv_heads = q_ref.shape[1], k_ref.shape[0]
    kv_width = kv_heads * HDIM
    spun = turned(both[:, : q_width + kv_width], cos_ref[...], sin_ref[...], 1)
    q_ref[...] = (spun[:, :q_width] * SCORE_SCALE).astype(BF16)
    for head in range(kv_heads):
        low = q_width + head * HDIM
        k_ref[head] = spun[:, low : low + HDIM].astype(BF16)
        low = low + kv_width
        v_ref[head] = both[:, low : low + HDIM].astype(BF16)


def project(x_sorted, gain, weights, cos, sin, q_width, kv_heads):
    rows, width = x_sorted.shape
    tile = 256
    columns = q_width + 2 * kv_heads * HDIM

    def row_block(lanes):
        return pl.BlockSpec((tile, lanes), lambda i: (i, 0))

    heads = pl.BlockSpec((kv_heads, tile, HDIM), lambda i: (0, i, 0))
    return pl.pallas_call(
        qkv_kernel,
        grid=(rows // tile,),
        in_specs=[
            row_block(width),
            pl.BlockSpec((1, width), lambda i: (0, 0)),
            pl.BlockSpec((width, columns), lambda i: (0, 0)),
            row_block(cos.shape[1]),
            row_block(cos.shape[1]),
        ],
        out_specs=[row_block(width), row_block(q_width), heads, heads],
        out_shape=[
            jax.ShapeDtypeStruct((rows, width), BF16),
            jax.ShapeDtypeStruct((rows, q_width), BF16),
            jax.ShapeDtypeStruct((kv_heads, rows, HDIM), BF16),
            jax.ShapeDtypeStruct((kv_heads, rows, HDIM), BF16),
        ],
        compiler_params=pltpu.CompilerParams(vmem_limit_bytes=VMEM_BYTES),
        cost_estimate=pl.CostEstimate(
            flops=rows * width * columns // 8,
            bytes_accessed=rows * width + width * columns,
            transcendentals=rows,
        ),
        name="project",
    )(x_sorted, gain, weights, cos, sin)


def mix_kernel(
    place_ref, mine_ref, theirs_ref, x_ref, gain_ref, own_ref, other_ref, m_ref, h_ref, w_ref
):
    shard = own_ref.shape[0] // (4 * LINE)
    half = w_ref.shape[1]

    @pl.when(pl.program_id(0) == 0)
    def _():
        for seq in range(2):

            def store(source, low, place):
                low = low + seq * 2 * LINE * shard
                w_ref[seq, pl.ds(place, shard), :] = source[low : low + shard, :]

            place_shards(place_ref, own_ref, other_ref, shard, store)

    mixed = jnp.dot(mine_ref[...], w_ref[0], preferred_element_type=F32)
    mixed = mixed + jnp.dot(theirs_ref[...], w_ref[1], preferred_element_type=F32)
    value = x_ref[...].astype(F32) + BRANCH_SCALE * mixed
    m_ref[...] = value
    scale = lax.rsqrt(jnp.mean(value * value, axis=-1, keepdims=True) + EPSILON)
    h_ref[...] = (value * scale * gain_ref[1:2, :]).astype(BF16)


def mix(places, mine, theirs, tokens, gains, own, other):
    rows, width = tokens.shape
    half = mine.shape[1]
    tile = 256

    def row_block(lanes):
        return pl.BlockSpec((tile, lanes), lambda i, p: (i, 0))

    def whole(shape):
        return pl.BlockSpec(shape, lambda i, p: (0,) * len(shape))

    return pl.pallas_call(
        mix_kernel,
        grid_spec=pltpu.PrefetchScalarGridSpec(
            num_scalar_prefetch=1,
            grid=(rows // tile,),
            in_specs=[
                row_block(half), row_block(half), row_block(width), whole(gains.shape),
                whole(own.shape), whole(other.shape),
            ],
            out_specs=[row_block(width), row_block(width), whole((2, half, width))],
        ),
        out_shape=[
            jax.ShapeDtypeStruct((rows, width), F32),
            jax.ShapeDtypeStruct((rows, width), BF16),
            jax.ShapeDtypeStruct((2, half, width), BF16),
        ],
        compiler_params=pltpu.CompilerParams(vmem_limit_bytes=VMEM_BYTES),
        cost_estimate=pl.CostEstimate(
            flops=rows * width * width // 8, bytes_accessed=rows * width, transcendentals=rows
        ),
        name="mix",
    )(places, mine, theirs, tokens, gains, own, other)


def token_grad_kernel(dq_ref, dk_ref, dv_ref, w_ref, own_ref, other_ref, mine_ref, sent_ref):
    q_width, kv_width = dq_ref.shape[1], dk_ref.shape[1]
    cuts = (0, q_width, q_width + kv_width, q_width + 2 * kv_width)
    grad = contract(dq_ref[...], w_ref[:, cuts[0] : cuts[1]], 1, 1)
    grad = grad + contract(dk_ref[...], w_ref[:, cuts[1] : cuts[2]], 1, 1)
    grad = (grad + contract(dv_ref[...], w_ref[:, cuts[2] : cuts[3]], 1, 1)).astype(BF16)
    for place_ref, out_ref in ((other_ref, sent_ref), (own_ref, mine_ref)):
        shape = (place_ref.shape[0], grad.shape[0])
        picked = lax.broadcasted_iota(jnp.int32, shape, 1) == place_ref[...]
        picked = jnp.where(picked, 1.0, 0.0).astype(BF16)
        out_ref[...] = jnp.dot(picked, grad, preferred_element_type=F32).astype(BF16)


def token_grad(grads, weights, own_places, other_places):
    rows, count = grads[0].shape[0], own_places.shape[0]
    width = weights.shape[0]
    columns = sum(grad.shape[1] for grad in grads)
    tile = width // 3

    def whole(array):
        return pl.BlockSpec(array.shape, lambda i: (0, 0))

    block = pl.BlockSpec((count, tile), lambda i: (0, i))
    return pl.pallas_call(
        token_grad_kernel,
        grid=(3,),
        in_specs=[whole(grad) for grad in grads]
        + [pl.BlockSpec((tile, columns), lambda i: (i, 0)), whole(own_places), whole(other_places)],
        out_specs=[block, block],
        out_shape=[jax.ShapeDtypeStruct((count, width), BF16)] * 2,
        compiler_params=pltpu.CompilerParams(vmem_limit_bytes=VMEM_BYTES),
        cost_estimate=pl.CostEstimate(
            flops=rows * width * columns // 8, bytes_accessed=rows * width, transcendentals=0
        ),
        name="token_grad",
    )(*grads, weights, own_places, other_places)


Q_TILE = 256


def windows(rows):
    longest = rows // 2
    for start in range(0, rows, Q_TILE):
        low = max(0, start - longest + 1) // Q_TILE * Q_TILE
        yield start, low, start + Q_TILE


def allowed_keys(start_ref, row, low, high):
    shape = (Q_TILE, high - low)
    rows = lax.broadcasted_iota(jnp.int32, shape, 0) + row
    keys = lax.broadcasted_iota(jnp.int32, shape, 1) + low
    return (keys <= rows) & (keys >= start_ref[row : row + Q_TILE, :])


def contract(left, right, left_dim, right_dim):
    return lax.dot_general(
        left, right, (((left_dim,), (right_dim,)), ((), ())), preferred_element_type=F32
    )


def probabilities(query, keys, allowed):
    scores = jnp.where(allowed, contract(query, keys, 1, 1), -1e30)
    expon = jnp.exp(scores - jnp.max(scores, axis=-1, keepdims=True))
    return expon * (1.0 / jnp.sum(expon, axis=-1, keepdims=True))


def attend_kernel(base, q_ref, k_ref, v_ref, start_ref, o_ref):
    pair = pl.program_id(0) + base
    ratio = QHEADS // KVHEADS
    for row, low, high in windows(q_ref.shape[0]):
        allowed = allowed_keys(start_ref, row, low, high)
        for side in range(2):
            head = (2 * pair + side) // ratio
            lanes = slice(side * HDIM, (side + 1) * HDIM)
            probs = probabilities(
                q_ref[row : row + Q_TILE, lanes], k_ref[head, low:high, :], allowed
            )
            mixed = contract(probs.astype(BF16), v_ref[head, low:high, :], 1, 0)
            o_ref[row : row + Q_TILE, lanes] = mixed.astype(BF16)


def attention_cost(rows, heads, products):
    area = sum(Q_TILE * (high - low) for _, low, high in windows(rows))
    return pl.CostEstimate(
        flops=products * heads * area * 16,
        bytes_accessed=8 * rows * heads * HDIM,
        transcendentals=heads * area,
    )


def attend(query, keys, values, starts, base, pairs):
    rows = query.shape[0]
    pair_block = pl.BlockSpec((rows, 2 * HDIM), lambda j: (0, j + base))
    whole = pl.BlockSpec(keys.shape, lambda j: (0, 0, 0))
    return pl.pallas_call(
        functools.partial(attend_kernel, base),
        grid=(pairs,),
        in_specs=[pair_block, whole, whole, pl.BlockSpec((rows, 1), lambda j: (0, 0))],
        out_specs=pl.BlockSpec((rows, 2 * HDIM), lambda j: (0, j)),
        out_shape=jax.ShapeDtypeStruct((rows, pairs * 2 * HDIM), BF16),
        compiler_params=pltpu.CompilerParams(vmem_limit_bytes=VMEM_BYTES),
        cost_estimate=attention_cost(rows, 2 * pairs, 2),
        name="attend",
    )(query, keys, values, starts)


def attend_back_kernel(
    q_ref, k_ref, v_ref, d_ref, start_ref, cos_ref, sin_ref,
    dq_ref, dk_ref, dv_ref, dk_sum, dv_sum,
):
    pair = pl.program_id(0)
    ratio = QHEADS // KVHEADS

    @pl.when(pair == 0)
    def _():
        dk_sum[...] = jnp.zeros_like(dk_sum)
        dv_sum[...] = jnp.zeros_like(dv_sum)

    for row, low, high in windows(q_ref.shape[0]):
        allowed = allowed_keys(start_ref, row, low, high)
        grads = []
        for side in range(2):
            head = (2 * pair + side) // ratio
            lanes = slice(side * HDIM, (side + 1) * HDIM)
            query = q_ref[row : row + Q_TILE, lanes]
            keys = k_ref[head, low:high, :]
            probs = probabilities(query, keys, allowed)
            grad_out = d_ref[row : row + Q_TILE, lanes]
            grad_probs = contract(grad_out, v_ref[head, low:high, :], 1, 1)
            inner = jnp.sum(probs * grad_probs, axis=-1, keepdims=True)
            grad_scores = (probs * (grad_probs - inner)).astype(BF16)
            grads.append(contract(grad_scores, keys, 1, 0) * SCORE_SCALE)
            dk_sum[head, low:high, :] += contract(grad_scores, query, 0, 0)
            dv_sum[head, low:high, :] += contract(probs.astype(BF16), grad_out, 0, 0)
        grad_query = jnp.concatenate(grads, axis=1).astype(BF16).astype(F32)
        dq_ref[row : row + Q_TILE, :] = turned(
            grad_query,
            cos_ref[row : row + Q_TILE, :],
            sin_ref[row : row + Q_TILE, :],
            -1,
        ).astype(BF16)

    @pl.when(pair == pl.num_programs(0) - 1)
    def _():
        heads = range(dk_sum.shape[0])
        grad_keys = jnp.concatenate([dk_sum[head] for head in heads], axis=1)
        grad_keys = grad_keys.astype(BF16).astype(F32)
        dk_ref[...] = turned(grad_keys, cos_ref[...], sin_ref[...], -1).astype(BF16)
        dv_ref[...] = jnp.concatenate([dv_sum[head] for head in heads], axis=1).astype(BF16)


def attend_back(query, keys, values, grad_out, starts, cos, sin):
    rows, lanes = query.shape
    pairs = lanes // (2 * HDIM)
    kv_heads = keys.shape[0]
    pair_block = pl.BlockSpec((rows, 2 * HDIM), lambda j: (0, j))
    whole = pl.BlockSpec(keys.shape, lambda j: (0, 0, 0))

    def fixed(lanes_of):
        return pl.BlockSpec((rows, lanes_of), lambda j: (0, 0))

    flat = kv_heads * HDIM
    return pl.pallas_call(
        attend_back_kernel,
        grid=(pairs,),
        in_specs=[
            pair_block, whole, whole, pair_block, fixed(1), fixed(2 * HDIM), fixed(2 * HDIM),
        ],
        out_specs=[pair_block, fixed(flat), fixed(flat)],
        out_shape=[
            jax.ShapeDtypeStruct(query.shape, BF16),
            jax.ShapeDtypeStruct((rows, flat), BF16),
            jax.ShapeDtypeStruct((rows, flat), BF16),
        ],
        scratch_shapes=[pltpu.VMEM(keys.shape, F32), pltpu.VMEM(keys.shape, F32)],
        compiler_params=pltpu.CompilerParams(vmem_limit_bytes=VMEM_BYTES),
        cost_estimate=attention_cost(rows, 2 * pairs, 5),
        name="attend_back",
    )(query, keys, values, grad_out, starts, cos, sin)


SLOTS = 2 * LINE - 1
SLOT_ORDER = (0, 3, 1, 2)
OWN, NEAR_X, NEAR_Y, FAR_Y, FAR_X = range(5)
FAR_TILES = (((NEAR_Y, 0), (FAR_Y, 0)), ((NEAR_X, 1), (FAR_X, 0)))
NEAR_TILES = (((NEAR_X, 0), (NEAR_Y, 1)), ((OWN, 0), (OWN, 1)))


def used_pieces(tiles):
    return sorted({piece for tile in tiles for piece, _ in tile})


def experts_kernel(tiles, half_rows, place_ref, *refs):
    used = used_pieces(tiles)
    sides = 2 * len(used)
    h_pieces, g_pieces, slots = refs[:sides], refs[sides : 2 * sides], refs[2 * sides : 2 * sides + SLOTS]
    select_ref = refs[2 * sides + SLOTS]
    (
        f_mine, f_other, d_mine, d_other, hid_a, hid_b, du_a, du_b, hcopy_ref, gcopy_ref,
        w_in, w_out, h_buf, g_buf, hidden, du_all, weight_sems, row_sems,
    ) = refs[-18:]
    width = h_buf.shape[2]
    half = slots[0].shape[1] // 3
    part = 2 * half
    step = pl.program_id(0)
    steps = 2 * len(tiles)

    def weight_copies(spot, slot):
        return (
            pltpu.make_async_copy(
                slots[slot].at[:, :part],
                w_in.at[:, spot * part : (spot + 1) * part],
                weight_sems.at[0, spot],
            ),
            pltpu.make_async_copy(
                slots[slot].at[:, part:],
                w_out.at[:, spot * half : (spot + 1) * half],
                weight_sems.at[1, spot],
            ),
        )

    def row_copies(number, buffer):
        side, tile = divmod(number, len(tiles))
        copies = []
        for spot, (piece, part_of) in enumerate(tiles[tile]):
            index = side * len(used) + used.index(piece)
            for kind, (pieces, held) in enumerate(((h_pieces, h_buf), (g_pieces, g_buf))):
                copies.append(
                    pltpu.make_async_copy(
                        pieces[index].at[pl.ds(part_of * half_rows, half_rows), :],
                        held.at[buffer, pl.ds(spot * half_rows, half_rows), :],
                        row_sems.at[buffer, 2 * kind + spot],
                    )
                )
        return copies

    def fetch(wanted, buffer):
        for number in range(steps):

            @pl.when(wanted == number)
            def _():
                for copy in row_copies(number, buffer):
                    copy.start()

    buffer = step % 2

    @pl.when(step == 0)
    def _():
        fetch(step, 0)
        for spot, expert in enumerate(SLOT_ORDER):
            for slot in range(expert, expert + LINE):

                @pl.when(slot == LINE - 1 + expert - place_ref[0])
                def _():
                    for copy in weight_copies(spot, slot):
                        copy.start()

        for spot in range(LINE):
            for copy in weight_copies(spot, LINE - 1):
                copy.wait()

    @pl.when(step + 1 < steps)
    def _():
        fetch(step + 1, 1 - buffer)

    for copy in row_copies(0, buffer):
        copy.wait()

    rows = h_buf[buffer]
    grads = g_buf[buffer, :, :width]
    hcopy_ref[...] = rows
    gcopy_ref[...] = grads
    gates = jnp.dot(g_buf[buffer, :, width:], select_ref[...], preferred_element_type=F32)
    for spot in range(LINE):
        units = slice(spot * half, (spot + 1) * half)
        both = jnp.dot(
            rows, w_in[:, spot * part : (spot + 1) * part], preferred_element_type=F32
        )
        back = jnp.dot(grads, w_out[:, units], preferred_element_type=F32)
        gate = gates[:, units]
        first, second = both[:, :half], both[:, half:]
        sigma = jax.nn.sigmoid(first)
        silu = first * sigma
        hidden[:, units] = (gate * (silu * second)).astype(BF16)
        back = back * (BRANCH_SCALE * gate)
        d_first = back * second * (sigma * (1.0 + first * (1.0 - sigma)))
        d_second = back * silu
        du_all[:, spot * part : spot * part + half] = d_first.astype(BF16)
        du_all[:, spot * part + half : (spot + 1) * part] = d_second.astype(BF16)
    hid_a[...] = hidden[:, : 2 * half]
    hid_b[...] = hidden[:, 2 * half :]
    du_a[...] = du_all[:, : 2 * part]
    du_b[...] = du_all[:, 2 * part :]
    ffn = contract(hidden[...], w_out[...], 1, 1).astype(BF16)
    back_rows = contract(du_all[...], w_in[...], 1, 1).astype(BF16)

    @pl.when(step < len(tiles))
    def _():
        f_mine[...] = ffn
        d_mine[...] = back_rows

    @pl.when(step >= len(tiles))
    def _():
        f_other[...] = ffn
        d_other[...] = back_rows


def run_experts(tiles, place, row_pieces, grad_pieces, slots, select, base, kept):
    used = used_pieces(tiles)
    sides = len(row_pieces) // 2
    wanted = used + [sides + piece for piece in used]
    rows = [row_pieces[piece] for piece in wanted]
    grads = [grad_pieces[piece] for piece in wanted]
    tile, width = row_pieces[OWN].shape
    wide = grad_pieces[OWN].shape[1]
    half = slots[0].shape[1] // 3
    part = 2 * half
    count = len(tiles)
    steps = 2 * count
    total = 8 * tile

    def late(lanes):
        return pl.BlockSpec((tile, lanes), lambda i, p: (i + base, 0))

    mine = pl.BlockSpec((tile, width), lambda i, p: (jnp.minimum(i, count - 1), 0))
    others = pl.BlockSpec((tile, width), lambda i, p: (jnp.maximum(i - count, 0), 0))
    anywhere = pl.BlockSpec(memory_space=pl.ANY)
    kept = list(kept)
    lead = 1 + 2 * len(wanted) + SLOTS + 1
    partial = jax.ShapeDtypeStruct((count * tile, width), BF16)
    lanes = [2 * half, 2 * half, 2 * part, 2 * part, width, width]
    return pl.pallas_call(
        functools.partial(experts_kernel, tiles, tile // 2),
        grid_spec=pltpu.PrefetchScalarGridSpec(
            num_scalar_prefetch=1,
            grid=(steps,),
            in_specs=[anywhere] * (2 * len(wanted) + SLOTS)
            + [pl.BlockSpec(select.shape, lambda i, p: (0, 0))]
            + [anywhere] * len(kept),
            out_specs=[mine, others, mine, others] + [late(n) for n in lanes],
            scratch_shapes=[
                pltpu.VMEM((width, LINE * part), BF16),
                pltpu.VMEM((width, LINE * half), BF16),
                pltpu.VMEM((2, tile, width), BF16),
                pltpu.VMEM((2, tile, wide), BF16),
                pltpu.VMEM((tile, LINE * half), BF16),
                pltpu.VMEM((tile, LINE * part), BF16),
                pltpu.SemaphoreType.DMA((2, LINE)),
                pltpu.SemaphoreType.DMA((2, 4)),
            ],
        ),
        out_shape=[partial] * 4 + [jax.ShapeDtypeStruct((total, n), BF16) for n in lanes],
        input_output_aliases={lead + i: 4 + i for i in range(len(kept))},
        compiler_params=pltpu.CompilerParams(vmem_limit_bytes=VMEM_BYTES),
        cost_estimate=pl.CostEstimate(
            flops=steps * tile * width * LINE * (part + half) // 4,
            bytes_accessed=2 * steps * tile * (6 * width + LINE * (part + half)),
            transcendentals=steps * tile * LINE * half,
        ),
        name="experts",
    )(place, *rows, *grads, *slots, select, *kept)


def qkv_grad_kernel(h_ref, dq_ref, dk_ref, dv_ref, gain_ref, o_ref):
    shard = o_ref.shape[-2]
    rows = h_ref[...]
    low = 0
    gains = jnp.broadcast_to(gain_ref[...], (PAD, gain_ref.shape[1])).T.astype(BF16)
    parts = [contract(rows, ref[...], 0, 0).astype(BF16) for ref in (dq_ref, dk_ref, dv_ref)]
    for part in parts + [gains]:
        for block in range(h_ref.shape[1] // shard):
            place = (block % 2, block // 2 % 2, 0, block // 4)
            o_ref[place + (slice(None), slice(low, low + part.shape[1]))] = part[
                block * shard : (block + 1) * shard
            ]
        low = low + part.shape[1]


def qkv_grad(normed, grads, gain_row, shard):
    rows, width = normed.shape
    columns = sum(grad.shape[1] for grad in grads)
    tile = width // 4
    planes = tile // (4 * shard)
    return pl.pallas_call(
        qkv_grad_kernel,
        grid=(4,),
        in_specs=[pl.BlockSpec((rows, tile), lambda i: (0, i))]
        + [pl.BlockSpec(grad.shape, lambda i: (0, 0)) for grad in grads]
        + [pl.BlockSpec((1, tile), lambda i: (0, i))],
        out_specs=pl.BlockSpec(
            (2, 2, 1, planes, shard, columns + PAD), lambda i: (0, 0, i // 2, i % 2, 0, 0)
        ),
        out_shape=jax.ShapeDtypeStruct((2, 2, 2, LINE, shard, columns + PAD), BF16),
        compiler_params=pltpu.CompilerParams(vmem_limit_bytes=VMEM_BYTES),
        cost_estimate=pl.CostEstimate(
            flops=rows * width * columns // 8,
            bytes_accessed=rows * width,
            transcendentals=0,
        ),
        name="qkv_grad",
    )(normed, *grads, gain_row)


def norm_back(value, gain, grad):
    scale = lax.rsqrt(jnp.mean(value * value, axis=-1, keepdims=True) + EPSILON)
    unit = value * scale
    grad_gain = jnp.sum(grad * unit, axis=0)
    scaled = grad * gain
    inner = jnp.mean(scaled * unit, axis=-1, keepdims=True)
    return scale * (scaled - unit * inner), grad_gain


def shards_plane(
    tokens,
    cotangent,
    positions,
    lengths,
    routes,
    logits,
    w_query,
    w_key,
    w_value,
    w_output,
    gain_attn,
    gain_ffn,
    w_in,
    w_out,
):
    seq = lax.axis_index("seq")
    data = lax.axis_index("dp")
    line, row_of, core = data // 4, (data // 2) % 2, data % 2
    tok_count, width = tokens.shape
    group_len = positions.shape[1]
    shard = w_query.shape[0]
    q_width = w_query.shape[1] // 2
    kv_width = w_key.shape[1] // 2
    kv_heads = kv_width // HDIM
    first_seq = seq == 0

    def ordered(mine, theirs, axis):
        low = jnp.where(first_seq, mine, theirs)
        high = jnp.where(first_seq, theirs, mine)
        return jnp.concatenate([low, high], axis=axis)

    def half_of(weights, which):
        half = weights.shape[1] // 2
        return lax.dynamic_slice_in_dim(weights, which * half, half, axis=1)

    def both_axes(value, pairs):
        return lax.ppermute(value, ("seq", "dp"), pairs)

    def device(s, d):
        return s * 4 * LINE + d

    straight, crossed = [], []
    for s in range(2):
        for d in range(4 * LINE):
            c = d % 2
            straight.append((device(s, d), device(c, d - c + s)))
            crossed.append((device(s, d), device(c, d - c + 1 - s)))
    crossed_back = [(there, here) for here, there in crossed]
    first_core = core == 0

    projections = (w_query, w_key, w_value)
    gain_columns = jnp.pad(jnp.stack([gain_attn, gain_ffn], axis=1), ((0, 0), (0, PAD - 2)))
    mine = jnp.concatenate([half_of(w, seq) for w in projections] + [gain_columns], axis=1)
    theirs = jnp.concatenate([half_of(w, 1 - seq) for w in projections] + [gain_columns], axis=1)
    theirs = swap_seq(theirs)
    qkv_width = q_width + 2 * kv_width
    pair = jnp.stack([jnp.where(first_seq, mine, theirs), jnp.where(first_seq, theirs, mine)])
    w_qkv = lax.all_gather(pair, "dp", axis=1, tiled=True).reshape(width, qkv_width + PAD)
    places_of = jnp.stack([line, row_of, core]).astype(jnp.int32)

    in_own = w_in[0]
    half = in_own.shape[1] // 2
    sent = jnp.concatenate(
        [lax.dynamic_slice_in_dim(in_own, seq * half, half, axis=1), w_out[0].T], axis=1
    )
    same = both_axes(sent, straight)
    cross = both_axes(lax.dynamic_slice_in_dim(in_own, (1 - seq) * half, half, axis=1), crossed)
    own_part = jnp.concatenate(
        [
            jnp.where(first_core, same[:, :half], cross),
            jnp.where(first_core, cross, same[:, :half]),
            same[:, half:],
        ],
        axis=1,
    )
    other_tokens = swap_seq(after(tokens, own_part))
    up_one, down_one = line_up(own_part), line_down(own_part)
    output_rows = jnp.concatenate(
        [w_output] + [swap_dp(w_output, 4 * step) for step in range(1, LINE)], axis=0
    )
    output_rows = jnp.concatenate([output_rows, swap_y(output_rows)], axis=0)
    output_rows = after(output_rows, other_tokens)
    output_rows = jnp.concatenate([output_rows, swap_seq(output_rows)], axis=0)
    output_others = swap_core(output_rows)

    experts_all = 4 * LINE
    gates = jax.nn.softmax(logits, axis=-1)
    named = routes[:, :, None] == jnp.arange(experts_all, dtype=jnp.int32)[None, None, :]
    gate_table = jnp.sum(jnp.where(named, gates[:, :, None], 0.0), axis=1)
    gate_high = lax.reduce_precision(gate_table, 8, 7)
    grad_rows = jnp.concatenate(
        [
            cotangent,
            gate_high.astype(BF16),
            (gate_table - gate_high).astype(BF16),
            jnp.zeros((tok_count, PAD - 2 * experts_all), BF16),
        ],
        axis=1,
    )
    grad_near = near_pieces(grad_rows, after(grad_rows, other_tokens))
    lane = jnp.arange(PAD, dtype=jnp.int32)[:, None]
    hosted = jnp.repeat(
        jnp.array(SLOT_ORDER, jnp.int32) * 4 + 2 * row_of + seq, half, total_repeat_length=LINE * half
    )
    select = ((lane % experts_all == hosted[None, :]) & (lane < 2 * experts_all)).astype(BF16)

    places = positions[0]
    ends = jnp.cumsum(lengths[0])
    ranks = jnp.arange(group_len, dtype=jnp.int32)
    reached = ranks[:, None] >= ends[None, :]
    starts = jnp.max(jnp.where(reached, ends[None, :], 0), axis=1)
    local = (ranks - starts).astype(F32)
    freqs = jnp.power(THETA, -jnp.arange(HDIM // 2, dtype=F32) * 2.0 / HDIM)
    angles = local[:, None] * freqs[None, :]
    cos, sin = jnp.cos(angles), jnp.sin(angles)
    cos = jnp.concatenate([cos, cos, cos, cos], axis=1)
    sin = jnp.concatenate([-sin, sin, -sin, sin], axis=1)
    start_column = starts[:, None]
    own_places = lax.dynamic_slice_in_dim(places, seq * tok_count, tok_count)
    other_places = lax.dynamic_slice_in_dim(places, (1 - seq) * tok_count, tok_count)
    sort_own = (ranks[:, None] == own_places[None, :]).astype(BF16)
    sort_other = (ranks[:, None] == other_places[None, :]).astype(BF16)

    def to_order(own, other):
        return (
            contract(sort_own, own, 1, 0) + contract(sort_other, other, 1, 0)
        ).astype(BF16)

    def from_order(sort, values):
        return contract(sort, values, 0, 0).astype(BF16)

    x_sorted = to_order(tokens, other_tokens)
    x_sorted, up_one, down_one = lax.optimization_barrier((x_sorted, up_one, down_one))
    up_two, down_two = line_up(up_one), line_down(down_one)
    gains = w_qkv[:, qkv_width : qkv_width + 2].astype(F32).T
    gain_one, gain_two = gains[0], gains[1]
    normed, query, keys, values = project(
        x_sorted, gain_one[None, :], w_qkv, cos, sin, q_width, kv_heads
    )
    pairs = q_width // (2 * HDIM)
    first_pairs = (pairs + 1) // 2
    mixed_one = attend(query, keys, values, start_column, 0, first_pairs)
    sent_one = swap_seq(from_order(sort_other, mixed_one))
    query_two, grad_near_x, grad_near_y = after((query, *grad_near), mixed_one)
    grad_near = (grad_near_x, grad_near_y)
    grad_far = far_pieces(*grad_near)
    mixed_two = attend(
        query_two, keys, values, start_column, first_pairs, pairs - first_pairs
    )
    sent_two = swap_seq(from_order(sort_other, mixed_two))
    mixed_mine = [from_order(sort_own, mixed_one), from_order(sort_own, mixed_two)]
    mixed_mine = jnp.concatenate(mixed_mine, axis=1)
    mixed_theirs = jnp.concatenate([sent_one, sent_two], axis=1)
    mixed_theirs, up_two, down_two = lax.optimization_barrier((mixed_theirs, up_two, down_two))
    up_three, down_three = line_up(up_two), line_down(down_two)
    inputs = tokens.astype(F32)
    middle, normed_ffn, output_parts = mix(
        places_of, mixed_mine, mixed_theirs, tokens, gains, output_rows, output_others
    )
    normed_ffn = after(normed_ffn, *grad_far)
    row_near = near_pieces(normed_ffn, normed_ffn)
    row_far = far_pieces(*row_near)
    slots = [up_three, up_two, up_one, own_part, down_one, down_two, down_three]
    row_pieces = with_cores(normed_ffn, *row_near, *row_far)
    grad_pieces = with_cores(*after((grad_rows, *grad_near, *grad_far), row_near[0]))
    place = line.astype(jnp.int32)[None]
    far = run_experts(FAR_TILES, place, row_pieces, grad_pieces, slots, select, 0, ())
    far_back = over_cores(far[2], far[3]).astype(BF16)
    back_y, back_x = far_links(far_back)
    near = run_experts(
        NEAR_TILES, after(place, far_back), row_pieces, grad_pieces, slots, select, 4, far[4:]
    )
    hid_a, hid_b, du_a, du_b, all_rows, all_grads = near[4:]

    def weight_grads(rows, grads, grad_both, hidden):
        inner = contract(rows, grad_both, 0, 0)
        outer = contract(grads, hidden, 0, 0) * BRANCH_SCALE
        return [
            jnp.concatenate(
                [inner[:, 2 * half * i : 2 * half * (i + 1)], outer[:, half * i : half * (i + 1)]],
                axis=1,
            ).astype(BF16)
            for i in range(2)
        ]

    rows_early, grads_early, back_y, back_x = lax.optimization_barrier(
        (all_rows, all_grads, back_y, back_x)
    )
    outer_grads = weight_grads(rows_early, grads_early, du_a, hid_a)
    grads_of = dict(zip(SLOT_ORDER[:2], outer_grads))
    far_line = (line_up(outer_grads[1]), line_down(outer_grads[0]))
    near_back = over_cores(after(near[2], *outer_grads), near[3])
    first, second = near_links(near_back, back_y, back_x)
    rows_late, grads_late = after((all_rows, all_grads), first, second)
    inner_grads = weight_grads(rows_late, grads_late, du_b, hid_b)
    grads_of.update(zip(SLOT_ORDER[2:], inner_grads))
    first, second = swap_seq(first), swap_y(second)
    near_back = after(near_back, *inner_grads)
    grad_normed_ffn = own_sum(near_back, back_y, back_x, first, second)

    def line_partial(first, *rest):
        value = grads_of[first]
        for where, expert in enumerate(rest):
            value = jnp.where(line > where, grads_of[expert], value)
        return value.astype(F32)

    def line_step(step, arrived):
        up, down = arrived
        last = LINE - 1
        right = line_partial(*range(last - step, LINE)) + up.astype(F32)
        left = grads_of[step]
        for where in range(step):
            left = jnp.where(line < last - where, grads_of[step - 1 - where], left)
        left = left.astype(F32) + down.astype(F32)
        return right.astype(BF16), left.astype(BF16)

    grad_final = cotangent.astype(F32)
    grad_norm, grad_gain_two = norm_back(middle, gain_two, grad_normed_ffn)
    grad_middle = grad_final + grad_norm
    grad_attn = (BRANCH_SCALE * grad_middle).astype(BF16)
    grad_mixed = contract(grad_attn, output_parts[0], 1, 1).astype(BF16)
    grad_other = contract(grad_attn, output_parts[1], 1, 1).astype(BF16)
    grad_other = swap_seq(grad_other)
    grad_w_output = contract(ordered(mixed_mine, mixed_theirs, 1), grad_attn, 0, 0)
    far_f, far_f_other, near_f, near_f_other = after(
        (far[0], far[1], near[0], near[1]), grad_mixed
    )
    far_ffn = over_cores(far_f, far_f_other).astype(BF16)
    ffn_y, ffn_x = far_links(far_ffn)
    near_ffn = over_cores(near_f, near_f_other)
    right, left = line_step(1, far_line)
    grad_other = after(grad_other, right, left, far_ffn)
    grad_sorted = to_order(grad_mixed, grad_other)
    mid_line = (line_up(right), line_down(left))
    grad_query, grad_keys, grad_values = attend_back(
        query, keys, values, grad_sorted, start_column, cos, sin
    )
    (grad_query, grad_keys, grad_values), mid_line, ffn_y, ffn_x = lax.optimization_barrier(
        ((grad_query, grad_keys, grad_values), mid_line, ffn_y, ffn_x)
    )
    right, left = line_step(2, mid_line)
    last_line = (line_up(right), line_down(left))
    first_ffn, second_ffn = near_links(near_ffn, ffn_y, ffn_x)
    first_ffn, second_ffn = swap_seq(first_ffn), swap_y(second_ffn)
    ffn = own_sum(near_ffn, ffn_y, ffn_x, first_ffn, second_ffn)
    output = (middle + BRANCH_SCALE * ffn).astype(BF16)
    grads_qkv = after((grad_query, grad_keys, grad_values), right, left)
    wide = qkv_grad(normed, grads_qkv, grad_gain_two[None, :], shard)
    grads_late = after(grads_qkv, wide)
    grad_normed, sent_normed = token_grad(
        grads_late, w_qkv, own_places[:, None], other_places[:, None]
    )
    grad_normed = grad_normed.astype(F32) + swap_seq(sent_normed).astype(F32)
    scale = lax.rsqrt(jnp.mean(inputs * inputs, axis=-1, keepdims=True) + EPSILON)
    unit = inputs * scale
    scaled = grad_normed * gain_one
    inner = jnp.mean(scaled * unit, axis=-1, keepdims=True)
    grad_tokens = grad_middle + scale * (scaled - unit * inner)

    summed_output = lax.psum_scatter(
        grad_w_output.astype(BF16), ("seq", "dp"), scatter_dimension=0, tiled=True
    )

    def chosen(value, which, axis):
        return lax.dynamic_index_in_dim(value, which, axis=axis, keepdims=False)

    kept = chosen(wide, core, 0).astype(F32)
    kept = kept + swap_core(chosen(wide, 1 - core, 0)).astype(F32)
    next_kept = chosen(kept, row_of, 0)
    next_kept = next_kept + swap_y(chosen(kept, 1 - row_of, 0).astype(BF16)).astype(F32)
    summed = chosen(next_kept, line, 1)
    sent_lines = [
        swap_dp(chosen(next_kept, line ^ step, 1).astype(BF16), 4 * step) for step in range(1, LINE)
    ]
    summed = summed + sum(value.astype(F32) for value in sent_lines)
    summed, last_line = lax.optimization_barrier((summed, last_line))
    part_grads = (
        line_partial(*range(LINE)) + last_line[0].astype(F32) + last_line[1].astype(F32)
    ).astype(BF16)
    same_grads = jnp.where(first_core, part_grads[:, :half], part_grads[:, half : 2 * half])
    cross_grads = jnp.where(first_core, part_grads[:, half : 2 * half], part_grads[:, :half])
    same_grads = jnp.concatenate([same_grads, part_grads[:, 2 * half :]], axis=1)
    same = both_axes(same_grads, straight)
    cross = both_axes(cross_grads, crossed_back)

    grad_w_in = ordered(same[:, :half], cross, 1)
    grad_w_out = same[:, half:].T
    kept_rows = chosen(summed, seq, 0)
    sent_rows = swap_seq(chosen(summed, 1 - seq, 0).astype(BF16)).astype(F32)
    cuts = (q_width, q_width + kv_width, qkv_width)
    pieces = [
        (a, b) for a, b in zip(jnp.split(kept_rows, cuts, axis=1), jnp.split(sent_rows, cuts, axis=1))
    ]
    grad_projections = [ordered(a, b, 1) for a, b in pieces[:3]]
    grad_gain_ffn = (pieces[3][0] + pieces[3][1])[:, 0]
    grad_gain_attn = sum(
        jnp.sum(grad * weight.astype(F32), axis=1)
        for grad, weight in zip(grad_projections, projections)
    ) / gain_attn.astype(F32)
    return (
        output,
        grad_tokens,
        grad_projections[0],
        grad_projections[1],
        grad_projections[2],
        summed_output.astype(F32),
        grad_gain_attn,
        grad_gain_ffn,
        grad_w_in.astype(F32)[None],
        grad_w_out.astype(F32)[None],
    )


def solution(mesh):
    placed = (
        P(("seq", "dp"), None),
        P(("seq", "dp"), None),
        P("dp", None),
        P("dp", None),
        P(("seq", "dp"), None),
        P(("seq", "dp"), None),
        P(("seq", "dp"), None),
        P(("seq", "dp"), None),
        P(("seq", "dp"), None),
        P(("seq", "dp"), None),
        P(("seq", "dp")),
        P(("seq", "dp")),
        P("dp", None, "seq"),
        P("dp", "seq", None),
    )
    return jax.shard_map(
        shards_plane if in_planes(mesh) else shards_general,
        mesh=mesh,
        in_specs=placed,
        out_specs=(
            P(("seq", "dp"), None),
            P(("seq", "dp"), None),
            P(("seq", "dp"), None),
            P(("seq", "dp"), None),
            P(("seq", "dp"), None),
            P(("seq", "dp"), None),
            P(("seq", "dp")),
            P(("seq", "dp")),
            P("dp", None, "seq"),
            P("dp", "seq", None),
        ),
        check_vma=False,
    )
```

```python
import functools

import jax
import jax.numpy as jnp
from jax import lax
from jax.experimental import pallas as pl
from jax.experimental.pallas import tpu as pltpu
from jax.sharding import PartitionSpec as P

QHEADS = 24
KVHEADS = 8
HDIM = 64
FF = 512
TOP = 8


EPSILON = 1e-06
BRANCH_SCALE = 0.22
SCORE_SCALE = 1.0 / 64.0
THETA = 10000.0


def rms_norm(value, gain):
    return value * lax.rsqrt(jnp.mean(value * value, axis=-1, keepdims=True) + EPSILON) * gain


def local_places(placing, seq_lengths):
    ends = jnp.cumsum(seq_lengths)
    segment = jnp.sum((placing[:, None] >= ends[None, :]).astype(jnp.int32), axis=1)
    starts = ends - seq_lengths
    member = segment[:, None] == jnp.arange(seq_lengths.shape[0], dtype=jnp.int32)[None, :]
    start_of = jnp.sum(jnp.where(member, starts[None, :], 0), axis=1)
    return (segment, placing - start_of)


def rotate(values, place, direction):
    half = values.shape[-1] // 2
    freqs = jnp.power(THETA, -jnp.arange(half, dtype=jnp.float32) * 2.0 / values.shape[-1])
    angles = place.astype(jnp.float32)[:, None] * freqs[None, :]
    cosine = jnp.cos(angles)[:, None, :]
    sine = direction * jnp.sin(angles)[:, None, :]
    first = values[..., :half]
    second = values[..., half:]
    return jnp.concatenate(
        [first * cosine - second * sine, second * cosine + first * sine], axis=-1
    )


def shards_general(
    tokens,
    cotangent,
    positions,
    lengths,
    routes,
    logits,
    w_query,
    w_key,
    w_value,
    w_output,
    gain_attn,
    gain_ffn,
    w_in,
    w_out,
):
    seq_count = lax.axis_size("seq")
    data_count = lax.axis_size("dp")
    tok_count = tokens.shape[0]
    group_len = positions.shape[1]
    local_experts = w_in.shape[0]
    experts_all = local_experts * data_count
    capacity = min(tok_count, 5 * tok_count * TOP // (4 * experts_all))
    heads_local = QHEADS // seq_count
    kv_local = KVHEADS // seq_count
    ratio = QHEADS // KVHEADS
    width = tokens.shape[1]
    query_full, key_full, value_full, output_full, gain_one, gain_two = (
        lax.all_gather(w_query, ("seq", "dp"), axis=0, tiled=True),
        lax.all_gather(w_key, ("seq", "dp"), axis=0, tiled=True),
        lax.all_gather(w_value, ("seq", "dp"), axis=0, tiled=True),
        lax.all_gather(w_output, ("seq", "dp"), axis=0, tiled=True),
        lax.all_gather(gain_attn, ("seq", "dp"), axis=0, tiled=True),
        lax.all_gather(gain_ffn, ("seq", "dp"), axis=0, tiled=True),
    )
    in_full, out_full = (
        lax.all_gather(w_in, "seq", axis=2, tiled=True),
        lax.all_gather(w_out, "seq", axis=1, tiled=True),
    )
    gain_one = gain_one.astype(jnp.float32)
    gain_two = gain_two.astype(jnp.float32)
    segment, place = local_places(positions[0], lengths[0])
    my_start = lax.axis_index("seq") * tok_count
    my_place = lax.dynamic_slice_in_dim(place, my_start, tok_count)
    inputs = tokens.astype(jnp.float32)
    normed = rms_norm(inputs, gain_one).astype(jnp.bfloat16)
    query_pre = jnp.dot(normed, query_full, preferred_element_type=jnp.float32)
    key_pre = jnp.dot(normed, key_full, preferred_element_type=jnp.float32)
    query_rot = (
        rotate(query_pre.reshape(tok_count, QHEADS, HDIM), my_place, 1.0)
        .reshape(tok_count, QHEADS * HDIM)
        .astype(jnp.bfloat16)
    )
    key_rot = (
        rotate(key_pre.reshape(tok_count, KVHEADS, HDIM), my_place, 1.0)
        .reshape(tok_count, KVHEADS * HDIM)
        .astype(jnp.bfloat16)
    )
    value_low = jnp.dot(normed, value_full, preferred_element_type=jnp.float32).astype(jnp.bfloat16)
    query_heads, key_heads, value_heads = (
        lax.all_to_all(query_rot, "seq", split_axis=1, concat_axis=0, tiled=True),
        lax.all_to_all(key_rot, "seq", split_axis=1, concat_axis=0, tiled=True),
        lax.all_to_all(value_low, "seq", split_axis=1, concat_axis=0, tiled=True),
    )
    keys_three = key_heads.reshape(group_len, kv_local, HDIM)
    values_three = value_heads.reshape(group_len, kv_local, HDIM)
    length = min(512, group_len)
    count = group_len // length

    def scores_of(query_block, seg_block, place_block):
        grouped = query_block.reshape(length, kv_local, ratio, HDIM)
        raw_scores = (
            jnp.einsum("qgrd,kgd->grqk", grouped, keys_three, preferred_element_type=jnp.float32)
            * SCORE_SCALE
        )
        allowed = (seg_block[:, None] == segment[None, :]) & (
            place[None, :] <= place_block[:, None]
        )
        return jnp.where(allowed[None, None], raw_scores, -1e30)

    def forward_block(pieces):
        query_block, seg_block, place_block = pieces
        scores = scores_of(query_block, seg_block, place_block)
        highest = jnp.max(scores, axis=-1, keepdims=True)
        expon = jnp.exp(scores - highest)
        totals = jnp.sum(expon, axis=-1, keepdims=True)
        probs = expon / totals
        mixed = jnp.einsum(
            "grqk,kgd->qgrd",
            probs.astype(jnp.bfloat16),
            values_three,
            preferred_element_type=jnp.float32,
        )
        return (
            mixed.reshape(length, heads_local * HDIM).astype(jnp.bfloat16),
            highest + jnp.log(totals),
            probs,
        )

    query_blocks = query_heads.reshape(count, length, heads_local * HDIM)
    seg_blocks = segment.reshape(count, length)
    place_blocks = place.reshape(count, length)
    block_args = (query_blocks, seg_blocks, place_blocks)

    def forward_light(pieces):
        mixed, lse_part, unused_probs = forward_block(pieces)
        return (mixed, lse_part)

    mixed_blocks, lse_blocks = lax.map(forward_light, block_args)
    mixed_heads = mixed_blocks.reshape(group_len, heads_local * HDIM)
    mixed_tokens = lax.all_to_all(mixed_heads, "seq", split_axis=0, concat_axis=1, tiled=True)
    attn = jnp.dot(mixed_tokens, output_full, preferred_element_type=jnp.float32)
    middle = inputs + BRANCH_SCALE * attn
    normed_ffn = rms_norm(middle, gain_two).astype(jnp.bfloat16)
    chosen = routes.reshape(-1)
    onehot = (chosen[:, None] == jnp.arange(experts_all, dtype=jnp.int32)[None, :]).astype(
        jnp.int32
    )
    ranking = jnp.sum(jnp.cumsum(onehot, axis=0) * onehot, axis=1) - 1
    target = chosen * capacity + ranking
    token_of = jnp.arange(tok_count * TOP, dtype=jnp.int32) // TOP
    gates = jax.nn.softmax(logits, axis=-1)
    source = jnp.full((experts_all * capacity,), tok_count, jnp.int32).at[target].set(token_of)
    slot_gate = jnp.zeros((experts_all * capacity,), jnp.float32).at[target].set(gates.reshape(-1))
    padded = jnp.concatenate([normed_ffn, jnp.zeros((1, width), jnp.bfloat16)], axis=0)
    outgoing = padded[source].reshape(data_count, local_experts * capacity, width)

    def expert_layout(arrived):
        return jnp.swapaxes(
            arrived.reshape(data_count, local_experts, capacity, width), 0, 1
        ).reshape(local_experts, data_count * capacity, width)

    def home_layout(values):
        return jnp.swapaxes(
            values.reshape(local_experts, data_count, capacity, width), 0, 1
        ).reshape(data_count, local_experts * capacity, width)

    def expert_forward(expert_rows):
        both = jnp.einsum("erd,edf->erf", expert_rows, in_full, preferred_element_type=jnp.float32)
        hidden = (jax.nn.silu(both[..., :FF]) * both[..., FF:]).astype(jnp.bfloat16)
        return (both, hidden)

    expert_rows = expert_layout(
        lax.all_to_all(outgoing, "dp", split_axis=0, concat_axis=0, tiled=True)
    )
    both, hidden = expert_forward(expert_rows)
    result = jnp.einsum(
        "erf,efd->erd", hidden, out_full, preferred_element_type=jnp.float32
    ).astype(jnp.bfloat16)
    returned = lax.all_to_all(
        home_layout(result), "dp", split_axis=0, concat_axis=0, tiled=True
    ).reshape(experts_all * capacity, width)
    picked = returned[target].reshape(tok_count, TOP, width).astype(jnp.float32)
    ffn = jnp.sum(picked * gates[:, :, None], axis=1)
    final = middle + BRANCH_SCALE * ffn
    output = final.astype(jnp.bfloat16)
    grad_final = cotangent.astype(jnp.float32)
    padded_grad = jnp.concatenate(
        [BRANCH_SCALE * grad_final, jnp.zeros((1, width), jnp.float32)], axis=0
    )
    grad_slots = (slot_gate[:, None] * padded_grad[source]).astype(jnp.bfloat16)
    grad_result = expert_layout(
        lax.all_to_all(
            grad_slots.reshape(data_count, local_experts * capacity, width),
            "dp",
            split_axis=0,
            concat_axis=0,
            tiled=True,
        )
    )
    rows_back = expert_layout(
        lax.all_to_all(outgoing, "dp", split_axis=0, concat_axis=0, tiled=True)
    )
    both_back, hidden_back = expert_forward(rows_back)
    grad_hidden = jnp.einsum(
        "erd,efd->erf", grad_result, out_full, preferred_element_type=jnp.float32
    )
    gate_part = both_back[..., :FF]
    up_part = both_back[..., FF:]
    sigma = jax.nn.sigmoid(gate_part)
    grad_gate = grad_hidden * up_part * sigma * (1.0 + gate_part * (1.0 - sigma))
    grad_up = grad_hidden * gate_part * sigma
    grad_both = jnp.concatenate([grad_gate, grad_up], axis=-1).astype(jnp.bfloat16)
    grad_out_local = jnp.einsum(
        "erf,erd->efd", hidden_back, grad_result, preferred_element_type=jnp.float32
    )
    grad_in_local = jnp.einsum(
        "erd,erf->edf", rows_back, grad_both, preferred_element_type=jnp.float32
    )
    grad_rows = jnp.einsum(
        "erf,edf->erd", grad_both, in_full, preferred_element_type=jnp.float32
    ).astype(jnp.bfloat16)
    grad_home = lax.all_to_all(
        home_layout(grad_rows), "dp", split_axis=0, concat_axis=0, tiled=True
    ).reshape(experts_all * capacity, width)
    grad_normed_ffn = jnp.sum(
        grad_home[target].reshape(tok_count, TOP, width).astype(jnp.float32), axis=1
    )
    grad_w_in, grad_w_out = (
        lax.psum_scatter(
            grad_in_local.astype(jnp.bfloat16), "seq", scatter_dimension=2, tiled=True
        ).astype(jnp.float32),
        lax.psum_scatter(
            grad_out_local.astype(jnp.bfloat16), "seq", scatter_dimension=1, tiled=True
        ).astype(jnp.float32),
    )
    unused_norm, norm_pull = jax.vjp(rms_norm, middle, gain_two)
    grad_middle_norm, grad_gain_two = norm_pull(grad_normed_ffn)
    grad_middle = grad_final + grad_middle_norm
    grad_attn = (BRANCH_SCALE * grad_middle).astype(jnp.bfloat16)
    grad_w_output = jnp.einsum(
        "te,td->ed", mixed_tokens, grad_attn, preferred_element_type=jnp.float32
    )
    grad_mixed = jnp.einsum(
        "td,ed->te", grad_attn, output_full, preferred_element_type=jnp.float32
    ).astype(jnp.bfloat16)
    grad_mixed_heads = lax.all_to_all(grad_mixed, "seq", split_axis=1, concat_axis=0, tiled=True)
    grad_blocks = grad_mixed_heads.reshape(count, length, heads_local * HDIM)
    back_args = (query_blocks, seg_blocks, place_blocks, lse_blocks, grad_blocks)

    def backward_block(carry, pieces):
        grad_keys, grad_values = carry
        query_block, seg_block, place_block, lse_block, grad_block = pieces[:5]
        probs = jnp.exp(scores_of(query_block, seg_block, place_block) - lse_block)
        grad_out = grad_block.reshape(length, kv_local, ratio, HDIM)
        grad_probs = jnp.einsum(
            "qgrd,kgd->grqk", grad_out, values_three, preferred_element_type=jnp.float32
        )
        grad_scores = (
            probs * (grad_probs - jnp.sum(probs * grad_probs, axis=-1, keepdims=True))
        ).astype(jnp.bfloat16)
        grad_query = SCORE_SCALE * jnp.einsum(
            "grqk,kgd->qgrd", grad_scores, keys_three, preferred_element_type=jnp.float32
        )
        grouped = query_block.reshape(length, kv_local, ratio, HDIM)
        grad_keys = grad_keys + SCORE_SCALE * jnp.einsum(
            "grqk,qgrd->kgd", grad_scores, grouped, preferred_element_type=jnp.float32
        )
        grad_values = grad_values + jnp.einsum(
            "grqk,qgrd->kgd",
            probs.astype(jnp.bfloat16),
            grad_out,
            preferred_element_type=jnp.float32,
        )
        return (
            (grad_keys, grad_values),
            grad_query.reshape(length, heads_local * HDIM).astype(jnp.bfloat16),
        )

    empty_keys = jnp.zeros((group_len, kv_local, HDIM), jnp.float32)
    (grad_keys, grad_values), grad_query_blocks = lax.scan(
        backward_block, (empty_keys, empty_keys), back_args
    )
    grad_query_heads = grad_query_blocks.reshape(group_len, heads_local * HDIM)
    grad_key_heads = grad_keys.reshape(group_len, kv_local * HDIM).astype(jnp.bfloat16)
    grad_value_heads = grad_values.reshape(group_len, kv_local * HDIM).astype(jnp.bfloat16)
    grad_query_tok, grad_key_tok, grad_value_tok = (
        lax.all_to_all(grad_query_heads, "seq", split_axis=0, concat_axis=1, tiled=True),
        lax.all_to_all(grad_key_heads, "seq", split_axis=0, concat_axis=1, tiled=True),
        lax.all_to_all(grad_value_heads, "seq", split_axis=0, concat_axis=1, tiled=True),
    )
    grad_query_pre = (
        rotate(grad_query_tok.astype(jnp.float32).reshape(tok_count, QHEADS, HDIM), my_place, -1.0)
        .reshape(tok_count, QHEADS * HDIM)
        .astype(jnp.bfloat16)
    )
    grad_key_pre = (
        rotate(grad_key_tok.astype(jnp.float32).reshape(tok_count, KVHEADS, HDIM), my_place, -1.0)
        .reshape(tok_count, KVHEADS * HDIM)
        .astype(jnp.bfloat16)
    )
    grad_w_query = jnp.einsum(
        "td,te->de", normed, grad_query_pre, preferred_element_type=jnp.float32
    )
    grad_w_key = jnp.einsum("td,te->de", normed, grad_key_pre, preferred_element_type=jnp.float32)
    grad_w_value = jnp.einsum(
        "td,te->de", normed, grad_value_tok, preferred_element_type=jnp.float32
    )
    grad_normed = jnp.einsum(
        "te,de->td", grad_query_pre, query_full, preferred_element_type=jnp.float32
    )
    grad_normed = grad_normed + jnp.einsum(
        "te,de->td", grad_key_pre, key_full, preferred_element_type=jnp.float32
    )
    grad_normed = grad_normed + jnp.einsum(
        "te,de->td", grad_value_tok, value_full, preferred_element_type=jnp.float32
    )
    unused_first, first_pull = jax.vjp(rms_norm, inputs, gain_one)
    grad_inputs_norm, grad_gain_one = first_pull(grad_normed)
    grad_tokens = grad_middle + grad_inputs_norm
    summed = (
        lax.psum_scatter(grad_w_query, ("seq", "dp"), scatter_dimension=0, tiled=True),
        lax.psum_scatter(grad_w_key, ("seq", "dp"), scatter_dimension=0, tiled=True),
        lax.psum_scatter(grad_w_value, ("seq", "dp"), scatter_dimension=0, tiled=True),
        lax.psum_scatter(grad_w_output, ("seq", "dp"), scatter_dimension=0, tiled=True),
        lax.psum_scatter(grad_gain_one, ("seq", "dp"), scatter_dimension=0, tiled=True),
        lax.psum_scatter(grad_gain_two, ("seq", "dp"), scatter_dimension=0, tiled=True),
    )
    return (
        output,
        grad_tokens,
        summed[0],
        summed[1],
        summed[2],
        summed[3],
        summed[4],
        summed[5],
        grad_w_in,
        grad_w_out,
    )


BF16 = jnp.bfloat16
F32 = jnp.float32
LINE = 4
PAD = 128
VMEM_BYTES = 60 * 1024 * 1024


def in_planes(mesh):
    return mesh.shape["seq"] == 2 and mesh.shape["dp"] == 4 * LINE


def swap_seq(value):
    return lax.ppermute(value, "seq", [(0, 1), (1, 0)])


def swap_dp(value, mask):
    return lax.ppermute(value, "dp", [(i, i ^ mask) for i in range(4 * LINE)])


def swap_core(value):
    return swap_dp(value, 1)


def swap_y(value):
    return swap_dp(value, 2)


def line_up(value):
    return lax.ppermute(value, "dp", [(i, i + 4) for i in range(4 * LINE - 4)])


def line_down(value):
    return lax.ppermute(value, "dp", [(i, i - 4) for i in range(4, 4 * LINE)])


def after(value, *others):
    return lax.optimization_barrier((value,) + others)[0]


def line_scatter(take, place):
    up = down = None
    for step in range(LINE - 1):
        far = jnp.minimum(LINE - 1 - step + place, LINE - 1)
        near = jnp.maximum(step - LINE + 1 + place, 0)
        right, left = take(far), take(near)
        if up is not None:
            right = right + up.astype(F32)
            left = left + down.astype(F32)
        up = line_up(right.astype(BF16))
        down = line_down(left.astype(BF16))
    return take(place) + up.astype(F32) + down.astype(F32)


def near_pieces(own, own_x):
    return swap_seq(own_x), swap_y(own)


def far_pieces(near_x, near_y):
    half = near_x.shape[0] // 2
    return swap_y(near_x[:half]), swap_seq(near_y[half:])


def with_cores(*pieces):
    return pieces + tuple(swap_core(piece) for piece in pieces)


def over_cores(mine, others):
    return mine.astype(F32) + swap_core(others).astype(F32)


def far_links(far):
    half = far.shape[0] // 2
    return swap_y(far[:half]), swap_seq(far[half:])


def near_links(near, from_y, from_x):
    half = from_y.shape[0] // 2
    first = (near[:half] + from_y[half:].astype(F32)).astype(BF16)
    second = (near[half : 2 * half] + from_x[half:].astype(F32)).astype(BF16)
    return first, second


def own_sum(near, from_y, from_x, first, second):
    half = from_y.shape[0] // 2
    low = near[2 * half : 3 * half] + from_y[:half].astype(F32) + first.astype(F32)
    high = near[3 * half :] + from_x[:half].astype(F32) + second.astype(F32)
    return jnp.concatenate([low, high], axis=0)


def turned(values, cos, sin, direction):
    lanes = values.shape[1]
    place = lax.broadcasted_iota(jnp.int32, values.shape, 1) % HDIM
    swapped = jnp.where(
        place < HDIM // 2,
        pltpu.roll(values, lanes - HDIM // 2, 1),
        pltpu.roll(values, HDIM // 2, 1),
    )
    times = lanes // cos.shape[1]
    cos = jnp.concatenate([cos] * times, axis=1)
    sin = jnp.concatenate([sin] * times, axis=1)
    if direction > 0:
        return values * cos + swapped * sin
    return values * cos - swapped * sin


def qkv_kernel(x_ref, gain_ref, w_ref, cos_ref, sin_ref, h_ref, q_ref, k_ref, v_ref):
    value = x_ref[...].astype(F32)
    scale = lax.rsqrt(jnp.mean(value * value, axis=-1, keepdims=True) + EPSILON)
    normed = (value * scale * gain_ref[...]).astype(BF16)
    h_ref[...] = normed
    q_width, kv_heads = q_ref.shape[1], k_ref.shape[0]
    kv_width = kv_heads * HDIM
    weights = w_ref[:, : q_width + 2 * kv_width]
    both = jnp.dot(normed, weights, preferred_element_type=F32)
    spun = turned(both[:, : q_width + kv_width], cos_ref[...], sin_ref[...], 1)
    q_ref[...] = (spun[:, :q_width] * SCORE_SCALE).astype(BF16)
    for head in range(kv_heads):
        low = q_width + head * HDIM
        k_ref[head] = spun[:, low : low + HDIM].astype(BF16)
        low = low + kv_width
        v_ref[head] = both[:, low : low + HDIM].astype(BF16)


def project(x_sorted, gain, weights, cos, sin, q_width, kv_heads):
    rows, width = x_sorted.shape
    tile = 256
    columns = q_width + 2 * kv_heads * HDIM

    def row_block(lanes):
        return pl.BlockSpec((tile, lanes), lambda i: (i, 0))

    heads = pl.BlockSpec((kv_heads, tile, HDIM), lambda i: (0, i, 0))
    return pl.pallas_call(
        qkv_kernel,
        grid=(rows // tile,),
        in_specs=[
            row_block(width),
            pl.BlockSpec((1, width), lambda i: (0, 0)),
            pl.BlockSpec((width, width), lambda i: (0, 1)),
            row_block(cos.shape[1]),
            row_block(cos.shape[1]),
        ],
        out_specs=[row_block(width), row_block(q_width), heads, heads],
        out_shape=[
            jax.ShapeDtypeStruct((rows, width), BF16),
            jax.ShapeDtypeStruct((rows, q_width), BF16),
            jax.ShapeDtypeStruct((kv_heads, rows, HDIM), BF16),
            jax.ShapeDtypeStruct((kv_heads, rows, HDIM), BF16),
        ],
        compiler_params=pltpu.CompilerParams(vmem_limit_bytes=VMEM_BYTES),
        cost_estimate=pl.CostEstimate(
            flops=rows * width * columns // 8,
            bytes_accessed=rows * width + width * columns,
            transcendentals=rows,
        ),
        name="project",
    )(x_sorted, gain, weights, cos, sin)


def mix_kernel(place_ref, mine_ref, theirs_ref, x_ref, gain_ref, w_ref, m_ref, h_ref, parts_ref):
    half = parts_ref.shape[1]

    @pl.when(pl.program_id(0) == 0)
    def _():
        for part in range(2):
            low = pl.multiple_of((place_ref[0] ^ part) * half, half)
            parts_ref[part] = w_ref[pl.ds(low, half), :]

    mixed = jnp.dot(mine_ref[...], parts_ref[0], preferred_element_type=F32)
    mixed = mixed + jnp.dot(theirs_ref[...], parts_ref[1], preferred_element_type=F32)
    value = x_ref[...].astype(F32) + BRANCH_SCALE * mixed
    m_ref[...] = value
    scale = lax.rsqrt(jnp.mean(value * value, axis=-1, keepdims=True) + EPSILON)
    h_ref[...] = (value * scale * gain_ref[...]).astype(BF16)


def mix(place, mine, theirs, tokens, gain, weights):
    rows, width = tokens.shape
    half = mine.shape[1]
    tile = 256

    def row_block(lanes):
        return pl.BlockSpec((tile, lanes), lambda i, p: (i, 0))

    def whole(shape):
        return pl.BlockSpec(shape, lambda i, p: (0,) * len(shape))

    return pl.pallas_call(
        mix_kernel,
        grid_spec=pltpu.PrefetchScalarGridSpec(
            num_scalar_prefetch=1,
            grid=(rows // tile,),
            in_specs=[
                row_block(half), row_block(half), row_block(width), whole(gain.shape),
                whole((width, width)),
            ],
            out_specs=[row_block(width), row_block(width), whole((2, half, width))],
        ),
        out_shape=[
            jax.ShapeDtypeStruct((rows, width), F32),
            jax.ShapeDtypeStruct((rows, width), BF16),
            jax.ShapeDtypeStruct((2, half, width), BF16),
        ],
        compiler_params=pltpu.CompilerParams(vmem_limit_bytes=VMEM_BYTES),
        cost_estimate=pl.CostEstimate(
            flops=rows * width * width // 8, bytes_accessed=rows * width, transcendentals=rows
        ),
        name="mix",
    )(place, mine, theirs, tokens, gain, weights)


def token_grad_kernel(dq_ref, dk_ref, dv_ref, w_ref, own_ref, other_ref, mine_ref, sent_ref):
    q_width, kv_width = dq_ref.shape[1], dk_ref.shape[1]
    cuts = (0, q_width, q_width + kv_width, q_width + 2 * kv_width)
    grad = contract(dq_ref[...], w_ref[:, cuts[0] : cuts[1]], 1, 1)
    grad = grad + contract(dk_ref[...], w_ref[:, cuts[1] : cuts[2]], 1, 1)
    grad = (grad + contract(dv_ref[...], w_ref[:, cuts[2] : cuts[3]], 1, 1)).astype(BF16)
    for place_ref, out_ref in ((other_ref, sent_ref), (own_ref, mine_ref)):
        shape = (place_ref.shape[0], grad.shape[0])
        picked = lax.broadcasted_iota(jnp.int32, shape, 1) == place_ref[...]
        picked = jnp.where(picked, 1.0, 0.0).astype(BF16)
        out_ref[...] = jnp.dot(picked, grad, preferred_element_type=F32).astype(BF16)


def token_grad(grads, weights, own_places, other_places):
    rows, count = grads[0].shape[0], own_places.shape[0]
    width = weights.shape[0]
    columns = sum(grad.shape[1] for grad in grads)
    tile = width // 3

    def whole(array):
        return pl.BlockSpec(array.shape, lambda i: (0, 0))

    block = pl.BlockSpec((count, tile), lambda i: (0, i))
    return pl.pallas_call(
        token_grad_kernel,
        grid=(3,),
        in_specs=[whole(grad) for grad in grads]
        + [pl.BlockSpec((tile, width), lambda i: (i, 1)), whole(own_places), whole(other_places)],
        out_specs=[block, block],
        out_shape=[jax.ShapeDtypeStruct((count, width), BF16)] * 2,
        compiler_params=pltpu.CompilerParams(vmem_limit_bytes=VMEM_BYTES),
        cost_estimate=pl.CostEstimate(
            flops=rows * width * columns // 8, bytes_accessed=rows * width, transcendentals=0
        ),
        name="token_grad",
    )(*grads, weights, own_places, other_places)


Q_TILE = 256


def windows(rows):
    longest = rows // 2
    for start in range(0, rows, Q_TILE):
        low = max(0, start - longest + 1) // Q_TILE * Q_TILE
        yield start, low, start + Q_TILE


def allowed_keys(start_ref, row, low, high):
    shape = (Q_TILE, high - low)
    rows = lax.broadcasted_iota(jnp.int32, shape, 0) + row
    keys = lax.broadcasted_iota(jnp.int32, shape, 1) + low
    return (keys <= rows) & (keys >= start_ref[row : row + Q_TILE, :])


def contract(left, right, left_dim, right_dim):
    return lax.dot_general(
        left, right, (((left_dim,), (right_dim,)), ((), ())), preferred_element_type=F32
    )


def probabilities(query, keys, allowed):
    scores = jnp.where(allowed, contract(query, keys, 1, 1), -1e30)
    expon = jnp.exp(scores - jnp.max(scores, axis=-1, keepdims=True))
    return expon * (1.0 / jnp.sum(expon, axis=-1, keepdims=True))


def attend_kernel(base, q_ref, k_ref, v_ref, start_ref, o_ref):
    pair = pl.program_id(0) + base
    ratio = QHEADS // KVHEADS
    for row, low, high in windows(q_ref.shape[0]):
        allowed = allowed_keys(start_ref, row, low, high)
        for side in range(2):
            head = (2 * pair + side) // ratio
            lanes = slice(side * HDIM, (side + 1) * HDIM)
            probs = probabilities(
                q_ref[row : row + Q_TILE, lanes], k_ref[head, low:high, :], allowed
            )
            mixed = contract(probs.astype(BF16), v_ref[head, low:high, :], 1, 0)
            o_ref[row : row + Q_TILE, lanes] = mixed.astype(BF16)


def attention_cost(rows, heads, products):
    area = sum(Q_TILE * (high - low) for _, low, high in windows(rows))
    return pl.CostEstimate(
        flops=products * heads * area * 16,
        bytes_accessed=8 * rows * heads * HDIM,
        transcendentals=heads * area,
    )


def attend(query, keys, values, starts, base, pairs):
    rows = query.shape[0]
    pair_block = pl.BlockSpec((rows, 2 * HDIM), lambda j: (0, j + base))
    whole = pl.BlockSpec(keys.shape, lambda j: (0, 0, 0))
    return pl.pallas_call(
        functools.partial(attend_kernel, base),
        grid=(pairs,),
        in_specs=[pair_block, whole, whole, pl.BlockSpec((rows, 1), lambda j: (0, 0))],
        out_specs=pl.BlockSpec((rows, 2 * HDIM), lambda j: (0, j)),
        out_shape=jax.ShapeDtypeStruct((rows, pairs * 2 * HDIM), BF16),
        compiler_params=pltpu.CompilerParams(vmem_limit_bytes=VMEM_BYTES),
        cost_estimate=attention_cost(rows, 2 * pairs, 2),
        name="attend",
    )(query, keys, values, starts)


def attend_back_kernel(
    q_ref, k_ref, v_ref, d_ref, start_ref, cos_ref, sin_ref,
    dq_ref, dk_ref, dv_ref, dk_sum, dv_sum,
):
    pair = pl.program_id(0)
    ratio = QHEADS // KVHEADS

    @pl.when(pair == 0)
    def _():
        dk_sum[...] = jnp.zeros_like(dk_sum)
        dv_sum[...] = jnp.zeros_like(dv_sum)

    for row, low, high in windows(q_ref.shape[0]):
        allowed = allowed_keys(start_ref, row, low, high)
        grads = []
        for side in range(2):
            head = (2 * pair + side) // ratio
            lanes = slice(side * HDIM, (side + 1) * HDIM)
            query = q_ref[row : row + Q_TILE, lanes]
            keys = k_ref[head, low:high, :]
            probs = probabilities(query, keys, allowed)
            grad_out = d_ref[row : row + Q_TILE, lanes]
            grad_probs = contract(grad_out, v_ref[head, low:high, :], 1, 1)
            inner = jnp.sum(probs * grad_probs, axis=-1, keepdims=True)
            grad_scores = (probs * (grad_probs - inner)).astype(BF16)
            grads.append(contract(grad_scores, keys, 1, 0) * SCORE_SCALE)
            dk_sum[head, low:high, :] += contract(grad_scores, query, 0, 0)
            dv_sum[head, low:high, :] += contract(probs.astype(BF16), grad_out, 0, 0)
        grad_query = jnp.concatenate(grads, axis=1).astype(BF16).astype(F32)
        dq_ref[row : row + Q_TILE, :] = turned(
            grad_query,
            cos_ref[row : row + Q_TILE, :],
            sin_ref[row : row + Q_TILE, :],
            -1,
        ).astype(BF16)

    @pl.when(pair == pl.num_programs(0) - 1)
    def _():
        heads = range(dk_sum.shape[0])
        grad_keys = jnp.concatenate([dk_sum[head] for head in heads], axis=1)
        grad_keys = grad_keys.astype(BF16).astype(F32)
        dk_ref[...] = turned(grad_keys, cos_ref[...], sin_ref[...], -1).astype(BF16)
        dv_ref[...] = jnp.concatenate([dv_sum[head] for head in heads], axis=1).astype(BF16)


def attend_back(query, keys, values, grad_out, starts, cos, sin):
    rows, lanes = query.shape
    pairs = lanes // (2 * HDIM)
    kv_heads = keys.shape[0]
    pair_block = pl.BlockSpec((rows, 2 * HDIM), lambda j: (0, j))
    whole = pl.BlockSpec(keys.shape, lambda j: (0, 0, 0))

    def fixed(lanes_of):
        return pl.BlockSpec((rows, lanes_of), lambda j: (0, 0))

    flat = kv_heads * HDIM
    return pl.pallas_call(
        attend_back_kernel,
        grid=(pairs,),
        in_specs=[
            pair_block, whole, whole, pair_block, fixed(1), fixed(2 * HDIM), fixed(2 * HDIM),
        ],
        out_specs=[pair_block, fixed(flat), fixed(flat)],
        out_shape=[
            jax.ShapeDtypeStruct(query.shape, BF16),
            jax.ShapeDtypeStruct((rows, flat), BF16),
            jax.ShapeDtypeStruct((rows, flat), BF16),
        ],
        scratch_shapes=[pltpu.VMEM(keys.shape, F32), pltpu.VMEM(keys.shape, F32)],
        compiler_params=pltpu.CompilerParams(vmem_limit_bytes=VMEM_BYTES),
        cost_estimate=attention_cost(rows, 2 * pairs, 5),
        name="attend_back",
    )(query, keys, values, grad_out, starts, cos, sin)


SLOTS = 2 * LINE - 1
SLOT_ORDER = (0, 3, 1, 2)
OWN, NEAR_X, NEAR_Y, FAR_Y, FAR_X = range(5)
FAR_TILES = (((NEAR_Y, 0), (FAR_Y, 0)), ((NEAR_X, 1), (FAR_X, 0)))
NEAR_TILES = (((NEAR_X, 0), (NEAR_Y, 1)), ((OWN, 0), (OWN, 1)))


def used_pieces(tiles):
    return sorted({piece for tile in tiles for piece, _ in tile})


def experts_kernel(tiles, half_rows, place_ref, *refs):
    used = used_pieces(tiles)
    sides = 2 * len(used)
    h_pieces, g_pieces, slots = refs[:sides], refs[sides : 2 * sides], refs[2 * sides : 2 * sides + SLOTS]
    select_ref = refs[2 * sides + SLOTS]
    (
        f_mine, f_other, d_mine, d_other, hid_a, hid_b, du_a, du_b, hcopy_ref, gcopy_ref,
        w_in, w_out, h_buf, g_buf, hidden, du_all, weight_sems, row_sems,
    ) = refs[-18:]
    width = h_buf.shape[2]
    half = slots[0].shape[1] // 3
    part = 2 * half
    step = pl.program_id(0)
    steps = 2 * len(tiles)

    def weight_copies(spot, slot):
        return (
            pltpu.make_async_copy(
                slots[slot].at[:, :part],
                w_in.at[:, spot * part : (spot + 1) * part],
                weight_sems.at[0, spot],
            ),
            pltpu.make_async_copy(
                slots[slot].at[:, part:],
                w_out.at[:, spot * half : (spot + 1) * half],
                weight_sems.at[1, spot],
            ),
        )

    def row_copies(number, buffer):
        side, tile = divmod(number, len(tiles))
        copies = []
        for spot, (piece, part_of) in enumerate(tiles[tile]):
            index = side * len(used) + used.index(piece)
            for kind, (pieces, held) in enumerate(((h_pieces, h_buf), (g_pieces, g_buf))):
                copies.append(
                    pltpu.make_async_copy(
                        pieces[index].at[pl.ds(part_of * half_rows, half_rows), :],
                        held.at[buffer, pl.ds(spot * half_rows, half_rows), :],
                        row_sems.at[buffer, 2 * kind + spot],
                    )
                )
        return copies

    def fetch(wanted, buffer):
        for number in range(steps):

            @pl.when(wanted == number)
            def _():
                for copy in row_copies(number, buffer):
                    copy.start()

    buffer = step % 2

    @pl.when(step == 0)
    def _():
        fetch(step, 0)
        for spot, expert in enumerate(SLOT_ORDER):
            for slot in range(expert, expert + LINE):

                @pl.when(slot == LINE - 1 + expert - place_ref[0])
                def _():
                    for copy in weight_copies(spot, slot):
                        copy.start()

        for spot in range(LINE):
            for copy in weight_copies(spot, LINE - 1):
                copy.wait()

    @pl.when(step + 1 < steps)
    def _():
        fetch(step + 1, 1 - buffer)

    for copy in row_copies(0, buffer):
        copy.wait()

    rows = h_buf[buffer]
    grads = g_buf[buffer, :, :width]
    hcopy_ref[...] = rows
    gcopy_ref[...] = grads
    gates = jnp.dot(g_buf[buffer, :, width:], select_ref[...], preferred_element_type=F32)
    for spot in range(LINE):
        units = slice(spot * half, (spot + 1) * half)
        both = jnp.dot(
            rows, w_in[:, spot * part : (spot + 1) * part], preferred_element_type=F32
        )
        back = jnp.dot(grads, w_out[:, units], preferred_element_type=F32)
        gate = gates[:, units]
        first, second = both[:, :half], both[:, half:]
        sigma = jax.nn.sigmoid(first)
        silu = first * sigma
        hidden[:, units] = (gate * (silu * second)).astype(BF16)
        back = back * (BRANCH_SCALE * gate)
        d_first = back * second * (sigma * (1.0 + first * (1.0 - sigma)))
        d_second = back * silu
        du_all[:, spot * part : spot * part + half] = d_first.astype(BF16)
        du_all[:, spot * part + half : (spot + 1) * part] = d_second.astype(BF16)
    hid_a[...] = hidden[:, : 2 * half]
    hid_b[...] = hidden[:, 2 * half :]
    du_a[...] = du_all[:, : 2 * part]
    du_b[...] = du_all[:, 2 * part :]
    ffn = contract(hidden[...], w_out[...], 1, 1).astype(BF16)
    back_rows = contract(du_all[...], w_in[...], 1, 1).astype(BF16)

    @pl.when(step < len(tiles))
    def _():
        f_mine[...] = ffn
        d_mine[...] = back_rows

    @pl.when(step >= len(tiles))
    def _():
        f_other[...] = ffn
        d_other[...] = back_rows


def run_experts(tiles, place, row_pieces, grad_pieces, slots, select, base, kept):
    used = used_pieces(tiles)
    sides = len(row_pieces) // 2
    wanted = used + [sides + piece for piece in used]
    rows = [row_pieces[piece] for piece in wanted]
    grads = [grad_pieces[piece] for piece in wanted]
    tile, width = row_pieces[OWN].shape
    wide = grad_pieces[OWN].shape[1]
    half = slots[0].shape[1] // 3
    part = 2 * half
    count = len(tiles)
    steps = 2 * count
    total = 8 * tile

    def late(lanes):
        return pl.BlockSpec((tile, lanes), lambda i, p: (i + base, 0))

    mine = pl.BlockSpec((tile, width), lambda i, p: (jnp.minimum(i, count - 1), 0))
    others = pl.BlockSpec((tile, width), lambda i, p: (jnp.maximum(i - count, 0), 0))
    anywhere = pl.BlockSpec(memory_space=pl.ANY)
    kept = list(kept)
    lead = 1 + 2 * len(wanted) + SLOTS + 1
    partial = jax.ShapeDtypeStruct((count * tile, width), BF16)
    lanes = [2 * half, 2 * half, 2 * part, 2 * part, width, width]
    return pl.pallas_call(
        functools.partial(experts_kernel, tiles, tile // 2),
        grid_spec=pltpu.PrefetchScalarGridSpec(
            num_scalar_prefetch=1,
            grid=(steps,),
            in_specs=[anywhere] * (2 * len(wanted) + SLOTS)
            + [pl.BlockSpec(select.shape, lambda i, p: (0, 0))]
            + [anywhere] * len(kept),
            out_specs=[mine, others, mine, others] + [late(n) for n in lanes],
            scratch_shapes=[
                pltpu.VMEM((width, LINE * part), BF16),
                pltpu.VMEM((width, LINE * half), BF16),
                pltpu.VMEM((2, tile, width), BF16),
                pltpu.VMEM((2, tile, wide), BF16),
                pltpu.VMEM((tile, LINE * half), BF16),
                pltpu.VMEM((tile, LINE * part), BF16),
                pltpu.SemaphoreType.DMA((2, LINE)),
                pltpu.SemaphoreType.DMA((2, 4)),
            ],
        ),
        out_shape=[partial] * 4 + [jax.ShapeDtypeStruct((total, n), BF16) for n in lanes],
        input_output_aliases={lead + i: 4 + i for i in range(len(kept))},
        compiler_params=pltpu.CompilerParams(vmem_limit_bytes=VMEM_BYTES),
        cost_estimate=pl.CostEstimate(
            flops=steps * tile * width * LINE * (part + half) // 4,
            bytes_accessed=2 * steps * tile * (6 * width + LINE * (part + half)),
            transcendentals=steps * tile * LINE * half,
        ),
        name="experts",
    )(place, *rows, *grads, *slots, select, *kept)


def qkv_grad_kernel(h_ref, dq_ref, dk_ref, dv_ref, gain_ref, o_ref):
    shard = o_ref.shape[-2]
    rows = h_ref[...]
    low = 0
    gains = jnp.broadcast_to(gain_ref[...], (PAD, gain_ref.shape[1])).T.astype(BF16)
    parts = [contract(rows, ref[...], 0, 0).astype(BF16) for ref in (dq_ref, dk_ref, dv_ref)]
    for part in parts + [gains]:
        for block in range(h_ref.shape[1] // shard):
            place = (block % 2, block // 2 % 2, 0, block // 4)
            o_ref[place + (slice(None), slice(low, low + part.shape[1]))] = part[
                block * shard : (block + 1) * shard
            ]
        low = low + part.shape[1]


def qkv_grad(normed, grads, gain_row, shard):
    rows, width = normed.shape
    columns = sum(grad.shape[1] for grad in grads)
    tile = width // 4
    planes = tile // (4 * shard)
    return pl.pallas_call(
        qkv_grad_kernel,
        grid=(4,),
        in_specs=[pl.BlockSpec((rows, tile), lambda i: (0, i))]
        + [pl.BlockSpec(grad.shape, lambda i: (0, 0)) for grad in grads]
        + [pl.BlockSpec((1, tile), lambda i: (0, i))],
        out_specs=pl.BlockSpec(
            (2, 2, 1, planes, shard, columns + PAD), lambda i: (0, 0, i // 2, i % 2, 0, 0)
        ),
        out_shape=jax.ShapeDtypeStruct((2, 2, 2, LINE, shard, columns + PAD), BF16),
        compiler_params=pltpu.CompilerParams(vmem_limit_bytes=VMEM_BYTES),
        cost_estimate=pl.CostEstimate(
            flops=rows * width * columns // 8,
            bytes_accessed=rows * width,
            transcendentals=0,
        ),
        name="qkv_grad",
    )(normed, *grads, gain_row)


def norm_back(value, gain, grad):
    scale = lax.rsqrt(jnp.mean(value * value, axis=-1, keepdims=True) + EPSILON)
    unit = value * scale
    grad_gain = jnp.sum(grad * unit, axis=0)
    scaled = grad * gain
    inner = jnp.mean(scaled * unit, axis=-1, keepdims=True)
    return scale * (scaled - unit * inner), grad_gain


def shards_plane(
    tokens,
    cotangent,
    positions,
    lengths,
    routes,
    logits,
    w_query,
    w_key,
    w_value,
    w_output,
    gain_attn,
    gain_ffn,
    w_in,
    w_out,
):
    seq = lax.axis_index("seq")
    data = lax.axis_index("dp")
    line, row_of, core = data // 4, (data // 2) % 2, data % 2
    tok_count, width = tokens.shape
    group_len = positions.shape[1]
    shard = w_query.shape[0]
    q_width = w_query.shape[1] // 2
    kv_width = w_key.shape[1] // 2
    kv_heads = kv_width // HDIM
    first_seq = seq == 0

    def ordered(mine, theirs, axis):
        low = jnp.where(first_seq, mine, theirs)
        high = jnp.where(first_seq, theirs, mine)
        return jnp.concatenate([low, high], axis=axis)

    def half_of(weights, which):
        half = weights.shape[1] // 2
        return lax.dynamic_slice_in_dim(weights, which * half, half, axis=1)

    def both_axes(value, pairs):
        return lax.ppermute(value, ("seq", "dp"), pairs)

    def device(s, d):
        return s * 4 * LINE + d

    straight, crossed = [], []
    for s in range(2):
        for d in range(4 * LINE):
            c = d % 2
            straight.append((device(s, d), device(c, d - c + s)))
            crossed.append((device(s, d), device(c, d - c + 1 - s)))
    crossed_back = [(there, here) for here, there in crossed]
    first_core = core == 0

    projections = (w_query, w_key, w_value)
    qkv_width = q_width + 2 * kv_width
    gain_columns = jnp.pad(
        jnp.stack([gain_attn, gain_ffn], axis=1), ((0, 0), (0, width - qkv_width - 2))
    )
    mine, theirs = [
        jnp.concatenate([w_output] + [half_of(w, which) for w in projections] + [gain_columns], axis=1)
        for which in (seq, 1 - seq)
    ]
    theirs = swap_seq(theirs)
    pair = jnp.stack([jnp.where(first_seq, mine, theirs), jnp.where(first_seq, theirs, mine)])
    gathered = lax.all_gather(pair, "dp", axis=1, tiled=True).reshape(width, 2 * width)

    in_own = w_in[0]
    half = in_own.shape[1] // 2
    sent = jnp.concatenate(
        [lax.dynamic_slice_in_dim(in_own, seq * half, half, axis=1), w_out[0].T], axis=1
    )
    same = both_axes(sent, straight)
    cross = both_axes(lax.dynamic_slice_in_dim(in_own, (1 - seq) * half, half, axis=1), crossed)
    own_part = jnp.concatenate(
        [
            jnp.where(first_core, same[:, :half], cross),
            jnp.where(first_core, cross, same[:, :half]),
            same[:, half:],
        ],
        axis=1,
    )
    other_tokens = swap_seq(after(tokens, own_part))
    up_one, down_one = line_up(own_part), line_down(own_part)
    experts_all = 4 * LINE
    gates = jax.nn.softmax(logits, axis=-1)
    named = routes[:, :, None] == jnp.arange(experts_all, dtype=jnp.int32)[None, None, :]
    gate_table = jnp.sum(jnp.where(named, gates[:, :, None], 0.0), axis=1)
    gate_high = lax.reduce_precision(gate_table, 8, 7)
    grad_rows = jnp.concatenate(
        [
            cotangent,
            gate_high.astype(BF16),
            (gate_table - gate_high).astype(BF16),
            jnp.zeros((tok_count, PAD - 2 * experts_all), BF16),
        ],
        axis=1,
    )
    grad_near = near_pieces(grad_rows, after(grad_rows, other_tokens))
    lane = jnp.arange(PAD, dtype=jnp.int32)[:, None]
    hosted = jnp.repeat(
        jnp.array(SLOT_ORDER, jnp.int32) * 4 + 2 * row_of + seq, half, total_repeat_length=LINE * half
    )
    select = ((lane % experts_all == hosted[None, :]) & (lane < 2 * experts_all)).astype(BF16)

    places = positions[0]
    ends = jnp.cumsum(lengths[0])
    ranks = jnp.arange(group_len, dtype=jnp.int32)
    reached = ranks[:, None] >= ends[None, :]
    starts = jnp.max(jnp.where(reached, ends[None, :], 0), axis=1)
    local = (ranks - starts).astype(F32)
    freqs = jnp.power(THETA, -jnp.arange(HDIM // 2, dtype=F32) * 2.0 / HDIM)
    angles = local[:, None] * freqs[None, :]
    cos, sin = jnp.cos(angles), jnp.sin(angles)
    cos = jnp.concatenate([cos, cos, cos, cos], axis=1)
    sin = jnp.concatenate([-sin, sin, -sin, sin], axis=1)
    start_column = starts[:, None]
    own_places = lax.dynamic_slice_in_dim(places, seq * tok_count, tok_count)
    other_places = lax.dynamic_slice_in_dim(places, (1 - seq) * tok_count, tok_count)
    sort_own = (ranks[:, None] == own_places[None, :]).astype(BF16)
    sort_other = (ranks[:, None] == other_places[None, :]).astype(BF16)

    def to_order(own, other):
        return (
            contract(sort_own, own, 1, 0) + contract(sort_other, other, 1, 0)
        ).astype(BF16)

    def from_order(sort, values):
        return contract(sort, values, 0, 0).astype(BF16)

    x_sorted = to_order(tokens, other_tokens)
    x_sorted, up_one, down_one = lax.optimization_barrier((x_sorted, up_one, down_one))
    up_two, down_two = line_up(up_one), line_down(down_one)
    gains = gathered[:, width + qkv_width : width + qkv_width + 2].astype(F32).T
    gain_one, gain_two = gains[0], gains[1]
    normed, query, keys, values = project(
        x_sorted, gain_one[None, :], gathered, cos, sin, q_width, kv_heads
    )
    pairs = q_width // (2 * HDIM)
    first_pairs = (pairs + 1) // 2
    mixed_one = attend(query, keys, values, start_column, 0, first_pairs)
    sent_one = swap_seq(from_order(sort_other, mixed_one))
    query_two, grad_near_x, grad_near_y = after((query, *grad_near), mixed_one)
    grad_near = (grad_near_x, grad_near_y)
    grad_far = far_pieces(*grad_near)
    mixed_two = attend(
        query_two, keys, values, start_column, first_pairs, pairs - first_pairs
    )
    sent_two = swap_seq(from_order(sort_other, mixed_two))
    mixed_mine = [from_order(sort_own, mixed_one), from_order(sort_own, mixed_two)]
    mixed_mine = jnp.concatenate(mixed_mine, axis=1)
    mixed_theirs = jnp.concatenate([sent_one, sent_two], axis=1)
    mixed_theirs, up_two, down_two = lax.optimization_barrier((mixed_theirs, up_two, down_two))
    up_three, down_three = line_up(up_two), line_down(down_two)
    inputs = tokens.astype(F32)
    middle, normed_ffn, output_parts = mix(
        seq.astype(jnp.int32)[None], mixed_mine, mixed_theirs, tokens, gain_two[None, :], gathered
    )
    normed_ffn = after(normed_ffn, *grad_far)
    row_near = near_pieces(normed_ffn, normed_ffn)
    row_far = far_pieces(*row_near)
    slots = [up_three, up_two, up_one, own_part, down_one, down_two, down_three]
    row_pieces = with_cores(normed_ffn, *row_near, *row_far)
    grad_pieces = with_cores(*after((grad_rows, *grad_near, *grad_far), row_near[0]))
    place = line.astype(jnp.int32)[None]
    far = run_experts(FAR_TILES, place, row_pieces, grad_pieces, slots, select, 0, ())
    far_back = over_cores(far[2], far[3]).astype(BF16)
    back_y, back_x = far_links(far_back)
    near = run_experts(
        NEAR_TILES, after(place, far_back), row_pieces, grad_pieces, slots, select, 4, far[4:]
    )
    hid_a, hid_b, du_a, du_b, all_rows, all_grads = near[4:]

    def weight_grads(rows, grads, grad_both, hidden):
        inner = contract(rows, grad_both, 0, 0)
        outer = contract(grads, hidden, 0, 0) * BRANCH_SCALE
        return [
            jnp.concatenate(
                [inner[:, 2 * half * i : 2 * half * (i + 1)], outer[:, half * i : half * (i + 1)]],
                axis=1,
            ).astype(BF16)
            for i in range(2)
        ]

    rows_early, grads_early, back_y, back_x = lax.optimization_barrier(
        (all_rows, all_grads, back_y, back_x)
    )
    outer_grads = weight_grads(rows_early, grads_early, du_a, hid_a)
    grads_of = dict(zip(SLOT_ORDER[:2], outer_grads))
    far_line = (line_up(outer_grads[1]), line_down(outer_grads[0]))
    near_back = over_cores(after(near[2], *outer_grads), near[3])
    first, second = near_links(near_back, back_y, back_x)
    rows_late, grads_late = after((all_rows, all_grads), first, second)
    inner_grads = weight_grads(rows_late, grads_late, du_b, hid_b)
    grads_of.update(zip(SLOT_ORDER[2:], inner_grads))
    first, second = swap_seq(first), swap_y(second)
    near_back = after(near_back, *inner_grads)
    grad_normed_ffn = own_sum(near_back, back_y, back_x, first, second)

    def line_partial(first, *rest):
        value = grads_of[first]
        for where, expert in enumerate(rest):
            value = jnp.where(line > where, grads_of[expert], value)
        return value.astype(F32)

    def line_step(step, arrived):
        up, down = arrived
        last = LINE - 1
        right = line_partial(*range(last - step, LINE)) + up.astype(F32)
        left = grads_of[step]
        for where in range(step):
            left = jnp.where(line < last - where, grads_of[step - 1 - where], left)
        left = left.astype(F32) + down.astype(F32)
        return right.astype(BF16), left.astype(BF16)

    grad_final = cotangent.astype(F32)
    grad_norm, grad_gain_two = norm_back(middle, gain_two, grad_normed_ffn)
    grad_middle = grad_final + grad_norm
    grad_attn = (BRANCH_SCALE * grad_middle).astype(BF16)
    grad_mixed = contract(grad_attn, output_parts[0], 1, 1).astype(BF16)
    grad_other = contract(grad_attn, output_parts[1], 1, 1).astype(BF16)
    grad_other = swap_seq(grad_other)
    grad_w_output = contract(ordered(mixed_mine, mixed_theirs, 1), grad_attn, 0, 0)
    far_f, far_f_other, near_f, near_f_other = after(
        (far[0], far[1], near[0], near[1]), grad_mixed
    )
    far_ffn = over_cores(far_f, far_f_other).astype(BF16)
    ffn_y, ffn_x = far_links(far_ffn)
    near_ffn = over_cores(near_f, near_f_other)
    right, left = line_step(1, far_line)
    grad_other = after(grad_other, right, left, far_ffn)
    grad_sorted = to_order(grad_mixed, grad_other)
    mid_line = (line_up(right), line_down(left))
    grad_query, grad_keys, grad_values = attend_back(
        query, keys, values, grad_sorted, start_column, cos, sin
    )
    (grad_query, grad_keys, grad_values), mid_line, ffn_y, ffn_x = lax.optimization_barrier(
        ((grad_query, grad_keys, grad_values), mid_line, ffn_y, ffn_x)
    )
    right, left = line_step(2, mid_line)
    last_line = (line_up(right), line_down(left))
    first_ffn, second_ffn = near_links(near_ffn, ffn_y, ffn_x)
    first_ffn, second_ffn = swap_seq(first_ffn), swap_y(second_ffn)
    ffn = own_sum(near_ffn, ffn_y, ffn_x, first_ffn, second_ffn)
    output = (middle + BRANCH_SCALE * ffn).astype(BF16)
    grads_qkv = after((grad_query, grad_keys, grad_values), right, left)
    wide = qkv_grad(normed, grads_qkv, grad_gain_two[None, :], shard)
    grads_late = after(grads_qkv, wide)
    grad_normed, sent_normed = token_grad(
        grads_late, gathered, own_places[:, None], other_places[:, None]
    )
    grad_normed = grad_normed.astype(F32) + swap_seq(sent_normed).astype(F32)
    scale = lax.rsqrt(jnp.mean(inputs * inputs, axis=-1, keepdims=True) + EPSILON)
    unit = inputs * scale
    scaled = grad_normed * gain_one
    inner = jnp.mean(scaled * unit, axis=-1, keepdims=True)
    grad_tokens = grad_middle + scale * (scaled - unit * inner)

    summed_output = lax.psum_scatter(
        grad_w_output.astype(BF16), ("seq", "dp"), scatter_dimension=0, tiled=True
    )

    def chosen(value, which, axis):
        return lax.dynamic_index_in_dim(value, which, axis=axis, keepdims=False)

    kept = chosen(wide, core, 0).astype(F32)
    kept = kept + swap_core(chosen(wide, 1 - core, 0)).astype(F32)
    next_kept = chosen(kept, row_of, 0)
    next_kept = next_kept + swap_y(chosen(kept, 1 - row_of, 0).astype(BF16)).astype(F32)
    next_kept, last_line = lax.optimization_barrier((next_kept, last_line))
    part_grads = (
        line_partial(*range(LINE)) + last_line[0].astype(F32) + last_line[1].astype(F32)
    ).astype(BF16)
    same_grads = jnp.where(first_core, part_grads[:, :half], part_grads[:, half : 2 * half])
    cross_grads = jnp.where(first_core, part_grads[:, half : 2 * half], part_grads[:, :half])
    same_grads = jnp.concatenate([same_grads, part_grads[:, 2 * half :]], axis=1)
    next_kept, same_grads, cross_grads = lax.optimization_barrier(
        (next_kept, same_grads, cross_grads)
    )
    same = both_axes(same_grads, straight)
    cross = both_axes(cross_grads, crossed_back)
    sent_lines = [
        swap_dp(chosen(next_kept, line ^ step, 1).astype(BF16), 4 * step) for step in range(1, LINE)
    ]
    summed = chosen(next_kept, line, 1) + sum(value.astype(F32) for value in sent_lines)
    summed, same, cross = lax.optimization_barrier((summed, same, cross))
    grad_w_in = ordered(same[:, :half], cross, 1)
    grad_w_out = same[:, half:].T
    kept_rows = chosen(summed, seq, 0)
    sent_rows = swap_seq(chosen(summed, 1 - seq, 0).astype(BF16)).astype(F32)
    cuts = (q_width, q_width + kv_width, qkv_width)
    pieces = [
        (a, b) for a, b in zip(jnp.split(kept_rows, cuts, axis=1), jnp.split(sent_rows, cuts, axis=1))
    ]
    grad_projections = [ordered(a, b, 1) for a, b in pieces[:3]]
    grad_gain_ffn = (pieces[3][0] + pieces[3][1])[:, 0]
    grad_gain_attn = sum(
        jnp.sum(grad * weight.astype(F32), axis=1)
        for grad, weight in zip(grad_projections, projections)
    ) / gain_attn.astype(F32)
    return (
        output,
        grad_tokens,
        grad_projections[0],
        grad_projections[1],
        grad_projections[2],
        summed_output.astype(F32),
        grad_gain_attn,
        grad_gain_ffn,
        grad_w_in.astype(F32)[None],
        grad_w_out.astype(F32)[None],
    )


def solution(mesh):
    placed = (
        P(("seq", "dp"), None),
        P(("seq", "dp"), None),
        P("dp", None),
        P("dp", None),
        P(("seq", "dp"), None),
        P(("seq", "dp"), None),
        P(("seq", "dp"), None),
        P(("seq", "dp"), None),
        P(("seq", "dp"), None),
        P(("seq", "dp"), None),
        P(("seq", "dp")),
        P(("seq", "dp")),
        P("dp", None, "seq"),
        P("dp", "seq", None),
    )
    return jax.shard_map(
        shards_plane if in_planes(mesh) else shards_general,
        mesh=mesh,
        in_specs=placed,
        out_specs=(
            P(("seq", "dp"), None),
            P(("seq", "dp"), None),
            P(("seq", "dp"), None),
            P(("seq", "dp"), None),
            P(("seq", "dp"), None),
            P(("seq", "dp"), None),
            P(("seq", "dp")),
            P(("seq", "dp")),
            P("dp", None, "seq"),
            P("dp", "seq", None),
        ),
        check_vma=False,
    )
```

```python
import functools

import jax
import jax.numpy as jnp
from jax import lax
from jax.experimental import pallas as pl
from jax.experimental.pallas import tpu as pltpu
from jax.sharding import PartitionSpec as P

QHEADS = 24
KVHEADS = 8
HDIM = 64
FF = 512
TOP = 8


EPSILON = 1e-06
BRANCH_SCALE = 0.22
SCORE_SCALE = 1.0 / 64.0
THETA = 10000.0


def rms_norm(value, gain):
    return value * lax.rsqrt(jnp.mean(value * value, axis=-1, keepdims=True) + EPSILON) * gain


def local_places(placing, seq_lengths):
    ends = jnp.cumsum(seq_lengths)
    segment = jnp.sum((placing[:, None] >= ends[None, :]).astype(jnp.int32), axis=1)
    starts = ends - seq_lengths
    member = segment[:, None] == jnp.arange(seq_lengths.shape[0], dtype=jnp.int32)[None, :]
    start_of = jnp.sum(jnp.where(member, starts[None, :], 0), axis=1)
    return (segment, placing - start_of)


def rotate(values, place, direction):
    half = values.shape[-1] // 2
    freqs = jnp.power(THETA, -jnp.arange(half, dtype=jnp.float32) * 2.0 / values.shape[-1])
    angles = place.astype(jnp.float32)[:, None] * freqs[None, :]
    cosine = jnp.cos(angles)[:, None, :]
    sine = direction * jnp.sin(angles)[:, None, :]
    first = values[..., :half]
    second = values[..., half:]
    return jnp.concatenate(
        [first * cosine - second * sine, second * cosine + first * sine], axis=-1
    )


def shards_general(
    tokens,
    cotangent,
    positions,
    lengths,
    routes,
    logits,
    w_query,
    w_key,
    w_value,
    w_output,
    gain_attn,
    gain_ffn,
    w_in,
    w_out,
):
    seq_count = lax.axis_size("seq")
    data_count = lax.axis_size("dp")
    tok_count = tokens.shape[0]
    group_len = positions.shape[1]
    local_experts = w_in.shape[0]
    experts_all = local_experts * data_count
    capacity = min(tok_count, 5 * tok_count * TOP // (4 * experts_all))
    heads_local = QHEADS // seq_count
    kv_local = KVHEADS // seq_count
    ratio = QHEADS // KVHEADS
    width = tokens.shape[1]
    query_full, key_full, value_full, output_full, gain_one, gain_two = (
        lax.all_gather(w_query, ("seq", "dp"), axis=0, tiled=True),
        lax.all_gather(w_key, ("seq", "dp"), axis=0, tiled=True),
        lax.all_gather(w_value, ("seq", "dp"), axis=0, tiled=True),
        lax.all_gather(w_output, ("seq", "dp"), axis=0, tiled=True),
        lax.all_gather(gain_attn, ("seq", "dp"), axis=0, tiled=True),
        lax.all_gather(gain_ffn, ("seq", "dp"), axis=0, tiled=True),
    )
    in_full, out_full = (
        lax.all_gather(w_in, "seq", axis=2, tiled=True),
        lax.all_gather(w_out, "seq", axis=1, tiled=True),
    )
    gain_one = gain_one.astype(jnp.float32)
    gain_two = gain_two.astype(jnp.float32)
    segment, place = local_places(positions[0], lengths[0])
    my_start = lax.axis_index("seq") * tok_count
    my_place = lax.dynamic_slice_in_dim(place, my_start, tok_count)
    inputs = tokens.astype(jnp.float32)
    normed = rms_norm(inputs, gain_one).astype(jnp.bfloat16)
    query_pre = jnp.dot(normed, query_full, preferred_element_type=jnp.float32)
    key_pre = jnp.dot(normed, key_full, preferred_element_type=jnp.float32)
    query_rot = (
        rotate(query_pre.reshape(tok_count, QHEADS, HDIM), my_place, 1.0)
        .reshape(tok_count, QHEADS * HDIM)
        .astype(jnp.bfloat16)
    )
    key_rot = (
        rotate(key_pre.reshape(tok_count, KVHEADS, HDIM), my_place, 1.0)
        .reshape(tok_count, KVHEADS * HDIM)
        .astype(jnp.bfloat16)
    )
    value_low = jnp.dot(normed, value_full, preferred_element_type=jnp.float32).astype(jnp.bfloat16)
    query_heads, key_heads, value_heads = (
        lax.all_to_all(query_rot, "seq", split_axis=1, concat_axis=0, tiled=True),
        lax.all_to_all(key_rot, "seq", split_axis=1, concat_axis=0, tiled=True),
        lax.all_to_all(value_low, "seq", split_axis=1, concat_axis=0, tiled=True),
    )
    keys_three = key_heads.reshape(group_len, kv_local, HDIM)
    values_three = value_heads.reshape(group_len, kv_local, HDIM)
    length = min(512, group_len)
    count = group_len // length

    def scores_of(query_block, seg_block, place_block):
        grouped = query_block.reshape(length, kv_local, ratio, HDIM)
        raw_scores = (
            jnp.einsum("qgrd,kgd->grqk", grouped, keys_three, preferred_element_type=jnp.float32)
            * SCORE_SCALE
        )
        allowed = (seg_block[:, None] == segment[None, :]) & (
            place[None, :] <= place_block[:, None]
        )
        return jnp.where(allowed[None, None], raw_scores, -1e30)

    def forward_block(pieces):
        query_block, seg_block, place_block = pieces
        scores = scores_of(query_block, seg_block, place_block)
        highest = jnp.max(scores, axis=-1, keepdims=True)
        expon = jnp.exp(scores - highest)
        totals = jnp.sum(expon, axis=-1, keepdims=True)
        probs = expon / totals
        mixed = jnp.einsum(
            "grqk,kgd->qgrd",
            probs.astype(jnp.bfloat16),
            values_three,
            preferred_element_type=jnp.float32,
        )
        return (
            mixed.reshape(length, heads_local * HDIM).astype(jnp.bfloat16),
            highest + jnp.log(totals),
            probs,
        )

    query_blocks = query_heads.reshape(count, length, heads_local * HDIM)
    seg_blocks = segment.reshape(count, length)
    place_blocks = place.reshape(count, length)
    block_args = (query_blocks, seg_blocks, place_blocks)

    def forward_light(pieces):
        mixed, lse_part, unused_probs = forward_block(pieces)
        return (mixed, lse_part)

    mixed_blocks, lse_blocks = lax.map(forward_light, block_args)
    mixed_heads = mixed_blocks.reshape(group_len, heads_local * HDIM)
    mixed_tokens = lax.all_to_all(mixed_heads, "seq", split_axis=0, concat_axis=1, tiled=True)
    attn = jnp.dot(mixed_tokens, output_full, preferred_element_type=jnp.float32)
    middle = inputs + BRANCH_SCALE * attn
    normed_ffn = rms_norm(middle, gain_two).astype(jnp.bfloat16)
    chosen = routes.reshape(-1)
    onehot = (chosen[:, None] == jnp.arange(experts_all, dtype=jnp.int32)[None, :]).astype(
        jnp.int32
    )
    ranking = jnp.sum(jnp.cumsum(onehot, axis=0) * onehot, axis=1) - 1
    target = chosen * capacity + ranking
    token_of = jnp.arange(tok_count * TOP, dtype=jnp.int32) // TOP
    gates = jax.nn.softmax(logits, axis=-1)
    source = jnp.full((experts_all * capacity,), tok_count, jnp.int32).at[target].set(token_of)
    slot_gate = jnp.zeros((experts_all * capacity,), jnp.float32).at[target].set(gates.reshape(-1))
    padded = jnp.concatenate([normed_ffn, jnp.zeros((1, width), jnp.bfloat16)], axis=0)
    outgoing = padded[source].reshape(data_count, local_experts * capacity, width)

    def expert_layout(arrived):
        return jnp.swapaxes(
            arrived.reshape(data_count, local_experts, capacity, width), 0, 1
        ).reshape(local_experts, data_count * capacity, width)

    def home_layout(values):
        return jnp.swapaxes(
            values.reshape(local_experts, data_count, capacity, width), 0, 1
        ).reshape(data_count, local_experts * capacity, width)

    def expert_forward(expert_rows):
        both = jnp.einsum("erd,edf->erf", expert_rows, in_full, preferred_element_type=jnp.float32)
        hidden = (jax.nn.silu(both[..., :FF]) * both[..., FF:]).astype(jnp.bfloat16)
        return (both, hidden)

    expert_rows = expert_layout(
        lax.all_to_all(outgoing, "dp", split_axis=0, concat_axis=0, tiled=True)
    )
    both, hidden = expert_forward(expert_rows)
    result = jnp.einsum(
        "erf,efd->erd", hidden, out_full, preferred_element_type=jnp.float32
    ).astype(jnp.bfloat16)
    returned = lax.all_to_all(
        home_layout(result), "dp", split_axis=0, concat_axis=0, tiled=True
    ).reshape(experts_all * capacity, width)
    picked = returned[target].reshape(tok_count, TOP, width).astype(jnp.float32)
    ffn = jnp.sum(picked * gates[:, :, None], axis=1)
    final = middle + BRANCH_SCALE * ffn
    output = final.astype(jnp.bfloat16)
    grad_final = cotangent.astype(jnp.float32)
    padded_grad = jnp.concatenate(
        [BRANCH_SCALE * grad_final, jnp.zeros((1, width), jnp.float32)], axis=0
    )
    grad_slots = (slot_gate[:, None] * padded_grad[source]).astype(jnp.bfloat16)
    grad_result = expert_layout(
        lax.all_to_all(
            grad_slots.reshape(data_count, local_experts * capacity, width),
            "dp",
            split_axis=0,
            concat_axis=0,
            tiled=True,
        )
    )
    rows_back = expert_layout(
        lax.all_to_all(outgoing, "dp", split_axis=0, concat_axis=0, tiled=True)
    )
    both_back, hidden_back = expert_forward(rows_back)
    grad_hidden = jnp.einsum(
        "erd,efd->erf", grad_result, out_full, preferred_element_type=jnp.float32
    )
    gate_part = both_back[..., :FF]
    up_part = both_back[..., FF:]
    sigma = jax.nn.sigmoid(gate_part)
    grad_gate = grad_hidden * up_part * sigma * (1.0 + gate_part * (1.0 - sigma))
    grad_up = grad_hidden * gate_part * sigma
    grad_both = jnp.concatenate([grad_gate, grad_up], axis=-1).astype(jnp.bfloat16)
    grad_out_local = jnp.einsum(
        "erf,erd->efd", hidden_back, grad_result, preferred_element_type=jnp.float32
    )
    grad_in_local = jnp.einsum(
        "erd,erf->edf", rows_back, grad_both, preferred_element_type=jnp.float32
    )
    grad_rows = jnp.einsum(
        "erf,edf->erd", grad_both, in_full, preferred_element_type=jnp.float32
    ).astype(jnp.bfloat16)
    grad_home = lax.all_to_all(
        home_layout(grad_rows), "dp", split_axis=0, concat_axis=0, tiled=True
    ).reshape(experts_all * capacity, width)
    grad_normed_ffn = jnp.sum(
        grad_home[target].reshape(tok_count, TOP, width).astype(jnp.float32), axis=1
    )
    grad_w_in, grad_w_out = (
        lax.psum_scatter(
            grad_in_local.astype(jnp.bfloat16), "seq", scatter_dimension=2, tiled=True
        ).astype(jnp.float32),
        lax.psum_scatter(
            grad_out_local.astype(jnp.bfloat16), "seq", scatter_dimension=1, tiled=True
        ).astype(jnp.float32),
    )
    unused_norm, norm_pull = jax.vjp(rms_norm, middle, gain_two)
    grad_middle_norm, grad_gain_two = norm_pull(grad_normed_ffn)
    grad_middle = grad_final + grad_middle_norm
    grad_attn = (BRANCH_SCALE * grad_middle).astype(jnp.bfloat16)
    grad_w_output = jnp.einsum(
        "te,td->ed", mixed_tokens, grad_attn, preferred_element_type=jnp.float32
    )
    grad_mixed = jnp.einsum(
        "td,ed->te", grad_attn, output_full, preferred_element_type=jnp.float32
    ).astype(jnp.bfloat16)
    grad_mixed_heads = lax.all_to_all(grad_mixed, "seq", split_axis=1, concat_axis=0, tiled=True)
    grad_blocks = grad_mixed_heads.reshape(count, length, heads_local * HDIM)
    back_args = (query_blocks, seg_blocks, place_blocks, lse_blocks, grad_blocks)

    def backward_block(carry, pieces):
        grad_keys, grad_values = carry
        query_block, seg_block, place_block, lse_block, grad_block = pieces[:5]
        probs = jnp.exp(scores_of(query_block, seg_block, place_block) - lse_block)
        grad_out = grad_block.reshape(length, kv_local, ratio, HDIM)
        grad_probs = jnp.einsum(
            "qgrd,kgd->grqk", grad_out, values_three, preferred_element_type=jnp.float32
        )
        grad_scores = (
            probs * (grad_probs - jnp.sum(probs * grad_probs, axis=-1, keepdims=True))
        ).astype(jnp.bfloat16)
        grad_query = SCORE_SCALE * jnp.einsum(
            "grqk,kgd->qgrd", grad_scores, keys_three, preferred_element_type=jnp.float32
        )
        grouped = query_block.reshape(length, kv_local, ratio, HDIM)
        grad_keys = grad_keys + SCORE_SCALE * jnp.einsum(
            "grqk,qgrd->kgd", grad_scores, grouped, preferred_element_type=jnp.float32
        )
        grad_values = grad_values + jnp.einsum(
            "grqk,qgrd->kgd",
            probs.astype(jnp.bfloat16),
            grad_out,
            preferred_element_type=jnp.float32,
        )
        return (
            (grad_keys, grad_values),
            grad_query.reshape(length, heads_local * HDIM).astype(jnp.bfloat16),
        )

    empty_keys = jnp.zeros((group_len, kv_local, HDIM), jnp.float32)
    (grad_keys, grad_values), grad_query_blocks = lax.scan(
        backward_block, (empty_keys, empty_keys), back_args
    )
    grad_query_heads = grad_query_blocks.reshape(group_len, heads_local * HDIM)
    grad_key_heads = grad_keys.reshape(group_len, kv_local * HDIM).astype(jnp.bfloat16)
    grad_value_heads = grad_values.reshape(group_len, kv_local * HDIM).astype(jnp.bfloat16)
    grad_query_tok, grad_key_tok, grad_value_tok = (
        lax.all_to_all(grad_query_heads, "seq", split_axis=0, concat_axis=1, tiled=True),
        lax.all_to_all(grad_key_heads, "seq", split_axis=0, concat_axis=1, tiled=True),
        lax.all_to_all(grad_value_heads, "seq", split_axis=0, concat_axis=1, tiled=True),
    )
    grad_query_pre = (
        rotate(grad_query_tok.astype(jnp.float32).reshape(tok_count, QHEADS, HDIM), my_place, -1.0)
        .reshape(tok_count, QHEADS * HDIM)
        .astype(jnp.bfloat16)
    )
    grad_key_pre = (
        rotate(grad_key_tok.astype(jnp.float32).reshape(tok_count, KVHEADS, HDIM), my_place, -1.0)
        .reshape(tok_count, KVHEADS * HDIM)
        .astype(jnp.bfloat16)
    )
    grad_w_query = jnp.einsum(
        "td,te->de", normed, grad_query_pre, preferred_element_type=jnp.float32
    )
    grad_w_key = jnp.einsum("td,te->de", normed, grad_key_pre, preferred_element_type=jnp.float32)
    grad_w_value = jnp.einsum(
        "td,te->de", normed, grad_value_tok, preferred_element_type=jnp.float32
    )
    grad_normed = jnp.einsum(
        "te,de->td", grad_query_pre, query_full, preferred_element_type=jnp.float32
    )
    grad_normed = grad_normed + jnp.einsum(
        "te,de->td", grad_key_pre, key_full, preferred_element_type=jnp.float32
    )
    grad_normed = grad_normed + jnp.einsum(
        "te,de->td", grad_value_tok, value_full, preferred_element_type=jnp.float32
    )
    unused_first, first_pull = jax.vjp(rms_norm, inputs, gain_one)
    grad_inputs_norm, grad_gain_one = first_pull(grad_normed)
    grad_tokens = grad_middle + grad_inputs_norm
    summed = (
        lax.psum_scatter(grad_w_query, ("seq", "dp"), scatter_dimension=0, tiled=True),
        lax.psum_scatter(grad_w_key, ("seq", "dp"), scatter_dimension=0, tiled=True),
        lax.psum_scatter(grad_w_value, ("seq", "dp"), scatter_dimension=0, tiled=True),
        lax.psum_scatter(grad_w_output, ("seq", "dp"), scatter_dimension=0, tiled=True),
        lax.psum_scatter(grad_gain_one, ("seq", "dp"), scatter_dimension=0, tiled=True),
        lax.psum_scatter(grad_gain_two, ("seq", "dp"), scatter_dimension=0, tiled=True),
    )
    return (
        output,
        grad_tokens,
        summed[0],
        summed[1],
        summed[2],
        summed[3],
        summed[4],
        summed[5],
        grad_w_in,
        grad_w_out,
    )


BF16 = jnp.bfloat16
F32 = jnp.float32
LINE = 4
PAD = 128
VMEM_BYTES = 60 * 1024 * 1024


def in_planes(mesh):
    return mesh.shape["seq"] == 2 and mesh.shape["dp"] == 4 * LINE


def swap_seq(value):
    return lax.ppermute(value, "seq", [(0, 1), (1, 0)])


def swap_dp(value, mask):
    return lax.ppermute(value, "dp", [(i, i ^ mask) for i in range(4 * LINE)])


def swap_core(value):
    return swap_dp(value, 1)


def swap_y(value):
    return swap_dp(value, 2)


def line_up(value):
    return lax.ppermute(value, "dp", [(i, i + 4) for i in range(4 * LINE - 4)])


def line_down(value):
    return lax.ppermute(value, "dp", [(i, i - 4) for i in range(4, 4 * LINE)])


def after(value, *others):
    return lax.optimization_barrier((value,) + others)[0]


def line_scatter(take, place):
    up = down = None
    for step in range(LINE - 1):
        far = jnp.minimum(LINE - 1 - step + place, LINE - 1)
        near = jnp.maximum(step - LINE + 1 + place, 0)
        right, left = take(far), take(near)
        if up is not None:
            right = right + up.astype(F32)
            left = left + down.astype(F32)
        up = line_up(right.astype(BF16))
        down = line_down(left.astype(BF16))
    return take(place) + up.astype(F32) + down.astype(F32)


def near_pieces(own, own_x):
    return swap_seq(own_x), swap_y(own)


def far_pieces(near_x, near_y):
    half = near_x.shape[0] // 2
    return swap_y(near_x[:half]), swap_seq(near_y[half:])


def with_cores(*pieces):
    return pieces + tuple(swap_core(piece) for piece in pieces)


def over_cores(mine, others):
    return mine.astype(F32) + swap_core(others).astype(F32)


def far_links(far):
    half = far.shape[0] // 2
    return swap_y(far[:half]), swap_seq(far[half:])


def near_links(near, from_y, from_x):
    half = from_y.shape[0] // 2
    first = (near[:half] + from_y[half:].astype(F32)).astype(BF16)
    second = (near[half : 2 * half] + from_x[half:].astype(F32)).astype(BF16)
    return first, second


def own_sum(near, from_y, from_x, first, second):
    half = from_y.shape[0] // 2
    low = near[2 * half : 3 * half] + from_y[:half].astype(F32) + first.astype(F32)
    high = near[3 * half :] + from_x[:half].astype(F32) + second.astype(F32)
    return jnp.concatenate([low, high], axis=0)


def turned(values, cos, sin, direction):
    lanes = values.shape[1]
    place = lax.broadcasted_iota(jnp.int32, values.shape, 1) % HDIM
    swapped = jnp.where(
        place < HDIM // 2,
        pltpu.roll(values, lanes - HDIM // 2, 1),
        pltpu.roll(values, HDIM // 2, 1),
    )
    times = lanes // cos.shape[1]
    cos = jnp.concatenate([cos] * times, axis=1)
    sin = jnp.concatenate([sin] * times, axis=1)
    if direction > 0:
        return values * cos + swapped * sin
    return values * cos - swapped * sin


def place_shards(place_ref, own_ref, other_ref, shard, store):
    for core in range(2):
        source = other_ref if core else own_ref
        for row in range(2):
            for line in range(LINE):
                index = (place_ref[0] ^ line) * 4 + (place_ref[1] ^ row) * 2 + (place_ref[2] ^ core)
                store(source, (row * LINE + line) * shard, pl.multiple_of(index * shard, shard))


def qkv_kernel(
    place_ref, x_ref, own_ref, other_ref, cos_ref, sin_ref,
    h_ref, q_ref, k_ref, v_ref, w_ref, gain_ref, columns_buf,
):
    q_width, kv_heads = q_ref.shape[1], k_ref.shape[0]
    kv_width = kv_heads * HDIM
    width, columns = w_ref.shape
    shard = own_ref.shape[0] // (2 * LINE)

    @pl.when(pl.program_id(0) == 0)
    def _():
        def store(source, low, place):
            for seq in range(2):
                first = seq * (columns + PAD)
                rows = pl.ds(pl.multiple_of(place + seq * (width // 2), shard), shard)
                w_ref[rows, :] = source[low : low + shard, first : first + columns]
                columns_buf[rows, :] = source[
                    low : low + shard, first + columns : first + columns + PAD
                ].astype(F32)

        place_shards(place_ref, own_ref, other_ref, shard, store)
        gain_ref[...] = columns_buf[...].T[: gain_ref.shape[0]]

    value = x_ref[...].astype(F32)
    scale = lax.rsqrt(jnp.mean(value * value, axis=-1, keepdims=True) + EPSILON)
    normed = (value * scale * gain_ref[0:1, :]).astype(BF16)
    h_ref[...] = normed
    both = jnp.dot(normed, w_ref[...], preferred_element_type=F32)
    spun = turned(both[:, : q_width + kv_width], cos_ref[...], sin_ref[...], 1)
    q_ref[...] = (spun[:, :q_width] * SCORE_SCALE).astype(BF16)
    for head in range(kv_heads):
        low = q_width + head * HDIM
        k_ref[head] = spun[:, low : low + HDIM].astype(BF16)
        low = low + kv_width
        v_ref[head] = both[:, low : low + HDIM].astype(BF16)


def project(places, x_sorted, own, other, cos, sin, q_width, kv_heads):
    rows, width = x_sorted.shape
    tile = 256
    columns = q_width + 2 * kv_heads * HDIM

    def row_block(lanes):
        return pl.BlockSpec((tile, lanes), lambda i, p: (i, 0))

    def whole(shape):
        return pl.BlockSpec(shape, lambda i, p: (0, 0))

    heads = pl.BlockSpec((kv_heads, tile, HDIM), lambda i, p: (0, i, 0))
    return pl.pallas_call(
        qkv_kernel,
        grid_spec=pltpu.PrefetchScalarGridSpec(
            num_scalar_prefetch=1,
            grid=(rows // tile,),
            in_specs=[
                row_block(width),
                whole(own.shape),
                whole(other.shape),
                row_block(cos.shape[1]),
                row_block(cos.shape[1]),
            ],
            out_specs=[
                row_block(width), row_block(q_width), heads, heads,
                whole((width, columns)), whole((8, width)),
            ],
            scratch_shapes=[pltpu.VMEM((width, PAD), F32)],
        ),
        out_shape=[
            jax.ShapeDtypeStruct((rows, width), BF16),
            jax.ShapeDtypeStruct((rows, q_width), BF16),
            jax.ShapeDtypeStruct((kv_heads, rows, HDIM), BF16),
            jax.ShapeDtypeStruct((kv_heads, rows, HDIM), BF16),
            jax.ShapeDtypeStruct((width, columns), BF16),
            jax.ShapeDtypeStruct((8, width), F32),
        ],
        compiler_params=pltpu.CompilerParams(vmem_limit_bytes=VMEM_BYTES),
        cost_estimate=pl.CostEstimate(
            flops=rows * width * columns // 8,
            bytes_accessed=rows * width + width * columns,
            transcendentals=rows,
        ),
        name="project",
    )(places, x_sorted, own, other, cos, sin)


def mix_kernel(place_ref, mine_ref, theirs_ref, x_ref, gain_ref, w_ref, m_ref, h_ref, parts_ref):
    half = parts_ref.shape[1]

    @pl.when(pl.program_id(0) == 0)
    def _():
        for part in range(2):
            low = pl.multiple_of((place_ref[0] ^ part) * half, half)
            parts_ref[part] = w_ref[pl.ds(low, half), :]

    mixed = jnp.dot(mine_ref[...], parts_ref[0], preferred_element_type=F32)
    mixed = mixed + jnp.dot(theirs_ref[...], parts_ref[1], preferred_element_type=F32)
    value = x_ref[...].astype(F32) + BRANCH_SCALE * mixed
    m_ref[...] = value
    scale = lax.rsqrt(jnp.mean(value * value, axis=-1, keepdims=True) + EPSILON)
    h_ref[...] = (value * scale * gain_ref[...]).astype(BF16)


def mix(place, mine, theirs, tokens, gain, weights):
    rows, width = tokens.shape
    half = mine.shape[1]
    tile = 256

    def row_block(lanes):
        return pl.BlockSpec((tile, lanes), lambda i, p: (i, 0))

    def whole(shape):
        return pl.BlockSpec(shape, lambda i, p: (0,) * len(shape))

    return pl.pallas_call(
        mix_kernel,
        grid_spec=pltpu.PrefetchScalarGridSpec(
            num_scalar_prefetch=1,
            grid=(rows // tile,),
            in_specs=[
                row_block(half), row_block(half), row_block(width), whole(gain.shape),
                whole((width, width)),
            ],
            out_specs=[row_block(width), row_block(width), whole((2, half, width))],
        ),
        out_shape=[
            jax.ShapeDtypeStruct((rows, width), F32),
            jax.ShapeDtypeStruct((rows, width), BF16),
            jax.ShapeDtypeStruct((2, half, width), BF16),
        ],
        compiler_params=pltpu.CompilerParams(vmem_limit_bytes=VMEM_BYTES),
        cost_estimate=pl.CostEstimate(
            flops=rows * width * width // 8, bytes_accessed=rows * width, transcendentals=rows
        ),
        name="mix",
    )(place, mine, theirs, tokens, gain, weights)


def token_grad_kernel(dq_ref, dk_ref, dv_ref, w_ref, own_ref, other_ref, mine_ref, sent_ref):
    q_width, kv_width = dq_ref.shape[1], dk_ref.shape[1]
    cuts = (0, q_width, q_width + kv_width, q_width + 2 * kv_width)
    grad = contract(dq_ref[...], w_ref[:, cuts[0] : cuts[1]], 1, 1)
    grad = grad + contract(dk_ref[...], w_ref[:, cuts[1] : cuts[2]], 1, 1)
    grad = (grad + contract(dv_ref[...], w_ref[:, cuts[2] : cuts[3]], 1, 1)).astype(BF16)
    for place_ref, out_ref in ((other_ref, sent_ref), (own_ref, mine_ref)):
        shape = (place_ref.shape[0], grad.shape[0])
        picked = lax.broadcasted_iota(jnp.int32, shape, 1) == place_ref[...]
        picked = jnp.where(picked, 1.0, 0.0).astype(BF16)
        out_ref[...] = jnp.dot(picked, grad, preferred_element_type=F32).astype(BF16)


def token_grad(grads, weights, own_places, other_places):
    rows, count = grads[0].shape[0], own_places.shape[0]
    width = weights.shape[0]
    columns = sum(grad.shape[1] for grad in grads)
    tile = width // 3

    def whole(array):
        return pl.BlockSpec(array.shape, lambda i: (0, 0))

    block = pl.BlockSpec((count, tile), lambda i: (0, i))
    return pl.pallas_call(
        token_grad_kernel,
        grid=(3,),
        in_specs=[whole(grad) for grad in grads]
        + [pl.BlockSpec((tile, columns), lambda i: (i, 0)), whole(own_places), whole(other_places)],
        out_specs=[block, block],
        out_shape=[jax.ShapeDtypeStruct((count, width), BF16)] * 2,
        compiler_params=pltpu.CompilerParams(vmem_limit_bytes=VMEM_BYTES),
        cost_estimate=pl.CostEstimate(
            flops=rows * width * columns // 8, bytes_accessed=rows * width, transcendentals=0
        ),
        name="token_grad",
    )(*grads, weights, own_places, other_places)


Q_TILE = 256


def windows(rows):
    longest = rows // 2
    for start in range(0, rows, Q_TILE):
        low = max(0, start - longest + 1) // Q_TILE * Q_TILE
        yield start, low, start + Q_TILE


def allowed_keys(start_ref, row, low, high):
    shape = (Q_TILE, high - low)
    rows = lax.broadcasted_iota(jnp.int32, shape, 0) + row
    keys = lax.broadcasted_iota(jnp.int32, shape, 1) + low
    return (keys <= rows) & (keys >= start_ref[row : row + Q_TILE, :])


def contract(left, right, left_dim, right_dim):
    return lax.dot_general(
        left, right, (((left_dim,), (right_dim,)), ((), ())), preferred_element_type=F32
    )


def probabilities(query, keys, allowed):
    scores = jnp.where(allowed, contract(query, keys, 1, 1), -1e30)
    expon = jnp.exp(scores - jnp.max(scores, axis=-1, keepdims=True))
    return expon * (1.0 / jnp.sum(expon, axis=-1, keepdims=True))


def attend_kernel(base, q_ref, k_ref, v_ref, start_ref, o_ref):
    pair = pl.program_id(0) + base
    ratio = QHEADS // KVHEADS
    for row, low, high in windows(q_ref.shape[0]):
        allowed = allowed_keys(start_ref, row, low, high)
        for side in range(2):
            head = (2 * pair + side) // ratio
            lanes = slice(side * HDIM, (side + 1) * HDIM)
            probs = probabilities(
                q_ref[row : row + Q_TILE, lanes], k_ref[head, low:high, :], allowed
            )
            mixed = contract(probs.astype(BF16), v_ref[head, low:high, :], 1, 0)
            o_ref[row : row + Q_TILE, lanes] = mixed.astype(BF16)


def attention_cost(rows, heads, products):
    area = sum(Q_TILE * (high - low) for _, low, high in windows(rows))
    return pl.CostEstimate(
        flops=products * heads * area * 16,
        bytes_accessed=8 * rows * heads * HDIM,
        transcendentals=heads * area,
    )


def attend(query, keys, values, starts, base, pairs):
    rows = query.shape[0]
    pair_block = pl.BlockSpec((rows, 2 * HDIM), lambda j: (0, j + base))
    whole = pl.BlockSpec(keys.shape, lambda j: (0, 0, 0))
    return pl.pallas_call(
        functools.partial(attend_kernel, base),
        grid=(pairs,),
        in_specs=[pair_block, whole, whole, pl.BlockSpec((rows, 1), lambda j: (0, 0))],
        out_specs=pl.BlockSpec((rows, 2 * HDIM), lambda j: (0, j)),
        out_shape=jax.ShapeDtypeStruct((rows, pairs * 2 * HDIM), BF16),
        compiler_params=pltpu.CompilerParams(vmem_limit_bytes=VMEM_BYTES),
        cost_estimate=attention_cost(rows, 2 * pairs, 2),
        name="attend",
    )(query, keys, values, starts)


def attend_back_kernel(
    q_ref, k_ref, v_ref, d_ref, start_ref, cos_ref, sin_ref,
    dq_ref, dk_ref, dv_ref, dk_sum, dv_sum,
):
    pair = pl.program_id(0)
    ratio = QHEADS // KVHEADS

    @pl.when(pair == 0)
    def _():
        dk_sum[...] = jnp.zeros_like(dk_sum)
        dv_sum[...] = jnp.zeros_like(dv_sum)

    for row, low, high in windows(q_ref.shape[0]):
        allowed = allowed_keys(start_ref, row, low, high)
        grads = []
        for side in range(2):
            head = (2 * pair + side) // ratio
            lanes = slice(side * HDIM, (side + 1) * HDIM)
            query = q_ref[row : row + Q_TILE, lanes]
            keys = k_ref[head, low:high, :]
            probs = probabilities(query, keys, allowed)
            grad_out = d_ref[row : row + Q_TILE, lanes]
            grad_probs = contract(grad_out, v_ref[head, low:high, :], 1, 1)
            inner = jnp.sum(probs * grad_probs, axis=-1, keepdims=True)
            grad_scores = (probs * (grad_probs - inner)).astype(BF16)
            grads.append(contract(grad_scores, keys, 1, 0) * SCORE_SCALE)
            dk_sum[head, low:high, :] += contract(grad_scores, query, 0, 0)
            dv_sum[head, low:high, :] += contract(probs.astype(BF16), grad_out, 0, 0)
        grad_query = jnp.concatenate(grads, axis=1).astype(BF16).astype(F32)
        dq_ref[row : row + Q_TILE, :] = turned(
            grad_query,
            cos_ref[row : row + Q_TILE, :],
            sin_ref[row : row + Q_TILE, :],
            -1,
        ).astype(BF16)

    @pl.when(pair == pl.num_programs(0) - 1)
    def _():
        heads = range(dk_sum.shape[0])
        grad_keys = jnp.concatenate([dk_sum[head] for head in heads], axis=1)
        grad_keys = grad_keys.astype(BF16).astype(F32)
        dk_ref[...] = turned(grad_keys, cos_ref[...], sin_ref[...], -1).astype(BF16)
        dv_ref[...] = jnp.concatenate([dv_sum[head] for head in heads], axis=1).astype(BF16)


def attend_back(query, keys, values, grad_out, starts, cos, sin):
    rows, lanes = query.shape
    pairs = lanes // (2 * HDIM)
    kv_heads = keys.shape[0]
    pair_block = pl.BlockSpec((rows, 2 * HDIM), lambda j: (0, j))
    whole = pl.BlockSpec(keys.shape, lambda j: (0, 0, 0))

    def fixed(lanes_of):
        return pl.BlockSpec((rows, lanes_of), lambda j: (0, 0))

    flat = kv_heads * HDIM
    return pl.pallas_call(
        attend_back_kernel,
        grid=(pairs,),
        in_specs=[
            pair_block, whole, whole, pair_block, fixed(1), fixed(2 * HDIM), fixed(2 * HDIM),
        ],
        out_specs=[pair_block, fixed(flat), fixed(flat)],
        out_shape=[
            jax.ShapeDtypeStruct(query.shape, BF16),
            jax.ShapeDtypeStruct((rows, flat), BF16),
            jax.ShapeDtypeStruct((rows, flat), BF16),
        ],
        scratch_shapes=[pltpu.VMEM(keys.shape, F32), pltpu.VMEM(keys.shape, F32)],
        compiler_params=pltpu.CompilerParams(vmem_limit_bytes=VMEM_BYTES),
        cost_estimate=attention_cost(rows, 2 * pairs, 5),
        name="attend_back",
    )(query, keys, values, grad_out, starts, cos, sin)


SLOTS = 2 * LINE - 1
SLOT_ORDER = (0, 3, 1, 2)
OWN, NEAR_X, NEAR_Y, FAR_Y, FAR_X = range(5)
FAR_TILES = (((NEAR_Y, 0), (FAR_Y, 0)), ((NEAR_X, 1), (FAR_X, 0)))
NEAR_TILES = (((NEAR_X, 0), (NEAR_Y, 1)), ((OWN, 0), (OWN, 1)))


def used_pieces(tiles):
    return sorted({piece for tile in tiles for piece, _ in tile})


def experts_kernel(tiles, half_rows, place_ref, *refs):
    used = used_pieces(tiles)
    sides = 2 * len(used)
    h_pieces, g_pieces, slots = refs[:sides], refs[sides : 2 * sides], refs[2 * sides : 2 * sides + SLOTS]
    select_ref = refs[2 * sides + SLOTS]
    (
        f_mine, f_other, d_mine, d_other, hid_a, hid_b, du_a, du_b, hcopy_ref, gcopy_ref,
        w_in, w_out, h_buf, g_buf, hidden, du_all, weight_sems, row_sems,
    ) = refs[-18:]
    width = h_buf.shape[2]
    half = slots[0].shape[1] // 3
    part = 2 * half
    step = pl.program_id(0)
    steps = 2 * len(tiles)

    def weight_copies(spot, slot):
        return (
            pltpu.make_async_copy(
                slots[slot].at[:, :part],
                w_in.at[:, spot * part : (spot + 1) * part],
                weight_sems.at[0, spot],
            ),
            pltpu.make_async_copy(
                slots[slot].at[:, part:],
                w_out.at[:, spot * half : (spot + 1) * half],
                weight_sems.at[1, spot],
            ),
        )

    def row_copies(number, buffer):
        side, tile = divmod(number, len(tiles))
        copies = []
        for spot, (piece, part_of) in enumerate(tiles[tile]):
            index = side * len(used) + used.index(piece)
            for kind, (pieces, held) in enumerate(((h_pieces, h_buf), (g_pieces, g_buf))):
                copies.append(
                    pltpu.make_async_copy(
                        pieces[index].at[pl.ds(part_of * half_rows, half_rows), :],
                        held.at[buffer, pl.ds(spot * half_rows, half_rows), :],
                        row_sems.at[buffer, 2 * kind + spot],
                    )
                )
        return copies

    def fetch(wanted, buffer):
        for number in range(steps):

            @pl.when(wanted == number)
            def _():
                for copy in row_copies(number, buffer):
                    copy.start()

    buffer = step % 2

    @pl.when(step == 0)
    def _():
        fetch(step, 0)
        for spot, expert in enumerate(SLOT_ORDER):
            for slot in range(expert, expert + LINE):

                @pl.when(slot == LINE - 1 + expert - place_ref[0])
                def _():
                    for copy in weight_copies(spot, slot):
                        copy.start()

        for spot in range(LINE):
            for copy in weight_copies(spot, LINE - 1):
                copy.wait()

    @pl.when(step + 1 < steps)
    def _():
        fetch(step + 1, 1 - buffer)

    for copy in row_copies(0, buffer):
        copy.wait()

    rows = h_buf[buffer]
    grads = g_buf[buffer, :, :width]
    hcopy_ref[...] = rows
    gcopy_ref[...] = grads
    gates = jnp.dot(g_buf[buffer, :, width:], select_ref[...], preferred_element_type=F32)
    for spot in range(LINE):
        units = slice(spot * half, (spot + 1) * half)
        both = jnp.dot(
            rows, w_in[:, spot * part : (spot + 1) * part], preferred_element_type=F32
        )
        back = jnp.dot(grads, w_out[:, units], preferred_element_type=F32)
        gate = gates[:, units]
        first, second = both[:, :half], both[:, half:]
        sigma = jax.nn.sigmoid(first)
        silu = first * sigma
        hidden[:, units] = (gate * (silu * second)).astype(BF16)
        back = back * (BRANCH_SCALE * gate)
        d_first = back * second * (sigma * (1.0 + first * (1.0 - sigma)))
        d_second = back * silu
        du_all[:, spot * part : spot * part + half] = d_first.astype(BF16)
        du_all[:, spot * part + half : (spot + 1) * part] = d_second.astype(BF16)
    hid_a[...] = hidden[:, : 2 * half]
    hid_b[...] = hidden[:, 2 * half :]
    du_a[...] = du_all[:, : 2 * part]
    du_b[...] = du_all[:, 2 * part :]
    ffn = contract(hidden[...], w_out[...], 1, 1).astype(BF16)
    back_rows = contract(du_all[...], w_in[...], 1, 1).astype(BF16)

    @pl.when(step < len(tiles))
    def _():
        f_mine[...] = ffn
        d_mine[...] = back_rows

    @pl.when(step >= len(tiles))
    def _():
        f_other[...] = ffn
        d_other[...] = back_rows


def run_experts(tiles, place, row_pieces, grad_pieces, slots, select, base, kept):
    used = used_pieces(tiles)
    sides = len(row_pieces) // 2
    wanted = used + [sides + piece for piece in used]
    rows = [row_pieces[piece] for piece in wanted]
    grads = [grad_pieces[piece] for piece in wanted]
    tile, width = row_pieces[OWN].shape
    wide = grad_pieces[OWN].shape[1]
    half = slots[0].shape[1] // 3
    part = 2 * half
    count = len(tiles)
    steps = 2 * count
    total = 8 * tile

    def late(lanes):
        return pl.BlockSpec((tile, lanes), lambda i, p: (i + base, 0))

    mine = pl.BlockSpec((tile, width), lambda i, p: (jnp.minimum(i, count - 1), 0))
    others = pl.BlockSpec((tile, width), lambda i, p: (jnp.maximum(i - count, 0), 0))
    anywhere = pl.BlockSpec(memory_space=pl.ANY)
    kept = list(kept)
    lead = 1 + 2 * len(wanted) + SLOTS + 1
    partial = jax.ShapeDtypeStruct((count * tile, width), BF16)
    lanes = [2 * half, 2 * half, 2 * part, 2 * part, width, width]
    return pl.pallas_call(
        functools.partial(experts_kernel, tiles, tile // 2),
        grid_spec=pltpu.PrefetchScalarGridSpec(
            num_scalar_prefetch=1,
            grid=(steps,),
            in_specs=[anywhere] * (2 * len(wanted) + SLOTS)
            + [pl.BlockSpec(select.shape, lambda i, p: (0, 0))]
            + [anywhere] * len(kept),
            out_specs=[mine, others, mine, others] + [late(n) for n in lanes],
            scratch_shapes=[
                pltpu.VMEM((width, LINE * part), BF16),
                pltpu.VMEM((width, LINE * half), BF16),
                pltpu.VMEM((2, tile, width), BF16),
                pltpu.VMEM((2, tile, wide), BF16),
                pltpu.VMEM((tile, LINE * half), BF16),
                pltpu.VMEM((tile, LINE * part), BF16),
                pltpu.SemaphoreType.DMA((2, LINE)),
                pltpu.SemaphoreType.DMA((2, 4)),
            ],
        ),
        out_shape=[partial] * 4 + [jax.ShapeDtypeStruct((total, n), BF16) for n in lanes],
        input_output_aliases={lead + i: 4 + i for i in range(len(kept))},
        compiler_params=pltpu.CompilerParams(vmem_limit_bytes=VMEM_BYTES),
        cost_estimate=pl.CostEstimate(
            flops=steps * tile * width * LINE * (part + half) // 4,
            bytes_accessed=2 * steps * tile * (6 * width + LINE * (part + half)),
            transcendentals=steps * tile * LINE * half,
        ),
        name="experts",
    )(place, *rows, *grads, *slots, select, *kept)


def qkv_grad_kernel(h_ref, dq_ref, dk_ref, dv_ref, gain_ref, o_ref):
    shard = o_ref.shape[-2]
    rows = h_ref[...]
    low = 0
    gains = jnp.broadcast_to(gain_ref[...], (PAD, gain_ref.shape[1])).T.astype(BF16)
    parts = [contract(rows, ref[...], 0, 0).astype(BF16) for ref in (dq_ref, dk_ref, dv_ref)]
    for part in parts + [gains]:
        for block in range(h_ref.shape[1] // shard):
            place = (block % 2, block // 2 % 2, 0, block // 4)
            o_ref[place + (slice(None), slice(low, low + part.shape[1]))] = part[
                block * shard : (block + 1) * shard
            ]
        low = low + part.shape[1]


def qkv_grad(normed, grads, gain_row, shard):
    rows, width = normed.shape
    columns = sum(grad.shape[1] for grad in grads)
    tile = width // 4
    planes = tile // (4 * shard)
    return pl.pallas_call(
        qkv_grad_kernel,
        grid=(4,),
        in_specs=[pl.BlockSpec((rows, tile), lambda i: (0, i))]
        + [pl.BlockSpec(grad.shape, lambda i: (0, 0)) for grad in grads]
        + [pl.BlockSpec((1, tile), lambda i: (0, i))],
        out_specs=pl.BlockSpec(
            (2, 2, 1, planes, shard, columns + PAD), lambda i: (0, 0, i // 2, i % 2, 0, 0)
        ),
        out_shape=jax.ShapeDtypeStruct((2, 2, 2, LINE, shard, columns + PAD), BF16),
        compiler_params=pltpu.CompilerParams(vmem_limit_bytes=VMEM_BYTES),
        cost_estimate=pl.CostEstimate(
            flops=rows * width * columns // 8,
            bytes_accessed=rows * width,
            transcendentals=0,
        ),
        name="qkv_grad",
    )(normed, *grads, gain_row)


def norm_back(value, gain, grad):
    scale = lax.rsqrt(jnp.mean(value * value, axis=-1, keepdims=True) + EPSILON)
    unit = value * scale
    grad_gain = jnp.sum(grad * unit, axis=0)
    scaled = grad * gain
    inner = jnp.mean(scaled * unit, axis=-1, keepdims=True)
    return scale * (scaled - unit * inner), grad_gain


def shards_plane(
    tokens,
    cotangent,
    positions,
    lengths,
    routes,
    logits,
    w_query,
    w_key,
    w_value,
    w_output,
    gain_attn,
    gain_ffn,
    w_in,
    w_out,
):
    seq = lax.axis_index("seq")
    data = lax.axis_index("dp")
    line, row_of, core = data // 4, (data // 2) % 2, data % 2
    tok_count, width = tokens.shape
    group_len = positions.shape[1]
    shard = w_query.shape[0]
    q_width = w_query.shape[1] // 2
    kv_width = w_key.shape[1] // 2
    kv_heads = kv_width // HDIM
    first_seq = seq == 0

    def ordered(mine, theirs, axis):
        low = jnp.where(first_seq, mine, theirs)
        high = jnp.where(first_seq, theirs, mine)
        return jnp.concatenate([low, high], axis=axis)

    def half_of(weights, which):
        half = weights.shape[1] // 2
        return lax.dynamic_slice_in_dim(weights, which * half, half, axis=1)

    def both_axes(value, pairs):
        return lax.ppermute(value, ("seq", "dp"), pairs)

    def device(s, d):
        return s * 4 * LINE + d

    straight, crossed = [], []
    for s in range(2):
        for d in range(4 * LINE):
            c = d % 2
            straight.append((device(s, d), device(c, d - c + s)))
            crossed.append((device(s, d), device(c, d - c + 1 - s)))
    crossed_back = [(there, here) for here, there in crossed]
    first_core = core == 0

    projections = (w_query, w_key, w_value)
    qkv_width = q_width + 2 * kv_width
    qkv_width = q_width + 2 * kv_width
    gain_columns = jnp.pad(jnp.stack([gain_attn, gain_ffn], axis=1), ((0, 0), (0, PAD - 2)))
    mine, theirs = [
        jnp.concatenate([half_of(w, which) for w in projections] + [gain_columns], axis=1)
        for which in (seq, 1 - seq)
    ]
    theirs = swap_seq(jnp.concatenate([theirs, w_output], axis=1))
    output_pair = ordered(w_output[None], theirs[None, :, qkv_width + PAD :], 0)
    block = ordered(mine, theirs[:, : qkv_width + PAD], 1)
    along = [block] + [swap_dp(block, 4 * step) for step in range(1, LINE)]
    places_of = jnp.stack([line, row_of, core]).astype(jnp.int32)

    in_own = w_in[0]
    half = in_own.shape[1] // 2
    sent = jnp.concatenate(
        [lax.dynamic_slice_in_dim(in_own, seq * half, half, axis=1), w_out[0].T], axis=1
    )
    same = both_axes(sent, straight)
    cross = both_axes(lax.dynamic_slice_in_dim(in_own, (1 - seq) * half, half, axis=1), crossed)
    same, cross, along = lax.optimization_barrier((same, cross, along))
    own_part = jnp.concatenate(
        [
            jnp.where(first_core, same[:, :half], cross),
            jnp.where(first_core, cross, same[:, :half]),
            same[:, half:],
        ],
        axis=1,
    )
    other_tokens = swap_seq(after(tokens, own_part))
    output_full = lax.all_gather(after(output_pair, own_part), "dp", axis=1, tiled=True)
    output_full = output_full.reshape(width, width)
    cut = width // 2
    lines = (line_up(own_part[:cut]), line_down(own_part[:cut]))
    qkv_rows = after(jnp.concatenate(along, axis=0), own_part)
    qkv_near, lines = lax.optimization_barrier((swap_y(qkv_rows), lines))
    late_part = after(own_part[cut:], lines)
    late_lines = (line_up(late_part), line_down(late_part))
    qkv_rows = jnp.concatenate([qkv_rows, qkv_near], axis=0)
    qkv_others = swap_core(qkv_rows)

    experts_all = 4 * LINE
    gates = jax.nn.softmax(logits, axis=-1)
    named = routes[:, :, None] == jnp.arange(experts_all, dtype=jnp.int32)[None, None, :]
    gate_table = jnp.sum(jnp.where(named, gates[:, :, None], 0.0), axis=1)
    gate_high = lax.reduce_precision(gate_table, 8, 7)
    grad_rows = jnp.concatenate(
        [
            cotangent,
            gate_high.astype(BF16),
            (gate_table - gate_high).astype(BF16),
            jnp.zeros((tok_count, PAD - 2 * experts_all), BF16),
        ],
        axis=1,
    )
    grad_near = near_pieces(grad_rows, after(grad_rows, other_tokens))
    lane = jnp.arange(PAD, dtype=jnp.int32)[:, None]
    hosted = jnp.repeat(
        jnp.array(SLOT_ORDER, jnp.int32) * 4 + 2 * row_of + seq, half, total_repeat_length=LINE * half
    )
    select = ((lane % experts_all == hosted[None, :]) & (lane < 2 * experts_all)).astype(BF16)

    places = positions[0]
    ends = jnp.cumsum(lengths[0])
    ranks = jnp.arange(group_len, dtype=jnp.int32)
    reached = ranks[:, None] >= ends[None, :]
    starts = jnp.max(jnp.where(reached, ends[None, :], 0), axis=1)
    local = (ranks - starts).astype(F32)
    freqs = jnp.power(THETA, -jnp.arange(HDIM // 2, dtype=F32) * 2.0 / HDIM)
    angles = local[:, None] * freqs[None, :]
    cos, sin = jnp.cos(angles), jnp.sin(angles)
    cos = jnp.concatenate([cos, cos, cos, cos], axis=1)
    sin = jnp.concatenate([-sin, sin, -sin, sin], axis=1)
    start_column = starts[:, None]
    own_places = lax.dynamic_slice_in_dim(places, seq * tok_count, tok_count)
    other_places = lax.dynamic_slice_in_dim(places, (1 - seq) * tok_count, tok_count)
    sort_own = (ranks[:, None] == own_places[None, :]).astype(BF16)
    sort_other = (ranks[:, None] == other_places[None, :]).astype(BF16)

    def to_order(own, other):
        return (
            contract(sort_own, own, 1, 0) + contract(sort_other, other, 1, 0)
        ).astype(BF16)

    def from_order(sort, values):
        return contract(sort, values, 0, 0).astype(BF16)

    x_sorted = to_order(tokens, other_tokens)
    normed, query, keys, values, w_qkv, gains = project(
        places_of, x_sorted, qkv_rows, qkv_others, cos, sin, q_width, kv_heads
    )
    gain_one, gain_two = gains[0], gains[1]
    query, late_lines = lax.optimization_barrier((query, late_lines))
    up_one = jnp.concatenate([lines[0], late_lines[0]], axis=0)
    down_one = jnp.concatenate([lines[1], late_lines[1]], axis=0)
    query, up_one, down_one = lax.optimization_barrier((query, up_one, down_one))
    up_two, down_two = line_up(up_one), line_down(down_one)
    pairs = q_width // (2 * HDIM)
    first_pairs = (pairs + 1) // 2
    mixed_one = attend(query, keys, values, start_column, 0, first_pairs)
    sent_one = swap_seq(from_order(sort_other, mixed_one))
    query_two, grad_near_x, grad_near_y = after((query, *grad_near), mixed_one)
    grad_near = (grad_near_x, grad_near_y)
    grad_far = far_pieces(*grad_near)
    mixed_two = attend(
        query_two, keys, values, start_column, first_pairs, pairs - first_pairs
    )
    sent_two = swap_seq(from_order(sort_other, mixed_two))
    mixed_mine = [from_order(sort_own, mixed_one), from_order(sort_own, mixed_two)]
    mixed_mine = jnp.concatenate(mixed_mine, axis=1)
    mixed_theirs = jnp.concatenate([sent_one, sent_two], axis=1)
    mixed_theirs, up_two, down_two = lax.optimization_barrier((mixed_theirs, up_two, down_two))
    up_three, down_three = line_up(up_two), line_down(down_two)
    inputs = tokens.astype(F32)
    middle, normed_ffn, output_parts = mix(
        seq.astype(jnp.int32)[None], mixed_mine, mixed_theirs, tokens, gain_two[None, :], output_full
    )
    normed_ffn = after(normed_ffn, *grad_far)
    row_near = near_pieces(normed_ffn, normed_ffn)
    row_far = far_pieces(*row_near)
    slots = [up_three, up_two, up_one, own_part, down_one, down_two, down_three]
    row_pieces = with_cores(normed_ffn, *row_near, *row_far)
    grad_pieces = with_cores(*after((grad_rows, *grad_near, *grad_far), row_near[0]))
    place = line.astype(jnp.int32)[None]
    far = run_experts(FAR_TILES, place, row_pieces, grad_pieces, slots, select, 0, ())
    far_back = over_cores(far[2], far[3]).astype(BF16)
    back_y, back_x = far_links(far_back)
    near = run_experts(
        NEAR_TILES, after(place, far_back), row_pieces, grad_pieces, slots, select, 4, far[4:]
    )
    hid_a, hid_b, du_a, du_b, all_rows, all_grads = near[4:]

    def weight_grads(rows, grads, grad_both, hidden):
        inner = contract(rows, grad_both, 0, 0)
        outer = contract(grads, hidden, 0, 0) * BRANCH_SCALE
        return [
            jnp.concatenate(
                [inner[:, 2 * half * i : 2 * half * (i + 1)], outer[:, half * i : half * (i + 1)]],
                axis=1,
            ).astype(BF16)
            for i in range(2)
        ]

    rows_early, grads_early, back_y, back_x = lax.optimization_barrier(
        (all_rows, all_grads, back_y, back_x)
    )
    outer_grads = weight_grads(rows_early, grads_early, du_a, hid_a)
    grads_of = dict(zip(SLOT_ORDER[:2], outer_grads))
    far_line = (line_up(outer_grads[1]), line_down(outer_grads[0]))
    near_back = over_cores(after(near[2], *outer_grads), near[3])
    first, second = near_links(near_back, back_y, back_x)
    rows_late, grads_late = after((all_rows, all_grads), first, second)
    inner_grads = weight_grads(rows_late, grads_late, du_b, hid_b)
    grads_of.update(zip(SLOT_ORDER[2:], inner_grads))
    first, second = swap_seq(first), swap_y(second)
    near_back = after(near_back, *inner_grads)
    grad_normed_ffn = own_sum(near_back, back_y, back_x, first, second)

    def line_partial(first, *rest):
        value = grads_of[first]
        for where, expert in enumerate(rest):
            value = jnp.where(line > where, grads_of[expert], value)
        return value.astype(F32)

    def line_step(step, arrived):
        up, down = arrived
        last = LINE - 1
        right = line_partial(*range(last - step, LINE)) + up.astype(F32)
        left = grads_of[step]
        for where in range(step):
            left = jnp.where(line < last - where, grads_of[step - 1 - where], left)
        left = left.astype(F32) + down.astype(F32)
        return right.astype(BF16), left.astype(BF16)

    grad_final = cotangent.astype(F32)
    grad_norm, grad_gain_two = norm_back(middle, gain_two, grad_normed_ffn)
    grad_middle = grad_final + grad_norm
    grad_attn = (BRANCH_SCALE * grad_middle).astype(BF16)
    grad_mixed = contract(grad_attn, output_parts[0], 1, 1).astype(BF16)
    grad_other = contract(grad_attn, output_parts[1], 1, 1).astype(BF16)
    grad_other = swap_seq(grad_other)
    grad_w_output = contract(ordered(mixed_mine, mixed_theirs, 1), grad_attn, 0, 0)
    far_f, far_f_other, near_f, near_f_other = after(
        (far[0], far[1], near[0], near[1]), grad_mixed
    )
    far_ffn = over_cores(far_f, far_f_other).astype(BF16)
    ffn_y, ffn_x = far_links(far_ffn)
    near_ffn = over_cores(near_f, near_f_other)
    right, left = line_step(1, far_line)
    grad_other = after(grad_other, right, left, far_ffn, grad_w_output)
    grad_sorted = to_order(grad_mixed, grad_other)
    mid_line = (line_up(right), line_down(left))
    grad_query, grad_keys, grad_values = attend_back(
        query, keys, values, grad_sorted, start_column, cos, sin
    )
    (grad_query, grad_keys, grad_values), mid_line, ffn_y, ffn_x = lax.optimization_barrier(
        ((grad_query, grad_keys, grad_values), mid_line, ffn_y, ffn_x)
    )
    right, left = line_step(2, mid_line)
    last_first = (line_up(right[:cut]), line_down(left[:cut]))
    first_ffn, second_ffn = near_links(near_ffn, ffn_y, ffn_x)
    first_ffn, second_ffn = swap_seq(first_ffn), swap_y(second_ffn)
    ffn = own_sum(near_ffn, ffn_y, ffn_x, first_ffn, second_ffn)
    output = (middle + BRANCH_SCALE * ffn).astype(BF16)
    grads_qkv = after((grad_query, grad_keys, grad_values), right, left)
    wide = qkv_grad(normed, grads_qkv, grad_gain_two[None, :], shard)


    def chosen(value, which, axis):
        return lax.dynamic_index_in_dim(value, which, axis=axis, keepdims=False)

    summed_output = lax.psum_scatter(
        grad_w_output.astype(BF16), ("seq", "dp"), scatter_dimension=0, tiled=True
    )
    kept = chosen(wide, core, 0).astype(F32)
    kept = kept + swap_core(chosen(wide, 1 - core, 0)).astype(F32)
    grads_late = after(grads_qkv, kept)
    grad_normed, sent_normed = token_grad(
        grads_late, w_qkv, own_places[:, None], other_places[:, None]
    )
    kept, sent_normed = lax.optimization_barrier((kept, sent_normed))
    right_late, left_late = after((right[cut:], left[cut:]), last_first, sent_normed)
    last_late = (line_up(right_late), line_down(left_late))
    grad_normed = grad_normed.astype(F32) + swap_seq(sent_normed).astype(F32)
    scale = lax.rsqrt(jnp.mean(inputs * inputs, axis=-1, keepdims=True) + EPSILON)
    unit = inputs * scale
    scaled = grad_normed * gain_one
    inner = jnp.mean(scaled * unit, axis=-1, keepdims=True)
    grad_tokens = grad_middle + scale * (scaled - unit * inner)
    next_kept = chosen(kept, row_of, 0)
    next_kept = next_kept + swap_y(chosen(kept, 1 - row_of, 0).astype(BF16)).astype(F32)
    next_kept, last_first, last_late, summed_output = lax.optimization_barrier(
        (next_kept, last_first, last_late, summed_output)
    )
    own_grads = line_partial(*range(LINE))
    part_grads = jnp.concatenate(
        [
            own + up.astype(F32) + down.astype(F32)
            for own, (up, down) in ((own_grads[:cut], last_first), (own_grads[cut:], last_late))
        ],
        axis=0,
    ).astype(BF16)
    same_grads = jnp.where(first_core, part_grads[:, :half], part_grads[:, half : 2 * half])
    cross_grads = jnp.where(first_core, part_grads[:, half : 2 * half], part_grads[:, :half])
    same_grads = jnp.concatenate([same_grads, part_grads[:, 2 * half :]], axis=1)
    next_kept, same_grads, cross_grads = lax.optimization_barrier(
        (next_kept, same_grads, cross_grads)
    )
    same = both_axes(same_grads, straight)
    cross = both_axes(cross_grads, crossed_back)
    sent_lines = [
        swap_dp(chosen(next_kept, line ^ step, 1).astype(BF16), 4 * step) for step in range(1, LINE)
    ]
    summed = chosen(next_kept, line, 1) + sum(value.astype(F32) for value in sent_lines)
    summed, same, cross = lax.optimization_barrier((summed, same, cross))
    grad_w_in = ordered(same[:, :half], cross, 1)
    grad_w_out = same[:, half:].T
    kept_rows = chosen(summed, seq, 0)
    sent_rows = swap_seq(chosen(summed, 1 - seq, 0).astype(BF16)).astype(F32)
    cuts = (q_width, q_width + kv_width, qkv_width)
    pieces = [
        (a, b) for a, b in zip(jnp.split(kept_rows, cuts, axis=1), jnp.split(sent_rows, cuts, axis=1))
    ]
    grad_projections = [ordered(a, b, 1) for a, b in pieces[:3]]
    grad_gain_ffn = (pieces[3][0] + pieces[3][1])[:, 0]
    grad_gain_attn = sum(
        jnp.sum(grad * weight.astype(F32), axis=1)
        for grad, weight in zip(grad_projections, projections)
    ) / gain_attn.astype(F32)
    return (
        output,
        grad_tokens,
        grad_projections[0],
        grad_projections[1],
        grad_projections[2],
        summed_output.astype(F32),
        grad_gain_attn,
        grad_gain_ffn,
        grad_w_in.astype(F32)[None],
        grad_w_out.astype(F32)[None],
    )


def solution(mesh):
    placed = (
        P(("seq", "dp"), None),
        P(("seq", "dp"), None),
        P("dp", None),
        P("dp", None),
        P(("seq", "dp"), None),
        P(("seq", "dp"), None),
        P(("seq", "dp"), None),
        P(("seq", "dp"), None),
        P(("seq", "dp"), None),
        P(("seq", "dp"), None),
        P(("seq", "dp")),
        P(("seq", "dp")),
        P("dp", None, "seq"),
        P("dp", "seq", None),
    )
    return jax.shard_map(
        shards_plane if in_planes(mesh) else shards_general,
        mesh=mesh,
        in_specs=placed,
        out_specs=(
            P(("seq", "dp"), None),
            P(("seq", "dp"), None),
            P(("seq", "dp"), None),
            P(("seq", "dp"), None),
            P(("seq", "dp"), None),
            P(("seq", "dp"), None),
            P(("seq", "dp")),
            P(("seq", "dp")),
            P("dp", None, "seq"),
            P("dp", "seq", None),
        ),
        check_vma=False,
    )
```

```python
import functools

import jax
import jax.numpy as jnp
from jax import lax
from jax.experimental import pallas as pl
from jax.experimental.pallas import tpu as pltpu
from jax.sharding import PartitionSpec as P

QHEADS = 24
KVHEADS = 8
HDIM = 64
FF = 512
TOP = 8


EPSILON = 1e-06
BRANCH_SCALE = 0.22
SCORE_SCALE = 1.0 / 64.0
THETA = 10000.0


def rms_norm(value, gain):
    return value * lax.rsqrt(jnp.mean(value * value, axis=-1, keepdims=True) + EPSILON) * gain


def local_places(placing, seq_lengths):
    ends = jnp.cumsum(seq_lengths)
    segment = jnp.sum((placing[:, None] >= ends[None, :]).astype(jnp.int32), axis=1)
    starts = ends - seq_lengths
    member = segment[:, None] == jnp.arange(seq_lengths.shape[0], dtype=jnp.int32)[None, :]
    start_of = jnp.sum(jnp.where(member, starts[None, :], 0), axis=1)
    return (segment, placing - start_of)


def rotate(values, place, direction):
    half = values.shape[-1] // 2
    freqs = jnp.power(THETA, -jnp.arange(half, dtype=jnp.float32) * 2.0 / values.shape[-1])
    angles = place.astype(jnp.float32)[:, None] * freqs[None, :]
    cosine = jnp.cos(angles)[:, None, :]
    sine = direction * jnp.sin(angles)[:, None, :]
    first = values[..., :half]
    second = values[..., half:]
    return jnp.concatenate(
        [first * cosine - second * sine, second * cosine + first * sine], axis=-1
    )


def shards_general(
    tokens,
    cotangent,
    positions,
    lengths,
    routes,
    logits,
    w_query,
    w_key,
    w_value,
    w_output,
    gain_attn,
    gain_ffn,
    w_in,
    w_out,
):
    seq_count = lax.axis_size("seq")
    data_count = lax.axis_size("dp")
    tok_count = tokens.shape[0]
    group_len = positions.shape[1]
    local_experts = w_in.shape[0]
    experts_all = local_experts * data_count
    capacity = min(tok_count, 5 * tok_count * TOP // (4 * experts_all))
    heads_local = QHEADS // seq_count
    kv_local = KVHEADS // seq_count
    ratio = QHEADS // KVHEADS
    width = tokens.shape[1]
    query_full, key_full, value_full, output_full, gain_one, gain_two = (
        lax.all_gather(w_query, ("seq", "dp"), axis=0, tiled=True),
        lax.all_gather(w_key, ("seq", "dp"), axis=0, tiled=True),
        lax.all_gather(w_value, ("seq", "dp"), axis=0, tiled=True),
        lax.all_gather(w_output, ("seq", "dp"), axis=0, tiled=True),
        lax.all_gather(gain_attn, ("seq", "dp"), axis=0, tiled=True),
        lax.all_gather(gain_ffn, ("seq", "dp"), axis=0, tiled=True),
    )
    in_full, out_full = (
        lax.all_gather(w_in, "seq", axis=2, tiled=True),
        lax.all_gather(w_out, "seq", axis=1, tiled=True),
    )
    gain_one = gain_one.astype(jnp.float32)
    gain_two = gain_two.astype(jnp.float32)
    segment, place = local_places(positions[0], lengths[0])
    my_start = lax.axis_index("seq") * tok_count
    my_place = lax.dynamic_slice_in_dim(place, my_start, tok_count)
    inputs = tokens.astype(jnp.float32)
    normed = rms_norm(inputs, gain_one).astype(jnp.bfloat16)
    query_pre = jnp.dot(normed, query_full, preferred_element_type=jnp.float32)
    key_pre = jnp.dot(normed, key_full, preferred_element_type=jnp.float32)
    query_rot = (
        rotate(query_pre.reshape(tok_count, QHEADS, HDIM), my_place, 1.0)
        .reshape(tok_count, QHEADS * HDIM)
        .astype(jnp.bfloat16)
    )
    key_rot = (
        rotate(key_pre.reshape(tok_count, KVHEADS, HDIM), my_place, 1.0)
        .reshape(tok_count, KVHEADS * HDIM)
        .astype(jnp.bfloat16)
    )
    value_low = jnp.dot(normed, value_full, preferred_element_type=jnp.float32).astype(jnp.bfloat16)
    query_heads, key_heads, value_heads = (
        lax.all_to_all(query_rot, "seq", split_axis=1, concat_axis=0, tiled=True),
        lax.all_to_all(key_rot, "seq", split_axis=1, concat_axis=0, tiled=True),
        lax.all_to_all(value_low, "seq", split_axis=1, concat_axis=0, tiled=True),
    )
    keys_three = key_heads.reshape(group_len, kv_local, HDIM)
    values_three = value_heads.reshape(group_len, kv_local, HDIM)
    length = min(512, group_len)
    count = group_len // length

    def scores_of(query_block, seg_block, place_block):
        grouped = query_block.reshape(length, kv_local, ratio, HDIM)
        raw_scores = (
            jnp.einsum("qgrd,kgd->grqk", grouped, keys_three, preferred_element_type=jnp.float32)
            * SCORE_SCALE
        )
        allowed = (seg_block[:, None] == segment[None, :]) & (
            place[None, :] <= place_block[:, None]
        )
        return jnp.where(allowed[None, None], raw_scores, -1e30)

    def forward_block(pieces):
        query_block, seg_block, place_block = pieces
        scores = scores_of(query_block, seg_block, place_block)
        highest = jnp.max(scores, axis=-1, keepdims=True)
        expon = jnp.exp(scores - highest)
        totals = jnp.sum(expon, axis=-1, keepdims=True)
        probs = expon / totals
        mixed = jnp.einsum(
            "grqk,kgd->qgrd",
            probs.astype(jnp.bfloat16),
            values_three,
            preferred_element_type=jnp.float32,
        )
        return (
            mixed.reshape(length, heads_local * HDIM).astype(jnp.bfloat16),
            highest + jnp.log(totals),
            probs,
        )

    query_blocks = query_heads.reshape(count, length, heads_local * HDIM)
    seg_blocks = segment.reshape(count, length)
    place_blocks = place.reshape(count, length)
    block_args = (query_blocks, seg_blocks, place_blocks)

    def forward_light(pieces):
        mixed, lse_part, unused_probs = forward_block(pieces)
        return (mixed, lse_part)

    mixed_blocks, lse_blocks = lax.map(forward_light, block_args)
    mixed_heads = mixed_blocks.reshape(group_len, heads_local * HDIM)
    mixed_tokens = lax.all_to_all(mixed_heads, "seq", split_axis=0, concat_axis=1, tiled=True)
    attn = jnp.dot(mixed_tokens, output_full, preferred_element_type=jnp.float32)
    middle = inputs + BRANCH_SCALE * attn
    normed_ffn = rms_norm(middle, gain_two).astype(jnp.bfloat16)
    chosen = routes.reshape(-1)
    onehot = (chosen[:, None] == jnp.arange(experts_all, dtype=jnp.int32)[None, :]).astype(
        jnp.int32
    )
    ranking = jnp.sum(jnp.cumsum(onehot, axis=0) * onehot, axis=1) - 1
    target = chosen * capacity + ranking
    token_of = jnp.arange(tok_count * TOP, dtype=jnp.int32) // TOP
    gates = jax.nn.softmax(logits, axis=-1)
    source = jnp.full((experts_all * capacity,), tok_count, jnp.int32).at[target].set(token_of)
    slot_gate = jnp.zeros((experts_all * capacity,), jnp.float32).at[target].set(gates.reshape(-1))
    padded = jnp.concatenate([normed_ffn, jnp.zeros((1, width), jnp.bfloat16)], axis=0)
    outgoing = padded[source].reshape(data_count, local_experts * capacity, width)

    def expert_layout(arrived):
        return jnp.swapaxes(
            arrived.reshape(data_count, local_experts, capacity, width), 0, 1
        ).reshape(local_experts, data_count * capacity, width)

    def home_layout(values):
        return jnp.swapaxes(
            values.reshape(local_experts, data_count, capacity, width), 0, 1
        ).reshape(data_count, local_experts * capacity, width)

    def expert_forward(expert_rows):
        both = jnp.einsum("erd,edf->erf", expert_rows, in_full, preferred_element_type=jnp.float32)
        hidden = (jax.nn.silu(both[..., :FF]) * both[..., FF:]).astype(jnp.bfloat16)
        return (both, hidden)

    expert_rows = expert_layout(
        lax.all_to_all(outgoing, "dp", split_axis=0, concat_axis=0, tiled=True)
    )
    both, hidden = expert_forward(expert_rows)
    result = jnp.einsum(
        "erf,efd->erd", hidden, out_full, preferred_element_type=jnp.float32
    ).astype(jnp.bfloat16)
    returned = lax.all_to_all(
        home_layout(result), "dp", split_axis=0, concat_axis=0, tiled=True
    ).reshape(experts_all * capacity, width)
    picked = returned[target].reshape(tok_count, TOP, width).astype(jnp.float32)
    ffn = jnp.sum(picked * gates[:, :, None], axis=1)
    final = middle + BRANCH_SCALE * ffn
    output = final.astype(jnp.bfloat16)
    grad_final = cotangent.astype(jnp.float32)
    padded_grad = jnp.concatenate(
        [BRANCH_SCALE * grad_final, jnp.zeros((1, width), jnp.float32)], axis=0
    )
    grad_slots = (slot_gate[:, None] * padded_grad[source]).astype(jnp.bfloat16)
    grad_result = expert_layout(
        lax.all_to_all(
            grad_slots.reshape(data_count, local_experts * capacity, width),
            "dp",
            split_axis=0,
            concat_axis=0,
            tiled=True,
        )
    )
    rows_back = expert_layout(
        lax.all_to_all(outgoing, "dp", split_axis=0, concat_axis=0, tiled=True)
    )
    both_back, hidden_back = expert_forward(rows_back)
    grad_hidden = jnp.einsum(
        "erd,efd->erf", grad_result, out_full, preferred_element_type=jnp.float32
    )
    gate_part = both_back[..., :FF]
    up_part = both_back[..., FF:]
    sigma = jax.nn.sigmoid(gate_part)
    grad_gate = grad_hidden * up_part * sigma * (1.0 + gate_part * (1.0 - sigma))
    grad_up = grad_hidden * gate_part * sigma
    grad_both = jnp.concatenate([grad_gate, grad_up], axis=-1).astype(jnp.bfloat16)
    grad_out_local = jnp.einsum(
        "erf,erd->efd", hidden_back, grad_result, preferred_element_type=jnp.float32
    )
    grad_in_local = jnp.einsum(
        "erd,erf->edf", rows_back, grad_both, preferred_element_type=jnp.float32
    )
    grad_rows = jnp.einsum(
        "erf,edf->erd", grad_both, in_full, preferred_element_type=jnp.float32
    ).astype(jnp.bfloat16)
    grad_home = lax.all_to_all(
        home_layout(grad_rows), "dp", split_axis=0, concat_axis=0, tiled=True
    ).reshape(experts_all * capacity, width)
    grad_normed_ffn = jnp.sum(
        grad_home[target].reshape(tok_count, TOP, width).astype(jnp.float32), axis=1
    )
    grad_w_in, grad_w_out = (
        lax.psum_scatter(
            grad_in_local.astype(jnp.bfloat16), "seq", scatter_dimension=2, tiled=True
        ).astype(jnp.float32),
        lax.psum_scatter(
            grad_out_local.astype(jnp.bfloat16), "seq", scatter_dimension=1, tiled=True
        ).astype(jnp.float32),
    )
    unused_norm, norm_pull = jax.vjp(rms_norm, middle, gain_two)
    grad_middle_norm, grad_gain_two = norm_pull(grad_normed_ffn)
    grad_middle = grad_final + grad_middle_norm
    grad_attn = (BRANCH_SCALE * grad_middle).astype(jnp.bfloat16)
    grad_w_output = jnp.einsum(
        "te,td->ed", mixed_tokens, grad_attn, preferred_element_type=jnp.float32
    )
    grad_mixed = jnp.einsum(
        "td,ed->te", grad_attn, output_full, preferred_element_type=jnp.float32
    ).astype(jnp.bfloat16)
    grad_mixed_heads = lax.all_to_all(grad_mixed, "seq", split_axis=1, concat_axis=0, tiled=True)
    grad_blocks = grad_mixed_heads.reshape(count, length, heads_local * HDIM)
    back_args = (query_blocks, seg_blocks, place_blocks, lse_blocks, grad_blocks)

    def backward_block(carry, pieces):
        grad_keys, grad_values = carry
        query_block, seg_block, place_block, lse_block, grad_block = pieces[:5]
        probs = jnp.exp(scores_of(query_block, seg_block, place_block) - lse_block)
        grad_out = grad_block.reshape(length, kv_local, ratio, HDIM)
        grad_probs = jnp.einsum(
            "qgrd,kgd->grqk", grad_out, values_three, preferred_element_type=jnp.float32
        )
        grad_scores = (
            probs * (grad_probs - jnp.sum(probs * grad_probs, axis=-1, keepdims=True))
        ).astype(jnp.bfloat16)
        grad_query = SCORE_SCALE * jnp.einsum(
            "grqk,kgd->qgrd", grad_scores, keys_three, preferred_element_type=jnp.float32
        )
        grouped = query_block.reshape(length, kv_local, ratio, HDIM)
        grad_keys = grad_keys + SCORE_SCALE * jnp.einsum(
            "grqk,qgrd->kgd", grad_scores, grouped, preferred_element_type=jnp.float32
        )
        grad_values = grad_values + jnp.einsum(
            "grqk,qgrd->kgd",
            probs.astype(jnp.bfloat16),
            grad_out,
            preferred_element_type=jnp.float32,
        )
        return (
            (grad_keys, grad_values),
            grad_query.reshape(length, heads_local * HDIM).astype(jnp.bfloat16),
        )

    empty_keys = jnp.zeros((group_len, kv_local, HDIM), jnp.float32)
    (grad_keys, grad_values), grad_query_blocks = lax.scan(
        backward_block, (empty_keys, empty_keys), back_args
    )
    grad_query_heads = grad_query_blocks.reshape(group_len, heads_local * HDIM)
    grad_key_heads = grad_keys.reshape(group_len, kv_local * HDIM).astype(jnp.bfloat16)
    grad_value_heads = grad_values.reshape(group_len, kv_local * HDIM).astype(jnp.bfloat16)
    grad_query_tok, grad_key_tok, grad_value_tok = (
        lax.all_to_all(grad_query_heads, "seq", split_axis=0, concat_axis=1, tiled=True),
        lax.all_to_all(grad_key_heads, "seq", split_axis=0, concat_axis=1, tiled=True),
        lax.all_to_all(grad_value_heads, "seq", split_axis=0, concat_axis=1, tiled=True),
    )
    grad_query_pre = (
        rotate(grad_query_tok.astype(jnp.float32).reshape(tok_count, QHEADS, HDIM), my_place, -1.0)
        .reshape(tok_count, QHEADS * HDIM)
        .astype(jnp.bfloat16)
    )
    grad_key_pre = (
        rotate(grad_key_tok.astype(jnp.float32).reshape(tok_count, KVHEADS, HDIM), my_place, -1.0)
        .reshape(tok_count, KVHEADS * HDIM)
        .astype(jnp.bfloat16)
    )
    grad_w_query = jnp.einsum(
        "td,te->de", normed, grad_query_pre, preferred_element_type=jnp.float32
    )
    grad_w_key = jnp.einsum("td,te->de", normed, grad_key_pre, preferred_element_type=jnp.float32)
    grad_w_value = jnp.einsum(
        "td,te->de", normed, grad_value_tok, preferred_element_type=jnp.float32
    )
    grad_normed = jnp.einsum(
        "te,de->td", grad_query_pre, query_full, preferred_element_type=jnp.float32
    )
    grad_normed = grad_normed + jnp.einsum(
        "te,de->td", grad_key_pre, key_full, preferred_element_type=jnp.float32
    )
    grad_normed = grad_normed + jnp.einsum(
        "te,de->td", grad_value_tok, value_full, preferred_element_type=jnp.float32
    )
    unused_first, first_pull = jax.vjp(rms_norm, inputs, gain_one)
    grad_inputs_norm, grad_gain_one = first_pull(grad_normed)
    grad_tokens = grad_middle + grad_inputs_norm
    summed = (
        lax.psum_scatter(grad_w_query, ("seq", "dp"), scatter_dimension=0, tiled=True),
        lax.psum_scatter(grad_w_key, ("seq", "dp"), scatter_dimension=0, tiled=True),
        lax.psum_scatter(grad_w_value, ("seq", "dp"), scatter_dimension=0, tiled=True),
        lax.psum_scatter(grad_w_output, ("seq", "dp"), scatter_dimension=0, tiled=True),
        lax.psum_scatter(grad_gain_one, ("seq", "dp"), scatter_dimension=0, tiled=True),
        lax.psum_scatter(grad_gain_two, ("seq", "dp"), scatter_dimension=0, tiled=True),
    )
    return (
        output,
        grad_tokens,
        summed[0],
        summed[1],
        summed[2],
        summed[3],
        summed[4],
        summed[5],
        grad_w_in,
        grad_w_out,
    )


BF16 = jnp.bfloat16
F32 = jnp.float32
LINE = 4
PAD = 128
VMEM_BYTES = 60 * 1024 * 1024


def in_planes(mesh):
    return mesh.shape["seq"] == 2 and mesh.shape["dp"] == 4 * LINE


def swap_seq(value):
    return lax.ppermute(value, "seq", [(0, 1), (1, 0)])


def swap_dp(value, mask):
    return lax.ppermute(value, "dp", [(i, i ^ mask) for i in range(4 * LINE)])


def swap_core(value):
    return swap_dp(value, 1)


def swap_y(value):
    return swap_dp(value, 2)


def line_up(value):
    return lax.ppermute(value, "dp", [(i, i + 4) for i in range(4 * LINE - 4)])


def line_down(value):
    return lax.ppermute(value, "dp", [(i, i - 4) for i in range(4, 4 * LINE)])


def after(value, *others):
    return lax.optimization_barrier((value,) + others)[0]


def line_scatter(take, place):
    up = down = None
    for step in range(LINE - 1):
        far = jnp.minimum(LINE - 1 - step + place, LINE - 1)
        near = jnp.maximum(step - LINE + 1 + place, 0)
        right, left = take(far), take(near)
        if up is not None:
            right = right + up.astype(F32)
            left = left + down.astype(F32)
        up = line_up(right.astype(BF16))
        down = line_down(left.astype(BF16))
    return take(place) + up.astype(F32) + down.astype(F32)


def near_pieces(own, own_x):
    return swap_seq(own_x), swap_y(own)


def far_pieces(near_x, near_y):
    half = near_x.shape[0] // 2
    return swap_y(near_x[:half]), swap_seq(near_y[half:])


def with_cores(*pieces):
    return pieces + tuple(swap_core(piece) for piece in pieces)


def over_cores(mine, others):
    return mine.astype(F32) + swap_core(others).astype(F32)


def far_links(far):
    half = far.shape[0] // 2
    return swap_y(far[:half]), swap_seq(far[half:])


def near_links(near, from_y, from_x):
    half = from_y.shape[0] // 2
    first = (near[:half] + from_y[half:].astype(F32)).astype(BF16)
    second = (near[half : 2 * half] + from_x[half:].astype(F32)).astype(BF16)
    return first, second


def own_sum(near, from_y, from_x, first, second):
    half = from_y.shape[0] // 2
    low = near[2 * half : 3 * half] + from_y[:half].astype(F32) + first.astype(F32)
    high = near[3 * half :] + from_x[:half].astype(F32) + second.astype(F32)
    return jnp.concatenate([low, high], axis=0)


def turned(values, cos, sin, direction):
    lanes = values.shape[1]
    place = lax.broadcasted_iota(jnp.int32, values.shape, 1) % HDIM
    swapped = jnp.where(
        place < HDIM // 2,
        pltpu.roll(values, lanes - HDIM // 2, 1),
        pltpu.roll(values, HDIM // 2, 1),
    )
    times = lanes // cos.shape[1]
    cos = jnp.concatenate([cos] * times, axis=1)
    sin = jnp.concatenate([sin] * times, axis=1)
    if direction > 0:
        return values * cos + swapped * sin
    return values * cos - swapped * sin


def place_shards(place_ref, own_ref, other_ref, shard, store):
    for core in range(2):
        source = other_ref if core else own_ref
        for row in range(2):
            for line in range(LINE):
                index = (place_ref[0] ^ line) * 4 + (place_ref[1] ^ row) * 2 + (place_ref[2] ^ core)
                store(source, (row * LINE + line) * shard, pl.multiple_of(index * shard, shard))


def qkv_kernel(
    place_ref, x_ref, own_ref, other_ref, cos_ref, sin_ref,
    h_ref, q_ref, k_ref, v_ref, w_ref, gain_ref, columns_buf,
):
    q_width, kv_heads = q_ref.shape[1], k_ref.shape[0]
    kv_width = kv_heads * HDIM
    width, columns = w_ref.shape
    shard = own_ref.shape[0] // (2 * LINE)

    @pl.when(pl.program_id(0) == 0)
    def _():
        def store(source, low, place):
            for seq in range(2):
                first = seq * (columns + PAD)
                rows = pl.ds(pl.multiple_of(place + seq * (width // 2), shard), shard)
                w_ref[rows, :] = source[low : low + shard, first : first + columns]
                columns_buf[rows, :] = source[
                    low : low + shard, first + columns : first + columns + PAD
                ].astype(F32)

        place_shards(place_ref, own_ref, other_ref, shard, store)
        gain_ref[...] = columns_buf[...].T[: gain_ref.shape[0]]

    value = x_ref[...].astype(F32)
    scale = lax.rsqrt(jnp.mean(value * value, axis=-1, keepdims=True) + EPSILON)
    normed = (value * scale * gain_ref[0:1, :]).astype(BF16)
    h_ref[...] = normed
    both = jnp.dot(normed, w_ref[...], preferred_element_type=F32)
    spun = turned(both[:, : q_width + kv_width], cos_ref[...], sin_ref[...], 1)
    q_ref[...] = (spun[:, :q_width] * SCORE_SCALE).astype(BF16)
    for head in range(kv_heads):
        low = q_width + head * HDIM
        k_ref[head] = spun[:, low : low + HDIM].astype(BF16)
        low = low + kv_width
        v_ref[head] = both[:, low : low + HDIM].astype(BF16)


def project(places, x_sorted, own, other, cos, sin, q_width, kv_heads):
    rows, width = x_sorted.shape
    tile = 256
    columns = q_width + 2 * kv_heads * HDIM

    def row_block(lanes):
        return pl.BlockSpec((tile, lanes), lambda i, p: (i, 0))

    def whole(shape):
        return pl.BlockSpec(shape, lambda i, p: (0, 0))

    heads = pl.BlockSpec((kv_heads, tile, HDIM), lambda i, p: (0, i, 0))
    return pl.pallas_call(
        qkv_kernel,
        grid_spec=pltpu.PrefetchScalarGridSpec(
            num_scalar_prefetch=1,
            grid=(rows // tile,),
            in_specs=[
                row_block(width),
                whole(own.shape),
                whole(other.shape),
                row_block(cos.shape[1]),
                row_block(cos.shape[1]),
            ],
            out_specs=[
                row_block(width), row_block(q_width), heads, heads,
                whole((width, columns)), whole((8, width)),
            ],
            scratch_shapes=[pltpu.VMEM((width, PAD), F32)],
        ),
        out_shape=[
            jax.ShapeDtypeStruct((rows, width), BF16),
            jax.ShapeDtypeStruct((rows, q_width), BF16),
            jax.ShapeDtypeStruct((kv_heads, rows, HDIM), BF16),
            jax.ShapeDtypeStruct((kv_heads, rows, HDIM), BF16),
            jax.ShapeDtypeStruct((width, columns), BF16),
            jax.ShapeDtypeStruct((8, width), F32),
        ],
        compiler_params=pltpu.CompilerParams(vmem_limit_bytes=VMEM_BYTES),
        cost_estimate=pl.CostEstimate(
            flops=rows * width * columns // 8,
            bytes_accessed=rows * width + width * columns,
            transcendentals=rows,
        ),
        name="project",
    )(places, x_sorted, own, other, cos, sin)


def mix_kernel(place_ref, mine_ref, theirs_ref, x_ref, gain_ref, w_ref, m_ref, h_ref, parts_ref):
    half = parts_ref.shape[1]

    @pl.when(pl.program_id(0) == 0)
    def _():
        for part in range(2):
            low = pl.multiple_of((place_ref[0] ^ part) * half, half)
            parts_ref[part] = w_ref[pl.ds(low, half), :]

    mixed = jnp.dot(mine_ref[...], parts_ref[0], preferred_element_type=F32)
    mixed = mixed + jnp.dot(theirs_ref[...], parts_ref[1], preferred_element_type=F32)
    value = x_ref[...].astype(F32) + BRANCH_SCALE * mixed
    m_ref[...] = value
    scale = lax.rsqrt(jnp.mean(value * value, axis=-1, keepdims=True) + EPSILON)
    h_ref[...] = (value * scale * gain_ref[...]).astype(BF16)


def mix(place, mine, theirs, tokens, gain, weights):
    rows, width = tokens.shape
    half = mine.shape[1]
    tile = 256

    def row_block(lanes):
        return pl.BlockSpec((tile, lanes), lambda i, p: (i, 0))

    def whole(shape):
        return pl.BlockSpec(shape, lambda i, p: (0,) * len(shape))

    return pl.pallas_call(
        mix_kernel,
        grid_spec=pltpu.PrefetchScalarGridSpec(
            num_scalar_prefetch=1,
            grid=(rows // tile,),
            in_specs=[
                row_block(half), row_block(half), row_block(width), whole(gain.shape),
                whole((width, width)),
            ],
            out_specs=[row_block(width), row_block(width), whole((2, half, width))],
        ),
        out_shape=[
            jax.ShapeDtypeStruct((rows, width), F32),
            jax.ShapeDtypeStruct((rows, width), BF16),
            jax.ShapeDtypeStruct((2, half, width), BF16),
        ],
        compiler_params=pltpu.CompilerParams(vmem_limit_bytes=VMEM_BYTES),
        cost_estimate=pl.CostEstimate(
            flops=rows * width * width // 8, bytes_accessed=rows * width, transcendentals=rows
        ),
        name="mix",
    )(place, mine, theirs, tokens, gain, weights)


def token_grad_kernel(dq_ref, dk_ref, dv_ref, w_ref, own_ref, other_ref, mine_ref, sent_ref):
    q_width, kv_width = dq_ref.shape[1], dk_ref.shape[1]
    cuts = (0, q_width, q_width + kv_width, q_width + 2 * kv_width)
    grad = contract(dq_ref[...], w_ref[:, cuts[0] : cuts[1]], 1, 1)
    grad = grad + contract(dk_ref[...], w_ref[:, cuts[1] : cuts[2]], 1, 1)
    grad = (grad + contract(dv_ref[...], w_ref[:, cuts[2] : cuts[3]], 1, 1)).astype(BF16)
    for place_ref, out_ref in ((other_ref, sent_ref), (own_ref, mine_ref)):
        shape = (place_ref.shape[0], grad.shape[0])
        picked = lax.broadcasted_iota(jnp.int32, shape, 1) == place_ref[...]
        picked = jnp.where(picked, 1.0, 0.0).astype(BF16)
        out_ref[...] = jnp.dot(picked, grad, preferred_element_type=F32).astype(BF16)


def token_grad(grads, weights, own_places, other_places):
    rows, count = grads[0].shape[0], own_places.shape[0]
    width = weights.shape[0]
    columns = sum(grad.shape[1] for grad in grads)
    tile = width // 3

    def whole(array):
        return pl.BlockSpec(array.shape, lambda i: (0, 0))

    block = pl.BlockSpec((count, tile), lambda i: (0, i))
    return pl.pallas_call(
        token_grad_kernel,
        grid=(3,),
        in_specs=[whole(grad) for grad in grads]
        + [pl.BlockSpec((tile, columns), lambda i: (i, 0)), whole(own_places), whole(other_places)],
        out_specs=[block, block],
        out_shape=[jax.ShapeDtypeStruct((count, width), BF16)] * 2,
        compiler_params=pltpu.CompilerParams(vmem_limit_bytes=VMEM_BYTES),
        cost_estimate=pl.CostEstimate(
            flops=rows * width * columns // 8, bytes_accessed=rows * width, transcendentals=0
        ),
        name="token_grad",
    )(*grads, weights, own_places, other_places)


Q_TILE = 256


def windows(rows):
    longest = rows // 2
    for start in range(0, rows, Q_TILE):
        low = max(0, start - longest + 1) // Q_TILE * Q_TILE
        yield start, low, start + Q_TILE


def allowed_keys(start_ref, row, low, high):
    shape = (Q_TILE, high - low)
    rows = lax.broadcasted_iota(jnp.int32, shape, 0) + row
    keys = lax.broadcasted_iota(jnp.int32, shape, 1) + low
    return (keys <= rows) & (keys >= start_ref[row : row + Q_TILE, :])


def contract(left, right, left_dim, right_dim):
    return lax.dot_general(
        left, right, (((left_dim,), (right_dim,)), ((), ())), preferred_element_type=F32
    )


def masked_scores(query, keys, allowed):
    return jnp.where(allowed, contract(query, keys, 1, 1), -1e30)


def attend_kernel(base, q_ref, k_ref, v_ref, start_ref, o_ref, level_ref):
    pair = pl.program_id(0) + base
    ratio = QHEADS // KVHEADS
    for row, low, high in windows(q_ref.shape[0]):
        allowed = allowed_keys(start_ref, row, low, high)
        for side in range(2):
            head = (2 * pair + side) // ratio
            lanes = slice(side * HDIM, (side + 1) * HDIM)
            scores = masked_scores(
                q_ref[row : row + Q_TILE, lanes], k_ref[head, low:high, :], allowed
            )
            highest = jnp.max(scores, axis=-1, keepdims=True)
            expon = jnp.exp(scores - highest)
            total = jnp.sum(expon, axis=-1, keepdims=True)
            level_ref[0, row : row + Q_TILE, side : side + 1] = highest + jnp.log(total)
            probs = expon * (1.0 / total)
            mixed = contract(probs.astype(BF16), v_ref[head, low:high, :], 1, 0)
            o_ref[row : row + Q_TILE, lanes] = mixed.astype(BF16)


def attention_cost(rows, heads, products):
    area = sum(Q_TILE * (high - low) for _, low, high in windows(rows))
    return pl.CostEstimate(
        flops=products * heads * area * 16,
        bytes_accessed=8 * rows * heads * HDIM,
        transcendentals=heads * area,
    )


def attend(query, keys, values, starts, base, pairs):
    rows = query.shape[0]
    pair_block = pl.BlockSpec((rows, 2 * HDIM), lambda j: (0, j + base))
    whole = pl.BlockSpec(keys.shape, lambda j: (0, 0, 0))
    return pl.pallas_call(
        functools.partial(attend_kernel, base),
        grid=(pairs,),
        in_specs=[pair_block, whole, whole, pl.BlockSpec((rows, 1), lambda j: (0, 0))],
        out_specs=[
            pl.BlockSpec((rows, 2 * HDIM), lambda j: (0, j)),
            pl.BlockSpec((1, rows, 2), lambda j: (j, 0, 0)),
        ],
        out_shape=[
            jax.ShapeDtypeStruct((rows, pairs * 2 * HDIM), BF16),
            jax.ShapeDtypeStruct((pairs, rows, 2), F32),
        ],
        compiler_params=pltpu.CompilerParams(vmem_limit_bytes=VMEM_BYTES),
        cost_estimate=attention_cost(rows, 2 * pairs, 2),
        name="attend",
    )(query, keys, values, starts)


def attend_back_kernel(
    q_ref, k_ref, v_ref, d_ref, level_ref, start_ref, cos_ref, sin_ref,
    dq_ref, dk_ref, dv_ref, dk_sum, dv_sum,
):
    pair = pl.program_id(0)
    ratio = QHEADS // KVHEADS

    @pl.when(pair == 0)
    def _():
        dk_sum[...] = jnp.zeros_like(dk_sum)
        dv_sum[...] = jnp.zeros_like(dv_sum)

    for row, low, high in windows(q_ref.shape[0]):
        allowed = allowed_keys(start_ref, row, low, high)
        grads = []
        for side in range(2):
            head = (2 * pair + side) // ratio
            lanes = slice(side * HDIM, (side + 1) * HDIM)
            query = q_ref[row : row + Q_TILE, lanes]
            keys = k_ref[head, low:high, :]
            probs = jnp.exp(
                masked_scores(query, keys, allowed)
                - level_ref[0, row : row + Q_TILE, side : side + 1]
            )
            grad_out = d_ref[row : row + Q_TILE, lanes]
            grad_probs = contract(grad_out, v_ref[head, low:high, :], 1, 1)
            inner = jnp.sum(probs * grad_probs, axis=-1, keepdims=True)
            grad_scores = (probs * (grad_probs - inner)).astype(BF16)
            grads.append(contract(grad_scores, keys, 1, 0) * SCORE_SCALE)
            dk_sum[head, low:high, :] += contract(grad_scores, query, 0, 0)
            dv_sum[head, low:high, :] += contract(probs.astype(BF16), grad_out, 0, 0)
        grad_query = jnp.concatenate(grads, axis=1).astype(BF16).astype(F32)
        dq_ref[row : row + Q_TILE, :] = turned(
            grad_query,
            cos_ref[row : row + Q_TILE, :],
            sin_ref[row : row + Q_TILE, :],
            -1,
        ).astype(BF16)

    @pl.when(pair == pl.num_programs(0) - 1)
    def _():
        heads = range(dk_sum.shape[0])
        grad_keys = jnp.concatenate([dk_sum[head] for head in heads], axis=1)
        grad_keys = grad_keys.astype(BF16).astype(F32)
        dk_ref[...] = turned(grad_keys, cos_ref[...], sin_ref[...], -1).astype(BF16)
        dv_ref[...] = jnp.concatenate([dv_sum[head] for head in heads], axis=1).astype(BF16)


def attend_back(query, keys, values, grad_out, levels, starts, cos, sin):
    rows, lanes = query.shape
    pairs = lanes // (2 * HDIM)
    kv_heads = keys.shape[0]
    pair_block = pl.BlockSpec((rows, 2 * HDIM), lambda j: (0, j))
    whole = pl.BlockSpec(keys.shape, lambda j: (0, 0, 0))

    def fixed(lanes_of):
        return pl.BlockSpec((rows, lanes_of), lambda j: (0, 0))

    flat = kv_heads * HDIM
    return pl.pallas_call(
        attend_back_kernel,
        grid=(pairs,),
        in_specs=[
            pair_block, whole, whole, pair_block,
            pl.BlockSpec((1, rows, 2), lambda j: (j, 0, 0)), fixed(1), fixed(2 * HDIM), fixed(2 * HDIM),
        ],
        out_specs=[pair_block, fixed(flat), fixed(flat)],
        out_shape=[
            jax.ShapeDtypeStruct(query.shape, BF16),
            jax.ShapeDtypeStruct((rows, flat), BF16),
            jax.ShapeDtypeStruct((rows, flat), BF16),
        ],
        scratch_shapes=[pltpu.VMEM(keys.shape, F32), pltpu.VMEM(keys.shape, F32)],
        compiler_params=pltpu.CompilerParams(vmem_limit_bytes=VMEM_BYTES),
        cost_estimate=attention_cost(rows, 2 * pairs, 5),
        name="attend_back",
    )(query, keys, values, grad_out, levels, starts, cos, sin)


SLOTS = 2 * LINE - 1
SLOT_ORDER = (0, 3, 1, 2)
OWN, NEAR_X, NEAR_Y, FAR_Y, FAR_X = range(5)
FAR_TILES = (((NEAR_Y, 0), (FAR_Y, 0)), ((NEAR_X, 1), (FAR_X, 0)))
NEAR_TILES = (((NEAR_X, 0), (NEAR_Y, 1)), ((OWN, 0), (OWN, 1)))


def used_pieces(tiles):
    return sorted({piece for tile in tiles for piece, _ in tile})


def experts_kernel(tiles, half_rows, place_ref, *refs):
    used = used_pieces(tiles)
    sides = 2 * len(used)
    h_pieces, g_pieces, slots = refs[:sides], refs[sides : 2 * sides], refs[2 * sides : 2 * sides + SLOTS]
    select_ref = refs[2 * sides + SLOTS]
    (
        f_mine, f_other, d_mine, d_other, hid_a, hid_b, du_a, du_b, hcopy_ref, gcopy_ref,
        w_in, w_out, h_buf, g_buf, hidden, du_all, weight_sems, row_sems,
    ) = refs[-18:]
    width = h_buf.shape[2]
    half = slots[0].shape[1] // 3
    part = 2 * half
    step = pl.program_id(0)
    steps = 2 * len(tiles)

    def weight_copies(spot, slot):
        return (
            pltpu.make_async_copy(
                slots[slot].at[:, :part],
                w_in.at[:, spot * part : (spot + 1) * part],
                weight_sems.at[0, spot],
            ),
            pltpu.make_async_copy(
                slots[slot].at[:, part:],
                w_out.at[:, spot * half : (spot + 1) * half],
                weight_sems.at[1, spot],
            ),
        )

    def row_copies(number, buffer):
        side, tile = divmod(number, len(tiles))
        copies = []
        for spot, (piece, part_of) in enumerate(tiles[tile]):
            index = side * len(used) + used.index(piece)
            for kind, (pieces, held) in enumerate(((h_pieces, h_buf), (g_pieces, g_buf))):
                copies.append(
                    pltpu.make_async_copy(
                        pieces[index].at[pl.ds(part_of * half_rows, half_rows), :],
                        held.at[buffer, pl.ds(spot * half_rows, half_rows), :],
                        row_sems.at[buffer, 2 * kind + spot],
                    )
                )
        return copies

    def fetch(wanted, buffer):
        for number in range(steps):

            @pl.when(wanted == number)
            def _():
                for copy in row_copies(number, buffer):
                    copy.start()

    buffer = step % 2

    @pl.when(step == 0)
    def _():
        fetch(step, 0)
        for spot, expert in enumerate(SLOT_ORDER):
            for slot in range(expert, expert + LINE):

                @pl.when(slot == LINE - 1 + expert - place_ref[0])
                def _():
                    for copy in weight_copies(spot, slot):
                        copy.start()

        for spot in range(LINE):
            for copy in weight_copies(spot, LINE - 1):
                copy.wait()

    @pl.when(step + 1 < steps)
    def _():
        fetch(step + 1, 1 - buffer)

    for copy in row_copies(0, buffer):
        copy.wait()

    rows = h_buf[buffer]
    grads = g_buf[buffer, :, :width]
    hcopy_ref[...] = rows
    gcopy_ref[...] = grads
    gates = jnp.dot(g_buf[buffer, :, width:], select_ref[...], preferred_element_type=F32)
    for spot in range(LINE):
        units = slice(spot * half, (spot + 1) * half)
        both = jnp.dot(
            rows, w_in[:, spot * part : (spot + 1) * part], preferred_element_type=F32
        )
        back = jnp.dot(grads, w_out[:, units], preferred_element_type=F32)
        gate = gates[:, units]
        first, second = both[:, :half], both[:, half:]
        sigma = jax.nn.sigmoid(first)
        silu = first * sigma
        hidden[:, units] = (gate * (silu * second)).astype(BF16)
        back = back * (BRANCH_SCALE * gate)
        d_first = back * second * (sigma * (1.0 + first * (1.0 - sigma)))
        d_second = back * silu
        du_all[:, spot * part : spot * part + half] = d_first.astype(BF16)
        du_all[:, spot * part + half : (spot + 1) * part] = d_second.astype(BF16)
    hid_a[...] = hidden[:, : 2 * half]
    hid_b[...] = hidden[:, 2 * half :]
    du_a[...] = du_all[:, : 2 * part]
    du_b[...] = du_all[:, 2 * part :]
    ffn = contract(hidden[...], w_out[...], 1, 1).astype(BF16)
    back_rows = contract(du_all[...], w_in[...], 1, 1).astype(BF16)

    @pl.when(step < len(tiles))
    def _():
        f_mine[...] = ffn
        d_mine[...] = back_rows

    @pl.when(step >= len(tiles))
    def _():
        f_other[...] = ffn
        d_other[...] = back_rows


def run_experts(tiles, place, row_pieces, grad_pieces, slots, select, base, kept):
    used = used_pieces(tiles)
    sides = len(row_pieces) // 2
    wanted = used + [sides + piece for piece in used]
    rows = [row_pieces[piece] for piece in wanted]
    grads = [grad_pieces[piece] for piece in wanted]
    tile, width = row_pieces[OWN].shape
    wide = grad_pieces[OWN].shape[1]
    half = slots[0].shape[1] // 3
    part = 2 * half
    count = len(tiles)
    steps = 2 * count
    total = 8 * tile

    def late(lanes):
        return pl.BlockSpec((tile, lanes), lambda i, p: (i + base, 0))

    mine = pl.BlockSpec((tile, width), lambda i, p: (jnp.minimum(i, count - 1), 0))
    others = pl.BlockSpec((tile, width), lambda i, p: (jnp.maximum(i - count, 0), 0))
    anywhere = pl.BlockSpec(memory_space=pl.ANY)
    kept = list(kept)
    lead = 1 + 2 * len(wanted) + SLOTS + 1
    partial = jax.ShapeDtypeStruct((count * tile, width), BF16)
    lanes = [2 * half, 2 * half, 2 * part, 2 * part, width, width]
    return pl.pallas_call(
        functools.partial(experts_kernel, tiles, tile // 2),
        grid_spec=pltpu.PrefetchScalarGridSpec(
            num_scalar_prefetch=1,
            grid=(steps,),
            in_specs=[anywhere] * (2 * len(wanted) + SLOTS)
            + [pl.BlockSpec(select.shape, lambda i, p: (0, 0))]
            + [anywhere] * len(kept),
            out_specs=[mine, others, mine, others] + [late(n) for n in lanes],
            scratch_shapes=[
                pltpu.VMEM((width, LINE * part), BF16),
                pltpu.VMEM((width, LINE * half), BF16),
                pltpu.VMEM((2, tile, width), BF16),
                pltpu.VMEM((2, tile, wide), BF16),
                pltpu.VMEM((tile, LINE * half), BF16),
                pltpu.VMEM((tile, LINE * part), BF16),
                pltpu.SemaphoreType.DMA((2, LINE)),
                pltpu.SemaphoreType.DMA((2, 4)),
            ],
        ),
        out_shape=[partial] * 4 + [jax.ShapeDtypeStruct((total, n), BF16) for n in lanes],
        input_output_aliases={lead + i: 4 + i for i in range(len(kept))},
        compiler_params=pltpu.CompilerParams(vmem_limit_bytes=VMEM_BYTES),
        cost_estimate=pl.CostEstimate(
            flops=steps * tile * width * LINE * (part + half) // 4,
            bytes_accessed=2 * steps * tile * (6 * width + LINE * (part + half)),
            transcendentals=steps * tile * LINE * half,
        ),
        name="experts",
    )(place, *rows, *grads, *slots, select, *kept)


def qkv_grad_kernel(h_ref, dq_ref, dk_ref, dv_ref, gain_ref, o_ref):
    shard = o_ref.shape[-2]
    rows = h_ref[...]
    low = 0
    gains = jnp.broadcast_to(gain_ref[...], (PAD, gain_ref.shape[1])).T.astype(BF16)
    parts = [contract(rows, ref[...], 0, 0).astype(BF16) for ref in (dq_ref, dk_ref, dv_ref)]
    for part in parts + [gains]:
        for block in range(h_ref.shape[1] // shard):
            place = (block % 2, block // 2 % 2, 0, block // 4)
            o_ref[place + (slice(None), slice(low, low + part.shape[1]))] = part[
                block * shard : (block + 1) * shard
            ]
        low = low + part.shape[1]


def qkv_grad(normed, grads, gain_row, shard):
    rows, width = normed.shape
    columns = sum(grad.shape[1] for grad in grads)
    tile = width // 4
    planes = tile // (4 * shard)
    return pl.pallas_call(
        qkv_grad_kernel,
        grid=(4,),
        in_specs=[pl.BlockSpec((rows, tile), lambda i: (0, i))]
        + [pl.BlockSpec(grad.shape, lambda i: (0, 0)) for grad in grads]
        + [pl.BlockSpec((1, tile), lambda i: (0, i))],
        out_specs=pl.BlockSpec(
            (2, 2, 1, planes, shard, columns + PAD), lambda i: (0, 0, i // 2, i % 2, 0, 0)
        ),
        out_shape=jax.ShapeDtypeStruct((2, 2, 2, LINE, shard, columns + PAD), BF16),
        compiler_params=pltpu.CompilerParams(vmem_limit_bytes=VMEM_BYTES),
        cost_estimate=pl.CostEstimate(
            flops=rows * width * columns // 8,
            bytes_accessed=rows * width,
            transcendentals=0,
        ),
        name="qkv_grad",
    )(normed, *grads, gain_row)


def norm_back(value, gain, grad):
    scale = lax.rsqrt(jnp.mean(value * value, axis=-1, keepdims=True) + EPSILON)
    unit = value * scale
    grad_gain = jnp.sum(grad * unit, axis=0)
    scaled = grad * gain
    inner = jnp.mean(scaled * unit, axis=-1, keepdims=True)
    return scale * (scaled - unit * inner), grad_gain


def shards_plane(
    tokens,
    cotangent,
    positions,
    lengths,
    routes,
    logits,
    w_query,
    w_key,
    w_value,
    w_output,
    gain_attn,
    gain_ffn,
    w_in,
    w_out,
):
    seq = lax.axis_index("seq")
    data = lax.axis_index("dp")
    line, row_of, core = data // 4, (data // 2) % 2, data % 2
    tok_count, width = tokens.shape
    group_len = positions.shape[1]
    shard = w_query.shape[0]
    q_width = w_query.shape[1] // 2
    kv_width = w_key.shape[1] // 2
    kv_heads = kv_width // HDIM
    first_seq = seq == 0

    def ordered(mine, theirs, axis):
        low = jnp.where(first_seq, mine, theirs)
        high = jnp.where(first_seq, theirs, mine)
        return jnp.concatenate([low, high], axis=axis)

    def half_of(weights, which):
        half = weights.shape[1] // 2
        return lax.dynamic_slice_in_dim(weights, which * half, half, axis=1)

    def both_axes(value, pairs):
        return lax.ppermute(value, ("seq", "dp"), pairs)

    def device(s, d):
        return s * 4 * LINE + d

    straight, crossed = [], []
    for s in range(2):
        for d in range(4 * LINE):
            c = d % 2
            straight.append((device(s, d), device(c, d - c + s)))
            crossed.append((device(s, d), device(c, d - c + 1 - s)))
    crossed_back = [(there, here) for here, there in crossed]
    first_core = core == 0

    projections = (w_query, w_key, w_value)
    qkv_width = q_width + 2 * kv_width
    qkv_width = q_width + 2 * kv_width
    gain_columns = jnp.pad(jnp.stack([gain_attn, gain_ffn], axis=1), ((0, 0), (0, PAD - 2)))
    mine, theirs = [
        jnp.concatenate([half_of(w, which) for w in projections] + [gain_columns], axis=1)
        for which in (seq, 1 - seq)
    ]
    theirs = swap_seq(jnp.concatenate([theirs, w_output], axis=1))
    output_pair = ordered(w_output[None], theirs[None, :, qkv_width + PAD :], 0)
    block = ordered(mine, theirs[:, : qkv_width + PAD], 1)
    along = [block] + [swap_dp(block, 4 * step) for step in range(1, LINE)]
    places_of = jnp.stack([line, row_of, core]).astype(jnp.int32)

    in_own = w_in[0]
    half = in_own.shape[1] // 2
    sent = jnp.concatenate(
        [lax.dynamic_slice_in_dim(in_own, seq * half, half, axis=1), w_out[0].T], axis=1
    )
    same = both_axes(sent, straight)
    cross = both_axes(lax.dynamic_slice_in_dim(in_own, (1 - seq) * half, half, axis=1), crossed)
    same, cross, along = lax.optimization_barrier((same, cross, along))
    own_part = jnp.concatenate(
        [
            jnp.where(first_core, same[:, :half], cross),
            jnp.where(first_core, cross, same[:, :half]),
            same[:, half:],
        ],
        axis=1,
    )
    other_tokens = swap_seq(after(tokens, own_part))
    output_full = lax.all_gather(after(output_pair, own_part), "dp", axis=1, tiled=True)
    output_full = output_full.reshape(width, width)
    cut = width // 2
    lines = (line_up(own_part[:cut]), line_down(own_part[:cut]))
    qkv_rows = after(jnp.concatenate(along, axis=0), own_part)
    qkv_near, lines = lax.optimization_barrier((swap_y(qkv_rows), lines))
    late_part = after(own_part[cut:], lines)
    late_lines = (line_up(late_part), line_down(late_part))
    qkv_rows = jnp.concatenate([qkv_rows, qkv_near], axis=0)
    qkv_others = swap_core(qkv_rows)

    experts_all = 4 * LINE
    gates = jax.nn.softmax(logits, axis=-1)
    named = routes[:, :, None] == jnp.arange(experts_all, dtype=jnp.int32)[None, None, :]
    gate_table = jnp.sum(jnp.where(named, gates[:, :, None], 0.0), axis=1)
    gate_high = lax.reduce_precision(gate_table, 8, 7)
    grad_rows = jnp.concatenate(
        [
            cotangent,
            gate_high.astype(BF16),
            (gate_table - gate_high).astype(BF16),
            jnp.zeros((tok_count, PAD - 2 * experts_all), BF16),
        ],
        axis=1,
    )
    grad_near = near_pieces(grad_rows, after(grad_rows, other_tokens))
    lane = jnp.arange(PAD, dtype=jnp.int32)[:, None]
    hosted = jnp.repeat(
        jnp.array(SLOT_ORDER, jnp.int32) * 4 + 2 * row_of + seq, half, total_repeat_length=LINE * half
    )
    select = ((lane % experts_all == hosted[None, :]) & (lane < 2 * experts_all)).astype(BF16)

    places = positions[0]
    ends = jnp.cumsum(lengths[0])
    ranks = jnp.arange(group_len, dtype=jnp.int32)
    reached = ranks[:, None] >= ends[None, :]
    starts = jnp.max(jnp.where(reached, ends[None, :], 0), axis=1)
    local = (ranks - starts).astype(F32)
    freqs = jnp.power(THETA, -jnp.arange(HDIM // 2, dtype=F32) * 2.0 / HDIM)
    angles = local[:, None] * freqs[None, :]
    cos, sin = jnp.cos(angles), jnp.sin(angles)
    cos = jnp.concatenate([cos, cos, cos, cos], axis=1)
    sin = jnp.concatenate([-sin, sin, -sin, sin], axis=1)
    start_column = starts[:, None]
    own_places = lax.dynamic_slice_in_dim(places, seq * tok_count, tok_count)
    other_places = lax.dynamic_slice_in_dim(places, (1 - seq) * tok_count, tok_count)
    sort_own = (ranks[:, None] == own_places[None, :]).astype(BF16)
    sort_other = (ranks[:, None] == other_places[None, :]).astype(BF16)

    def to_order(own, other):
        return (
            contract(sort_own, own, 1, 0) + contract(sort_other, other, 1, 0)
        ).astype(BF16)

    def from_order(sort, values):
        return contract(sort, values, 0, 0).astype(BF16)

    x_sorted = to_order(tokens, other_tokens)
    normed, query, keys, values, w_qkv, gains = project(
        places_of, x_sorted, qkv_rows, qkv_others, cos, sin, q_width, kv_heads
    )
    gain_one, gain_two = gains[0], gains[1]
    pairs = q_width // (2 * HDIM)
    first_pairs = 2 * pairs // 3
    mixed_one, levels_one = attend(query, keys, values, start_column, 0, first_pairs)
    sent_one = swap_seq(from_order(sort_other, mixed_one))
    lines, late_lines = after((lines, late_lines), mixed_one)
    up_one = jnp.concatenate([lines[0], late_lines[0]], axis=0)
    down_one = jnp.concatenate([lines[1], late_lines[1]], axis=0)
    query_two, grad_near_x, grad_near_y, up_one, down_one = after(
        (query, *grad_near, up_one, down_one), mixed_one
    )
    up_two, down_two = line_up(up_one), line_down(down_one)
    grad_near = (grad_near_x, grad_near_y)
    grad_far = far_pieces(*grad_near)
    mixed_two, levels_two = attend(
        query_two, keys, values, start_column, first_pairs, pairs - first_pairs
    )
    sent_two = swap_seq(from_order(sort_other, mixed_two))
    mixed_mine = [from_order(sort_own, mixed_one), from_order(sort_own, mixed_two)]
    mixed_mine = jnp.concatenate(mixed_mine, axis=1)
    mixed_theirs = jnp.concatenate([sent_one, sent_two], axis=1)
    inputs = tokens.astype(F32)
    middle, normed_ffn, output_parts = mix(
        seq.astype(jnp.int32)[None], mixed_mine, mixed_theirs, tokens, gain_two[None, :], output_full
    )
    normed_ffn = after(normed_ffn, *grad_far)
    up_two, down_two = after((up_two, down_two), normed_ffn)
    up_three, down_three = line_up(up_two), line_down(down_two)
    row_near = near_pieces(normed_ffn, normed_ffn)
    row_far = far_pieces(*row_near)
    slots = [up_three, up_two, up_one, own_part, down_one, down_two, down_three]
    row_pieces = with_cores(normed_ffn, *row_near, *row_far)
    grad_pieces = with_cores(*after((grad_rows, *grad_near, *grad_far), row_near[0]))
    place = line.astype(jnp.int32)[None]
    far = run_experts(FAR_TILES, place, row_pieces, grad_pieces, slots, select, 0, ())
    far_back = over_cores(far[2], far[3]).astype(BF16)
    back_y, back_x = far_links(far_back)
    near = run_experts(
        NEAR_TILES, after(place, far_back), row_pieces, grad_pieces, slots, select, 4, far[4:]
    )
    hid_a, hid_b, du_a, du_b, all_rows, all_grads = near[4:]

    def weight_grads(rows, grads, grad_both, hidden):
        inner = contract(rows, grad_both, 0, 0)
        outer = contract(grads, hidden, 0, 0) * BRANCH_SCALE
        return [
            jnp.concatenate(
                [inner[:, 2 * half * i : 2 * half * (i + 1)], outer[:, half * i : half * (i + 1)]],
                axis=1,
            ).astype(BF16)
            for i in range(2)
        ]

    rows_early, grads_early, back_y, back_x = lax.optimization_barrier(
        (all_rows, all_grads, back_y, back_x)
    )
    outer_grads = weight_grads(rows_early, grads_early, du_a, hid_a)
    grads_of = dict(zip(SLOT_ORDER[:2], outer_grads))
    far_line = (line_up(outer_grads[1]), line_down(outer_grads[0]))
    near_back = over_cores(after(near[2], *outer_grads), near[3])
    first, second = near_links(near_back, back_y, back_x)
    rows_late, grads_late = after((all_rows, all_grads), first, second)
    inner_grads = weight_grads(rows_late, grads_late, du_b, hid_b)
    grads_of.update(zip(SLOT_ORDER[2:], inner_grads))
    first, second = swap_seq(first), swap_y(second)
    near_back = after(near_back, *inner_grads)
    grad_normed_ffn = own_sum(near_back, back_y, back_x, first, second)

    def line_partial(first, *rest):
        value = grads_of[first]
        for where, expert in enumerate(rest):
            value = jnp.where(line > where, grads_of[expert], value)
        return value.astype(F32)

    def line_step(step, arrived):
        up, down = arrived
        last = LINE - 1
        right = line_partial(*range(last - step, LINE)) + up.astype(F32)
        left = grads_of[step]
        for where in range(step):
            left = jnp.where(line < last - where, grads_of[step - 1 - where], left)
        left = left.astype(F32) + down.astype(F32)
        return right.astype(BF16), left.astype(BF16)

    grad_final = cotangent.astype(F32)
    grad_norm, grad_gain_two = norm_back(middle, gain_two, grad_normed_ffn)
    grad_middle = grad_final + grad_norm
    grad_attn = (BRANCH_SCALE * grad_middle).astype(BF16)
    grad_mixed = contract(grad_attn, output_parts[0], 1, 1).astype(BF16)
    grad_other = contract(grad_attn, output_parts[1], 1, 1).astype(BF16)
    grad_other = swap_seq(grad_other)
    grad_w_output = contract(ordered(mixed_mine, mixed_theirs, 1), grad_attn, 0, 0)
    far_f, far_f_other, near_f, near_f_other = after(
        (far[0], far[1], near[0], near[1]), grad_mixed
    )
    far_ffn = over_cores(far_f, far_f_other).astype(BF16)
    ffn_y, ffn_x = far_links(far_ffn)
    near_ffn = over_cores(near_f, near_f_other)
    right, left = line_step(1, far_line)
    grad_other = after(grad_other, right, left, far_ffn, grad_w_output)
    grad_sorted = to_order(grad_mixed, grad_other)
    mid_line = (line_up(right), line_down(left))
    grad_query, grad_keys, grad_values = attend_back(
        query,
        keys,
        values,
        grad_sorted,
        jnp.concatenate([levels_one, levels_two], axis=0),
        start_column,
        cos,
        sin,
    )
    (grad_query, grad_keys, grad_values), mid_line, ffn_y, ffn_x = lax.optimization_barrier(
        ((grad_query, grad_keys, grad_values), mid_line, ffn_y, ffn_x)
    )
    right, left = line_step(2, mid_line)
    third = width // 3
    last_first = (line_up(right[:third]), line_down(left[:third]))
    first_ffn, second_ffn = near_links(near_ffn, ffn_y, ffn_x)
    first_ffn, second_ffn = swap_seq(first_ffn), swap_y(second_ffn)
    ffn = own_sum(near_ffn, ffn_y, ffn_x, first_ffn, second_ffn)
    output = (middle + BRANCH_SCALE * ffn).astype(BF16)
    grads_qkv = after((grad_query, grad_keys, grad_values), right, left)
    wide = qkv_grad(normed, grads_qkv, grad_gain_two[None, :], shard)


    def chosen(value, which, axis):
        return lax.dynamic_index_in_dim(value, which, axis=axis, keepdims=False)

    summed_output = lax.psum_scatter(
        grad_w_output.astype(BF16), ("seq", "dp"), scatter_dimension=0, tiled=True
    )
    kept = chosen(wide, core, 0).astype(F32)
    kept = kept + swap_core(chosen(wide, 1 - core, 0)).astype(F32)
    grads_late = after(grads_qkv, kept)
    grad_normed, sent_normed = token_grad(
        grads_late, w_qkv, own_places[:, None], other_places[:, None]
    )
    kept, sent_normed = lax.optimization_barrier((kept, sent_normed))
    right_mid, left_mid = after((right[third : 2 * third], left[third : 2 * third]), last_first)
    last_mid = (line_up(right_mid), line_down(left_mid))
    right_late, left_late = after(
        (right[2 * third :], left[2 * third :]), last_mid, sent_normed
    )
    last_late = (line_up(right_late), line_down(left_late))
    grad_normed = grad_normed.astype(F32) + swap_seq(sent_normed).astype(F32)
    scale = lax.rsqrt(jnp.mean(inputs * inputs, axis=-1, keepdims=True) + EPSILON)
    unit = inputs * scale
    scaled = grad_normed * gain_one
    inner = jnp.mean(scaled * unit, axis=-1, keepdims=True)
    grad_tokens = grad_middle + scale * (scaled - unit * inner)
    next_kept = chosen(kept, row_of, 0)
    next_kept = next_kept + swap_y(chosen(kept, 1 - row_of, 0).astype(BF16)).astype(F32)
    next_kept, last_first, last_mid, last_late, summed_output = lax.optimization_barrier(
        (next_kept, last_first, last_mid, last_late, summed_output)
    )
    own_grads = line_partial(*range(LINE))
    part_grads = jnp.concatenate(
        [
            own + up.astype(F32) + down.astype(F32)
            for own, (up, down) in zip(
                jnp.split(own_grads, 3, axis=0), (last_first, last_mid, last_late)
            )
        ],
        axis=0,
    ).astype(BF16)
    same_grads = jnp.where(first_core, part_grads[:, :half], part_grads[:, half : 2 * half])
    cross_grads = jnp.where(first_core, part_grads[:, half : 2 * half], part_grads[:, :half])
    same_grads = jnp.concatenate([same_grads, part_grads[:, 2 * half :]], axis=1)
    next_kept, same_grads, cross_grads = lax.optimization_barrier(
        (next_kept, same_grads, cross_grads)
    )
    same = both_axes(same_grads, straight)
    cross = both_axes(cross_grads, crossed_back)
    sent_lines = [
        swap_dp(chosen(next_kept, line ^ step, 1).astype(BF16), 4 * step) for step in range(1, LINE)
    ]
    summed = chosen(next_kept, line, 1) + sum(value.astype(F32) for value in sent_lines)
    summed, same, cross = lax.optimization_barrier((summed, same, cross))
    grad_w_in = ordered(same[:, :half], cross, 1)
    grad_w_out = same[:, half:].T
    kept_rows = chosen(summed, seq, 0)
    sent_rows = swap_seq(chosen(summed, 1 - seq, 0).astype(BF16)).astype(F32)
    cuts = (q_width, q_width + kv_width, qkv_width)
    pieces = [
        (a, b) for a, b in zip(jnp.split(kept_rows, cuts, axis=1), jnp.split(sent_rows, cuts, axis=1))
    ]
    grad_projections = [ordered(a, b, 1) for a, b in pieces[:3]]
    grad_gain_ffn = (pieces[3][0] + pieces[3][1])[:, 0]
    grad_gain_attn = sum(
        jnp.sum(grad * weight.astype(F32), axis=1)
        for grad, weight in zip(grad_projections, projections)
    ) / gain_attn.astype(F32)
    return (
        output,
        grad_tokens,
        grad_projections[0],
        grad_projections[1],
        grad_projections[2],
        summed_output.astype(F32),
        grad_gain_attn,
        grad_gain_ffn,
        grad_w_in.astype(F32)[None],
        grad_w_out.astype(F32)[None],
    )


def solution(mesh):
    placed = (
        P(("seq", "dp"), None),
        P(("seq", "dp"), None),
        P("dp", None),
        P("dp", None),
        P(("seq", "dp"), None),
        P(("seq", "dp"), None),
        P(("seq", "dp"), None),
        P(("seq", "dp"), None),
        P(("seq", "dp"), None),
        P(("seq", "dp"), None),
        P(("seq", "dp")),
        P(("seq", "dp")),
        P("dp", None, "seq"),
        P("dp", "seq", None),
    )
    return jax.shard_map(
        shards_plane if in_planes(mesh) else shards_general,
        mesh=mesh,
        in_specs=placed,
        out_specs=(
            P(("seq", "dp"), None),
            P(("seq", "dp"), None),
            P(("seq", "dp"), None),
            P(("seq", "dp"), None),
            P(("seq", "dp"), None),
            P(("seq", "dp"), None),
            P(("seq", "dp")),
            P(("seq", "dp")),
            P("dp", None, "seq"),
            P("dp", "seq", None),
        ),
        check_vma=False,
    )
```

```python
import functools

import jax
import jax.numpy as jnp
from jax import lax
from jax.experimental import pallas as pl
from jax.experimental.pallas import tpu as pltpu
from jax.sharding import PartitionSpec as P

QHEADS = 24
KVHEADS = 8
HDIM = 64
FF = 512
TOP = 8


EPSILON = 1e-06
BRANCH_SCALE = 0.22
SCORE_SCALE = 1.0 / 64.0
THETA = 10000.0


def rms_norm(value, gain):
    return value * lax.rsqrt(jnp.mean(value * value, axis=-1, keepdims=True) + EPSILON) * gain


def local_places(placing, seq_lengths):
    ends = jnp.cumsum(seq_lengths)
    segment = jnp.sum((placing[:, None] >= ends[None, :]).astype(jnp.int32), axis=1)
    starts = ends - seq_lengths
    member = segment[:, None] == jnp.arange(seq_lengths.shape[0], dtype=jnp.int32)[None, :]
    start_of = jnp.sum(jnp.where(member, starts[None, :], 0), axis=1)
    return (segment, placing - start_of)


def rotate(values, place, direction):
    half = values.shape[-1] // 2
    freqs = jnp.power(THETA, -jnp.arange(half, dtype=jnp.float32) * 2.0 / values.shape[-1])
    angles = place.astype(jnp.float32)[:, None] * freqs[None, :]
    cosine = jnp.cos(angles)[:, None, :]
    sine = direction * jnp.sin(angles)[:, None, :]
    first = values[..., :half]
    second = values[..., half:]
    return jnp.concatenate(
        [first * cosine - second * sine, second * cosine + first * sine], axis=-1
    )


def shards_general(
    tokens,
    cotangent,
    positions,
    lengths,
    routes,
    logits,
    w_query,
    w_key,
    w_value,
    w_output,
    gain_attn,
    gain_ffn,
    w_in,
    w_out,
):
    seq_count = lax.axis_size("seq")
    data_count = lax.axis_size("dp")
    tok_count = tokens.shape[0]
    group_len = positions.shape[1]
    local_experts = w_in.shape[0]
    experts_all = local_experts * data_count
    capacity = min(tok_count, 5 * tok_count * TOP // (4 * experts_all))
    heads_local = QHEADS // seq_count
    kv_local = KVHEADS // seq_count
    ratio = QHEADS // KVHEADS
    width = tokens.shape[1]
    query_full, key_full, value_full, output_full, gain_one, gain_two = (
        lax.all_gather(w_query, ("seq", "dp"), axis=0, tiled=True),
        lax.all_gather(w_key, ("seq", "dp"), axis=0, tiled=True),
        lax.all_gather(w_value, ("seq", "dp"), axis=0, tiled=True),
        lax.all_gather(w_output, ("seq", "dp"), axis=0, tiled=True),
        lax.all_gather(gain_attn, ("seq", "dp"), axis=0, tiled=True),
        lax.all_gather(gain_ffn, ("seq", "dp"), axis=0, tiled=True),
    )
    in_full, out_full = (
        lax.all_gather(w_in, "seq", axis=2, tiled=True),
        lax.all_gather(w_out, "seq", axis=1, tiled=True),
    )
    gain_one = gain_one.astype(jnp.float32)
    gain_two = gain_two.astype(jnp.float32)
    segment, place = local_places(positions[0], lengths[0])
    my_start = lax.axis_index("seq") * tok_count
    my_place = lax.dynamic_slice_in_dim(place, my_start, tok_count)
    inputs = tokens.astype(jnp.float32)
    normed = rms_norm(inputs, gain_one).astype(jnp.bfloat16)
    query_pre = jnp.dot(normed, query_full, preferred_element_type=jnp.float32)
    key_pre = jnp.dot(normed, key_full, preferred_element_type=jnp.float32)
    query_rot = (
        rotate(query_pre.reshape(tok_count, QHEADS, HDIM), my_place, 1.0)
        .reshape(tok_count, QHEADS * HDIM)
        .astype(jnp.bfloat16)
    )
    key_rot = (
        rotate(key_pre.reshape(tok_count, KVHEADS, HDIM), my_place, 1.0)
        .reshape(tok_count, KVHEADS * HDIM)
        .astype(jnp.bfloat16)
    )
    value_low = jnp.dot(normed, value_full, preferred_element_type=jnp.float32).astype(jnp.bfloat16)
    query_heads, key_heads, value_heads = (
        lax.all_to_all(query_rot, "seq", split_axis=1, concat_axis=0, tiled=True),
        lax.all_to_all(key_rot, "seq", split_axis=1, concat_axis=0, tiled=True),
        lax.all_to_all(value_low, "seq", split_axis=1, concat_axis=0, tiled=True),
    )
    keys_three = key_heads.reshape(group_len, kv_local, HDIM)
    values_three = value_heads.reshape(group_len, kv_local, HDIM)
    length = min(512, group_len)
    count = group_len // length

    def scores_of(query_block, seg_block, place_block):
        grouped = query_block.reshape(length, kv_local, ratio, HDIM)
        raw_scores = (
            jnp.einsum("qgrd,kgd->grqk", grouped, keys_three, preferred_element_type=jnp.float32)
            * SCORE_SCALE
        )
        allowed = (seg_block[:, None] == segment[None, :]) & (
            place[None, :] <= place_block[:, None]
        )
        return jnp.where(allowed[None, None], raw_scores, -1e30)

    def forward_block(pieces):
        query_block, seg_block, place_block = pieces
        scores = scores_of(query_block, seg_block, place_block)
        highest = jnp.max(scores, axis=-1, keepdims=True)
        expon = jnp.exp(scores - highest)
        totals = jnp.sum(expon, axis=-1, keepdims=True)
        probs = expon / totals
        mixed = jnp.einsum(
            "grqk,kgd->qgrd",
            probs.astype(jnp.bfloat16),
            values_three,
            preferred_element_type=jnp.float32,
        )
        return (
            mixed.reshape(length, heads_local * HDIM).astype(jnp.bfloat16),
            highest + jnp.log(totals),
            probs,
        )

    query_blocks = query_heads.reshape(count, length, heads_local * HDIM)
    seg_blocks = segment.reshape(count, length)
    place_blocks = place.reshape(count, length)
    block_args = (query_blocks, seg_blocks, place_blocks)

    def forward_light(pieces):
        mixed, lse_part, unused_probs = forward_block(pieces)
        return (mixed, lse_part)

    mixed_blocks, lse_blocks = lax.map(forward_light, block_args)
    mixed_heads = mixed_blocks.reshape(group_len, heads_local * HDIM)
    mixed_tokens = lax.all_to_all(mixed_heads, "seq", split_axis=0, concat_axis=1, tiled=True)
    attn = jnp.dot(mixed_tokens, output_full, preferred_element_type=jnp.float32)
    middle = inputs + BRANCH_SCALE * attn
    normed_ffn = rms_norm(middle, gain_two).astype(jnp.bfloat16)
    chosen = routes.reshape(-1)
    onehot = (chosen[:, None] == jnp.arange(experts_all, dtype=jnp.int32)[None, :]).astype(
        jnp.int32
    )
    ranking = jnp.sum(jnp.cumsum(onehot, axis=0) * onehot, axis=1) - 1
    target = chosen * capacity + ranking
    token_of = jnp.arange(tok_count * TOP, dtype=jnp.int32) // TOP
    gates = jax.nn.softmax(logits, axis=-1)
    source = jnp.full((experts_all * capacity,), tok_count, jnp.int32).at[target].set(token_of)
    slot_gate = jnp.zeros((experts_all * capacity,), jnp.float32).at[target].set(gates.reshape(-1))
    padded = jnp.concatenate([normed_ffn, jnp.zeros((1, width), jnp.bfloat16)], axis=0)
    outgoing = padded[source].reshape(data_count, local_experts * capacity, width)

    def expert_layout(arrived):
        return jnp.swapaxes(
            arrived.reshape(data_count, local_experts, capacity, width), 0, 1
        ).reshape(local_experts, data_count * capacity, width)

    def home_layout(values):
        return jnp.swapaxes(
            values.reshape(local_experts, data_count, capacity, width), 0, 1
        ).reshape(data_count, local_experts * capacity, width)

    def expert_forward(expert_rows):
        both = jnp.einsum("erd,edf->erf", expert_rows, in_full, preferred_element_type=jnp.float32)
        hidden = (jax.nn.silu(both[..., :FF]) * both[..., FF:]).astype(jnp.bfloat16)
        return (both, hidden)

    expert_rows = expert_layout(
        lax.all_to_all(outgoing, "dp", split_axis=0, concat_axis=0, tiled=True)
    )
    both, hidden = expert_forward(expert_rows)
    result = jnp.einsum(
        "erf,efd->erd", hidden, out_full, preferred_element_type=jnp.float32
    ).astype(jnp.bfloat16)
    returned = lax.all_to_all(
        home_layout(result), "dp", split_axis=0, concat_axis=0, tiled=True
    ).reshape(experts_all * capacity, width)
    picked = returned[target].reshape(tok_count, TOP, width).astype(jnp.float32)
    ffn = jnp.sum(picked * gates[:, :, None], axis=1)
    final = middle + BRANCH_SCALE * ffn
    output = final.astype(jnp.bfloat16)
    grad_final = cotangent.astype(jnp.float32)
    padded_grad = jnp.concatenate(
        [BRANCH_SCALE * grad_final, jnp.zeros((1, width), jnp.float32)], axis=0
    )
    grad_slots = (slot_gate[:, None] * padded_grad[source]).astype(jnp.bfloat16)
    grad_result = expert_layout(
        lax.all_to_all(
            grad_slots.reshape(data_count, local_experts * capacity, width),
            "dp",
            split_axis=0,
            concat_axis=0,
            tiled=True,
        )
    )
    rows_back = expert_layout(
        lax.all_to_all(outgoing, "dp", split_axis=0, concat_axis=0, tiled=True)
    )
    both_back, hidden_back = expert_forward(rows_back)
    grad_hidden = jnp.einsum(
        "erd,efd->erf", grad_result, out_full, preferred_element_type=jnp.float32
    )
    gate_part = both_back[..., :FF]
    up_part = both_back[..., FF:]
    sigma = jax.nn.sigmoid(gate_part)
    grad_gate = grad_hidden * up_part * sigma * (1.0 + gate_part * (1.0 - sigma))
    grad_up = grad_hidden * gate_part * sigma
    grad_both = jnp.concatenate([grad_gate, grad_up], axis=-1).astype(jnp.bfloat16)
    grad_out_local = jnp.einsum(
        "erf,erd->efd", hidden_back, grad_result, preferred_element_type=jnp.float32
    )
    grad_in_local = jnp.einsum(
        "erd,erf->edf", rows_back, grad_both, preferred_element_type=jnp.float32
    )
    grad_rows = jnp.einsum(
        "erf,edf->erd", grad_both, in_full, preferred_element_type=jnp.float32
    ).astype(jnp.bfloat16)
    grad_home = lax.all_to_all(
        home_layout(grad_rows), "dp", split_axis=0, concat_axis=0, tiled=True
    ).reshape(experts_all * capacity, width)
    grad_normed_ffn = jnp.sum(
        grad_home[target].reshape(tok_count, TOP, width).astype(jnp.float32), axis=1
    )
    grad_w_in, grad_w_out = (
        lax.psum_scatter(
            grad_in_local.astype(jnp.bfloat16), "seq", scatter_dimension=2, tiled=True
        ).astype(jnp.float32),
        lax.psum_scatter(
            grad_out_local.astype(jnp.bfloat16), "seq", scatter_dimension=1, tiled=True
        ).astype(jnp.float32),
    )
    unused_norm, norm_pull = jax.vjp(rms_norm, middle, gain_two)
    grad_middle_norm, grad_gain_two = norm_pull(grad_normed_ffn)
    grad_middle = grad_final + grad_middle_norm
    grad_attn = (BRANCH_SCALE * grad_middle).astype(jnp.bfloat16)
    grad_w_output = jnp.einsum(
        "te,td->ed", mixed_tokens, grad_attn, preferred_element_type=jnp.float32
    )
    grad_mixed = jnp.einsum(
        "td,ed->te", grad_attn, output_full, preferred_element_type=jnp.float32
    ).astype(jnp.bfloat16)
    grad_mixed_heads = lax.all_to_all(grad_mixed, "seq", split_axis=1, concat_axis=0, tiled=True)
    grad_blocks = grad_mixed_heads.reshape(count, length, heads_local * HDIM)
    back_args = (query_blocks, seg_blocks, place_blocks, lse_blocks, grad_blocks)

    def backward_block(carry, pieces):
        grad_keys, grad_values = carry
        query_block, seg_block, place_block, lse_block, grad_block = pieces[:5]
        probs = jnp.exp(scores_of(query_block, seg_block, place_block) - lse_block)
        grad_out = grad_block.reshape(length, kv_local, ratio, HDIM)
        grad_probs = jnp.einsum(
            "qgrd,kgd->grqk", grad_out, values_three, preferred_element_type=jnp.float32
        )
        grad_scores = (
            probs * (grad_probs - jnp.sum(probs * grad_probs, axis=-1, keepdims=True))
        ).astype(jnp.bfloat16)
        grad_query = SCORE_SCALE * jnp.einsum(
            "grqk,kgd->qgrd", grad_scores, keys_three, preferred_element_type=jnp.float32
        )
        grouped = query_block.reshape(length, kv_local, ratio, HDIM)
        grad_keys = grad_keys + SCORE_SCALE * jnp.einsum(
            "grqk,qgrd->kgd", grad_scores, grouped, preferred_element_type=jnp.float32
        )
        grad_values = grad_values + jnp.einsum(
            "grqk,qgrd->kgd",
            probs.astype(jnp.bfloat16),
            grad_out,
            preferred_element_type=jnp.float32,
        )
        return (
            (grad_keys, grad_values),
            grad_query.reshape(length, heads_local * HDIM).astype(jnp.bfloat16),
        )

    empty_keys = jnp.zeros((group_len, kv_local, HDIM), jnp.float32)
    (grad_keys, grad_values), grad_query_blocks = lax.scan(
        backward_block, (empty_keys, empty_keys), back_args
    )
    grad_query_heads = grad_query_blocks.reshape(group_len, heads_local * HDIM)
    grad_key_heads = grad_keys.reshape(group_len, kv_local * HDIM).astype(jnp.bfloat16)
    grad_value_heads = grad_values.reshape(group_len, kv_local * HDIM).astype(jnp.bfloat16)
    grad_query_tok, grad_key_tok, grad_value_tok = (
        lax.all_to_all(grad_query_heads, "seq", split_axis=0, concat_axis=1, tiled=True),
        lax.all_to_all(grad_key_heads, "seq", split_axis=0, concat_axis=1, tiled=True),
        lax.all_to_all(grad_value_heads, "seq", split_axis=0, concat_axis=1, tiled=True),
    )
    grad_query_pre = (
        rotate(grad_query_tok.astype(jnp.float32).reshape(tok_count, QHEADS, HDIM), my_place, -1.0)
        .reshape(tok_count, QHEADS * HDIM)
        .astype(jnp.bfloat16)
    )
    grad_key_pre = (
        rotate(grad_key_tok.astype(jnp.float32).reshape(tok_count, KVHEADS, HDIM), my_place, -1.0)
        .reshape(tok_count, KVHEADS * HDIM)
        .astype(jnp.bfloat16)
    )
    grad_w_query = jnp.einsum(
        "td,te->de", normed, grad_query_pre, preferred_element_type=jnp.float32
    )
    grad_w_key = jnp.einsum("td,te->de", normed, grad_key_pre, preferred_element_type=jnp.float32)
    grad_w_value = jnp.einsum(
        "td,te->de", normed, grad_value_tok, preferred_element_type=jnp.float32
    )
    grad_normed = jnp.einsum(
        "te,de->td", grad_query_pre, query_full, preferred_element_type=jnp.float32
    )
    grad_normed = grad_normed + jnp.einsum(
        "te,de->td", grad_key_pre, key_full, preferred_element_type=jnp.float32
    )
    grad_normed = grad_normed + jnp.einsum(
        "te,de->td", grad_value_tok, value_full, preferred_element_type=jnp.float32
    )
    unused_first, first_pull = jax.vjp(rms_norm, inputs, gain_one)
    grad_inputs_norm, grad_gain_one = first_pull(grad_normed)
    grad_tokens = grad_middle + grad_inputs_norm
    summed = (
        lax.psum_scatter(grad_w_query, ("seq", "dp"), scatter_dimension=0, tiled=True),
        lax.psum_scatter(grad_w_key, ("seq", "dp"), scatter_dimension=0, tiled=True),
        lax.psum_scatter(grad_w_value, ("seq", "dp"), scatter_dimension=0, tiled=True),
        lax.psum_scatter(grad_w_output, ("seq", "dp"), scatter_dimension=0, tiled=True),
        lax.psum_scatter(grad_gain_one, ("seq", "dp"), scatter_dimension=0, tiled=True),
        lax.psum_scatter(grad_gain_two, ("seq", "dp"), scatter_dimension=0, tiled=True),
    )
    return (
        output,
        grad_tokens,
        summed[0],
        summed[1],
        summed[2],
        summed[3],
        summed[4],
        summed[5],
        grad_w_in,
        grad_w_out,
    )


BF16 = jnp.bfloat16
F32 = jnp.float32
LINE = 4
PAD = 128
VMEM_BYTES = 60 * 1024 * 1024


def in_planes(mesh):
    return mesh.shape["seq"] == 2 and mesh.shape["dp"] == 4 * LINE


def swap_seq(value):
    return lax.ppermute(value, "seq", [(0, 1), (1, 0)])


def swap_dp(value, mask):
    return lax.ppermute(value, "dp", [(i, i ^ mask) for i in range(4 * LINE)])


def swap_core(value):
    return swap_dp(value, 1)


def swap_y(value):
    return swap_dp(value, 2)


def line_up(value):
    return lax.ppermute(value, "dp", [(i, i + 4) for i in range(4 * LINE - 4)])


def line_down(value):
    return lax.ppermute(value, "dp", [(i, i - 4) for i in range(4, 4 * LINE)])


def after(value, *others):
    return lax.optimization_barrier((value,) + others)[0]


def line_scatter(take, place):
    up = down = None
    for step in range(LINE - 1):
        far = jnp.minimum(LINE - 1 - step + place, LINE - 1)
        near = jnp.maximum(step - LINE + 1 + place, 0)
        right, left = take(far), take(near)
        if up is not None:
            right = right + up.astype(F32)
            left = left + down.astype(F32)
        up = line_up(right.astype(BF16))
        down = line_down(left.astype(BF16))
    return take(place) + up.astype(F32) + down.astype(F32)


def near_pieces(own, own_x):
    return swap_seq(own_x), swap_y(own)


def far_pieces(near_x, near_y):
    half = near_x.shape[0] // 2
    return swap_y(near_x[:half]), swap_seq(near_y[half:])


def with_cores(*pieces):
    return pieces + tuple(swap_core(piece) for piece in pieces)


def over_cores(mine, others):
    return mine.astype(F32) + swap_core(others).astype(F32)


def far_links(far):
    half = far.shape[0] // 2
    return swap_y(far[:half]), swap_seq(far[half:])


def near_links(near, from_y, from_x):
    half = from_y.shape[0] // 2
    first = (near[:half] + from_y[half:].astype(F32)).astype(BF16)
    second = (near[half : 2 * half] + from_x[half:].astype(F32)).astype(BF16)
    return first, second


def own_sum(near, from_y, from_x, first, second):
    half = from_y.shape[0] // 2
    low = near[2 * half : 3 * half] + from_y[:half].astype(F32) + first.astype(F32)
    high = near[3 * half :] + from_x[:half].astype(F32) + second.astype(F32)
    return jnp.concatenate([low, high], axis=0)


def turned(values, cos, sin, direction):
    lanes = values.shape[1]
    place = lax.broadcasted_iota(jnp.int32, values.shape, 1) % HDIM
    swapped = jnp.where(
        place < HDIM // 2,
        pltpu.roll(values, lanes - HDIM // 2, 1),
        pltpu.roll(values, HDIM // 2, 1),
    )
    times = lanes // cos.shape[1]
    cos = jnp.concatenate([cos] * times, axis=1)
    sin = jnp.concatenate([sin] * times, axis=1)
    if direction > 0:
        return values * cos + swapped * sin
    return values * cos - swapped * sin


def place_shards(place_ref, own_ref, other_ref, shard, store):
    for core in range(2):
        source = other_ref if core else own_ref
        for row in range(2):
            for line in range(LINE):
                index = (place_ref[0] ^ line) * 4 + (place_ref[1] ^ row) * 2 + (place_ref[2] ^ core)
                store(source, (row * LINE + line) * shard, pl.multiple_of(index * shard, shard))


def qkv_kernel(
    place_ref, x_ref, own_ref, other_ref, cos_ref, sin_ref,
    h_ref, q_ref, k_ref, v_ref, w_ref, gain_ref, columns_buf,
):
    q_width, kv_heads = q_ref.shape[1], k_ref.shape[0]
    kv_width = kv_heads * HDIM
    width, columns = w_ref.shape
    shard = own_ref.shape[0] // (2 * LINE)

    @pl.when(pl.program_id(0) == 0)
    def _():
        def store(source, low, place):
            for seq in range(2):
                first = seq * (columns + PAD)
                rows = pl.ds(pl.multiple_of(place + seq * (width // 2), shard), shard)
                w_ref[rows, :] = source[low : low + shard, first : first + columns]
                columns_buf[rows, :] = source[
                    low : low + shard, first + columns : first + columns + PAD
                ].astype(F32)

        place_shards(place_ref, own_ref, other_ref, shard, store)
        gain_ref[...] = columns_buf[...].T[: gain_ref.shape[0]]

    value = x_ref[...].astype(F32)
    scale = lax.rsqrt(jnp.mean(value * value, axis=-1, keepdims=True) + EPSILON)
    normed = (value * scale * gain_ref[0:1, :]).astype(BF16)
    h_ref[...] = normed
    both = jnp.dot(normed, w_ref[...], preferred_element_type=F32)
    spun = turned(both[:, : q_width + kv_width], cos_ref[...], sin_ref[...], 1)
    q_ref[...] = (spun[:, :q_width] * SCORE_SCALE).astype(BF16)
    for head in range(kv_heads):
        low = q_width + head * HDIM
        k_ref[head] = spun[:, low : low + HDIM].astype(BF16)
        low = low + kv_width
        v_ref[head] = both[:, low : low + HDIM].astype(BF16)


def project(places, x_sorted, own, other, cos, sin, q_width, kv_heads):
    rows, width = x_sorted.shape
    tile = 256
    columns = q_width + 2 * kv_heads * HDIM

    def row_block(lanes):
        return pl.BlockSpec((tile, lanes), lambda i, p: (i, 0))

    def whole(shape):
        return pl.BlockSpec(shape, lambda i, p: (0, 0))

    heads = pl.BlockSpec((kv_heads, tile, HDIM), lambda i, p: (0, i, 0))
    return pl.pallas_call(
        qkv_kernel,
        grid_spec=pltpu.PrefetchScalarGridSpec(
            num_scalar_prefetch=1,
            grid=(rows // tile,),
            in_specs=[
                row_block(width),
                whole(own.shape),
                whole(other.shape),
                row_block(cos.shape[1]),
                row_block(cos.shape[1]),
            ],
            out_specs=[
                row_block(width), row_block(q_width), heads, heads,
                whole((width, columns)), whole((8, width)),
            ],
            scratch_shapes=[pltpu.VMEM((width, PAD), F32)],
        ),
        out_shape=[
            jax.ShapeDtypeStruct((rows, width), BF16),
            jax.ShapeDtypeStruct((rows, q_width), BF16),
            jax.ShapeDtypeStruct((kv_heads, rows, HDIM), BF16),
            jax.ShapeDtypeStruct((kv_heads, rows, HDIM), BF16),
            jax.ShapeDtypeStruct((width, columns), BF16),
            jax.ShapeDtypeStruct((8, width), F32),
        ],
        compiler_params=pltpu.CompilerParams(vmem_limit_bytes=VMEM_BYTES),
        cost_estimate=pl.CostEstimate(
            flops=rows * width * columns // 8,
            bytes_accessed=rows * width + width * columns,
            transcendentals=rows,
        ),
        name="project",
    )(places, x_sorted, own, other, cos, sin)


def mix_kernel(place_ref, mine_ref, theirs_ref, x_ref, gain_ref, w_ref, m_ref, h_ref, parts_ref):
    half = parts_ref.shape[1]

    @pl.when(pl.program_id(0) == 0)
    def _():
        for part in range(2):
            low = pl.multiple_of((place_ref[0] ^ part) * half, half)
            parts_ref[part] = w_ref[pl.ds(low, half), :]

    mixed = jnp.dot(mine_ref[...], parts_ref[0], preferred_element_type=F32)
    mixed = mixed + jnp.dot(theirs_ref[...], parts_ref[1], preferred_element_type=F32)
    value = x_ref[...].astype(F32) + BRANCH_SCALE * mixed
    m_ref[...] = value
    scale = lax.rsqrt(jnp.mean(value * value, axis=-1, keepdims=True) + EPSILON)
    h_ref[...] = (value * scale * gain_ref[...]).astype(BF16)


def mix(place, mine, theirs, tokens, gain, weights):
    rows, width = tokens.shape
    half = mine.shape[1]
    tile = 256

    def row_block(lanes):
        return pl.BlockSpec((tile, lanes), lambda i, p: (i, 0))

    def whole(shape):
        return pl.BlockSpec(shape, lambda i, p: (0,) * len(shape))

    return pl.pallas_call(
        mix_kernel,
        grid_spec=pltpu.PrefetchScalarGridSpec(
            num_scalar_prefetch=1,
            grid=(rows // tile,),
            in_specs=[
                row_block(half), row_block(half), row_block(width), whole(gain.shape),
                whole((width, width)),
            ],
            out_specs=[row_block(width), row_block(width), whole((2, half, width))],
        ),
        out_shape=[
            jax.ShapeDtypeStruct((rows, width), F32),
            jax.ShapeDtypeStruct((rows, width), BF16),
            jax.ShapeDtypeStruct((2, half, width), BF16),
        ],
        compiler_params=pltpu.CompilerParams(vmem_limit_bytes=VMEM_BYTES),
        cost_estimate=pl.CostEstimate(
            flops=rows * width * width // 8, bytes_accessed=rows * width, transcendentals=rows
        ),
        name="mix",
    )(place, mine, theirs, tokens, gain, weights)


def token_grad_kernel(dq_ref, dk_ref, dv_ref, w_ref, own_ref, other_ref, mine_ref, sent_ref):
    q_width, kv_width = dq_ref.shape[1], dk_ref.shape[1]
    cuts = (0, q_width, q_width + kv_width, q_width + 2 * kv_width)
    grad = contract(dq_ref[...], w_ref[:, cuts[0] : cuts[1]], 1, 1)
    grad = grad + contract(dk_ref[...], w_ref[:, cuts[1] : cuts[2]], 1, 1)
    grad = (grad + contract(dv_ref[...], w_ref[:, cuts[2] : cuts[3]], 1, 1)).astype(BF16)
    for place_ref, out_ref in ((other_ref, sent_ref), (own_ref, mine_ref)):
        shape = (place_ref.shape[0], grad.shape[0])
        picked = lax.broadcasted_iota(jnp.int32, shape, 1) == place_ref[...]
        picked = jnp.where(picked, 1.0, 0.0).astype(BF16)
        out_ref[...] = jnp.dot(picked, grad, preferred_element_type=F32).astype(BF16)


def token_grad(grads, weights, own_places, other_places):
    rows, count = grads[0].shape[0], own_places.shape[0]
    width = weights.shape[0]
    columns = sum(grad.shape[1] for grad in grads)
    tile = width // 3

    def whole(array):
        return pl.BlockSpec(array.shape, lambda i: (0, 0))

    block = pl.BlockSpec((count, tile), lambda i: (0, i))
    return pl.pallas_call(
        token_grad_kernel,
        grid=(3,),
        in_specs=[whole(grad) for grad in grads]
        + [pl.BlockSpec((tile, columns), lambda i: (i, 0)), whole(own_places), whole(other_places)],
        out_specs=[block, block],
        out_shape=[jax.ShapeDtypeStruct((count, width), BF16)] * 2,
        compiler_params=pltpu.CompilerParams(vmem_limit_bytes=VMEM_BYTES),
        cost_estimate=pl.CostEstimate(
            flops=rows * width * columns // 8, bytes_accessed=rows * width, transcendentals=0
        ),
        name="token_grad",
    )(*grads, weights, own_places, other_places)


Q_TILE = 256


def windows(rows):
    longest = rows // 2
    for start in range(0, rows, Q_TILE):
        low = max(0, start - longest + 1) // Q_TILE * Q_TILE
        yield start, low, start + Q_TILE


def allowed_keys(start_ref, row, low, high):
    shape = (Q_TILE, high - low)
    rows = lax.broadcasted_iota(jnp.int32, shape, 0) + row
    keys = lax.broadcasted_iota(jnp.int32, shape, 1) + low
    return (keys <= rows) & (keys >= start_ref[row : row + Q_TILE, :])


def contract(left, right, left_dim, right_dim):
    return lax.dot_general(
        left, right, (((left_dim,), (right_dim,)), ((), ())), preferred_element_type=F32
    )


def masked_scores(query, keys, allowed):
    return jnp.where(allowed, contract(query, keys, 1, 1), -1e30)


def attend_kernel(base, q_ref, k_ref, v_ref, start_ref, o_ref, level_ref):
    pair = pl.program_id(0) + base
    ratio = QHEADS // KVHEADS
    for row, low, high in windows(q_ref.shape[0]):
        allowed = allowed_keys(start_ref, row, low, high)
        for side in range(2):
            head = (2 * pair + side) // ratio
            lanes = slice(side * HDIM, (side + 1) * HDIM)
            scores = masked_scores(
                q_ref[row : row + Q_TILE, lanes], k_ref[head, low:high, :], allowed
            )
            highest = jnp.max(scores, axis=-1, keepdims=True)
            expon = jnp.exp(scores - highest)
            total = jnp.sum(expon, axis=-1, keepdims=True)
            level_ref[0, row : row + Q_TILE, side : side + 1] = highest + jnp.log(total)
            probs = expon * (1.0 / total)
            mixed = contract(probs.astype(BF16), v_ref[head, low:high, :], 1, 0)
            o_ref[row : row + Q_TILE, lanes] = mixed.astype(BF16)


def attention_cost(rows, heads, products):
    area = sum(Q_TILE * (high - low) for _, low, high in windows(rows))
    return pl.CostEstimate(
        flops=products * heads * area * 16,
        bytes_accessed=8 * rows * heads * HDIM,
        transcendentals=heads * area,
    )


def attend(query, keys, values, starts, base, pairs):
    rows = query.shape[0]
    pair_block = pl.BlockSpec((rows, 2 * HDIM), lambda j: (0, j + base))
    whole = pl.BlockSpec(keys.shape, lambda j: (0, 0, 0))
    return pl.pallas_call(
        functools.partial(attend_kernel, base),
        grid=(pairs,),
        in_specs=[pair_block, whole, whole, pl.BlockSpec((rows, 1), lambda j: (0, 0))],
        out_specs=[
            pl.BlockSpec((rows, 2 * HDIM), lambda j: (0, j)),
            pl.BlockSpec((1, rows, 2), lambda j: (j, 0, 0)),
        ],
        out_shape=[
            jax.ShapeDtypeStruct((rows, pairs * 2 * HDIM), BF16),
            jax.ShapeDtypeStruct((pairs, rows, 2), F32),
        ],
        compiler_params=pltpu.CompilerParams(vmem_limit_bytes=VMEM_BYTES),
        cost_estimate=attention_cost(rows, 2 * pairs, 2),
        name="attend",
    )(query, keys, values, starts)


def attend_back_kernel(
    q_ref, k_ref, v_ref, d_ref, level_ref, start_ref, cos_ref, sin_ref,
    dq_ref, dk_ref, dv_ref, dk_sum, dv_sum,
):
    pair = pl.program_id(0)
    ratio = QHEADS // KVHEADS

    @pl.when(pair == 0)
    def _():
        dk_sum[...] = jnp.zeros_like(dk_sum)
        dv_sum[...] = jnp.zeros_like(dv_sum)

    for row, low, high in windows(q_ref.shape[0]):
        allowed = allowed_keys(start_ref, row, low, high)
        grads = []
        for side in range(2):
            head = (2 * pair + side) // ratio
            lanes = slice(side * HDIM, (side + 1) * HDIM)
            query = q_ref[row : row + Q_TILE, lanes]
            keys = k_ref[head, low:high, :]
            probs = jnp.exp(
                masked_scores(query, keys, allowed)
                - level_ref[0, row : row + Q_TILE, side : side + 1]
            )
            grad_out = d_ref[row : row + Q_TILE, lanes]
            grad_probs = contract(grad_out, v_ref[head, low:high, :], 1, 1)
            inner = jnp.sum(probs * grad_probs, axis=-1, keepdims=True)
            grad_scores = (probs * (grad_probs - inner)).astype(BF16)
            grads.append(contract(grad_scores, keys, 1, 0) * SCORE_SCALE)
            dk_sum[head, low:high, :] += contract(grad_scores, query, 0, 0)
            dv_sum[head, low:high, :] += contract(probs.astype(BF16), grad_out, 0, 0)
        grad_query = jnp.concatenate(grads, axis=1).astype(BF16).astype(F32)
        dq_ref[row : row + Q_TILE, :] = turned(
            grad_query,
            cos_ref[row : row + Q_TILE, :],
            sin_ref[row : row + Q_TILE, :],
            -1,
        ).astype(BF16)

    @pl.when(pair == pl.num_programs(0) - 1)
    def _():
        heads = range(dk_sum.shape[0])
        grad_keys = jnp.concatenate([dk_sum[head] for head in heads], axis=1)
        grad_keys = grad_keys.astype(BF16).astype(F32)
        dk_ref[...] = turned(grad_keys, cos_ref[...], sin_ref[...], -1).astype(BF16)
        dv_ref[...] = jnp.concatenate([dv_sum[head] for head in heads], axis=1).astype(BF16)


def attend_back(query, keys, values, grad_out, levels, starts, cos, sin):
    rows, lanes = query.shape
    pairs = lanes // (2 * HDIM)
    kv_heads = keys.shape[0]
    pair_block = pl.BlockSpec((rows, 2 * HDIM), lambda j: (0, j))
    whole = pl.BlockSpec(keys.shape, lambda j: (0, 0, 0))

    def fixed(lanes_of):
        return pl.BlockSpec((rows, lanes_of), lambda j: (0, 0))

    flat = kv_heads * HDIM
    return pl.pallas_call(
        attend_back_kernel,
        grid=(pairs,),
        in_specs=[
            pair_block, whole, whole, pair_block,
            pl.BlockSpec((1, rows, 2), lambda j: (j, 0, 0)), fixed(1), fixed(2 * HDIM), fixed(2 * HDIM),
        ],
        out_specs=[pair_block, fixed(flat), fixed(flat)],
        out_shape=[
            jax.ShapeDtypeStruct(query.shape, BF16),
            jax.ShapeDtypeStruct((rows, flat), BF16),
            jax.ShapeDtypeStruct((rows, flat), BF16),
        ],
        scratch_shapes=[pltpu.VMEM(keys.shape, F32), pltpu.VMEM(keys.shape, F32)],
        compiler_params=pltpu.CompilerParams(vmem_limit_bytes=VMEM_BYTES),
        cost_estimate=attention_cost(rows, 2 * pairs, 5),
        name="attend_back",
    )(query, keys, values, grad_out, levels, starts, cos, sin)


SLOTS = 2 * LINE - 1
SLOT_ORDER = (0, 3, 1, 2)
OWN, NEAR_X, NEAR_Y, FAR_Y, FAR_X = range(5)
FAR_TILES = (((NEAR_Y, 0), (FAR_Y, 0)), ((NEAR_X, 1), (FAR_X, 0)))
NEAR_TILES = (((NEAR_X, 0), (NEAR_Y, 1)), ((OWN, 0), (OWN, 1)))


def used_pieces(tiles):
    return sorted({piece for tile in tiles for piece, _ in tile})


def experts_kernel(tiles, half_rows, place_ref, *refs):
    used = used_pieces(tiles)
    sides = 2 * len(used)
    h_pieces, g_pieces, slots = refs[:sides], refs[sides : 2 * sides], refs[2 * sides : 2 * sides + SLOTS]
    select_ref = refs[2 * sides + SLOTS]
    (
        f_mine, f_other, d_mine, d_other, hid_a, hid_b, du_a, du_b, hcopy_ref, gcopy_ref,
        w_in, w_out, h_buf, g_buf, hidden, du_all, weight_sems, row_sems,
    ) = refs[-18:]
    width = h_buf.shape[2]
    half = slots[0].shape[1] // 3
    part = 2 * half
    step = pl.program_id(0)
    steps = 2 * len(tiles)

    def weight_copies(spot, slot):
        return (
            pltpu.make_async_copy(
                slots[slot].at[:, :part],
                w_in.at[:, spot * part : (spot + 1) * part],
                weight_sems.at[0, spot],
            ),
            pltpu.make_async_copy(
                slots[slot].at[:, part:],
                w_out.at[:, spot * half : (spot + 1) * half],
                weight_sems.at[1, spot],
            ),
        )

    def row_copies(number, buffer):
        side, tile = divmod(number, len(tiles))
        copies = []
        for spot, (piece, part_of) in enumerate(tiles[tile]):
            index = side * len(used) + used.index(piece)
            for kind, (pieces, held) in enumerate(((h_pieces, h_buf), (g_pieces, g_buf))):
                copies.append(
                    pltpu.make_async_copy(
                        pieces[index].at[pl.ds(part_of * half_rows, half_rows), :],
                        held.at[buffer, pl.ds(spot * half_rows, half_rows), :],
                        row_sems.at[buffer, 2 * kind + spot],
                    )
                )
        return copies

    def fetch(wanted, buffer):
        for number in range(steps):

            @pl.when(wanted == number)
            def _():
                for copy in row_copies(number, buffer):
                    copy.start()

    buffer = step % 2

    @pl.when(step == 0)
    def _():
        fetch(step, 0)
        for spot, expert in enumerate(SLOT_ORDER):
            for slot in range(expert, expert + LINE):

                @pl.when(slot == LINE - 1 + expert - place_ref[0])
                def _():
                    for copy in weight_copies(spot, slot):
                        copy.start()

        for spot in range(LINE):
            for copy in weight_copies(spot, LINE - 1):
                copy.wait()

    @pl.when(step + 1 < steps)
    def _():
        fetch(step + 1, 1 - buffer)

    for copy in row_copies(0, buffer):
        copy.wait()

    rows = h_buf[buffer]
    grads = g_buf[buffer, :, :width]
    hcopy_ref[...] = rows
    gcopy_ref[...] = grads
    gates = jnp.dot(g_buf[buffer, :, width:], select_ref[...], preferred_element_type=F32)
    for spot in range(LINE):
        units = slice(spot * half, (spot + 1) * half)
        both = jnp.dot(
            rows, w_in[:, spot * part : (spot + 1) * part], preferred_element_type=F32
        )
        back = jnp.dot(grads, w_out[:, units], preferred_element_type=F32)
        gate = gates[:, units]
        first, second = both[:, :half], both[:, half:]
        sigma = jax.nn.sigmoid(first)
        silu = first * sigma
        hidden[:, units] = (gate * (silu * second)).astype(BF16)
        back = back * (BRANCH_SCALE * gate)
        d_first = back * second * (sigma * (1.0 + first * (1.0 - sigma)))
        d_second = back * silu
        du_all[:, spot * part : spot * part + half] = d_first.astype(BF16)
        du_all[:, spot * part + half : (spot + 1) * part] = d_second.astype(BF16)
    hid_a[...] = hidden[:, : 2 * half]
    hid_b[...] = hidden[:, 2 * half :]
    du_a[...] = du_all[:, : 2 * part]
    du_b[...] = du_all[:, 2 * part :]
    ffn = contract(hidden[...], w_out[...], 1, 1).astype(BF16)
    back_rows = contract(du_all[...], w_in[...], 1, 1).astype(BF16)

    @pl.when(step < len(tiles))
    def _():
        f_mine[...] = ffn
        d_mine[...] = back_rows

    @pl.when(step >= len(tiles))
    def _():
        f_other[...] = ffn
        d_other[...] = back_rows


def run_experts(tiles, place, row_pieces, grad_pieces, slots, select, base, kept):
    used = used_pieces(tiles)
    sides = len(row_pieces) // 2
    wanted = used + [sides + piece for piece in used]
    rows = [row_pieces[piece] for piece in wanted]
    grads = [grad_pieces[piece] for piece in wanted]
    tile, width = row_pieces[OWN].shape
    wide = grad_pieces[OWN].shape[1]
    half = slots[0].shape[1] // 3
    part = 2 * half
    count = len(tiles)
    steps = 2 * count
    total = 8 * tile

    def late(lanes):
        return pl.BlockSpec((tile, lanes), lambda i, p: (i + base, 0))

    mine = pl.BlockSpec((tile, width), lambda i, p: (jnp.minimum(i, count - 1), 0))
    others = pl.BlockSpec((tile, width), lambda i, p: (jnp.maximum(i - count, 0), 0))
    anywhere = pl.BlockSpec(memory_space=pl.ANY)
    kept = list(kept)
    lead = 1 + 2 * len(wanted) + SLOTS + 1
    partial = jax.ShapeDtypeStruct((count * tile, width), BF16)
    lanes = [2 * half, 2 * half, 2 * part, 2 * part, width, width]
    return pl.pallas_call(
        functools.partial(experts_kernel, tiles, tile // 2),
        grid_spec=pltpu.PrefetchScalarGridSpec(
            num_scalar_prefetch=1,
            grid=(steps,),
            in_specs=[anywhere] * (2 * len(wanted) + SLOTS)
            + [pl.BlockSpec(select.shape, lambda i, p: (0, 0))]
            + [anywhere] * len(kept),
            out_specs=[mine, others, mine, others] + [late(n) for n in lanes],
            scratch_shapes=[
                pltpu.VMEM((width, LINE * part), BF16),
                pltpu.VMEM((width, LINE * half), BF16),
                pltpu.VMEM((2, tile, width), BF16),
                pltpu.VMEM((2, tile, wide), BF16),
                pltpu.VMEM((tile, LINE * half), BF16),
                pltpu.VMEM((tile, LINE * part), BF16),
                pltpu.SemaphoreType.DMA((2, LINE)),
                pltpu.SemaphoreType.DMA((2, 4)),
            ],
        ),
        out_shape=[partial] * 4 + [jax.ShapeDtypeStruct((total, n), BF16) for n in lanes],
        input_output_aliases={lead + i: 4 + i for i in range(len(kept))},
        compiler_params=pltpu.CompilerParams(vmem_limit_bytes=VMEM_BYTES),
        cost_estimate=pl.CostEstimate(
            flops=steps * tile * width * LINE * (part + half) // 4,
            bytes_accessed=2 * steps * tile * (6 * width + LINE * (part + half)),
            transcendentals=steps * tile * LINE * half,
        ),
        name="experts",
    )(place, *rows, *grads, *slots, select, *kept)


def qkv_grad_kernel(h_ref, dq_ref, dk_ref, dv_ref, gain_ref, o_ref):
    shard = o_ref.shape[-2]
    rows = h_ref[...]
    low = 0
    gains = jnp.broadcast_to(gain_ref[...], (PAD, gain_ref.shape[1])).T.astype(BF16)
    parts = [contract(rows, ref[...], 0, 0).astype(BF16) for ref in (dq_ref, dk_ref, dv_ref)]
    for part in parts + [gains]:
        for block in range(h_ref.shape[1] // shard):
            place = (block % 2, block // 2 % 2, 0, block // 4)
            o_ref[place + (slice(None), slice(low, low + part.shape[1]))] = part[
                block * shard : (block + 1) * shard
            ]
        low = low + part.shape[1]


def qkv_grad(normed, grads, gain_row, shard):
    rows, width = normed.shape
    columns = sum(grad.shape[1] for grad in grads)
    tile = width // 4
    planes = tile // (4 * shard)
    return pl.pallas_call(
        qkv_grad_kernel,
        grid=(4,),
        in_specs=[pl.BlockSpec((rows, tile), lambda i: (0, i))]
        + [pl.BlockSpec(grad.shape, lambda i: (0, 0)) for grad in grads]
        + [pl.BlockSpec((1, tile), lambda i: (0, i))],
        out_specs=pl.BlockSpec(
            (2, 2, 1, planes, shard, columns + PAD), lambda i: (0, 0, i // 2, i % 2, 0, 0)
        ),
        out_shape=jax.ShapeDtypeStruct((2, 2, 2, LINE, shard, columns + PAD), BF16),
        compiler_params=pltpu.CompilerParams(vmem_limit_bytes=VMEM_BYTES),
        cost_estimate=pl.CostEstimate(
            flops=rows * width * columns // 8,
            bytes_accessed=rows * width,
            transcendentals=0,
        ),
        name="qkv_grad",
    )(normed, *grads, gain_row)


def norm_back(value, gain, grad):
    scale = lax.rsqrt(jnp.mean(value * value, axis=-1, keepdims=True) + EPSILON)
    unit = value * scale
    grad_gain = jnp.sum(grad * unit, axis=0)
    scaled = grad * gain
    inner = jnp.mean(scaled * unit, axis=-1, keepdims=True)
    return scale * (scaled - unit * inner), grad_gain


def shards_plane(
    tokens,
    cotangent,
    positions,
    lengths,
    routes,
    logits,
    w_query,
    w_key,
    w_value,
    w_output,
    gain_attn,
    gain_ffn,
    w_in,
    w_out,
):
    seq = lax.axis_index("seq")
    data = lax.axis_index("dp")
    line, row_of, core = data // 4, (data // 2) % 2, data % 2
    tok_count, width = tokens.shape
    group_len = positions.shape[1]
    shard = w_query.shape[0]
    q_width = w_query.shape[1] // 2
    kv_width = w_key.shape[1] // 2
    kv_heads = kv_width // HDIM
    first_seq = seq == 0

    def ordered(mine, theirs, axis):
        low = jnp.where(first_seq, mine, theirs)
        high = jnp.where(first_seq, theirs, mine)
        return jnp.concatenate([low, high], axis=axis)

    def half_of(weights, which):
        half = weights.shape[1] // 2
        return lax.dynamic_slice_in_dim(weights, which * half, half, axis=1)

    def both_axes(value, pairs):
        return lax.ppermute(value, ("seq", "dp"), pairs)

    def device(s, d):
        return s * 4 * LINE + d

    straight, crossed = [], []
    for s in range(2):
        for d in range(4 * LINE):
            c = d % 2
            straight.append((device(s, d), device(c, d - c + s)))
            crossed.append((device(s, d), device(c, d - c + 1 - s)))
    crossed_back = [(there, here) for here, there in crossed]
    first_core = core == 0

    projections = (w_query, w_key, w_value)
    qkv_width = q_width + 2 * kv_width
    qkv_width = q_width + 2 * kv_width
    gain_columns = jnp.pad(jnp.stack([gain_attn, gain_ffn], axis=1), ((0, 0), (0, PAD - 2)))
    mine, theirs = [
        jnp.concatenate([half_of(w, which) for w in projections] + [gain_columns], axis=1)
        for which in (seq, 1 - seq)
    ]
    theirs = swap_seq(jnp.concatenate([theirs, w_output], axis=1))
    output_pair = ordered(w_output[None], theirs[None, :, qkv_width + PAD :], 0)
    block = ordered(mine, theirs[:, : qkv_width + PAD], 1)
    along = [block] + [swap_dp(block, 4 * step) for step in range(1, LINE)]
    places_of = jnp.stack([line, row_of, core]).astype(jnp.int32)

    in_own = w_in[0]
    half = in_own.shape[1] // 2
    sent = jnp.concatenate(
        [lax.dynamic_slice_in_dim(in_own, seq * half, half, axis=1), w_out[0].T], axis=1
    )
    same = both_axes(sent, straight)
    cross = both_axes(lax.dynamic_slice_in_dim(in_own, (1 - seq) * half, half, axis=1), crossed)
    same, cross, along = lax.optimization_barrier((same, cross, along))
    own_part = jnp.concatenate(
        [
            jnp.where(first_core, same[:, :half], cross),
            jnp.where(first_core, cross, same[:, :half]),
            same[:, half:],
        ],
        axis=1,
    )
    other_tokens = swap_seq(after(tokens, own_part))
    cut = width // 2
    lines = (line_up(own_part[:cut]), line_down(own_part[:cut]))
    qkv_rows = after(jnp.concatenate(along, axis=0), own_part)
    qkv_near, lines = lax.optimization_barrier((swap_y(qkv_rows), lines))
    late_part = after(own_part[cut:], lines)
    late_lines = (line_up(late_part), line_down(late_part))
    qkv_rows = jnp.concatenate([qkv_rows, qkv_near], axis=0)
    qkv_others = swap_core(qkv_rows)

    experts_all = 4 * LINE
    gates = jax.nn.softmax(logits, axis=-1)
    named = routes[:, :, None] == jnp.arange(experts_all, dtype=jnp.int32)[None, None, :]
    gate_table = jnp.sum(jnp.where(named, gates[:, :, None], 0.0), axis=1)
    gate_high = lax.reduce_precision(gate_table, 8, 7)
    grad_rows = jnp.concatenate(
        [
            cotangent,
            gate_high.astype(BF16),
            (gate_table - gate_high).astype(BF16),
            jnp.zeros((tok_count, PAD - 2 * experts_all), BF16),
        ],
        axis=1,
    )
    grad_near = near_pieces(grad_rows, after(grad_rows, other_tokens))
    lane = jnp.arange(PAD, dtype=jnp.int32)[:, None]
    hosted = jnp.repeat(
        jnp.array(SLOT_ORDER, jnp.int32) * 4 + 2 * row_of + seq, half, total_repeat_length=LINE * half
    )
    select = ((lane % experts_all == hosted[None, :]) & (lane < 2 * experts_all)).astype(BF16)

    places = positions[0]
    ends = jnp.cumsum(lengths[0])
    ranks = jnp.arange(group_len, dtype=jnp.int32)
    reached = ranks[:, None] >= ends[None, :]
    starts = jnp.max(jnp.where(reached, ends[None, :], 0), axis=1)
    local = (ranks - starts).astype(F32)
    freqs = jnp.power(THETA, -jnp.arange(HDIM // 2, dtype=F32) * 2.0 / HDIM)
    angles = local[:, None] * freqs[None, :]
    cos, sin = jnp.cos(angles), jnp.sin(angles)
    cos = jnp.concatenate([cos, cos, cos, cos], axis=1)
    sin = jnp.concatenate([-sin, sin, -sin, sin], axis=1)
    start_column = starts[:, None]
    own_places = lax.dynamic_slice_in_dim(places, seq * tok_count, tok_count)
    other_places = lax.dynamic_slice_in_dim(places, (1 - seq) * tok_count, tok_count)
    sort_own = (ranks[:, None] == own_places[None, :]).astype(BF16)
    sort_other = (ranks[:, None] == other_places[None, :]).astype(BF16)

    def to_order(own, other):
        return (
            contract(sort_own, own, 1, 0) + contract(sort_other, other, 1, 0)
        ).astype(BF16)

    def from_order(sort, values):
        return contract(sort, values, 0, 0).astype(BF16)

    x_sorted = to_order(tokens, other_tokens)
    x_sorted, late_lines = lax.optimization_barrier((x_sorted, late_lines))
    up_one = jnp.concatenate([lines[0], late_lines[0]], axis=0)
    down_one = jnp.concatenate([lines[1], late_lines[1]], axis=0)
    x_sorted, up_one, down_one = lax.optimization_barrier((x_sorted, up_one, down_one))
    up_two, down_two = line_up(up_one), line_down(down_one)
    normed, query, keys, values, w_qkv, gains = project(
        places_of, x_sorted, qkv_rows, qkv_others, cos, sin, q_width, kv_heads
    )
    gain_one, gain_two = gains[0], gains[1]
    output_full = lax.all_gather(after(output_pair, query), "dp", axis=1, tiled=True)
    output_full = output_full.reshape(width, width)
    mixed_sorted, levels = attend(
        query, keys, values, start_column, 0, q_width // (2 * HDIM)
    )
    mixed_sorted, grad_near = lax.optimization_barrier((mixed_sorted, grad_near))
    mixed_theirs = swap_seq(from_order(sort_other, mixed_sorted))
    mixed_mine = from_order(sort_own, mixed_sorted)
    grad_near = after(grad_near, mixed_theirs)
    grad_far = far_pieces(*grad_near)
    inputs = tokens.astype(F32)
    middle, normed_ffn, output_parts = mix(
        seq.astype(jnp.int32)[None], mixed_mine, mixed_theirs, tokens, gain_two[None, :], output_full
    )
    up_two, down_two = after((up_two, down_two), normed_ffn)
    up_three, down_three = line_up(up_two), line_down(down_two)
    row_near = near_pieces(normed_ffn, normed_ffn)
    row_far = far_pieces(*row_near)
    slots = [up_three, up_two, up_one, own_part, down_one, down_two, down_three]
    row_pieces = with_cores(normed_ffn, *row_near, *row_far)
    grad_pieces = with_cores(*after((grad_rows, *grad_near, *grad_far), row_near[0]))
    place = line.astype(jnp.int32)[None]
    far = run_experts(FAR_TILES, place, row_pieces, grad_pieces, slots, select, 0, ())
    far_back = over_cores(far[2], far[3]).astype(BF16)
    back_y, back_x = far_links(far_back)
    near = run_experts(
        NEAR_TILES, after(place, far_back), row_pieces, grad_pieces, slots, select, 4, far[4:]
    )
    hid_a, hid_b, du_a, du_b, all_rows, all_grads = near[4:]

    def weight_grads(rows, grads, grad_both, hidden):
        inner = contract(rows, grad_both, 0, 0)
        outer = contract(grads, hidden, 0, 0) * BRANCH_SCALE
        return [
            jnp.concatenate(
                [inner[:, 2 * half * i : 2 * half * (i + 1)], outer[:, half * i : half * (i + 1)]],
                axis=1,
            ).astype(BF16)
            for i in range(2)
        ]

    rows_early, grads_early, back_y, back_x = lax.optimization_barrier(
        (all_rows, all_grads, back_y, back_x)
    )
    outer_grads = weight_grads(rows_early, grads_early, du_a, hid_a)
    grads_of = dict(zip(SLOT_ORDER[:2], outer_grads))
    far_line = (line_up(outer_grads[1]), line_down(outer_grads[0]))
    near_back = over_cores(after(near[2], *outer_grads), near[3])
    first, second = near_links(near_back, back_y, back_x)
    rows_late, grads_late = after((all_rows, all_grads), first, second)
    inner_grads = weight_grads(rows_late, grads_late, du_b, hid_b)
    grads_of.update(zip(SLOT_ORDER[2:], inner_grads))
    first, second = swap_seq(first), swap_y(second)
    near_back = after(near_back, *inner_grads)
    grad_normed_ffn = own_sum(near_back, back_y, back_x, first, second)

    def line_partial(first, *rest):
        value = grads_of[first]
        for where, expert in enumerate(rest):
            value = jnp.where(line > where, grads_of[expert], value)
        return value.astype(F32)

    def line_step(step, arrived):
        up, down = arrived
        last = LINE - 1
        right = line_partial(*range(last - step, LINE)) + up.astype(F32)
        left = grads_of[step]
        for where in range(step):
            left = jnp.where(line < last - where, grads_of[step - 1 - where], left)
        left = left.astype(F32) + down.astype(F32)
        return right.astype(BF16), left.astype(BF16)

    grad_final = cotangent.astype(F32)
    grad_norm, grad_gain_two = norm_back(middle, gain_two, grad_normed_ffn)
    grad_middle = grad_final + grad_norm
    grad_attn = (BRANCH_SCALE * grad_middle).astype(BF16)
    grad_mixed = contract(grad_attn, output_parts[0], 1, 1).astype(BF16)
    grad_other = contract(grad_attn, output_parts[1], 1, 1).astype(BF16)
    grad_other = swap_seq(grad_other)
    grad_w_output = contract(ordered(mixed_mine, mixed_theirs, 1), grad_attn, 0, 0)
    far_f, far_f_other, near_f, near_f_other = after(
        (far[0], far[1], near[0], near[1]), grad_mixed
    )
    far_ffn = over_cores(far_f, far_f_other).astype(BF16)
    ffn_y, ffn_x = far_links(far_ffn)
    near_ffn = over_cores(near_f, near_f_other)
    right, left = line_step(1, far_line)
    grad_other = after(grad_other, right, left, far_ffn, grad_w_output)
    grad_sorted = to_order(grad_mixed, grad_other)
    mid_line = (line_up(right), line_down(left))
    grad_query, grad_keys, grad_values = attend_back(
        query,
        keys,
        values,
        grad_sorted,
        levels,
        start_column,
        cos,
        sin,
    )
    (grad_query, grad_keys, grad_values), mid_line, ffn_y, ffn_x = lax.optimization_barrier(
        ((grad_query, grad_keys, grad_values), mid_line, ffn_y, ffn_x)
    )
    right, left = line_step(2, mid_line)
    last_first = (line_up(right[:cut]), line_down(left[:cut]))
    first_ffn, second_ffn = near_links(near_ffn, ffn_y, ffn_x)
    first_ffn, second_ffn = swap_seq(first_ffn), swap_y(second_ffn)
    grads_qkv = after((grad_query, grad_keys, grad_values), right, left)
    wide = qkv_grad(normed, grads_qkv, grad_gain_two[None, :], shard)


    def chosen(value, which, axis):
        return lax.dynamic_index_in_dim(value, which, axis=axis, keepdims=False)

    summed_output = lax.psum_scatter(
        grad_w_output.astype(BF16), ("seq", "dp"), scatter_dimension=0, tiled=True
    )
    kept = chosen(wide, core, 0).astype(F32)
    kept = kept + swap_core(chosen(wide, 1 - core, 0)).astype(F32)
    grads_late = after(grads_qkv, kept)
    grad_normed, sent_normed = token_grad(
        grads_late, w_qkv, own_places[:, None], other_places[:, None]
    )
    kept, sent_normed = lax.optimization_barrier((kept, sent_normed))
    right_late, left_late = after((right[cut:], left[cut:]), last_first, sent_normed)
    last_late = (line_up(right_late), line_down(left_late))
    grad_normed = grad_normed.astype(F32) + swap_seq(sent_normed).astype(F32)
    scale = lax.rsqrt(jnp.mean(inputs * inputs, axis=-1, keepdims=True) + EPSILON)
    unit = inputs * scale
    scaled = grad_normed * gain_one
    inner = jnp.mean(scaled * unit, axis=-1, keepdims=True)
    grad_tokens = grad_middle + scale * (scaled - unit * inner)
    next_kept = chosen(kept, row_of, 0)
    next_kept = next_kept + swap_y(chosen(kept, 1 - row_of, 0).astype(BF16)).astype(F32)
    next_kept, last_first, last_late, summed_output = lax.optimization_barrier(
        (next_kept, last_first, last_late, summed_output)
    )
    own_grads = line_partial(*range(LINE))
    part_grads = jnp.concatenate(
        [
            own + up.astype(F32) + down.astype(F32)
            for own, (up, down) in ((own_grads[:cut], last_first), (own_grads[cut:], last_late))
        ],
        axis=0,
    ).astype(BF16)
    same_grads = jnp.where(first_core, part_grads[:, :half], part_grads[:, half : 2 * half])
    cross_grads = jnp.where(first_core, part_grads[:, half : 2 * half], part_grads[:, :half])
    same_grads = jnp.concatenate([same_grads, part_grads[:, 2 * half :]], axis=1)
    next_kept, same_grads, cross_grads = lax.optimization_barrier(
        (next_kept, same_grads, cross_grads)
    )
    same = both_axes(same_grads, straight)
    cross = both_axes(cross_grads, crossed_back)
    kept_half = chosen(next_kept, seq, 0)
    sent_half = swap_seq(chosen(next_kept, 1 - seq, 0).astype(BF16)).astype(F32)
    cuts = (q_width, q_width + kv_width, qkv_width)
    pieces = list(zip(jnp.split(kept_half, cuts, axis=2), jnp.split(sent_half, cuts, axis=2)))
    full = jnp.concatenate(
        [ordered(a, b, 2) for a, b in pieces[:3]] + [pieces[3][0] + pieces[3][1]], axis=2
    )
    low = full.astype(BF16)
    sent_lines = [
        swap_dp(chosen(low, line ^ step, 0), 4 * step) for step in range(1, LINE)
    ]
    first_ffn, second_ffn = after((first_ffn, second_ffn), low)
    ffn = own_sum(near_ffn, ffn_y, ffn_x, first_ffn, second_ffn)
    output = (middle + BRANCH_SCALE * ffn).astype(BF16)
    summed = chosen(full, line, 0) + sum(value.astype(F32) for value in sent_lines)
    grad_w_in = ordered(same[:, :half], cross, 1)
    grad_w_out = same[:, half:].T
    cuts = (2 * q_width, 2 * (q_width + kv_width), 2 * qkv_width)
    grad_projections = jnp.split(summed, cuts, axis=1)
    grad_gain_ffn = grad_projections[3][:, 0]
    grad_gain_attn = sum(
        jnp.sum(grad * weight.astype(F32), axis=1)
        for grad, weight in zip(grad_projections[:3], projections)
    ) / gain_attn.astype(F32)
    return (
        output,
        grad_tokens,
        grad_projections[0],
        grad_projections[1],
        grad_projections[2],
        summed_output.astype(F32),
        grad_gain_attn,
        grad_gain_ffn,
        grad_w_in.astype(F32)[None],
        grad_w_out.astype(F32)[None],
    )


def solution(mesh):
    placed = (
        P(("seq", "dp"), None),
        P(("seq", "dp"), None),
        P("dp", None),
        P("dp", None),
        P(("seq", "dp"), None),
        P(("seq", "dp"), None),
        P(("seq", "dp"), None),
        P(("seq", "dp"), None),
        P(("seq", "dp"), None),
        P(("seq", "dp"), None),
        P(("seq", "dp")),
        P(("seq", "dp")),
        P("dp", None, "seq"),
        P("dp", "seq", None),
    )
    return jax.shard_map(
        shards_plane if in_planes(mesh) else shards_general,
        mesh=mesh,
        in_specs=placed,
        out_specs=(
            P(("seq", "dp"), None),
            P(("seq", "dp"), None),
            P(("seq", "dp"), None),
            P(("seq", "dp"), None),
            P(("seq", "dp"), None),
            P(("seq", "dp"), None),
            P(("seq", "dp")),
            P(("seq", "dp")),
            P("dp", None, "seq"),
            P("dp", "seq", None),
        ),
        check_vma=False,
    )
```

```python
import functools

import jax
import jax.numpy as jnp
from jax import lax
from jax.experimental import pallas as pl
from jax.experimental.pallas import tpu as pltpu
from jax.sharding import PartitionSpec as P

QHEADS = 24
KVHEADS = 8
HDIM = 64
FF = 512
TOP = 8


EPSILON = 1e-06
BRANCH_SCALE = 0.22
SCORE_SCALE = 1.0 / 64.0
THETA = 10000.0


def rms_norm(value, gain):
    return value * lax.rsqrt(jnp.mean(value * value, axis=-1, keepdims=True) + EPSILON) * gain


def local_places(placing, seq_lengths):
    ends = jnp.cumsum(seq_lengths)
    segment = jnp.sum((placing[:, None] >= ends[None, :]).astype(jnp.int32), axis=1)
    starts = ends - seq_lengths
    member = segment[:, None] == jnp.arange(seq_lengths.shape[0], dtype=jnp.int32)[None, :]
    start_of = jnp.sum(jnp.where(member, starts[None, :], 0), axis=1)
    return (segment, placing - start_of)


def rotate(values, place, direction):
    half = values.shape[-1] // 2
    freqs = jnp.power(THETA, -jnp.arange(half, dtype=jnp.float32) * 2.0 / values.shape[-1])
    angles = place.astype(jnp.float32)[:, None] * freqs[None, :]
    cosine = jnp.cos(angles)[:, None, :]
    sine = direction * jnp.sin(angles)[:, None, :]
    first = values[..., :half]
    second = values[..., half:]
    return jnp.concatenate(
        [first * cosine - second * sine, second * cosine + first * sine], axis=-1
    )


def shards_general(
    tokens,
    cotangent,
    positions,
    lengths,
    routes,
    logits,
    w_query,
    w_key,
    w_value,
    w_output,
    gain_attn,
    gain_ffn,
    w_in,
    w_out,
):
    seq_count = lax.axis_size("seq")
    data_count = lax.axis_size("dp")
    tok_count = tokens.shape[0]
    group_len = positions.shape[1]
    local_experts = w_in.shape[0]
    experts_all = local_experts * data_count
    capacity = min(tok_count, 5 * tok_count * TOP // (4 * experts_all))
    heads_local = QHEADS // seq_count
    kv_local = KVHEADS // seq_count
    ratio = QHEADS // KVHEADS
    width = tokens.shape[1]
    query_full, key_full, value_full, output_full, gain_one, gain_two = (
        lax.all_gather(w_query, ("seq", "dp"), axis=0, tiled=True),
        lax.all_gather(w_key, ("seq", "dp"), axis=0, tiled=True),
        lax.all_gather(w_value, ("seq", "dp"), axis=0, tiled=True),
        lax.all_gather(w_output, ("seq", "dp"), axis=0, tiled=True),
        lax.all_gather(gain_attn, ("seq", "dp"), axis=0, tiled=True),
        lax.all_gather(gain_ffn, ("seq", "dp"), axis=0, tiled=True),
    )
    in_full, out_full = (
        lax.all_gather(w_in, "seq", axis=2, tiled=True),
        lax.all_gather(w_out, "seq", axis=1, tiled=True),
    )
    gain_one = gain_one.astype(jnp.float32)
    gain_two = gain_two.astype(jnp.float32)
    segment, place = local_places(positions[0], lengths[0])
    my_start = lax.axis_index("seq") * tok_count
    my_place = lax.dynamic_slice_in_dim(place, my_start, tok_count)
    inputs = tokens.astype(jnp.float32)
    normed = rms_norm(inputs, gain_one).astype(jnp.bfloat16)
    query_pre = jnp.dot(normed, query_full, preferred_element_type=jnp.float32)
    key_pre = jnp.dot(normed, key_full, preferred_element_type=jnp.float32)
    query_rot = (
        rotate(query_pre.reshape(tok_count, QHEADS, HDIM), my_place, 1.0)
        .reshape(tok_count, QHEADS * HDIM)
        .astype(jnp.bfloat16)
    )
    key_rot = (
        rotate(key_pre.reshape(tok_count, KVHEADS, HDIM), my_place, 1.0)
        .reshape(tok_count, KVHEADS * HDIM)
        .astype(jnp.bfloat16)
    )
    value_low = jnp.dot(normed, value_full, preferred_element_type=jnp.float32).astype(jnp.bfloat16)
    query_heads, key_heads, value_heads = (
        lax.all_to_all(query_rot, "seq", split_axis=1, concat_axis=0, tiled=True),
        lax.all_to_all(key_rot, "seq", split_axis=1, concat_axis=0, tiled=True),
        lax.all_to_all(value_low, "seq", split_axis=1, concat_axis=0, tiled=True),
    )
    keys_three = key_heads.reshape(group_len, kv_local, HDIM)
    values_three = value_heads.reshape(group_len, kv_local, HDIM)
    length = min(512, group_len)
    count = group_len // length

    def scores_of(query_block, seg_block, place_block):
        grouped = query_block.reshape(length, kv_local, ratio, HDIM)
        raw_scores = (
            jnp.einsum("qgrd,kgd->grqk", grouped, keys_three, preferred_element_type=jnp.float32)
            * SCORE_SCALE
        )
        allowed = (seg_block[:, None] == segment[None, :]) & (
            place[None, :] <= place_block[:, None]
        )
        return jnp.where(allowed[None, None], raw_scores, -1e30)

    def forward_block(pieces):
        query_block, seg_block, place_block = pieces
        scores = scores_of(query_block, seg_block, place_block)
        highest = jnp.max(scores, axis=-1, keepdims=True)
        expon = jnp.exp(scores - highest)
        totals = jnp.sum(expon, axis=-1, keepdims=True)
        probs = expon / totals
        mixed = jnp.einsum(
            "grqk,kgd->qgrd",
            probs.astype(jnp.bfloat16),
            values_three,
            preferred_element_type=jnp.float32,
        )
        return (
            mixed.reshape(length, heads_local * HDIM).astype(jnp.bfloat16),
            highest + jnp.log(totals),
            probs,
        )

    query_blocks = query_heads.reshape(count, length, heads_local * HDIM)
    seg_blocks = segment.reshape(count, length)
    place_blocks = place.reshape(count, length)
    block_args = (query_blocks, seg_blocks, place_blocks)

    def forward_light(pieces):
        mixed, lse_part, unused_probs = forward_block(pieces)
        return (mixed, lse_part)

    mixed_blocks, lse_blocks = lax.map(forward_light, block_args)
    mixed_heads = mixed_blocks.reshape(group_len, heads_local * HDIM)
    mixed_tokens = lax.all_to_all(mixed_heads, "seq", split_axis=0, concat_axis=1, tiled=True)
    attn = jnp.dot(mixed_tokens, output_full, preferred_element_type=jnp.float32)
    middle = inputs + BRANCH_SCALE * attn
    normed_ffn = rms_norm(middle, gain_two).astype(jnp.bfloat16)
    chosen = routes.reshape(-1)
    onehot = (chosen[:, None] == jnp.arange(experts_all, dtype=jnp.int32)[None, :]).astype(
        jnp.int32
    )
    ranking = jnp.sum(jnp.cumsum(onehot, axis=0) * onehot, axis=1) - 1
    target = chosen * capacity + ranking
    token_of = jnp.arange(tok_count * TOP, dtype=jnp.int32) // TOP
    gates = jax.nn.softmax(logits, axis=-1)
    source = jnp.full((experts_all * capacity,), tok_count, jnp.int32).at[target].set(token_of)
    slot_gate = jnp.zeros((experts_all * capacity,), jnp.float32).at[target].set(gates.reshape(-1))
    padded = jnp.concatenate([normed_ffn, jnp.zeros((1, width), jnp.bfloat16)], axis=0)
    outgoing = padded[source].reshape(data_count, local_experts * capacity, width)

    def expert_layout(arrived):
        return jnp.swapaxes(
            arrived.reshape(data_count, local_experts, capacity, width), 0, 1
        ).reshape(local_experts, data_count * capacity, width)

    def home_layout(values):
        return jnp.swapaxes(
            values.reshape(local_experts, data_count, capacity, width), 0, 1
        ).reshape(data_count, local_experts * capacity, width)

    def expert_forward(expert_rows):
        both = jnp.einsum("erd,edf->erf", expert_rows, in_full, preferred_element_type=jnp.float32)
        hidden = (jax.nn.silu(both[..., :FF]) * both[..., FF:]).astype(jnp.bfloat16)
        return (both, hidden)

    expert_rows = expert_layout(
        lax.all_to_all(outgoing, "dp", split_axis=0, concat_axis=0, tiled=True)
    )
    both, hidden = expert_forward(expert_rows)
    result = jnp.einsum(
        "erf,efd->erd", hidden, out_full, preferred_element_type=jnp.float32
    ).astype(jnp.bfloat16)
    returned = lax.all_to_all(
        home_layout(result), "dp", split_axis=0, concat_axis=0, tiled=True
    ).reshape(experts_all * capacity, width)
    picked = returned[target].reshape(tok_count, TOP, width).astype(jnp.float32)
    ffn = jnp.sum(picked * gates[:, :, None], axis=1)
    final = middle + BRANCH_SCALE * ffn
    output = final.astype(jnp.bfloat16)
    grad_final = cotangent.astype(jnp.float32)
    padded_grad = jnp.concatenate(
        [BRANCH_SCALE * grad_final, jnp.zeros((1, width), jnp.float32)], axis=0
    )
    grad_slots = (slot_gate[:, None] * padded_grad[source]).astype(jnp.bfloat16)
    grad_result = expert_layout(
        lax.all_to_all(
            grad_slots.reshape(data_count, local_experts * capacity, width),
            "dp",
            split_axis=0,
            concat_axis=0,
            tiled=True,
        )
    )
    rows_back = expert_layout(
        lax.all_to_all(outgoing, "dp", split_axis=0, concat_axis=0, tiled=True)
    )
    both_back, hidden_back = expert_forward(rows_back)
    grad_hidden = jnp.einsum(
        "erd,efd->erf", grad_result, out_full, preferred_element_type=jnp.float32
    )
    gate_part = both_back[..., :FF]
    up_part = both_back[..., FF:]
    sigma = jax.nn.sigmoid(gate_part)
    grad_gate = grad_hidden * up_part * sigma * (1.0 + gate_part * (1.0 - sigma))
    grad_up = grad_hidden * gate_part * sigma
    grad_both = jnp.concatenate([grad_gate, grad_up], axis=-1).astype(jnp.bfloat16)
    grad_out_local = jnp.einsum(
        "erf,erd->efd", hidden_back, grad_result, preferred_element_type=jnp.float32
    )
    grad_in_local = jnp.einsum(
        "erd,erf->edf", rows_back, grad_both, preferred_element_type=jnp.float32
    )
    grad_rows = jnp.einsum(
        "erf,edf->erd", grad_both, in_full, preferred_element_type=jnp.float32
    ).astype(jnp.bfloat16)
    grad_home = lax.all_to_all(
        home_layout(grad_rows), "dp", split_axis=0, concat_axis=0, tiled=True
    ).reshape(experts_all * capacity, width)
    grad_normed_ffn = jnp.sum(
        grad_home[target].reshape(tok_count, TOP, width).astype(jnp.float32), axis=1
    )
    grad_w_in, grad_w_out = (
        lax.psum_scatter(
            grad_in_local.astype(jnp.bfloat16), "seq", scatter_dimension=2, tiled=True
        ).astype(jnp.float32),
        lax.psum_scatter(
            grad_out_local.astype(jnp.bfloat16), "seq", scatter_dimension=1, tiled=True
        ).astype(jnp.float32),
    )
    unused_norm, norm_pull = jax.vjp(rms_norm, middle, gain_two)
    grad_middle_norm, grad_gain_two = norm_pull(grad_normed_ffn)
    grad_middle = grad_final + grad_middle_norm
    grad_attn = (BRANCH_SCALE * grad_middle).astype(jnp.bfloat16)
    grad_w_output = jnp.einsum(
        "te,td->ed", mixed_tokens, grad_attn, preferred_element_type=jnp.float32
    )
    grad_mixed = jnp.einsum(
        "td,ed->te", grad_attn, output_full, preferred_element_type=jnp.float32
    ).astype(jnp.bfloat16)
    grad_mixed_heads = lax.all_to_all(grad_mixed, "seq", split_axis=1, concat_axis=0, tiled=True)
    grad_blocks = grad_mixed_heads.reshape(count, length, heads_local * HDIM)
    back_args = (query_blocks, seg_blocks, place_blocks, lse_blocks, grad_blocks)

    def backward_block(carry, pieces):
        grad_keys, grad_values = carry
        query_block, seg_block, place_block, lse_block, grad_block = pieces[:5]
        probs = jnp.exp(scores_of(query_block, seg_block, place_block) - lse_block)
        grad_out = grad_block.reshape(length, kv_local, ratio, HDIM)
        grad_probs = jnp.einsum(
            "qgrd,kgd->grqk", grad_out, values_three, preferred_element_type=jnp.float32
        )
        grad_scores = (
            probs * (grad_probs - jnp.sum(probs * grad_probs, axis=-1, keepdims=True))
        ).astype(jnp.bfloat16)
        grad_query = SCORE_SCALE * jnp.einsum(
            "grqk,kgd->qgrd", grad_scores, keys_three, preferred_element_type=jnp.float32
        )
        grouped = query_block.reshape(length, kv_local, ratio, HDIM)
        grad_keys = grad_keys + SCORE_SCALE * jnp.einsum(
            "grqk,qgrd->kgd", grad_scores, grouped, preferred_element_type=jnp.float32
        )
        grad_values = grad_values + jnp.einsum(
            "grqk,qgrd->kgd",
            probs.astype(jnp.bfloat16),
            grad_out,
            preferred_element_type=jnp.float32,
        )
        return (
            (grad_keys, grad_values),
            grad_query.reshape(length, heads_local * HDIM).astype(jnp.bfloat16),
        )

    empty_keys = jnp.zeros((group_len, kv_local, HDIM), jnp.float32)
    (grad_keys, grad_values), grad_query_blocks = lax.scan(
        backward_block, (empty_keys, empty_keys), back_args
    )
    grad_query_heads = grad_query_blocks.reshape(group_len, heads_local * HDIM)
    grad_key_heads = grad_keys.reshape(group_len, kv_local * HDIM).astype(jnp.bfloat16)
    grad_value_heads = grad_values.reshape(group_len, kv_local * HDIM).astype(jnp.bfloat16)
    grad_query_tok, grad_key_tok, grad_value_tok = (
        lax.all_to_all(grad_query_heads, "seq", split_axis=0, concat_axis=1, tiled=True),
        lax.all_to_all(grad_key_heads, "seq", split_axis=0, concat_axis=1, tiled=True),
        lax.all_to_all(grad_value_heads, "seq", split_axis=0, concat_axis=1, tiled=True),
    )
    grad_query_pre = (
        rotate(grad_query_tok.astype(jnp.float32).reshape(tok_count, QHEADS, HDIM), my_place, -1.0)
        .reshape(tok_count, QHEADS * HDIM)
        .astype(jnp.bfloat16)
    )
    grad_key_pre = (
        rotate(grad_key_tok.astype(jnp.float32).reshape(tok_count, KVHEADS, HDIM), my_place, -1.0)
        .reshape(tok_count, KVHEADS * HDIM)
        .astype(jnp.bfloat16)
    )
    grad_w_query = jnp.einsum(
        "td,te->de", normed, grad_query_pre, preferred_element_type=jnp.float32
    )
    grad_w_key = jnp.einsum("td,te->de", normed, grad_key_pre, preferred_element_type=jnp.float32)
    grad_w_value = jnp.einsum(
        "td,te->de", normed, grad_value_tok, preferred_element_type=jnp.float32
    )
    grad_normed = jnp.einsum(
        "te,de->td", grad_query_pre, query_full, preferred_element_type=jnp.float32
    )
    grad_normed = grad_normed + jnp.einsum(
        "te,de->td", grad_key_pre, key_full, preferred_element_type=jnp.float32
    )
    grad_normed = grad_normed + jnp.einsum(
        "te,de->td", grad_value_tok, value_full, preferred_element_type=jnp.float32
    )
    unused_first, first_pull = jax.vjp(rms_norm, inputs, gain_one)
    grad_inputs_norm, grad_gain_one = first_pull(grad_normed)
    grad_tokens = grad_middle + grad_inputs_norm
    summed = (
        lax.psum_scatter(grad_w_query, ("seq", "dp"), scatter_dimension=0, tiled=True),
        lax.psum_scatter(grad_w_key, ("seq", "dp"), scatter_dimension=0, tiled=True),
        lax.psum_scatter(grad_w_value, ("seq", "dp"), scatter_dimension=0, tiled=True),
        lax.psum_scatter(grad_w_output, ("seq", "dp"), scatter_dimension=0, tiled=True),
        lax.psum_scatter(grad_gain_one, ("seq", "dp"), scatter_dimension=0, tiled=True),
        lax.psum_scatter(grad_gain_two, ("seq", "dp"), scatter_dimension=0, tiled=True),
    )
    return (
        output,
        grad_tokens,
        summed[0],
        summed[1],
        summed[2],
        summed[3],
        summed[4],
        summed[5],
        grad_w_in,
        grad_w_out,
    )


BF16 = jnp.bfloat16
F32 = jnp.float32
LINE = 4
PAD = 128
VMEM_BYTES = 60 * 1024 * 1024


def in_planes(mesh):
    return mesh.shape["seq"] == 2 and mesh.shape["dp"] == 4 * LINE


def swap_seq(value):
    return lax.ppermute(value, "seq", [(0, 1), (1, 0)])


def swap_dp(value, mask):
    return lax.ppermute(value, "dp", [(i, i ^ mask) for i in range(4 * LINE)])


def swap_core(value):
    return swap_dp(value, 1)


def swap_y(value):
    return swap_dp(value, 2)


def line_up(value):
    return lax.ppermute(value, "dp", [(i, i + 4) for i in range(4 * LINE - 4)])


def line_down(value):
    return lax.ppermute(value, "dp", [(i, i - 4) for i in range(4, 4 * LINE)])


def after(value, *others):
    return lax.optimization_barrier((value,) + others)[0]


def line_scatter(take, place):
    up = down = None
    for step in range(LINE - 1):
        far = jnp.minimum(LINE - 1 - step + place, LINE - 1)
        near = jnp.maximum(step - LINE + 1 + place, 0)
        right, left = take(far), take(near)
        if up is not None:
            right = right + up.astype(F32)
            left = left + down.astype(F32)
        up = line_up(right.astype(BF16))
        down = line_down(left.astype(BF16))
    return take(place) + up.astype(F32) + down.astype(F32)


def near_pieces(own, own_x):
    return swap_seq(own_x), swap_y(own)


def far_pieces(near_x, near_y):
    half = near_x.shape[0] // 2
    return swap_y(near_x[:half]), swap_seq(near_y[half:])


def with_cores(*pieces):
    return pieces + tuple(swap_core(piece) for piece in pieces)


def over_cores(mine, others):
    return mine.astype(F32) + swap_core(others).astype(F32)


def far_links(far):
    half = far.shape[0] // 2
    return swap_y(far[:half]), swap_seq(far[half:])


def near_links(near, from_y, from_x):
    half = from_y.shape[0] // 2
    first = (near[:half] + from_y[half:].astype(F32)).astype(BF16)
    second = (near[half : 2 * half] + from_x[half:].astype(F32)).astype(BF16)
    return first, second


def own_sum(near, from_y, from_x, first, second):
    half = from_y.shape[0] // 2
    low = near[2 * half : 3 * half] + from_y[:half].astype(F32) + first.astype(F32)
    high = near[3 * half :] + from_x[:half].astype(F32) + second.astype(F32)
    return jnp.concatenate([low, high], axis=0)


def turned(values, cos, sin, direction):
    lanes = values.shape[1]
    place = lax.broadcasted_iota(jnp.int32, values.shape, 1) % HDIM
    swapped = jnp.where(
        place < HDIM // 2,
        pltpu.roll(values, lanes - HDIM // 2, 1),
        pltpu.roll(values, HDIM // 2, 1),
    )
    times = lanes // cos.shape[1]
    cos = jnp.concatenate([cos] * times, axis=1)
    sin = jnp.concatenate([sin] * times, axis=1)
    if direction > 0:
        return values * cos + swapped * sin
    return values * cos - swapped * sin


def place_shards(place_ref, own_ref, other_ref, shard, store):
    for core in range(2):
        source = other_ref if core else own_ref
        for row in range(2):
            for line in range(LINE):
                index = (place_ref[0] ^ line) * 4 + (place_ref[1] ^ row) * 2 + (place_ref[2] ^ core)
                store(source, (row * LINE + line) * shard, pl.multiple_of(index * shard, shard))


def qkv_kernel(
    place_ref, x_ref, own_ref, other_ref, cos_ref, sin_ref,
    h_ref, q_ref, k_ref, v_ref, w_ref, gain_ref, columns_buf,
):
    q_width, kv_heads = q_ref.shape[1], k_ref.shape[0]
    kv_width = kv_heads * HDIM
    width, columns = w_ref.shape
    shard = own_ref.shape[0] // (2 * LINE)

    @pl.when(pl.program_id(0) == 0)
    def _():
        def store(source, low, place):
            for seq in range(2):
                first = seq * (columns + PAD)
                rows = pl.ds(pl.multiple_of(place + seq * (width // 2), shard), shard)
                w_ref[rows, :] = source[low : low + shard, first : first + columns]
                columns_buf[rows, :] = source[
                    low : low + shard, first + columns : first + columns + PAD
                ].astype(F32)

        place_shards(place_ref, own_ref, other_ref, shard, store)
        gain_ref[...] = columns_buf[...].T[: gain_ref.shape[0]]

    value = x_ref[...].astype(F32)
    scale = lax.rsqrt(jnp.mean(value * value, axis=-1, keepdims=True) + EPSILON)
    normed = (value * scale * gain_ref[0:1, :]).astype(BF16)
    h_ref[...] = normed
    both = jnp.dot(normed, w_ref[...], preferred_element_type=F32)
    spun = turned(both[:, : q_width + kv_width], cos_ref[...], sin_ref[...], 1)
    q_ref[...] = (spun[:, :q_width] * SCORE_SCALE).astype(BF16)
    for head in range(kv_heads):
        low = q_width + head * HDIM
        k_ref[head] = spun[:, low : low + HDIM].astype(BF16)
        low = low + kv_width
        v_ref[head] = both[:, low : low + HDIM].astype(BF16)


def project(places, x_sorted, own, other, cos, sin, q_width, kv_heads):
    rows, width = x_sorted.shape
    tile = 256
    columns = q_width + 2 * kv_heads * HDIM

    def row_block(lanes):
        return pl.BlockSpec((tile, lanes), lambda i, p: (i, 0))

    def whole(shape):
        return pl.BlockSpec(shape, lambda i, p: (0, 0))

    heads = pl.BlockSpec((kv_heads, tile, HDIM), lambda i, p: (0, i, 0))
    return pl.pallas_call(
        qkv_kernel,
        grid_spec=pltpu.PrefetchScalarGridSpec(
            num_scalar_prefetch=1,
            grid=(rows // tile,),
            in_specs=[
                row_block(width),
                whole(own.shape),
                whole(other.shape),
                row_block(cos.shape[1]),
                row_block(cos.shape[1]),
            ],
            out_specs=[
                row_block(width), row_block(q_width), heads, heads,
                whole((width, columns)), whole((8, width)),
            ],
            scratch_shapes=[pltpu.VMEM((width, PAD), F32)],
        ),
        out_shape=[
            jax.ShapeDtypeStruct((rows, width), BF16),
            jax.ShapeDtypeStruct((rows, q_width), BF16),
            jax.ShapeDtypeStruct((kv_heads, rows, HDIM), BF16),
            jax.ShapeDtypeStruct((kv_heads, rows, HDIM), BF16),
            jax.ShapeDtypeStruct((width, columns), BF16),
            jax.ShapeDtypeStruct((8, width), F32),
        ],
        compiler_params=pltpu.CompilerParams(vmem_limit_bytes=VMEM_BYTES),
        cost_estimate=pl.CostEstimate(
            flops=rows * width * columns // 8,
            bytes_accessed=rows * width + width * columns,
            transcendentals=rows,
        ),
        name="project",
    )(places, x_sorted, own, other, cos, sin)


def mix_kernel(
    place_ref, mine_ref, theirs_ref, x_ref, gain_ref, own_ref, other_ref, m_ref, h_ref, parts_ref
):
    shard = own_ref.shape[0] // (2 * LINE)
    width = parts_ref.shape[2]

    @pl.when(pl.program_id(0) == 0)
    def _():
        for seq in range(2):

            def store(source, low, place):
                parts_ref[place_ref[3] ^ seq, pl.ds(place, shard), :] = source[
                    low : low + shard, seq * width : (seq + 1) * width
                ]

            place_shards(place_ref, own_ref, other_ref, shard, store)

    mixed = jnp.dot(mine_ref[...], parts_ref[0], preferred_element_type=F32)
    mixed = mixed + jnp.dot(theirs_ref[...], parts_ref[1], preferred_element_type=F32)
    value = x_ref[...].astype(F32) + BRANCH_SCALE * mixed
    m_ref[...] = value
    scale = lax.rsqrt(jnp.mean(value * value, axis=-1, keepdims=True) + EPSILON)
    h_ref[...] = (value * scale * gain_ref[1:2, :]).astype(BF16)


def mix(places, mine, theirs, tokens, gains, own, other):
    rows, width = tokens.shape
    half = mine.shape[1]
    tile = 256

    def row_block(lanes):
        return pl.BlockSpec((tile, lanes), lambda i, p: (i, 0))

    def whole(shape):
        return pl.BlockSpec(shape, lambda i, p: (0,) * len(shape))

    return pl.pallas_call(
        mix_kernel,
        grid_spec=pltpu.PrefetchScalarGridSpec(
            num_scalar_prefetch=1,
            grid=(rows // tile,),
            in_specs=[
                row_block(half), row_block(half), row_block(width), whole(gains.shape),
                whole(own.shape), whole(other.shape),
            ],
            out_specs=[row_block(width), row_block(width), whole((2, half, width))],
        ),
        out_shape=[
            jax.ShapeDtypeStruct((rows, width), F32),
            jax.ShapeDtypeStruct((rows, width), BF16),
            jax.ShapeDtypeStruct((2, half, width), BF16),
        ],
        compiler_params=pltpu.CompilerParams(vmem_limit_bytes=VMEM_BYTES),
        cost_estimate=pl.CostEstimate(
            flops=rows * width * width // 8, bytes_accessed=rows * width, transcendentals=rows
        ),
        name="mix",
    )(places, mine, theirs, tokens, gains, own, other)


def token_grad_kernel(dq_ref, dk_ref, dv_ref, w_ref, own_ref, other_ref, mine_ref, sent_ref):
    q_width, kv_width = dq_ref.shape[1], dk_ref.shape[1]
    cuts = (0, q_width, q_width + kv_width, q_width + 2 * kv_width)
    grad = contract(dq_ref[...], w_ref[:, cuts[0] : cuts[1]], 1, 1)
    grad = grad + contract(dk_ref[...], w_ref[:, cuts[1] : cuts[2]], 1, 1)
    grad = (grad + contract(dv_ref[...], w_ref[:, cuts[2] : cuts[3]], 1, 1)).astype(BF16)
    for place_ref, out_ref in ((other_ref, sent_ref), (own_ref, mine_ref)):
        shape = (place_ref.shape[0], grad.shape[0])
        picked = lax.broadcasted_iota(jnp.int32, shape, 1) == place_ref[...]
        picked = jnp.where(picked, 1.0, 0.0).astype(BF16)
        out_ref[...] = jnp.dot(picked, grad, preferred_element_type=F32).astype(BF16)


def token_grad(grads, weights, own_places, other_places):
    rows, count = grads[0].shape[0], own_places.shape[0]
    width = weights.shape[0]
    columns = sum(grad.shape[1] for grad in grads)
    tile = width // 3

    def whole(array):
        return pl.BlockSpec(array.shape, lambda i: (0, 0))

    block = pl.BlockSpec((count, tile), lambda i: (0, i))
    return pl.pallas_call(
        token_grad_kernel,
        grid=(3,),
        in_specs=[whole(grad) for grad in grads]
        + [pl.BlockSpec((tile, columns), lambda i: (i, 0)), whole(own_places), whole(other_places)],
        out_specs=[block, block],
        out_shape=[jax.ShapeDtypeStruct((count, width), BF16)] * 2,
        compiler_params=pltpu.CompilerParams(vmem_limit_bytes=VMEM_BYTES),
        cost_estimate=pl.CostEstimate(
            flops=rows * width * columns // 8, bytes_accessed=rows * width, transcendentals=0
        ),
        name="token_grad",
    )(*grads, weights, own_places, other_places)


Q_TILE = 256


def windows(rows):
    longest = rows // 2
    for start in range(0, rows, Q_TILE):
        low = max(0, start - longest + 1) // Q_TILE * Q_TILE
        yield start, low, start + Q_TILE


def allowed_keys(start_ref, row, low, high):
    shape = (Q_TILE, high - low)
    rows = lax.broadcasted_iota(jnp.int32, shape, 0) + row
    keys = lax.broadcasted_iota(jnp.int32, shape, 1) + low
    return (keys <= rows) & (keys >= start_ref[row : row + Q_TILE, :])


def contract(left, right, left_dim, right_dim):
    return lax.dot_general(
        left, right, (((left_dim,), (right_dim,)), ((), ())), preferred_element_type=F32
    )


def masked_scores(query, keys, allowed):
    return jnp.where(allowed, contract(query, keys, 1, 1), -1e30)


def attend_kernel(base, q_ref, k_ref, v_ref, start_ref, o_ref, level_ref):
    pair = pl.program_id(0) + base
    ratio = QHEADS // KVHEADS
    for row, low, high in windows(q_ref.shape[0]):
        allowed = allowed_keys(start_ref, row, low, high)
        for side in range(2):
            head = (2 * pair + side) // ratio
            lanes = slice(side * HDIM, (side + 1) * HDIM)
            scores = masked_scores(
                q_ref[row : row + Q_TILE, lanes], k_ref[head, low:high, :], allowed
            )
            highest = jnp.max(scores, axis=-1, keepdims=True)
            expon = jnp.exp(scores - highest)
            total = jnp.sum(expon, axis=-1, keepdims=True)
            level_ref[0, row : row + Q_TILE, side : side + 1] = highest + jnp.log(total)
            probs = expon * (1.0 / total)
            mixed = contract(probs.astype(BF16), v_ref[head, low:high, :], 1, 0)
            o_ref[row : row + Q_TILE, lanes] = mixed.astype(BF16)


def attention_cost(rows, heads, products):
    area = sum(Q_TILE * (high - low) for _, low, high in windows(rows))
    return pl.CostEstimate(
        flops=products * heads * area * 16,
        bytes_accessed=8 * rows * heads * HDIM,
        transcendentals=heads * area,
    )


def attend(query, keys, values, starts, base, pairs):
    rows = query.shape[0]
    pair_block = pl.BlockSpec((rows, 2 * HDIM), lambda j: (0, j + base))
    whole = pl.BlockSpec(keys.shape, lambda j: (0, 0, 0))
    return pl.pallas_call(
        functools.partial(attend_kernel, base),
        grid=(pairs,),
        in_specs=[pair_block, whole, whole, pl.BlockSpec((rows, 1), lambda j: (0, 0))],
        out_specs=[
            pl.BlockSpec((rows, 2 * HDIM), lambda j: (0, j)),
            pl.BlockSpec((1, rows, 2), lambda j: (j, 0, 0)),
        ],
        out_shape=[
            jax.ShapeDtypeStruct((rows, pairs * 2 * HDIM), BF16),
            jax.ShapeDtypeStruct((pairs, rows, 2), F32),
        ],
        compiler_params=pltpu.CompilerParams(vmem_limit_bytes=VMEM_BYTES),
        cost_estimate=attention_cost(rows, 2 * pairs, 2),
        name="attend",
    )(query, keys, values, starts)


def attend_back_kernel(
    q_ref, k_ref, v_ref, d_ref, level_ref, start_ref, cos_ref, sin_ref,
    dq_ref, dk_ref, dv_ref, dk_sum, dv_sum,
):
    pair = pl.program_id(0)
    ratio = QHEADS // KVHEADS

    @pl.when(pair == 0)
    def _():
        dk_sum[...] = jnp.zeros_like(dk_sum)
        dv_sum[...] = jnp.zeros_like(dv_sum)

    for row, low, high in windows(q_ref.shape[0]):
        allowed = allowed_keys(start_ref, row, low, high)
        grads = []
        for side in range(2):
            head = (2 * pair + side) // ratio
            lanes = slice(side * HDIM, (side + 1) * HDIM)
            query = q_ref[row : row + Q_TILE, lanes]
            keys = k_ref[head, low:high, :]
            probs = jnp.exp(
                masked_scores(query, keys, allowed)
                - level_ref[0, row : row + Q_TILE, side : side + 1]
            )
            grad_out = d_ref[row : row + Q_TILE, lanes]
            grad_probs = contract(grad_out, v_ref[head, low:high, :], 1, 1)
            inner = jnp.sum(probs * grad_probs, axis=-1, keepdims=True)
            grad_scores = (probs * (grad_probs - inner)).astype(BF16)
            grads.append(contract(grad_scores, keys, 1, 0) * SCORE_SCALE)
            dk_sum[head, low:high, :] += contract(grad_scores, query, 0, 0)
            dv_sum[head, low:high, :] += contract(probs.astype(BF16), grad_out, 0, 0)
        grad_query = jnp.concatenate(grads, axis=1).astype(BF16).astype(F32)
        dq_ref[row : row + Q_TILE, :] = turned(
            grad_query,
            cos_ref[row : row + Q_TILE, :],
            sin_ref[row : row + Q_TILE, :],
            -1,
        ).astype(BF16)

    @pl.when(pair == pl.num_programs(0) - 1)
    def _():
        heads = range(dk_sum.shape[0])
        grad_keys = jnp.concatenate([dk_sum[head] for head in heads], axis=1)
        grad_keys = grad_keys.astype(BF16).astype(F32)
        dk_ref[...] = turned(grad_keys, cos_ref[...], sin_ref[...], -1).astype(BF16)
        dv_ref[...] = jnp.concatenate([dv_sum[head] for head in heads], axis=1).astype(BF16)


def attend_back(query, keys, values, grad_out, levels, starts, cos, sin):
    rows, lanes = query.shape
    pairs = lanes // (2 * HDIM)
    kv_heads = keys.shape[0]
    pair_block = pl.BlockSpec((rows, 2 * HDIM), lambda j: (0, j))
    whole = pl.BlockSpec(keys.shape, lambda j: (0, 0, 0))

    def fixed(lanes_of):
        return pl.BlockSpec((rows, lanes_of), lambda j: (0, 0))

    flat = kv_heads * HDIM
    return pl.pallas_call(
        attend_back_kernel,
        grid=(pairs,),
        in_specs=[
            pair_block, whole, whole, pair_block,
            pl.BlockSpec((1, rows, 2), lambda j: (j, 0, 0)), fixed(1), fixed(2 * HDIM), fixed(2 * HDIM),
        ],
        out_specs=[pair_block, fixed(flat), fixed(flat)],
        out_shape=[
            jax.ShapeDtypeStruct(query.shape, BF16),
            jax.ShapeDtypeStruct((rows, flat), BF16),
            jax.ShapeDtypeStruct((rows, flat), BF16),
        ],
        scratch_shapes=[pltpu.VMEM(keys.shape, F32), pltpu.VMEM(keys.shape, F32)],
        compiler_params=pltpu.CompilerParams(vmem_limit_bytes=VMEM_BYTES),
        cost_estimate=attention_cost(rows, 2 * pairs, 5),
        name="attend_back",
    )(query, keys, values, grad_out, levels, starts, cos, sin)


SLOTS = 2 * LINE - 1
SLOT_ORDER = (0, 3, 1, 2)
OWN, NEAR_X, NEAR_Y, FAR_Y, FAR_X = range(5)
FAR_TILES = (((NEAR_Y, 0), (FAR_Y, 0)), ((NEAR_X, 1), (FAR_X, 0)))
NEAR_TILES = (((NEAR_X, 0), (NEAR_Y, 1)), ((OWN, 0), (OWN, 1)))


def used_pieces(tiles):
    return sorted({piece for tile in tiles for piece, _ in tile})


def experts_kernel(tiles, half_rows, place_ref, *refs):
    used = used_pieces(tiles)
    sides = 2 * len(used)
    h_pieces, g_pieces, slots = refs[:sides], refs[sides : 2 * sides], refs[2 * sides : 2 * sides + SLOTS]
    select_ref = refs[2 * sides + SLOTS]
    (
        f_mine, f_other, d_mine, d_other, hid_a, hid_b, du_a, du_b, hcopy_ref, gcopy_ref,
        w_in, w_out, h_buf, g_buf, hidden, du_all, weight_sems, row_sems,
    ) = refs[-18:]
    width = h_buf.shape[2]
    half = slots[0].shape[1] // 3
    part = 2 * half
    step = pl.program_id(0)
    steps = 2 * len(tiles)

    def weight_copies(spot, slot):
        return (
            pltpu.make_async_copy(
                slots[slot].at[:, :part],
                w_in.at[:, spot * part : (spot + 1) * part],
                weight_sems.at[0, spot],
            ),
            pltpu.make_async_copy(
                slots[slot].at[:, part:],
                w_out.at[:, spot * half : (spot + 1) * half],
                weight_sems.at[1, spot],
            ),
        )

    def row_copies(number, buffer):
        side, tile = divmod(number, len(tiles))
        copies = []
        for spot, (piece, part_of) in enumerate(tiles[tile]):
            index = side * len(used) + used.index(piece)
            for kind, (pieces, held) in enumerate(((h_pieces, h_buf), (g_pieces, g_buf))):
                copies.append(
                    pltpu.make_async_copy(
                        pieces[index].at[pl.ds(part_of * half_rows, half_rows), :],
                        held.at[buffer, pl.ds(spot * half_rows, half_rows), :],
                        row_sems.at[buffer, 2 * kind + spot],
                    )
                )
        return copies

    def fetch(wanted, buffer):
        for number in range(steps):

            @pl.when(wanted == number)
            def _():
                for copy in row_copies(number, buffer):
                    copy.start()

    buffer = step % 2

    @pl.when(step == 0)
    def _():
        fetch(step, 0)
        for spot, expert in enumerate(SLOT_ORDER):
            for slot in range(expert, expert + LINE):

                @pl.when(slot == LINE - 1 + expert - place_ref[0])
                def _():
                    for copy in weight_copies(spot, slot):
                        copy.start()

        for spot in range(LINE):
            for copy in weight_copies(spot, LINE - 1):
                copy.wait()

    @pl.when(step + 1 < steps)
    def _():
        fetch(step + 1, 1 - buffer)

    for copy in row_copies(0, buffer):
        copy.wait()

    rows = h_buf[buffer]
    grads = g_buf[buffer, :, :width]
    hcopy_ref[...] = rows
    gcopy_ref[...] = grads
    gates = jnp.dot(g_buf[buffer, :, width:], select_ref[...], preferred_element_type=F32)
    for spot in range(LINE):
        units = slice(spot * half, (spot + 1) * half)
        both = jnp.dot(
            rows, w_in[:, spot * part : (spot + 1) * part], preferred_element_type=F32
        )
        back = jnp.dot(grads, w_out[:, units], preferred_element_type=F32)
        gate = gates[:, units]
        first, second = both[:, :half], both[:, half:]
        sigma = jax.nn.sigmoid(first)
        silu = first * sigma
        hidden[:, units] = (gate * (silu * second)).astype(BF16)
        back = back * (BRANCH_SCALE * gate)
        d_first = back * second * (sigma * (1.0 + first * (1.0 - sigma)))
        d_second = back * silu
        du_all[:, spot * part : spot * part + half] = d_first.astype(BF16)
        du_all[:, spot * part + half : (spot + 1) * part] = d_second.astype(BF16)
    hid_a[...] = hidden[:, : 2 * half]
    hid_b[...] = hidden[:, 2 * half :]
    du_a[...] = du_all[:, : 2 * part]
    du_b[...] = du_all[:, 2 * part :]
    ffn = contract(hidden[...], w_out[...], 1, 1).astype(BF16)
    back_rows = contract(du_all[...], w_in[...], 1, 1).astype(BF16)

    @pl.when(step < len(tiles))
    def _():
        f_mine[...] = ffn
        d_mine[...] = back_rows

    @pl.when(step >= len(tiles))
    def _():
        f_other[...] = ffn
        d_other[...] = back_rows


def run_experts(tiles, place, row_pieces, grad_pieces, slots, select, base, kept):
    used = used_pieces(tiles)
    sides = len(row_pieces) // 2
    wanted = used + [sides + piece for piece in used]
    rows = [row_pieces[piece] for piece in wanted]
    grads = [grad_pieces[piece] for piece in wanted]
    tile, width = row_pieces[OWN].shape
    wide = grad_pieces[OWN].shape[1]
    half = slots[0].shape[1] // 3
    part = 2 * half
    count = len(tiles)
    steps = 2 * count
    total = 8 * tile

    def late(lanes):
        return pl.BlockSpec((tile, lanes), lambda i, p: (i + base, 0))

    mine = pl.BlockSpec((tile, width), lambda i, p: (jnp.minimum(i, count - 1), 0))
    others = pl.BlockSpec((tile, width), lambda i, p: (jnp.maximum(i - count, 0), 0))
    anywhere = pl.BlockSpec(memory_space=pl.ANY)
    kept = list(kept)
    lead = 1 + 2 * len(wanted) + SLOTS + 1
    partial = jax.ShapeDtypeStruct((count * tile, width), BF16)
    lanes = [2 * half, 2 * half, 2 * part, 2 * part, width, width]
    return pl.pallas_call(
        functools.partial(experts_kernel, tiles, tile // 2),
        grid_spec=pltpu.PrefetchScalarGridSpec(
            num_scalar_prefetch=1,
            grid=(steps,),
            in_specs=[anywhere] * (2 * len(wanted) + SLOTS)
            + [pl.BlockSpec(select.shape, lambda i, p: (0, 0))]
            + [anywhere] * len(kept),
            out_specs=[mine, others, mine, others] + [late(n) for n in lanes],
            scratch_shapes=[
                pltpu.VMEM((width, LINE * part), BF16),
                pltpu.VMEM((width, LINE * half), BF16),
                pltpu.VMEM((2, tile, width), BF16),
                pltpu.VMEM((2, tile, wide), BF16),
                pltpu.VMEM((tile, LINE * half), BF16),
                pltpu.VMEM((tile, LINE * part), BF16),
                pltpu.SemaphoreType.DMA((2, LINE)),
                pltpu.SemaphoreType.DMA((2, 4)),
            ],
        ),
        out_shape=[partial] * 4 + [jax.ShapeDtypeStruct((total, n), BF16) for n in lanes],
        input_output_aliases={lead + i: 4 + i for i in range(len(kept))},
        compiler_params=pltpu.CompilerParams(vmem_limit_bytes=VMEM_BYTES),
        cost_estimate=pl.CostEstimate(
            flops=steps * tile * width * LINE * (part + half) // 4,
            bytes_accessed=2 * steps * tile * (6 * width + LINE * (part + half)),
            transcendentals=steps * tile * LINE * half,
        ),
        name="experts",
    )(place, *rows, *grads, *slots, select, *kept)


def qkv_grad_kernel(h_ref, dq_ref, dk_ref, dv_ref, gain_ref, o_ref):
    shard = o_ref.shape[-2]
    rows = h_ref[...]
    low = 0
    gains = jnp.broadcast_to(gain_ref[...], (PAD, gain_ref.shape[1])).T.astype(BF16)
    parts = [contract(rows, ref[...], 0, 0).astype(BF16) for ref in (dq_ref, dk_ref, dv_ref)]
    for part in parts + [gains]:
        for block in range(h_ref.shape[1] // shard):
            place = (block % 2, block // 2 % 2, 0, block // 4)
            o_ref[place + (slice(None), slice(low, low + part.shape[1]))] = part[
                block * shard : (block + 1) * shard
            ]
        low = low + part.shape[1]


def qkv_grad(normed, grads, gain_row, shard):
    rows, width = normed.shape
    columns = sum(grad.shape[1] for grad in grads)
    tile = width // 4
    planes = tile // (4 * shard)
    return pl.pallas_call(
        qkv_grad_kernel,
        grid=(4,),
        in_specs=[pl.BlockSpec((rows, tile), lambda i: (0, i))]
        + [pl.BlockSpec(grad.shape, lambda i: (0, 0)) for grad in grads]
        + [pl.BlockSpec((1, tile), lambda i: (0, i))],
        out_specs=pl.BlockSpec(
            (2, 2, 1, planes, shard, columns + PAD), lambda i: (0, 0, i // 2, i % 2, 0, 0)
        ),
        out_shape=jax.ShapeDtypeStruct((2, 2, 2, LINE, shard, columns + PAD), BF16),
        compiler_params=pltpu.CompilerParams(vmem_limit_bytes=VMEM_BYTES),
        cost_estimate=pl.CostEstimate(
            flops=rows * width * columns // 8,
            bytes_accessed=rows * width,
            transcendentals=0,
        ),
        name="qkv_grad",
    )(normed, *grads, gain_row)


def norm_back(value, gain, grad):
    scale = lax.rsqrt(jnp.mean(value * value, axis=-1, keepdims=True) + EPSILON)
    unit = value * scale
    grad_gain = jnp.sum(grad * unit, axis=0)
    scaled = grad * gain
    inner = jnp.mean(scaled * unit, axis=-1, keepdims=True)
    return scale * (scaled - unit * inner), grad_gain


def shards_plane(
    tokens,
    cotangent,
    positions,
    lengths,
    routes,
    logits,
    w_query,
    w_key,
    w_value,
    w_output,
    gain_attn,
    gain_ffn,
    w_in,
    w_out,
):
    seq = lax.axis_index("seq")
    data = lax.axis_index("dp")
    line, row_of, core = data // 4, (data // 2) % 2, data % 2
    tok_count, width = tokens.shape
    group_len = positions.shape[1]
    shard = w_query.shape[0]
    q_width = w_query.shape[1] // 2
    kv_width = w_key.shape[1] // 2
    kv_heads = kv_width // HDIM
    first_seq = seq == 0

    def ordered(mine, theirs, axis):
        low = jnp.where(first_seq, mine, theirs)
        high = jnp.where(first_seq, theirs, mine)
        return jnp.concatenate([low, high], axis=axis)

    def half_of(weights, which):
        half = weights.shape[1] // 2
        return lax.dynamic_slice_in_dim(weights, which * half, half, axis=1)

    def both_axes(value, pairs):
        return lax.ppermute(value, ("seq", "dp"), pairs)

    def device(s, d):
        return s * 4 * LINE + d

    straight, crossed = [], []
    for s in range(2):
        for d in range(4 * LINE):
            c = d % 2
            straight.append((device(s, d), device(c, d - c + s)))
            crossed.append((device(s, d), device(c, d - c + 1 - s)))
    crossed_back = [(there, here) for here, there in crossed]
    first_core = core == 0

    projections = (w_query, w_key, w_value)
    qkv_width = q_width + 2 * kv_width
    qkv_width = q_width + 2 * kv_width
    gain_columns = jnp.pad(jnp.stack([gain_attn, gain_ffn], axis=1), ((0, 0), (0, PAD - 2)))
    mine, theirs = [
        jnp.concatenate([half_of(w, which) for w in projections] + [gain_columns], axis=1)
        for which in (seq, 1 - seq)
    ]
    theirs = swap_seq(jnp.concatenate([theirs, w_output], axis=1))
    block = jnp.concatenate(
        [
            ordered(mine, theirs[:, : qkv_width + PAD], 1),
            ordered(w_output, theirs[:, qkv_width + PAD :], 1),
        ],
        axis=1,
    )
    along = [block] + [swap_dp(block, 4 * step) for step in range(1, LINE)]
    places_of = jnp.stack([line, row_of, core, seq]).astype(jnp.int32)

    in_own = w_in[0]
    half = in_own.shape[1] // 2
    sent = jnp.concatenate(
        [lax.dynamic_slice_in_dim(in_own, seq * half, half, axis=1), w_out[0].T], axis=1
    )
    same = both_axes(sent, straight)
    cross = both_axes(lax.dynamic_slice_in_dim(in_own, (1 - seq) * half, half, axis=1), crossed)
    same, cross, along = lax.optimization_barrier((same, cross, along))
    own_part = jnp.concatenate(
        [
            jnp.where(first_core, same[:, :half], cross),
            jnp.where(first_core, cross, same[:, :half]),
            same[:, half:],
        ],
        axis=1,
    )
    other_tokens = swap_seq(after(tokens, own_part))
    cut = width // 2
    lines = (line_up(own_part[:cut]), line_down(own_part[:cut]))
    split = 2 * (qkv_width + PAD)
    qkv_rows = after(jnp.concatenate([piece[:, :split] for piece in along], axis=0), own_part)
    qkv_near, lines = lax.optimization_barrier((swap_y(qkv_rows), lines))
    late_part = after(own_part[cut:], lines)
    late_lines = (line_up(late_part), line_down(late_part))
    qkv_rows = jnp.concatenate([qkv_rows, qkv_near], axis=0)
    qkv_others = swap_core(qkv_rows)

    experts_all = 4 * LINE
    gates = jax.nn.softmax(logits, axis=-1)
    named = routes[:, :, None] == jnp.arange(experts_all, dtype=jnp.int32)[None, None, :]
    gate_table = jnp.sum(jnp.where(named, gates[:, :, None], 0.0), axis=1)
    gate_high = lax.reduce_precision(gate_table, 8, 7)
    grad_rows = jnp.concatenate(
        [
            cotangent,
            gate_high.astype(BF16),
            (gate_table - gate_high).astype(BF16),
            jnp.zeros((tok_count, PAD - 2 * experts_all), BF16),
        ],
        axis=1,
    )
    grad_near = near_pieces(grad_rows, after(grad_rows, other_tokens))
    lane = jnp.arange(PAD, dtype=jnp.int32)[:, None]
    hosted = jnp.repeat(
        jnp.array(SLOT_ORDER, jnp.int32) * 4 + 2 * row_of + seq, half, total_repeat_length=LINE * half
    )
    select = ((lane % experts_all == hosted[None, :]) & (lane < 2 * experts_all)).astype(BF16)

    places = positions[0]
    ends = jnp.cumsum(lengths[0])
    ranks = jnp.arange(group_len, dtype=jnp.int32)
    reached = ranks[:, None] >= ends[None, :]
    starts = jnp.max(jnp.where(reached, ends[None, :], 0), axis=1)
    local = (ranks - starts).astype(F32)
    freqs = jnp.power(THETA, -jnp.arange(HDIM // 2, dtype=F32) * 2.0 / HDIM)
    angles = local[:, None] * freqs[None, :]
    cos, sin = jnp.cos(angles), jnp.sin(angles)
    cos = jnp.concatenate([cos, cos, cos, cos], axis=1)
    sin = jnp.concatenate([-sin, sin, -sin, sin], axis=1)
    start_column = starts[:, None]
    own_places = lax.dynamic_slice_in_dim(places, seq * tok_count, tok_count)
    other_places = lax.dynamic_slice_in_dim(places, (1 - seq) * tok_count, tok_count)
    sort_own = (ranks[:, None] == own_places[None, :]).astype(BF16)
    sort_other = (ranks[:, None] == other_places[None, :]).astype(BF16)

    def to_order(own, other):
        return (
            contract(sort_own, own, 1, 0) + contract(sort_other, other, 1, 0)
        ).astype(BF16)

    def from_order(sort, values):
        return contract(sort, values, 0, 0).astype(BF16)

    x_sorted = to_order(tokens, other_tokens)
    normed, query, keys, values, w_qkv, gains = project(
        places_of, x_sorted, qkv_rows, qkv_others, cos, sin, q_width, kv_heads
    )
    gain_one, gain_two = gains[0], gains[1]
    output_rows = after(jnp.concatenate([piece[:, split:] for piece in along], axis=0), query)
    output_near = swap_y(output_rows)
    query, late_lines = lax.optimization_barrier((query, late_lines))
    up_one = jnp.concatenate([lines[0], late_lines[0]], axis=0)
    down_one = jnp.concatenate([lines[1], late_lines[1]], axis=0)
    query, up_one, down_one = lax.optimization_barrier((query, up_one, down_one))
    up_two, down_two = line_up(up_one), line_down(down_one)
    pairs = q_width // (2 * HDIM)
    first_pairs = (pairs + 1) // 2
    mixed_one, levels_one = attend(query, keys, values, start_column, 0, first_pairs)
    sent_one = swap_seq(from_order(sort_other, mixed_one))
    output_rows, output_near = after((output_rows, output_near), mixed_one)
    output_rows = jnp.concatenate([output_rows, output_near], axis=0)
    output_others = swap_core(output_rows)
    query_two, grad_near_x, grad_near_y = after((query, *grad_near), mixed_one)
    grad_near = (grad_near_x, grad_near_y)
    grad_far = far_pieces(*grad_near)
    mixed_two, levels_two = attend(
        query_two, keys, values, start_column, first_pairs, pairs - first_pairs
    )
    sent_two = swap_seq(from_order(sort_other, mixed_two))
    mixed_mine = [from_order(sort_own, mixed_one), from_order(sort_own, mixed_two)]
    mixed_mine = jnp.concatenate(mixed_mine, axis=1)
    mixed_theirs = jnp.concatenate([sent_one, sent_two], axis=1)
    mixed_theirs, up_two, down_two = lax.optimization_barrier((mixed_theirs, up_two, down_two))
    up_three, down_three = line_up(up_two), line_down(down_two)
    inputs = tokens.astype(F32)
    middle, normed_ffn, output_parts = mix(
        places_of, mixed_mine, mixed_theirs, tokens, gains, output_rows, output_others
    )
    normed_ffn = after(normed_ffn, *grad_far)
    row_near = near_pieces(normed_ffn, normed_ffn)
    row_far = far_pieces(*row_near)
    slots = [up_three, up_two, up_one, own_part, down_one, down_two, down_three]
    row_pieces = with_cores(normed_ffn, *row_near, *row_far)
    grad_pieces = with_cores(*after((grad_rows, *grad_near, *grad_far), row_near[0]))
    place = line.astype(jnp.int32)[None]
    far = run_experts(FAR_TILES, place, row_pieces, grad_pieces, slots, select, 0, ())
    far_back = over_cores(far[2], far[3]).astype(BF16)
    back_y, back_x = far_links(far_back)
    near = run_experts(
        NEAR_TILES, after(place, far_back), row_pieces, grad_pieces, slots, select, 4, far[4:]
    )
    hid_a, hid_b, du_a, du_b, all_rows, all_grads = near[4:]

    def weight_grads(rows, grads, grad_both, hidden):
        inner = contract(rows, grad_both, 0, 0)
        outer = contract(grads, hidden, 0, 0) * BRANCH_SCALE
        return [
            jnp.concatenate(
                [inner[:, 2 * half * i : 2 * half * (i + 1)], outer[:, half * i : half * (i + 1)]],
                axis=1,
            ).astype(BF16)
            for i in range(2)
        ]

    rows_early, grads_early, back_y, back_x = lax.optimization_barrier(
        (all_rows, all_grads, back_y, back_x)
    )
    outer_grads = weight_grads(rows_early, grads_early, du_a, hid_a)
    grads_of = dict(zip(SLOT_ORDER[:2], outer_grads))
    far_line = (line_up(outer_grads[1]), line_down(outer_grads[0]))
    near_back = over_cores(after(near[2], *outer_grads), near[3])
    first, second = near_links(near_back, back_y, back_x)
    rows_late, grads_late = after((all_rows, all_grads), first, second)
    inner_grads = weight_grads(rows_late, grads_late, du_b, hid_b)
    grads_of.update(zip(SLOT_ORDER[2:], inner_grads))
    first, second = swap_seq(first), swap_y(second)
    near_back = after(near_back, *inner_grads)
    grad_normed_ffn = own_sum(near_back, back_y, back_x, first, second)

    def line_partial(first, *rest):
        value = grads_of[first]
        for where, expert in enumerate(rest):
            value = jnp.where(line > where, grads_of[expert], value)
        return value.astype(F32)

    def line_step(step, arrived):
        up, down = arrived
        last = LINE - 1
        right = line_partial(*range(last - step, LINE)) + up.astype(F32)
        left = grads_of[step]
        for where in range(step):
            left = jnp.where(line < last - where, grads_of[step - 1 - where], left)
        left = left.astype(F32) + down.astype(F32)
        return right.astype(BF16), left.astype(BF16)

    grad_final = cotangent.astype(F32)
    grad_norm, grad_gain_two = norm_back(middle, gain_two, grad_normed_ffn)
    grad_middle = grad_final + grad_norm
    grad_attn = (BRANCH_SCALE * grad_middle).astype(BF16)
    grad_mixed = contract(grad_attn, output_parts[0], 1, 1).astype(BF16)
    grad_other = contract(grad_attn, output_parts[1], 1, 1).astype(BF16)
    grad_other = swap_seq(grad_other)
    grad_w_output = contract(ordered(mixed_mine, mixed_theirs, 1), grad_attn, 0, 0)
    far_f, far_f_other, near_f, near_f_other = after(
        (far[0], far[1], near[0], near[1]), grad_mixed
    )
    far_ffn = over_cores(far_f, far_f_other).astype(BF16)
    ffn_y, ffn_x = far_links(far_ffn)
    near_ffn = over_cores(near_f, near_f_other)
    right, left = line_step(1, far_line)
    grad_other = after(grad_other, right, left, far_ffn, grad_w_output)
    grad_sorted = to_order(grad_mixed, grad_other)
    mid_line = (line_up(right), line_down(left))
    grad_query, grad_keys, grad_values = attend_back(
        query,
        keys,
        values,
        grad_sorted,
        jnp.concatenate([levels_one, levels_two], axis=0),
        start_column,
        cos,
        sin,
    )
    (grad_query, grad_keys, grad_values), mid_line, ffn_y, ffn_x = lax.optimization_barrier(
        ((grad_query, grad_keys, grad_values), mid_line, ffn_y, ffn_x)
    )
    right, left = line_step(2, mid_line)
    last_first = (line_up(right[:cut]), line_down(left[:cut]))
    first_ffn, second_ffn = near_links(near_ffn, ffn_y, ffn_x)
    first_ffn, second_ffn = swap_seq(first_ffn), swap_y(second_ffn)
    ffn = own_sum(near_ffn, ffn_y, ffn_x, first_ffn, second_ffn)
    output = (middle + BRANCH_SCALE * ffn).astype(BF16)
    grads_qkv = after((grad_query, grad_keys, grad_values), right, left)
    wide = qkv_grad(normed, grads_qkv, grad_gain_two[None, :], shard)


    def chosen(value, which, axis):
        return lax.dynamic_index_in_dim(value, which, axis=axis, keepdims=False)

    summed_output = lax.psum_scatter(
        grad_w_output.astype(BF16), ("seq", "dp"), scatter_dimension=0, tiled=True
    )
    kept = chosen(wide, core, 0).astype(F32)
    kept = kept + swap_core(chosen(wide, 1 - core, 0)).astype(F32)
    grads_late = after(grads_qkv, kept)
    grad_normed, sent_normed = token_grad(
        grads_late, w_qkv, own_places[:, None], other_places[:, None]
    )
    kept, sent_normed = lax.optimization_barrier((kept, sent_normed))
    right_late, left_late = after((right[cut:], left[cut:]), last_first, sent_normed)
    last_late = (line_up(right_late), line_down(left_late))
    grad_normed = grad_normed.astype(F32) + swap_seq(sent_normed).astype(F32)
    scale = lax.rsqrt(jnp.mean(inputs * inputs, axis=-1, keepdims=True) + EPSILON)
    unit = inputs * scale
    scaled = grad_normed * gain_one
    inner = jnp.mean(scaled * unit, axis=-1, keepdims=True)
    grad_tokens = grad_middle + scale * (scaled - unit * inner)
    next_kept = chosen(kept, row_of, 0)
    next_kept = next_kept + swap_y(chosen(kept, 1 - row_of, 0).astype(BF16)).astype(F32)
    next_kept, last_first, last_late, summed_output = lax.optimization_barrier(
        (next_kept, last_first, last_late, summed_output)
    )
    own_grads = line_partial(*range(LINE))
    part_grads = jnp.concatenate(
        [
            own + up.astype(F32) + down.astype(F32)
            for own, (up, down) in ((own_grads[:cut], last_first), (own_grads[cut:], last_late))
        ],
        axis=0,
    ).astype(BF16)
    same_grads = jnp.where(first_core, part_grads[:, :half], part_grads[:, half : 2 * half])
    cross_grads = jnp.where(first_core, part_grads[:, half : 2 * half], part_grads[:, :half])
    same_grads = jnp.concatenate([same_grads, part_grads[:, 2 * half :]], axis=1)
    next_kept, same_grads, cross_grads = lax.optimization_barrier(
        (next_kept, same_grads, cross_grads)
    )
    same = both_axes(same_grads, straight)
    cross = both_axes(cross_grads, crossed_back)
    sent_lines = [
        swap_dp(chosen(next_kept, line ^ step, 1).astype(BF16), 4 * step) for step in range(1, LINE)
    ]
    summed = chosen(next_kept, line, 1) + sum(value.astype(F32) for value in sent_lines)
    summed, same, cross = lax.optimization_barrier((summed, same, cross))
    grad_w_in = ordered(same[:, :half], cross, 1)
    grad_w_out = same[:, half:].T
    kept_rows = chosen(summed, seq, 0)
    sent_rows = swap_seq(chosen(summed, 1 - seq, 0).astype(BF16)).astype(F32)
    cuts = (q_width, q_width + kv_width, qkv_width)
    pieces = [
        (a, b) for a, b in zip(jnp.split(kept_rows, cuts, axis=1), jnp.split(sent_rows, cuts, axis=1))
    ]
    grad_projections = [ordered(a, b, 1) for a, b in pieces[:3]]
    grad_gain_ffn = (pieces[3][0] + pieces[3][1])[:, 0]
    grad_gain_attn = sum(
        jnp.sum(grad * weight.astype(F32), axis=1)
        for grad, weight in zip(grad_projections, projections)
    ) / gain_attn.astype(F32)
    return (
        output,
        grad_tokens,
        grad_projections[0],
        grad_projections[1],
        grad_projections[2],
        summed_output.astype(F32),
        grad_gain_attn,
        grad_gain_ffn,
        grad_w_in.astype(F32)[None],
        grad_w_out.astype(F32)[None],
    )


def solution(mesh):
    placed = (
        P(("seq", "dp"), None),
        P(("seq", "dp"), None),
        P("dp", None),
        P("dp", None),
        P(("seq", "dp"), None),
        P(("seq", "dp"), None),
        P(("seq", "dp"), None),
        P(("seq", "dp"), None),
        P(("seq", "dp"), None),
        P(("seq", "dp"), None),
        P(("seq", "dp")),
        P(("seq", "dp")),
        P("dp", None, "seq"),
        P("dp", "seq", None),
    )
    return jax.shard_map(
        shards_plane if in_planes(mesh) else shards_general,
        mesh=mesh,
        in_specs=placed,
        out_specs=(
            P(("seq", "dp"), None),
            P(("seq", "dp"), None),
            P(("seq", "dp"), None),
            P(("seq", "dp"), None),
            P(("seq", "dp"), None),
            P(("seq", "dp"), None),
            P(("seq", "dp")),
            P(("seq", "dp")),
            P("dp", None, "seq"),
            P("dp", "seq", None),
        ),
        check_vma=False,
    )
```

```python
import functools

import jax
import jax.numpy as jnp
from jax import lax
from jax.experimental import pallas as pl
from jax.experimental.pallas import tpu as pltpu
from jax.sharding import PartitionSpec as P

QHEADS = 24
KVHEADS = 8
HDIM = 64
FF = 512
TOP = 8


EPSILON = 1e-06
BRANCH_SCALE = 0.22
SCORE_SCALE = 1.0 / 64.0
THETA = 10000.0


def rms_norm(value, gain):
    return value * lax.rsqrt(jnp.mean(value * value, axis=-1, keepdims=True) + EPSILON) * gain


def local_places(placing, seq_lengths):
    ends = jnp.cumsum(seq_lengths)
    segment = jnp.sum((placing[:, None] >= ends[None, :]).astype(jnp.int32), axis=1)
    starts = ends - seq_lengths
    member = segment[:, None] == jnp.arange(seq_lengths.shape[0], dtype=jnp.int32)[None, :]
    start_of = jnp.sum(jnp.where(member, starts[None, :], 0), axis=1)
    return (segment, placing - start_of)


def rotate(values, place, direction):
    half = values.shape[-1] // 2
    freqs = jnp.power(THETA, -jnp.arange(half, dtype=jnp.float32) * 2.0 / values.shape[-1])
    angles = place.astype(jnp.float32)[:, None] * freqs[None, :]
    cosine = jnp.cos(angles)[:, None, :]
    sine = direction * jnp.sin(angles)[:, None, :]
    first = values[..., :half]
    second = values[..., half:]
    return jnp.concatenate(
        [first * cosine - second * sine, second * cosine + first * sine], axis=-1
    )


def shards_general(
    tokens,
    cotangent,
    positions,
    lengths,
    routes,
    logits,
    w_query,
    w_key,
    w_value,
    w_output,
    gain_attn,
    gain_ffn,
    w_in,
    w_out,
):
    seq_count = lax.axis_size("seq")
    data_count = lax.axis_size("dp")
    tok_count = tokens.shape[0]
    group_len = positions.shape[1]
    local_experts = w_in.shape[0]
    experts_all = local_experts * data_count
    capacity = min(tok_count, 5 * tok_count * TOP // (4 * experts_all))
    heads_local = QHEADS // seq_count
    kv_local = KVHEADS // seq_count
    ratio = QHEADS // KVHEADS
    width = tokens.shape[1]
    query_full, key_full, value_full, output_full, gain_one, gain_two = (
        lax.all_gather(w_query, ("seq", "dp"), axis=0, tiled=True),
        lax.all_gather(w_key, ("seq", "dp"), axis=0, tiled=True),
        lax.all_gather(w_value, ("seq", "dp"), axis=0, tiled=True),
        lax.all_gather(w_output, ("seq", "dp"), axis=0, tiled=True),
        lax.all_gather(gain_attn, ("seq", "dp"), axis=0, tiled=True),
        lax.all_gather(gain_ffn, ("seq", "dp"), axis=0, tiled=True),
    )
    in_full, out_full = (
        lax.all_gather(w_in, "seq", axis=2, tiled=True),
        lax.all_gather(w_out, "seq", axis=1, tiled=True),
    )
    gain_one = gain_one.astype(jnp.float32)
    gain_two = gain_two.astype(jnp.float32)
    segment, place = local_places(positions[0], lengths[0])
    my_start = lax.axis_index("seq") * tok_count
    my_place = lax.dynamic_slice_in_dim(place, my_start, tok_count)
    inputs = tokens.astype(jnp.float32)
    normed = rms_norm(inputs, gain_one).astype(jnp.bfloat16)
    query_pre = jnp.dot(normed, query_full, preferred_element_type=jnp.float32)
    key_pre = jnp.dot(normed, key_full, preferred_element_type=jnp.float32)
    query_rot = (
        rotate(query_pre.reshape(tok_count, QHEADS, HDIM), my_place, 1.0)
        .reshape(tok_count, QHEADS * HDIM)
        .astype(jnp.bfloat16)
    )
    key_rot = (
        rotate(key_pre.reshape(tok_count, KVHEADS, HDIM), my_place, 1.0)
        .reshape(tok_count, KVHEADS * HDIM)
        .astype(jnp.bfloat16)
    )
    value_low = jnp.dot(normed, value_full, preferred_element_type=jnp.float32).astype(jnp.bfloat16)
    query_heads, key_heads, value_heads = (
        lax.all_to_all(query_rot, "seq", split_axis=1, concat_axis=0, tiled=True),
        lax.all_to_all(key_rot, "seq", split_axis=1, concat_axis=0, tiled=True),
        lax.all_to_all(value_low, "seq", split_axis=1, concat_axis=0, tiled=True),
    )
    keys_three = key_heads.reshape(group_len, kv_local, HDIM)
    values_three = value_heads.reshape(group_len, kv_local, HDIM)
    length = min(512, group_len)
    count = group_len // length

    def scores_of(query_block, seg_block, place_block):
        grouped = query_block.reshape(length, kv_local, ratio, HDIM)
        raw_scores = (
            jnp.einsum("qgrd,kgd->grqk", grouped, keys_three, preferred_element_type=jnp.float32)
            * SCORE_SCALE
        )
        allowed = (seg_block[:, None] == segment[None, :]) & (
            place[None, :] <= place_block[:, None]
        )
        return jnp.where(allowed[None, None], raw_scores, -1e30)

    def forward_block(pieces):
        query_block, seg_block, place_block = pieces
        scores = scores_of(query_block, seg_block, place_block)
        highest = jnp.max(scores, axis=-1, keepdims=True)
        expon = jnp.exp(scores - highest)
        totals = jnp.sum(expon, axis=-1, keepdims=True)
        probs = expon / totals
        mixed = jnp.einsum(
            "grqk,kgd->qgrd",
            probs.astype(jnp.bfloat16),
            values_three,
            preferred_element_type=jnp.float32,
        )
        return (
            mixed.reshape(length, heads_local * HDIM).astype(jnp.bfloat16),
            highest + jnp.log(totals),
            probs,
        )

    query_blocks = query_heads.reshape(count, length, heads_local * HDIM)
    seg_blocks = segment.reshape(count, length)
    place_blocks = place.reshape(count, length)
    block_args = (query_blocks, seg_blocks, place_blocks)

    def forward_light(pieces):
        mixed, lse_part, unused_probs = forward_block(pieces)
        return (mixed, lse_part)

    mixed_blocks, lse_blocks = lax.map(forward_light, block_args)
    mixed_heads = mixed_blocks.reshape(group_len, heads_local * HDIM)
    mixed_tokens = lax.all_to_all(mixed_heads, "seq", split_axis=0, concat_axis=1, tiled=True)
    attn = jnp.dot(mixed_tokens, output_full, preferred_element_type=jnp.float32)
    middle = inputs + BRANCH_SCALE * attn
    normed_ffn = rms_norm(middle, gain_two).astype(jnp.bfloat16)
    chosen = routes.reshape(-1)
    onehot = (chosen[:, None] == jnp.arange(experts_all, dtype=jnp.int32)[None, :]).astype(
        jnp.int32
    )
    ranking = jnp.sum(jnp.cumsum(onehot, axis=0) * onehot, axis=1) - 1
    target = chosen * capacity + ranking
    token_of = jnp.arange(tok_count * TOP, dtype=jnp.int32) // TOP
    gates = jax.nn.softmax(logits, axis=-1)
    source = jnp.full((experts_all * capacity,), tok_count, jnp.int32).at[target].set(token_of)
    slot_gate = jnp.zeros((experts_all * capacity,), jnp.float32).at[target].set(gates.reshape(-1))
    padded = jnp.concatenate([normed_ffn, jnp.zeros((1, width), jnp.bfloat16)], axis=0)
    outgoing = padded[source].reshape(data_count, local_experts * capacity, width)

    def expert_layout(arrived):
        return jnp.swapaxes(
            arrived.reshape(data_count, local_experts, capacity, width), 0, 1
        ).reshape(local_experts, data_count * capacity, width)

    def home_layout(values):
        return jnp.swapaxes(
            values.reshape(local_experts, data_count, capacity, width), 0, 1
        ).reshape(data_count, local_experts * capacity, width)

    def expert_forward(expert_rows):
        both = jnp.einsum("erd,edf->erf", expert_rows, in_full, preferred_element_type=jnp.float32)
        hidden = (jax.nn.silu(both[..., :FF]) * both[..., FF:]).astype(jnp.bfloat16)
        return (both, hidden)

    expert_rows = expert_layout(
        lax.all_to_all(outgoing, "dp", split_axis=0, concat_axis=0, tiled=True)
    )
    both, hidden = expert_forward(expert_rows)
    result = jnp.einsum(
        "erf,efd->erd", hidden, out_full, preferred_element_type=jnp.float32
    ).astype(jnp.bfloat16)
    returned = lax.all_to_all(
        home_layout(result), "dp", split_axis=0, concat_axis=0, tiled=True
    ).reshape(experts_all * capacity, width)
    picked = returned[target].reshape(tok_count, TOP, width).astype(jnp.float32)
    ffn = jnp.sum(picked * gates[:, :, None], axis=1)
    final = middle + BRANCH_SCALE * ffn
    output = final.astype(jnp.bfloat16)
    grad_final = cotangent.astype(jnp.float32)
    padded_grad = jnp.concatenate(
        [BRANCH_SCALE * grad_final, jnp.zeros((1, width), jnp.float32)], axis=0
    )
    grad_slots = (slot_gate[:, None] * padded_grad[source]).astype(jnp.bfloat16)
    grad_result = expert_layout(
        lax.all_to_all(
            grad_slots.reshape(data_count, local_experts * capacity, width),
            "dp",
            split_axis=0,
            concat_axis=0,
            tiled=True,
        )
    )
    rows_back = expert_layout(
        lax.all_to_all(outgoing, "dp", split_axis=0, concat_axis=0, tiled=True)
    )
    both_back, hidden_back = expert_forward(rows_back)
    grad_hidden = jnp.einsum(
        "erd,efd->erf", grad_result, out_full, preferred_element_type=jnp.float32
    )
    gate_part = both_back[..., :FF]
    up_part = both_back[..., FF:]
    sigma = jax.nn.sigmoid(gate_part)
    grad_gate = grad_hidden * up_part * sigma * (1.0 + gate_part * (1.0 - sigma))
    grad_up = grad_hidden * gate_part * sigma
    grad_both = jnp.concatenate([grad_gate, grad_up], axis=-1).astype(jnp.bfloat16)
    grad_out_local = jnp.einsum(
        "erf,erd->efd", hidden_back, grad_result, preferred_element_type=jnp.float32
    )
    grad_in_local = jnp.einsum(
        "erd,erf->edf", rows_back, grad_both, preferred_element_type=jnp.float32
    )
    grad_rows = jnp.einsum(
        "erf,edf->erd", grad_both, in_full, preferred_element_type=jnp.float32
    ).astype(jnp.bfloat16)
    grad_home = lax.all_to_all(
        home_layout(grad_rows), "dp", split_axis=0, concat_axis=0, tiled=True
    ).reshape(experts_all * capacity, width)
    grad_normed_ffn = jnp.sum(
        grad_home[target].reshape(tok_count, TOP, width).astype(jnp.float32), axis=1
    )
    grad_w_in, grad_w_out = (
        lax.psum_scatter(
            grad_in_local.astype(jnp.bfloat16), "seq", scatter_dimension=2, tiled=True
        ).astype(jnp.float32),
        lax.psum_scatter(
            grad_out_local.astype(jnp.bfloat16), "seq", scatter_dimension=1, tiled=True
        ).astype(jnp.float32),
    )
    unused_norm, norm_pull = jax.vjp(rms_norm, middle, gain_two)
    grad_middle_norm, grad_gain_two = norm_pull(grad_normed_ffn)
    grad_middle = grad_final + grad_middle_norm
    grad_attn = (BRANCH_SCALE * grad_middle).astype(jnp.bfloat16)
    grad_w_output = jnp.einsum(
        "te,td->ed", mixed_tokens, grad_attn, preferred_element_type=jnp.float32
    )
    grad_mixed = jnp.einsum(
        "td,ed->te", grad_attn, output_full, preferred_element_type=jnp.float32
    ).astype(jnp.bfloat16)
    grad_mixed_heads = lax.all_to_all(grad_mixed, "seq", split_axis=1, concat_axis=0, tiled=True)
    grad_blocks = grad_mixed_heads.reshape(count, length, heads_local * HDIM)
    back_args = (query_blocks, seg_blocks, place_blocks, lse_blocks, grad_blocks)

    def backward_block(carry, pieces):
        grad_keys, grad_values = carry
        query_block, seg_block, place_block, lse_block, grad_block = pieces[:5]
        probs = jnp.exp(scores_of(query_block, seg_block, place_block) - lse_block)
        grad_out = grad_block.reshape(length, kv_local, ratio, HDIM)
        grad_probs = jnp.einsum(
            "qgrd,kgd->grqk", grad_out, values_three, preferred_element_type=jnp.float32
        )
        grad_scores = (
            probs * (grad_probs - jnp.sum(probs * grad_probs, axis=-1, keepdims=True))
        ).astype(jnp.bfloat16)
        grad_query = SCORE_SCALE * jnp.einsum(
            "grqk,kgd->qgrd", grad_scores, keys_three, preferred_element_type=jnp.float32
        )
        grouped = query_block.reshape(length, kv_local, ratio, HDIM)
        grad_keys = grad_keys + SCORE_SCALE * jnp.einsum(
            "grqk,qgrd->kgd", grad_scores, grouped, preferred_element_type=jnp.float32
        )
        grad_values = grad_values + jnp.einsum(
            "grqk,qgrd->kgd",
            probs.astype(jnp.bfloat16),
            grad_out,
            preferred_element_type=jnp.float32,
        )
        return (
            (grad_keys, grad_values),
            grad_query.reshape(length, heads_local * HDIM).astype(jnp.bfloat16),
        )

    empty_keys = jnp.zeros((group_len, kv_local, HDIM), jnp.float32)
    (grad_keys, grad_values), grad_query_blocks = lax.scan(
        backward_block, (empty_keys, empty_keys), back_args
    )
    grad_query_heads = grad_query_blocks.reshape(group_len, heads_local * HDIM)
    grad_key_heads = grad_keys.reshape(group_len, kv_local * HDIM).astype(jnp.bfloat16)
    grad_value_heads = grad_values.reshape(group_len, kv_local * HDIM).astype(jnp.bfloat16)
    grad_query_tok, grad_key_tok, grad_value_tok = (
        lax.all_to_all(grad_query_heads, "seq", split_axis=0, concat_axis=1, tiled=True),
        lax.all_to_all(grad_key_heads, "seq", split_axis=0, concat_axis=1, tiled=True),
        lax.all_to_all(grad_value_heads, "seq", split_axis=0, concat_axis=1, tiled=True),
    )
    grad_query_pre = (
        rotate(grad_query_tok.astype(jnp.float32).reshape(tok_count, QHEADS, HDIM), my_place, -1.0)
        .reshape(tok_count, QHEADS * HDIM)
        .astype(jnp.bfloat16)
    )
    grad_key_pre = (
        rotate(grad_key_tok.astype(jnp.float32).reshape(tok_count, KVHEADS, HDIM), my_place, -1.0)
        .reshape(tok_count, KVHEADS * HDIM)
        .astype(jnp.bfloat16)
    )
    grad_w_query = jnp.einsum(
        "td,te->de", normed, grad_query_pre, preferred_element_type=jnp.float32
    )
    grad_w_key = jnp.einsum("td,te->de", normed, grad_key_pre, preferred_element_type=jnp.float32)
    grad_w_value = jnp.einsum(
        "td,te->de", normed, grad_value_tok, preferred_element_type=jnp.float32
    )
    grad_normed = jnp.einsum(
        "te,de->td", grad_query_pre, query_full, preferred_element_type=jnp.float32
    )
    grad_normed = grad_normed + jnp.einsum(
        "te,de->td", grad_key_pre, key_full, preferred_element_type=jnp.float32
    )
    grad_normed = grad_normed + jnp.einsum(
        "te,de->td", grad_value_tok, value_full, preferred_element_type=jnp.float32
    )
    unused_first, first_pull = jax.vjp(rms_norm, inputs, gain_one)
    grad_inputs_norm, grad_gain_one = first_pull(grad_normed)
    grad_tokens = grad_middle + grad_inputs_norm
    summed = (
        lax.psum_scatter(grad_w_query, ("seq", "dp"), scatter_dimension=0, tiled=True),
        lax.psum_scatter(grad_w_key, ("seq", "dp"), scatter_dimension=0, tiled=True),
        lax.psum_scatter(grad_w_value, ("seq", "dp"), scatter_dimension=0, tiled=True),
        lax.psum_scatter(grad_w_output, ("seq", "dp"), scatter_dimension=0, tiled=True),
        lax.psum_scatter(grad_gain_one, ("seq", "dp"), scatter_dimension=0, tiled=True),
        lax.psum_scatter(grad_gain_two, ("seq", "dp"), scatter_dimension=0, tiled=True),
    )
    return (
        output,
        grad_tokens,
        summed[0],
        summed[1],
        summed[2],
        summed[3],
        summed[4],
        summed[5],
        grad_w_in,
        grad_w_out,
    )


BF16 = jnp.bfloat16
F32 = jnp.float32
LINE = 4
PAD = 128
VMEM_BYTES = 60 * 1024 * 1024


def in_planes(mesh):
    return mesh.shape["seq"] == 2 and mesh.shape["dp"] == 4 * LINE


def swap_seq(value):
    return lax.ppermute(value, "seq", [(0, 1), (1, 0)])


def swap_dp(value, mask):
    return lax.ppermute(value, "dp", [(i, i ^ mask) for i in range(4 * LINE)])


def swap_core(value):
    return swap_dp(value, 1)


def swap_y(value):
    return swap_dp(value, 2)


def line_up(value):
    return lax.ppermute(value, "dp", [(i, i + 4) for i in range(4 * LINE - 4)])


def line_down(value):
    return lax.ppermute(value, "dp", [(i, i - 4) for i in range(4, 4 * LINE)])


def after(value, *others):
    return lax.optimization_barrier((value,) + others)[0]


def line_scatter(take, place):
    up = down = None
    for step in range(LINE - 1):
        far = jnp.minimum(LINE - 1 - step + place, LINE - 1)
        near = jnp.maximum(step - LINE + 1 + place, 0)
        right, left = take(far), take(near)
        if up is not None:
            right = right + up.astype(F32)
            left = left + down.astype(F32)
        up = line_up(right.astype(BF16))
        down = line_down(left.astype(BF16))
    return take(place) + up.astype(F32) + down.astype(F32)


def near_pieces(own, own_x):
    return swap_seq(own_x), swap_y(own)


def far_pieces(near_x, near_y):
    half = near_x.shape[0] // 2
    return swap_y(near_x[:half]), swap_seq(near_y[half:])


def with_cores(*pieces):
    return pieces + tuple(swap_core(piece) for piece in pieces)


def over_cores(mine, others):
    return mine.astype(F32) + swap_core(others).astype(F32)


def far_links(far):
    half = far.shape[0] // 2
    return swap_y(far[:half]), swap_seq(far[half:])


def near_links(near, from_y, from_x):
    half = from_y.shape[0] // 2
    first = (near[:half] + from_y[half:].astype(F32)).astype(BF16)
    second = (near[half : 2 * half] + from_x[half:].astype(F32)).astype(BF16)
    return first, second


def own_sum(near, from_y, from_x, first, second):
    half = from_y.shape[0] // 2
    low = near[2 * half : 3 * half] + from_y[:half].astype(F32) + first.astype(F32)
    high = near[3 * half :] + from_x[:half].astype(F32) + second.astype(F32)
    return jnp.concatenate([low, high], axis=0)


def turned(values, cos, sin, direction):
    lanes = values.shape[1]
    place = lax.broadcasted_iota(jnp.int32, values.shape, 1) % HDIM
    swapped = jnp.where(
        place < HDIM // 2,
        pltpu.roll(values, lanes - HDIM // 2, 1),
        pltpu.roll(values, HDIM // 2, 1),
    )
    times = lanes // cos.shape[1]
    cos = jnp.concatenate([cos] * times, axis=1)
    sin = jnp.concatenate([sin] * times, axis=1)
    if direction > 0:
        return values * cos + swapped * sin
    return values * cos - swapped * sin


def qkv_kernel(x_ref, gain_ref, w_ref, cos_ref, sin_ref, h_ref, q_ref, k_ref, v_ref):
    value = x_ref[...].astype(F32)
    scale = lax.rsqrt(jnp.mean(value * value, axis=-1, keepdims=True) + EPSILON)
    normed = (value * scale * gain_ref[...]).astype(BF16)
    h_ref[...] = normed
    both = jnp.dot(normed, w_ref[...], preferred_element_type=F32)
    q_width, kv_heads = q_ref.shape[1], k_ref.shape[0]
    kv_width = kv_heads * HDIM
    spun = turned(both[:, : q_width + kv_width], cos_ref[...], sin_ref[...], 1)
    q_ref[...] = (spun[:, :q_width] * SCORE_SCALE).astype(BF16)
    for head in range(kv_heads):
        low = q_width + head * HDIM
        k_ref[head] = spun[:, low : low + HDIM].astype(BF16)
        low = low + kv_width
        v_ref[head] = both[:, low : low + HDIM].astype(BF16)


def project(x_sorted, gain, weights, cos, sin, q_width, kv_heads):
    rows, width = x_sorted.shape
    tile = 256
    columns = q_width + 2 * kv_heads * HDIM

    def row_block(lanes):
        return pl.BlockSpec((tile, lanes), lambda i: (i, 0))

    heads = pl.BlockSpec((kv_heads, tile, HDIM), lambda i: (0, i, 0))
    return pl.pallas_call(
        qkv_kernel,
        grid=(rows // tile,),
        in_specs=[
            row_block(width),
            pl.BlockSpec((1, width), lambda i: (0, 0)),
            pl.BlockSpec((width, columns), lambda i: (0, 0)),
            row_block(cos.shape[1]),
            row_block(cos.shape[1]),
        ],
        out_specs=[row_block(width), row_block(q_width), heads, heads],
        out_shape=[
            jax.ShapeDtypeStruct((rows, width), BF16),
            jax.ShapeDtypeStruct((rows, q_width), BF16),
            jax.ShapeDtypeStruct((kv_heads, rows, HDIM), BF16),
            jax.ShapeDtypeStruct((kv_heads, rows, HDIM), BF16),
        ],
        compiler_params=pltpu.CompilerParams(vmem_limit_bytes=VMEM_BYTES),
        cost_estimate=pl.CostEstimate(
            flops=rows * width * columns // 8,
            bytes_accessed=rows * width + width * columns,
            transcendentals=rows,
        ),
        name="project",
    )(x_sorted, gain, weights, cos, sin)


def token_grad_kernel(dq_ref, dk_ref, dv_ref, w_ref, own_ref, other_ref, mine_ref, sent_ref):
    q_width, kv_width = dq_ref.shape[1], dk_ref.shape[1]
    cuts = (0, q_width, q_width + kv_width, q_width + 2 * kv_width)
    grad = contract(dq_ref[...], w_ref[:, cuts[0] : cuts[1]], 1, 1)
    grad = grad + contract(dk_ref[...], w_ref[:, cuts[1] : cuts[2]], 1, 1)
    grad = (grad + contract(dv_ref[...], w_ref[:, cuts[2] : cuts[3]], 1, 1)).astype(BF16)
    for place_ref, out_ref in ((other_ref, sent_ref), (own_ref, mine_ref)):
        shape = (place_ref.shape[0], grad.shape[0])
        picked = lax.broadcasted_iota(jnp.int32, shape, 1) == place_ref[...]
        picked = jnp.where(picked, 1.0, 0.0).astype(BF16)
        out_ref[...] = jnp.dot(picked, grad, preferred_element_type=F32).astype(BF16)


def token_grad(grads, weights, own_places, other_places):
    rows, count = grads[0].shape[0], own_places.shape[0]
    width = weights.shape[0]
    columns = sum(grad.shape[1] for grad in grads)
    tile = width // 3

    def whole(array):
        return pl.BlockSpec(array.shape, lambda i: (0, 0))

    block = pl.BlockSpec((count, tile), lambda i: (0, i))
    return pl.pallas_call(
        token_grad_kernel,
        grid=(3,),
        in_specs=[whole(grad) for grad in grads]
        + [pl.BlockSpec((tile, columns), lambda i: (i, 0)), whole(own_places), whole(other_places)],
        out_specs=[block, block],
        out_shape=[jax.ShapeDtypeStruct((count, width), BF16)] * 2,
        compiler_params=pltpu.CompilerParams(vmem_limit_bytes=VMEM_BYTES),
        cost_estimate=pl.CostEstimate(
            flops=rows * width * columns // 8, bytes_accessed=rows * width, transcendentals=0
        ),
        name="token_grad",
    )(*grads, weights, own_places, other_places)


Q_TILE = 256


def windows(rows):
    longest = rows // 2
    for start in range(0, rows, Q_TILE):
        low = max(0, start - longest + 1) // Q_TILE * Q_TILE
        yield start, low, start + Q_TILE


def allowed_keys(start_ref, row, low, high):
    shape = (Q_TILE, high - low)
    rows = lax.broadcasted_iota(jnp.int32, shape, 0) + row
    keys = lax.broadcasted_iota(jnp.int32, shape, 1) + low
    return (keys <= rows) & (keys >= start_ref[row : row + Q_TILE, :])


def contract(left, right, left_dim, right_dim):
    return lax.dot_general(
        left, right, (((left_dim,), (right_dim,)), ((), ())), preferred_element_type=F32
    )


def masked_scores(query, keys, allowed):
    return jnp.where(allowed, contract(query, keys, 1, 1), -1e30)


def attend_kernel(base, q_ref, k_ref, v_ref, start_ref, o_ref, level_ref):
    pair = pl.program_id(0) + base
    ratio = QHEADS // KVHEADS
    for row, low, high in windows(q_ref.shape[0]):
        allowed = allowed_keys(start_ref, row, low, high)
        for side in range(2):
            head = (2 * pair + side) // ratio
            lanes = slice(side * HDIM, (side + 1) * HDIM)
            scores = masked_scores(
                q_ref[row : row + Q_TILE, lanes], k_ref[head, low:high, :], allowed
            )
            highest = jnp.max(scores, axis=-1, keepdims=True)
            expon = jnp.exp(scores - highest)
            total = jnp.sum(expon, axis=-1, keepdims=True)
            level_ref[0, row : row + Q_TILE, side : side + 1] = highest + jnp.log(total)
            probs = expon * (1.0 / total)
            mixed = contract(probs.astype(BF16), v_ref[head, low:high, :], 1, 0)
            o_ref[row : row + Q_TILE, lanes] = mixed.astype(BF16)


def attention_cost(rows, heads, products):
    area = sum(Q_TILE * (high - low) for _, low, high in windows(rows))
    return pl.CostEstimate(
        flops=products * heads * area * 16,
        bytes_accessed=8 * rows * heads * HDIM,
        transcendentals=heads * area,
    )


def attend(query, keys, values, starts, base, pairs):
    rows = query.shape[0]
    pair_block = pl.BlockSpec((rows, 2 * HDIM), lambda j: (0, j + base))
    whole = pl.BlockSpec(keys.shape, lambda j: (0, 0, 0))
    return pl.pallas_call(
        functools.partial(attend_kernel, base),
        grid=(pairs,),
        in_specs=[pair_block, whole, whole, pl.BlockSpec((rows, 1), lambda j: (0, 0))],
        out_specs=[
            pl.BlockSpec((rows, 2 * HDIM), lambda j: (0, j)),
            pl.BlockSpec((1, rows, 2), lambda j: (j, 0, 0)),
        ],
        out_shape=[
            jax.ShapeDtypeStruct((rows, pairs * 2 * HDIM), BF16),
            jax.ShapeDtypeStruct((pairs, rows, 2), F32),
        ],
        compiler_params=pltpu.CompilerParams(vmem_limit_bytes=VMEM_BYTES),
        cost_estimate=attention_cost(rows, 2 * pairs, 2),
        name="attend",
    )(query, keys, values, starts)


def attend_back_kernel(
    q_ref, k_ref, v_ref, d_ref, level_ref, start_ref, cos_ref, sin_ref,
    dq_ref, dk_ref, dv_ref, dk_sum, dv_sum,
):
    pair = pl.program_id(0)
    ratio = QHEADS // KVHEADS

    @pl.when(pair == 0)
    def _():
        dk_sum[...] = jnp.zeros_like(dk_sum)
        dv_sum[...] = jnp.zeros_like(dv_sum)

    for row, low, high in windows(q_ref.shape[0]):
        allowed = allowed_keys(start_ref, row, low, high)
        grads = []
        for side in range(2):
            head = (2 * pair + side) // ratio
            lanes = slice(side * HDIM, (side + 1) * HDIM)
            query = q_ref[row : row + Q_TILE, lanes]
            keys = k_ref[head, low:high, :]
            probs = jnp.exp(
                masked_scores(query, keys, allowed)
                - level_ref[0, row : row + Q_TILE, side : side + 1]
            )
            grad_out = d_ref[row : row + Q_TILE, lanes]
            grad_probs = contract(grad_out, v_ref[head, low:high, :], 1, 1)
            inner = jnp.sum(probs * grad_probs, axis=-1, keepdims=True)
            grad_scores = (probs * (grad_probs - inner)).astype(BF16)
            grads.append(contract(grad_scores, keys, 1, 0) * SCORE_SCALE)
            dk_sum[head, low:high, :] += contract(grad_scores, query, 0, 0)
            dv_sum[head, low:high, :] += contract(probs.astype(BF16), grad_out, 0, 0)
        grad_query = jnp.concatenate(grads, axis=1).astype(BF16).astype(F32)
        dq_ref[row : row + Q_TILE, :] = turned(
            grad_query,
            cos_ref[row : row + Q_TILE, :],
            sin_ref[row : row + Q_TILE, :],
            -1,
        ).astype(BF16)

    @pl.when(pair == pl.num_programs(0) - 1)
    def _():
        heads = range(dk_sum.shape[0])
        grad_keys = jnp.concatenate([dk_sum[head] for head in heads], axis=1)
        grad_keys = grad_keys.astype(BF16).astype(F32)
        dk_ref[...] = turned(grad_keys, cos_ref[...], sin_ref[...], -1).astype(BF16)
        dv_ref[...] = jnp.concatenate([dv_sum[head] for head in heads], axis=1).astype(BF16)


def attend_back(query, keys, values, grad_out, levels, starts, cos, sin):
    rows, lanes = query.shape
    pairs = lanes // (2 * HDIM)
    kv_heads = keys.shape[0]
    pair_block = pl.BlockSpec((rows, 2 * HDIM), lambda j: (0, j))
    whole = pl.BlockSpec(keys.shape, lambda j: (0, 0, 0))

    def fixed(lanes_of):
        return pl.BlockSpec((rows, lanes_of), lambda j: (0, 0))

    flat = kv_heads * HDIM
    return pl.pallas_call(
        attend_back_kernel,
        grid=(pairs,),
        in_specs=[
            pair_block, whole, whole, pair_block,
            pl.BlockSpec((1, rows, 2), lambda j: (j, 0, 0)), fixed(1), fixed(2 * HDIM), fixed(2 * HDIM),
        ],
        out_specs=[pair_block, fixed(flat), fixed(flat)],
        out_shape=[
            jax.ShapeDtypeStruct(query.shape, BF16),
            jax.ShapeDtypeStruct((rows, flat), BF16),
            jax.ShapeDtypeStruct((rows, flat), BF16),
        ],
        scratch_shapes=[pltpu.VMEM(keys.shape, F32), pltpu.VMEM(keys.shape, F32)],
        compiler_params=pltpu.CompilerParams(vmem_limit_bytes=VMEM_BYTES),
        cost_estimate=attention_cost(rows, 2 * pairs, 5),
        name="attend_back",
    )(query, keys, values, grad_out, levels, starts, cos, sin)


SLOTS = 2 * LINE - 1
SLOT_ORDER = (0, 3, 1, 2)
OWN, NEAR_X, NEAR_Y, FAR_Y, FAR_X = range(5)
FAR_TILES = (((NEAR_Y, 0), (FAR_Y, 0)), ((NEAR_X, 1), (FAR_X, 0)))
NEAR_TILES = (((NEAR_X, 0), (NEAR_Y, 1)), ((OWN, 0), (OWN, 1)))


def used_pieces(tiles):
    return sorted({piece for tile in tiles for piece, _ in tile})


def experts_kernel(tiles, half_rows, place_ref, *refs):
    used = used_pieces(tiles)
    sides = 2 * len(used)
    h_pieces, g_pieces, slots = refs[:sides], refs[sides : 2 * sides], refs[2 * sides : 2 * sides + SLOTS]
    select_ref = refs[2 * sides + SLOTS]
    (
        f_mine, f_other, d_mine, d_other, hid_a, hid_b, du_a, du_b, hcopy_ref, gcopy_ref,
        w_in, w_out, h_buf, g_buf, hidden, du_all, weight_sems, row_sems,
    ) = refs[-18:]
    width = h_buf.shape[2]
    half = slots[0].shape[1] // 3
    part = 2 * half
    step = pl.program_id(0)
    steps = 2 * len(tiles)

    def weight_copies(spot, slot):
        return (
            pltpu.make_async_copy(
                slots[slot].at[:, :part],
                w_in.at[:, spot * part : (spot + 1) * part],
                weight_sems.at[0, spot],
            ),
            pltpu.make_async_copy(
                slots[slot].at[:, part:],
                w_out.at[:, spot * half : (spot + 1) * half],
                weight_sems.at[1, spot],
            ),
        )

    def row_copies(number, buffer):
        side, tile = divmod(number, len(tiles))
        copies = []
        for spot, (piece, part_of) in enumerate(tiles[tile]):
            index = side * len(used) + used.index(piece)
            for kind, (pieces, held) in enumerate(((h_pieces, h_buf), (g_pieces, g_buf))):
                copies.append(
                    pltpu.make_async_copy(
                        pieces[index].at[pl.ds(part_of * half_rows, half_rows), :],
                        held.at[buffer, pl.ds(spot * half_rows, half_rows), :],
                        row_sems.at[buffer, 2 * kind + spot],
                    )
                )
        return copies

    def fetch(wanted, buffer):
        for number in range(steps):

            @pl.when(wanted == number)
            def _():
                for copy in row_copies(number, buffer):
                    copy.start()

    buffer = step % 2

    @pl.when(step == 0)
    def _():
        fetch(step, 0)
        for spot, expert in enumerate(SLOT_ORDER):
            for slot in range(expert, expert + LINE):

                @pl.when(slot == LINE - 1 + expert - place_ref[0])
                def _():
                    for copy in weight_copies(spot, slot):
                        copy.start()

        for spot in range(LINE):
            for copy in weight_copies(spot, LINE - 1):
                copy.wait()

    @pl.when(step + 1 < steps)
    def _():
        fetch(step + 1, 1 - buffer)

    for copy in row_copies(0, buffer):
        copy.wait()

    rows = h_buf[buffer]
    grads = g_buf[buffer, :, :width]
    hcopy_ref[...] = rows
    gcopy_ref[...] = grads
    gates = jnp.dot(g_buf[buffer, :, width:], select_ref[...], preferred_element_type=F32)
    for spot in range(LINE):
        units = slice(spot * half, (spot + 1) * half)
        both = jnp.dot(
            rows, w_in[:, spot * part : (spot + 1) * part], preferred_element_type=F32
        )
        back = jnp.dot(grads, w_out[:, units], preferred_element_type=F32)
        gate = gates[:, units]
        first, second = both[:, :half], both[:, half:]
        sigma = jax.nn.sigmoid(first)
        silu = first * sigma
        hidden[:, units] = (gate * (silu * second)).astype(BF16)
        back = back * (BRANCH_SCALE * gate)
        d_first = back * second * (sigma * (1.0 + first * (1.0 - sigma)))
        d_second = back * silu
        du_all[:, spot * part : spot * part + half] = d_first.astype(BF16)
        du_all[:, spot * part + half : (spot + 1) * part] = d_second.astype(BF16)
    hid_a[...] = hidden[:, : 2 * half]
    hid_b[...] = hidden[:, 2 * half :]
    du_a[...] = du_all[:, : 2 * part]
    du_b[...] = du_all[:, 2 * part :]
    ffn = contract(hidden[...], w_out[...], 1, 1).astype(BF16)
    back_rows = contract(du_all[...], w_in[...], 1, 1).astype(BF16)

    @pl.when(step < len(tiles))
    def _():
        f_mine[...] = ffn
        d_mine[...] = back_rows

    @pl.when(step >= len(tiles))
    def _():
        f_other[...] = ffn
        d_other[...] = back_rows


def run_experts(tiles, place, row_pieces, grad_pieces, slots, select, base, kept):
    used = used_pieces(tiles)
    sides = len(row_pieces) // 2
    wanted = used + [sides + piece for piece in used]
    rows = [row_pieces[piece] for piece in wanted]
    grads = [grad_pieces[piece] for piece in wanted]
    tile, width = row_pieces[OWN].shape
    wide = grad_pieces[OWN].shape[1]
    half = slots[0].shape[1] // 3
    part = 2 * half
    count = len(tiles)
    steps = 2 * count
    total = 8 * tile

    def late(lanes):
        return pl.BlockSpec((tile, lanes), lambda i, p: (i + base, 0))

    mine = pl.BlockSpec((tile, width), lambda i, p: (jnp.minimum(i, count - 1), 0))
    others = pl.BlockSpec((tile, width), lambda i, p: (jnp.maximum(i - count, 0), 0))
    anywhere = pl.BlockSpec(memory_space=pl.ANY)
    kept = list(kept)
    lead = 1 + 2 * len(wanted) + SLOTS + 1
    partial = jax.ShapeDtypeStruct((count * tile, width), BF16)
    lanes = [2 * half, 2 * half, 2 * part, 2 * part, width, width]
    return pl.pallas_call(
        functools.partial(experts_kernel, tiles, tile // 2),
        grid_spec=pltpu.PrefetchScalarGridSpec(
            num_scalar_prefetch=1,
            grid=(steps,),
            in_specs=[anywhere] * (2 * len(wanted) + SLOTS)
            + [pl.BlockSpec(select.shape, lambda i, p: (0, 0))]
            + [anywhere] * len(kept),
            out_specs=[mine, others, mine, others] + [late(n) for n in lanes],
            scratch_shapes=[
                pltpu.VMEM((width, LINE * part), BF16),
                pltpu.VMEM((width, LINE * half), BF16),
                pltpu.VMEM((2, tile, width), BF16),
                pltpu.VMEM((2, tile, wide), BF16),
                pltpu.VMEM((tile, LINE * half), BF16),
                pltpu.VMEM((tile, LINE * part), BF16),
                pltpu.SemaphoreType.DMA((2, LINE)),
                pltpu.SemaphoreType.DMA((2, 4)),
            ],
        ),
        out_shape=[partial] * 4 + [jax.ShapeDtypeStruct((total, n), BF16) for n in lanes],
        input_output_aliases={lead + i: 4 + i for i in range(len(kept))},
        compiler_params=pltpu.CompilerParams(vmem_limit_bytes=VMEM_BYTES),
        cost_estimate=pl.CostEstimate(
            flops=steps * tile * width * LINE * (part + half) // 4,
            bytes_accessed=2 * steps * tile * (6 * width + LINE * (part + half)),
            transcendentals=steps * tile * LINE * half,
        ),
        name="experts",
    )(place, *rows, *grads, *slots, select, *kept)


def qkv_grad_kernel(h_ref, dq_ref, dk_ref, dv_ref, gain_ref, o_ref):
    shard = o_ref.shape[-2]
    rows = h_ref[...]
    low = 0
    gains = jnp.broadcast_to(gain_ref[...], (PAD, gain_ref.shape[1])).T.astype(BF16)
    parts = [contract(rows, ref[...], 0, 0).astype(BF16) for ref in (dq_ref, dk_ref, dv_ref)]
    for part in parts + [gains]:
        for block in range(h_ref.shape[1] // shard):
            place = (block % 2, block // 2 % 2, 0, block // 4)
            o_ref[place + (slice(None), slice(low, low + part.shape[1]))] = part[
                block * shard : (block + 1) * shard
            ]
        low = low + part.shape[1]


def qkv_grad(normed, grads, gain_row, shard):
    rows, width = normed.shape
    columns = sum(grad.shape[1] for grad in grads)
    tile = width // 4
    planes = tile // (4 * shard)
    return pl.pallas_call(
        qkv_grad_kernel,
        grid=(4,),
        in_specs=[pl.BlockSpec((rows, tile), lambda i: (0, i))]
        + [pl.BlockSpec(grad.shape, lambda i: (0, 0)) for grad in grads]
        + [pl.BlockSpec((1, tile), lambda i: (0, i))],
        out_specs=pl.BlockSpec(
            (2, 2, 1, planes, shard, columns + PAD), lambda i: (0, 0, i // 2, i % 2, 0, 0)
        ),
        out_shape=jax.ShapeDtypeStruct((2, 2, 2, LINE, shard, columns + PAD), BF16),
        compiler_params=pltpu.CompilerParams(vmem_limit_bytes=VMEM_BYTES),
        cost_estimate=pl.CostEstimate(
            flops=rows * width * columns // 8,
            bytes_accessed=rows * width,
            transcendentals=0,
        ),
        name="qkv_grad",
    )(normed, *grads, gain_row)


def norm_back(value, gain, grad):
    scale = lax.rsqrt(jnp.mean(value * value, axis=-1, keepdims=True) + EPSILON)
    unit = value * scale
    grad_gain = jnp.sum(grad * unit, axis=0)
    scaled = grad * gain
    inner = jnp.mean(scaled * unit, axis=-1, keepdims=True)
    return scale * (scaled - unit * inner), grad_gain


def shards_plane(
    tokens,
    cotangent,
    positions,
    lengths,
    routes,
    logits,
    w_query,
    w_key,
    w_value,
    w_output,
    gain_attn,
    gain_ffn,
    w_in,
    w_out,
):
    seq = lax.axis_index("seq")
    data = lax.axis_index("dp")
    line, row_of, core = data // 4, (data // 2) % 2, data % 2
    tok_count, width = tokens.shape
    group_len = positions.shape[1]
    shard = w_query.shape[0]
    q_width = w_query.shape[1] // 2
    kv_width = w_key.shape[1] // 2
    kv_heads = kv_width // HDIM
    first_seq = seq == 0

    def ordered(mine, theirs, axis):
        low = jnp.where(first_seq, mine, theirs)
        high = jnp.where(first_seq, theirs, mine)
        return jnp.concatenate([low, high], axis=axis)

    def half_of(weights, which):
        half = weights.shape[1] // 2
        return lax.dynamic_slice_in_dim(weights, which * half, half, axis=1)

    def both_axes(value, pairs):
        return lax.ppermute(value, ("seq", "dp"), pairs)

    def device(s, d):
        return s * 4 * LINE + d

    straight, crossed = [], []
    for s in range(2):
        for d in range(4 * LINE):
            c = d % 2
            straight.append((device(s, d), device(c, d - c + s)))
            crossed.append((device(s, d), device(c, d - c + 1 - s)))
    crossed_back = [(there, here) for here, there in crossed]
    first_core = core == 0

    projections = (w_query, w_key, w_value)
    qkv_width = q_width + 2 * kv_width
    gain_columns = jnp.pad(jnp.stack([gain_attn, gain_ffn], axis=1), ((0, 0), (0, PAD - 2)))
    mine = jnp.concatenate([half_of(w, seq) for w in projections] + [gain_columns], axis=1)
    theirs = jnp.concatenate([half_of(w, 1 - seq) for w in projections] + [gain_columns], axis=1)
    theirs = swap_seq(theirs)
    pair = jnp.stack([jnp.where(first_seq, mine, theirs), jnp.where(first_seq, theirs, mine)])
    qkv_width = q_width + 2 * kv_width
    w_qkv = lax.all_gather(pair, "dp", axis=1, tiled=True).reshape(width, qkv_width + PAD)
    output_full = lax.all_gather(w_output, ("seq", "dp"), axis=0, tiled=True)

    in_own = w_in[0]
    half = in_own.shape[1] // 2
    sent = jnp.concatenate(
        [lax.dynamic_slice_in_dim(in_own, seq * half, half, axis=1), w_out[0].T], axis=1
    )
    same = both_axes(sent, straight)
    cross = both_axes(lax.dynamic_slice_in_dim(in_own, (1 - seq) * half, half, axis=1), crossed)
    own_part = jnp.concatenate(
        [
            jnp.where(first_core, same[:, :half], cross),
            jnp.where(first_core, cross, same[:, :half]),
            same[:, half:],
        ],
        axis=1,
    )
    other_tokens = swap_seq(after(tokens, own_part))
    up_one, down_one = line_up(own_part), line_down(own_part)
    cut = width // 2

    experts_all = 4 * LINE
    gates = jax.nn.softmax(logits, axis=-1)
    named = routes[:, :, None] == jnp.arange(experts_all, dtype=jnp.int32)[None, None, :]
    gate_table = jnp.sum(jnp.where(named, gates[:, :, None], 0.0), axis=1)
    gate_high = lax.reduce_precision(gate_table, 8, 7)
    grad_rows = jnp.concatenate(
        [
            cotangent,
            gate_high.astype(BF16),
            (gate_table - gate_high).astype(BF16),
            jnp.zeros((tok_count, PAD - 2 * experts_all), BF16),
        ],
        axis=1,
    )
    grad_near = near_pieces(grad_rows, after(grad_rows, other_tokens))
    lane = jnp.arange(PAD, dtype=jnp.int32)[:, None]
    hosted = jnp.repeat(
        jnp.array(SLOT_ORDER, jnp.int32) * 4 + 2 * row_of + seq, half, total_repeat_length=LINE * half
    )
    select = ((lane % experts_all == hosted[None, :]) & (lane < 2 * experts_all)).astype(BF16)

    places = positions[0]
    ends = jnp.cumsum(lengths[0])
    ranks = jnp.arange(group_len, dtype=jnp.int32)
    reached = ranks[:, None] >= ends[None, :]
    starts = jnp.max(jnp.where(reached, ends[None, :], 0), axis=1)
    local = (ranks - starts).astype(F32)
    freqs = jnp.power(THETA, -jnp.arange(HDIM // 2, dtype=F32) * 2.0 / HDIM)
    angles = local[:, None] * freqs[None, :]
    cos, sin = jnp.cos(angles), jnp.sin(angles)
    cos = jnp.concatenate([cos, cos, cos, cos], axis=1)
    sin = jnp.concatenate([-sin, sin, -sin, sin], axis=1)
    start_column = starts[:, None]
    own_places = lax.dynamic_slice_in_dim(places, seq * tok_count, tok_count)
    other_places = lax.dynamic_slice_in_dim(places, (1 - seq) * tok_count, tok_count)
    sort_own = (ranks[:, None] == own_places[None, :]).astype(BF16)
    sort_other = (ranks[:, None] == other_places[None, :]).astype(BF16)

    def to_order(own, other):
        return (
            contract(sort_own, own, 1, 0) + contract(sort_other, other, 1, 0)
        ).astype(BF16)

    def from_order(sort, values):
        return contract(sort, values, 0, 0).astype(BF16)

    x_sorted = to_order(tokens, other_tokens)
    gains = w_qkv[:, qkv_width : qkv_width + 2].astype(F32).T
    gain_one, gain_two = gains[0], gains[1]
    x_sorted, up_one, down_one = lax.optimization_barrier((x_sorted, up_one, down_one))
    up_two, down_two = line_up(up_one), line_down(down_one)
    normed, query, keys, values = project(
        x_sorted, gain_one[None, :], w_qkv, cos, sin, q_width, kv_heads
    )
    pairs = q_width // (2 * HDIM)
    first_pairs = (pairs + 1) // 2
    mixed_one, levels_one = attend(query, keys, values, start_column, 0, first_pairs)
    sent_one = swap_seq(from_order(sort_other, mixed_one))
    query_two, grad_near_x, grad_near_y = after((query, *grad_near), mixed_one)
    grad_near = (grad_near_x, grad_near_y)
    grad_far = far_pieces(*grad_near)
    mixed_two, levels_two = attend(
        query_two, keys, values, start_column, first_pairs, pairs - first_pairs
    )
    sent_two = swap_seq(from_order(sort_other, mixed_two))
    mixed_mine = [from_order(sort_own, mixed_one), from_order(sort_own, mixed_two)]
    mixed = ordered(
        jnp.concatenate(mixed_mine, axis=1), jnp.concatenate([sent_one, sent_two], axis=1), 1
    )
    mixed, up_two, down_two = lax.optimization_barrier((mixed, up_two, down_two))
    up_three, down_three = line_up(up_two), line_down(down_two)
    inputs = tokens.astype(F32)
    attn = jnp.dot(mixed, output_full, preferred_element_type=F32)
    middle = inputs + BRANCH_SCALE * attn
    normed_ffn = rms_norm(middle, gain_two).astype(BF16)

    normed_ffn = after(normed_ffn, *grad_far)
    row_near = near_pieces(normed_ffn, normed_ffn)
    row_far = far_pieces(*row_near)
    slots = [up_three, up_two, up_one, own_part, down_one, down_two, down_three]
    row_pieces = with_cores(normed_ffn, *row_near, *row_far)
    grad_pieces = with_cores(*after((grad_rows, *grad_near, *grad_far), row_near[0]))
    place = line.astype(jnp.int32)[None]
    far = run_experts(FAR_TILES, place, row_pieces, grad_pieces, slots, select, 0, ())
    far_back = over_cores(far[2], far[3]).astype(BF16)
    back_y, back_x = far_links(far_back)
    near = run_experts(
        NEAR_TILES, after(place, far_back), row_pieces, grad_pieces, slots, select, 4, far[4:]
    )
    hid_a, hid_b, du_a, du_b, all_rows, all_grads = near[4:]

    def weight_grads(rows, grads, grad_both, hidden):
        inner = contract(rows, grad_both, 0, 0)
        outer = contract(grads, hidden, 0, 0) * BRANCH_SCALE
        return [
            jnp.concatenate(
                [inner[:, 2 * half * i : 2 * half * (i + 1)], outer[:, half * i : half * (i + 1)]],
                axis=1,
            ).astype(BF16)
            for i in range(2)
        ]

    rows_early, grads_early, back_y, back_x = lax.optimization_barrier(
        (all_rows, all_grads, back_y, back_x)
    )
    outer_grads = weight_grads(rows_early, grads_early, du_a, hid_a)
    grads_of = dict(zip(SLOT_ORDER[:2], outer_grads))
    far_line = (line_up(outer_grads[1]), line_down(outer_grads[0]))
    near_back = over_cores(after(near[2], *outer_grads), near[3])
    first, second = near_links(near_back, back_y, back_x)
    rows_late, grads_late = after((all_rows, all_grads), first, second)
    inner_grads = weight_grads(rows_late, grads_late, du_b, hid_b)
    grads_of.update(zip(SLOT_ORDER[2:], inner_grads))
    first, second = swap_seq(first), swap_y(second)
    near_back = after(near_back, *inner_grads)
    grad_normed_ffn = own_sum(near_back, back_y, back_x, first, second)

    def line_partial(first, *rest):
        value = grads_of[first]
        for where, expert in enumerate(rest):
            value = jnp.where(line > where, grads_of[expert], value)
        return value.astype(F32)

    def line_step(step, arrived):
        up, down = arrived
        last = LINE - 1
        right = line_partial(*range(last - step, LINE)) + up.astype(F32)
        left = grads_of[step]
        for where in range(step):
            left = jnp.where(line < last - where, grads_of[step - 1 - where], left)
        left = left.astype(F32) + down.astype(F32)
        return right.astype(BF16), left.astype(BF16)

    grad_final = cotangent.astype(F32)
    grad_norm, grad_gain_two = norm_back(middle, gain_two, grad_normed_ffn)
    grad_middle = grad_final + grad_norm
    grad_attn = (BRANCH_SCALE * grad_middle).astype(BF16)
    grad_mixed = contract(grad_attn, output_full, 1, 1).astype(BF16)
    grad_w_output = contract(mixed, grad_attn, 0, 0)
    grad_other = swap_seq(half_of(grad_mixed, 1 - seq))
    far_f, far_f_other, near_f, near_f_other = after(
        (far[0], far[1], near[0], near[1]), grad_mixed
    )
    far_ffn = over_cores(far_f, far_f_other).astype(BF16)
    ffn_y, ffn_x = far_links(far_ffn)
    near_ffn = over_cores(near_f, near_f_other)
    right, left = line_step(1, far_line)
    grad_other = after(grad_other, right, left, far_ffn, grad_w_output)
    grad_sorted = to_order(half_of(grad_mixed, seq), grad_other)
    mid_line = (line_up(right), line_down(left))
    grad_query, grad_keys, grad_values = attend_back(
        query,
        keys,
        values,
        grad_sorted,
        jnp.concatenate([levels_one, levels_two], axis=0),
        start_column,
        cos,
        sin,
    )
    (grad_query, grad_keys, grad_values), mid_line, ffn_y, ffn_x = lax.optimization_barrier(
        ((grad_query, grad_keys, grad_values), mid_line, ffn_y, ffn_x)
    )
    right, left = line_step(2, mid_line)
    last_first = (line_up(right[:cut]), line_down(left[:cut]))
    first_ffn, second_ffn = near_links(near_ffn, ffn_y, ffn_x)
    first_ffn, second_ffn = swap_seq(first_ffn), swap_y(second_ffn)
    ffn = own_sum(near_ffn, ffn_y, ffn_x, first_ffn, second_ffn)
    output = (middle + BRANCH_SCALE * ffn).astype(BF16)
    grads_qkv = after((grad_query, grad_keys, grad_values), right, left)
    wide = qkv_grad(normed, grads_qkv, grad_gain_two[None, :], shard)


    def chosen(value, which, axis):
        return lax.dynamic_index_in_dim(value, which, axis=axis, keepdims=False)

    summed_output = lax.psum_scatter(
        grad_w_output.astype(BF16), ("seq", "dp"), scatter_dimension=0, tiled=True
    )
    kept = chosen(wide, core, 0).astype(F32)
    kept = kept + swap_core(chosen(wide, 1 - core, 0)).astype(F32)
    grads_late = after(grads_qkv, kept)
    grad_normed, sent_normed = token_grad(
        grads_late, w_qkv, own_places[:, None], other_places[:, None]
    )
    kept, sent_normed = lax.optimization_barrier((kept, sent_normed))
    right_late, left_late = after((right[cut:], left[cut:]), last_first, sent_normed)
    last_late = (line_up(right_late), line_down(left_late))
    grad_normed = grad_normed.astype(F32) + swap_seq(sent_normed).astype(F32)
    scale = lax.rsqrt(jnp.mean(inputs * inputs, axis=-1, keepdims=True) + EPSILON)
    unit = inputs * scale
    scaled = grad_normed * gain_one
    inner = jnp.mean(scaled * unit, axis=-1, keepdims=True)
    grad_tokens = grad_middle + scale * (scaled - unit * inner)
    next_kept = chosen(kept, row_of, 0)
    next_kept = next_kept + swap_y(chosen(kept, 1 - row_of, 0).astype(BF16)).astype(F32)
    next_kept, last_first, last_late, summed_output = lax.optimization_barrier(
        (next_kept, last_first, last_late, summed_output)
    )
    own_grads = line_partial(*range(LINE))
    part_grads = jnp.concatenate(
        [
            own + up.astype(F32) + down.astype(F32)
            for own, (up, down) in ((own_grads[:cut], last_first), (own_grads[cut:], last_late))
        ],
        axis=0,
    ).astype(BF16)
    same_grads = jnp.where(first_core, part_grads[:, :half], part_grads[:, half : 2 * half])
    cross_grads = jnp.where(first_core, part_grads[:, half : 2 * half], part_grads[:, :half])
    same_grads = jnp.concatenate([same_grads, part_grads[:, 2 * half :]], axis=1)
    next_kept, same_grads, cross_grads = lax.optimization_barrier(
        (next_kept, same_grads, cross_grads)
    )
    same = both_axes(same_grads, straight)
    cross = both_axes(cross_grads, crossed_back)
    sent_lines = [
        swap_dp(chosen(next_kept, line ^ step, 1).astype(BF16), 4 * step) for step in range(1, LINE)
    ]
    summed = chosen(next_kept, line, 1) + sum(value.astype(F32) for value in sent_lines)
    summed, same, cross = lax.optimization_barrier((summed, same, cross))
    grad_w_in = ordered(same[:, :half], cross, 1)
    grad_w_out = same[:, half:].T
    kept_rows = chosen(summed, seq, 0)
    sent_rows = swap_seq(chosen(summed, 1 - seq, 0).astype(BF16)).astype(F32)
    cuts = (q_width, q_width + kv_width, qkv_width)
    pieces = [
        (a, b) for a, b in zip(jnp.split(kept_rows, cuts, axis=1), jnp.split(sent_rows, cuts, axis=1))
    ]
    grad_projections = [ordered(a, b, 1) for a, b in pieces[:3]]
    grad_gain_ffn = (pieces[3][0] + pieces[3][1])[:, 0]
    grad_gain_attn = sum(
        jnp.sum(grad * weight.astype(F32), axis=1)
        for grad, weight in zip(grad_projections, projections)
    ) / gain_attn.astype(F32)
    return (
        output,
        grad_tokens,
        grad_projections[0],
        grad_projections[1],
        grad_projections[2],
        summed_output.astype(F32),
        grad_gain_attn,
        grad_gain_ffn,
        grad_w_in.astype(F32)[None],
        grad_w_out.astype(F32)[None],
    )


def solution(mesh):
    placed = (
        P(("seq", "dp"), None),
        P(("seq", "dp"), None),
        P("dp", None),
        P("dp", None),
        P(("seq", "dp"), None),
        P(("seq", "dp"), None),
        P(("seq", "dp"), None),
        P(("seq", "dp"), None),
        P(("seq", "dp"), None),
        P(("seq", "dp"), None),
        P(("seq", "dp")),
        P(("seq", "dp")),
        P("dp", None, "seq"),
        P("dp", "seq", None),
    )
    return jax.shard_map(
        shards_plane if in_planes(mesh) else shards_general,
        mesh=mesh,
        in_specs=placed,
        out_specs=(
            P(("seq", "dp"), None),
            P(("seq", "dp"), None),
            P(("seq", "dp"), None),
            P(("seq", "dp"), None),
            P(("seq", "dp"), None),
            P(("seq", "dp"), None),
            P(("seq", "dp")),
            P(("seq", "dp")),
            P("dp", None, "seq"),
            P("dp", "seq", None),
        ),
        check_vma=False,
    )
```

```python
import functools

import jax
import jax.numpy as jnp
from jax import lax
from jax.experimental import pallas as pl
from jax.experimental.pallas import tpu as pltpu
from jax.sharding import PartitionSpec as P

QHEADS = 24
KVHEADS = 8
HDIM = 64
FF = 512
TOP = 8


EPSILON = 1e-06
BRANCH_SCALE = 0.22
SCORE_SCALE = 1.0 / 64.0
THETA = 10000.0


def rms_norm(value, gain):
    return value * lax.rsqrt(jnp.mean(value * value, axis=-1, keepdims=True) + EPSILON) * gain


def local_places(placing, seq_lengths):
    ends = jnp.cumsum(seq_lengths)
    segment = jnp.sum((placing[:, None] >= ends[None, :]).astype(jnp.int32), axis=1)
    starts = ends - seq_lengths
    member = segment[:, None] == jnp.arange(seq_lengths.shape[0], dtype=jnp.int32)[None, :]
    start_of = jnp.sum(jnp.where(member, starts[None, :], 0), axis=1)
    return (segment, placing - start_of)


def rotate(values, place, direction):
    half = values.shape[-1] // 2
    freqs = jnp.power(THETA, -jnp.arange(half, dtype=jnp.float32) * 2.0 / values.shape[-1])
    angles = place.astype(jnp.float32)[:, None] * freqs[None, :]
    cosine = jnp.cos(angles)[:, None, :]
    sine = direction * jnp.sin(angles)[:, None, :]
    first = values[..., :half]
    second = values[..., half:]
    return jnp.concatenate(
        [first * cosine - second * sine, second * cosine + first * sine], axis=-1
    )


def shards_general(
    tokens,
    cotangent,
    positions,
    lengths,
    routes,
    logits,
    w_query,
    w_key,
    w_value,
    w_output,
    gain_attn,
    gain_ffn,
    w_in,
    w_out,
):
    seq_count = lax.axis_size("seq")
    data_count = lax.axis_size("dp")
    tok_count = tokens.shape[0]
    group_len = positions.shape[1]
    local_experts = w_in.shape[0]
    experts_all = local_experts * data_count
    capacity = min(tok_count, 5 * tok_count * TOP // (4 * experts_all))
    heads_local = QHEADS // seq_count
    kv_local = KVHEADS // seq_count
    ratio = QHEADS // KVHEADS
    width = tokens.shape[1]
    query_full, key_full, value_full, output_full, gain_one, gain_two = (
        lax.all_gather(w_query, ("seq", "dp"), axis=0, tiled=True),
        lax.all_gather(w_key, ("seq", "dp"), axis=0, tiled=True),
        lax.all_gather(w_value, ("seq", "dp"), axis=0, tiled=True),
        lax.all_gather(w_output, ("seq", "dp"), axis=0, tiled=True),
        lax.all_gather(gain_attn, ("seq", "dp"), axis=0, tiled=True),
        lax.all_gather(gain_ffn, ("seq", "dp"), axis=0, tiled=True),
    )
    in_full, out_full = (
        lax.all_gather(w_in, "seq", axis=2, tiled=True),
        lax.all_gather(w_out, "seq", axis=1, tiled=True),
    )
    gain_one = gain_one.astype(jnp.float32)
    gain_two = gain_two.astype(jnp.float32)
    segment, place = local_places(positions[0], lengths[0])
    my_start = lax.axis_index("seq") * tok_count
    my_place = lax.dynamic_slice_in_dim(place, my_start, tok_count)
    inputs = tokens.astype(jnp.float32)
    normed = rms_norm(inputs, gain_one).astype(jnp.bfloat16)
    query_pre = jnp.dot(normed, query_full, preferred_element_type=jnp.float32)
    key_pre = jnp.dot(normed, key_full, preferred_element_type=jnp.float32)
    query_rot = (
        rotate(query_pre.reshape(tok_count, QHEADS, HDIM), my_place, 1.0)
        .reshape(tok_count, QHEADS * HDIM)
        .astype(jnp.bfloat16)
    )
    key_rot = (
        rotate(key_pre.reshape(tok_count, KVHEADS, HDIM), my_place, 1.0)
        .reshape(tok_count, KVHEADS * HDIM)
        .astype(jnp.bfloat16)
    )
    value_low = jnp.dot(normed, value_full, preferred_element_type=jnp.float32).astype(jnp.bfloat16)
    query_heads, key_heads, value_heads = (
        lax.all_to_all(query_rot, "seq", split_axis=1, concat_axis=0, tiled=True),
        lax.all_to_all(key_rot, "seq", split_axis=1, concat_axis=0, tiled=True),
        lax.all_to_all(value_low, "seq", split_axis=1, concat_axis=0, tiled=True),
    )
    keys_three = key_heads.reshape(group_len, kv_local, HDIM)
    values_three = value_heads.reshape(group_len, kv_local, HDIM)
    length = min(512, group_len)
    count = group_len // length

    def scores_of(query_block, seg_block, place_block):
        grouped = query_block.reshape(length, kv_local, ratio, HDIM)
        raw_scores = (
            jnp.einsum("qgrd,kgd->grqk", grouped, keys_three, preferred_element_type=jnp.float32)
            * SCORE_SCALE
        )
        allowed = (seg_block[:, None] == segment[None, :]) & (
            place[None, :] <= place_block[:, None]
        )
        return jnp.where(allowed[None, None], raw_scores, -1e30)

    def forward_block(pieces):
        query_block, seg_block, place_block = pieces
        scores = scores_of(query_block, seg_block, place_block)
        highest = jnp.max(scores, axis=-1, keepdims=True)
        expon = jnp.exp(scores - highest)
        totals = jnp.sum(expon, axis=-1, keepdims=True)
        probs = expon / totals
        mixed = jnp.einsum(
            "grqk,kgd->qgrd",
            probs.astype(jnp.bfloat16),
            values_three,
            preferred_element_type=jnp.float32,
        )
        return (
            mixed.reshape(length, heads_local * HDIM).astype(jnp.bfloat16),
            highest + jnp.log(totals),
            probs,
        )

    query_blocks = query_heads.reshape(count, length, heads_local * HDIM)
    seg_blocks = segment.reshape(count, length)
    place_blocks = place.reshape(count, length)
    block_args = (query_blocks, seg_blocks, place_blocks)

    def forward_light(pieces):
        mixed, lse_part, unused_probs = forward_block(pieces)
        return (mixed, lse_part)

    mixed_blocks, lse_blocks = lax.map(forward_light, block_args)
    mixed_heads = mixed_blocks.reshape(group_len, heads_local * HDIM)
    mixed_tokens = lax.all_to_all(mixed_heads, "seq", split_axis=0, concat_axis=1, tiled=True)
    attn = jnp.dot(mixed_tokens, output_full, preferred_element_type=jnp.float32)
    middle = inputs + BRANCH_SCALE * attn
    normed_ffn = rms_norm(middle, gain_two).astype(jnp.bfloat16)
    chosen = routes.reshape(-1)
    onehot = (chosen[:, None] == jnp.arange(experts_all, dtype=jnp.int32)[None, :]).astype(
        jnp.int32
    )
    ranking = jnp.sum(jnp.cumsum(onehot, axis=0) * onehot, axis=1) - 1
    target = chosen * capacity + ranking
    token_of = jnp.arange(tok_count * TOP, dtype=jnp.int32) // TOP
    gates = jax.nn.softmax(logits, axis=-1)
    source = jnp.full((experts_all * capacity,), tok_count, jnp.int32).at[target].set(token_of)
    slot_gate = jnp.zeros((experts_all * capacity,), jnp.float32).at[target].set(gates.reshape(-1))
    padded = jnp.concatenate([normed_ffn, jnp.zeros((1, width), jnp.bfloat16)], axis=0)
    outgoing = padded[source].reshape(data_count, local_experts * capacity, width)

    def expert_layout(arrived):
        return jnp.swapaxes(
            arrived.reshape(data_count, local_experts, capacity, width), 0, 1
        ).reshape(local_experts, data_count * capacity, width)

    def home_layout(values):
        return jnp.swapaxes(
            values.reshape(local_experts, data_count, capacity, width), 0, 1
        ).reshape(data_count, local_experts * capacity, width)

    def expert_forward(expert_rows):
        both = jnp.einsum("erd,edf->erf", expert_rows, in_full, preferred_element_type=jnp.float32)
        hidden = (jax.nn.silu(both[..., :FF]) * both[..., FF:]).astype(jnp.bfloat16)
        return (both, hidden)

    expert_rows = expert_layout(
        lax.all_to_all(outgoing, "dp", split_axis=0, concat_axis=0, tiled=True)
    )
    both, hidden = expert_forward(expert_rows)
    result = jnp.einsum(
        "erf,efd->erd", hidden, out_full, preferred_element_type=jnp.float32
    ).astype(jnp.bfloat16)
    returned = lax.all_to_all(
        home_layout(result), "dp", split_axis=0, concat_axis=0, tiled=True
    ).reshape(experts_all * capacity, width)
    picked = returned[target].reshape(tok_count, TOP, width).astype(jnp.float32)
    ffn = jnp.sum(picked * gates[:, :, None], axis=1)
    final = middle + BRANCH_SCALE * ffn
    output = final.astype(jnp.bfloat16)
    grad_final = cotangent.astype(jnp.float32)
    padded_grad = jnp.concatenate(
        [BRANCH_SCALE * grad_final, jnp.zeros((1, width), jnp.float32)], axis=0
    )
    grad_slots = (slot_gate[:, None] * padded_grad[source]).astype(jnp.bfloat16)
    grad_result = expert_layout(
        lax.all_to_all(
            grad_slots.reshape(data_count, local_experts * capacity, width),
            "dp",
            split_axis=0,
            concat_axis=0,
            tiled=True,
        )
    )
    rows_back = expert_layout(
        lax.all_to_all(outgoing, "dp", split_axis=0, concat_axis=0, tiled=True)
    )
    both_back, hidden_back = expert_forward(rows_back)
    grad_hidden = jnp.einsum(
        "erd,efd->erf", grad_result, out_full, preferred_element_type=jnp.float32
    )
    gate_part = both_back[..., :FF]
    up_part = both_back[..., FF:]
    sigma = jax.nn.sigmoid(gate_part)
    grad_gate = grad_hidden * up_part * sigma * (1.0 + gate_part * (1.0 - sigma))
    grad_up = grad_hidden * gate_part * sigma
    grad_both = jnp.concatenate([grad_gate, grad_up], axis=-1).astype(jnp.bfloat16)
    grad_out_local = jnp.einsum(
        "erf,erd->efd", hidden_back, grad_result, preferred_element_type=jnp.float32
    )
    grad_in_local = jnp.einsum(
        "erd,erf->edf", rows_back, grad_both, preferred_element_type=jnp.float32
    )
    grad_rows = jnp.einsum(
        "erf,edf->erd", grad_both, in_full, preferred_element_type=jnp.float32
    ).astype(jnp.bfloat16)
    grad_home = lax.all_to_all(
        home_layout(grad_rows), "dp", split_axis=0, concat_axis=0, tiled=True
    ).reshape(experts_all * capacity, width)
    grad_normed_ffn = jnp.sum(
        grad_home[target].reshape(tok_count, TOP, width).astype(jnp.float32), axis=1
    )
    grad_w_in, grad_w_out = (
        lax.psum_scatter(
            grad_in_local.astype(jnp.bfloat16), "seq", scatter_dimension=2, tiled=True
        ).astype(jnp.float32),
        lax.psum_scatter(
            grad_out_local.astype(jnp.bfloat16), "seq", scatter_dimension=1, tiled=True
        ).astype(jnp.float32),
    )
    unused_norm, norm_pull = jax.vjp(rms_norm, middle, gain_two)
    grad_middle_norm, grad_gain_two = norm_pull(grad_normed_ffn)
    grad_middle = grad_final + grad_middle_norm
    grad_attn = (BRANCH_SCALE * grad_middle).astype(jnp.bfloat16)
    grad_w_output = jnp.einsum(
        "te,td->ed", mixed_tokens, grad_attn, preferred_element_type=jnp.float32
    )
    grad_mixed = jnp.einsum(
        "td,ed->te", grad_attn, output_full, preferred_element_type=jnp.float32
    ).astype(jnp.bfloat16)
    grad_mixed_heads = lax.all_to_all(grad_mixed, "seq", split_axis=1, concat_axis=0, tiled=True)
    grad_blocks = grad_mixed_heads.reshape(count, length, heads_local * HDIM)
    back_args = (query_blocks, seg_blocks, place_blocks, lse_blocks, grad_blocks)

    def backward_block(carry, pieces):
        grad_keys, grad_values = carry
        query_block, seg_block, place_block, lse_block, grad_block = pieces[:5]
        probs = jnp.exp(scores_of(query_block, seg_block, place_block) - lse_block)
        grad_out = grad_block.reshape(length, kv_local, ratio, HDIM)
        grad_probs = jnp.einsum(
            "qgrd,kgd->grqk", grad_out, values_three, preferred_element_type=jnp.float32
        )
        grad_scores = (
            probs * (grad_probs - jnp.sum(probs * grad_probs, axis=-1, keepdims=True))
        ).astype(jnp.bfloat16)
        grad_query = SCORE_SCALE * jnp.einsum(
            "grqk,kgd->qgrd", grad_scores, keys_three, preferred_element_type=jnp.float32
        )
        grouped = query_block.reshape(length, kv_local, ratio, HDIM)
        grad_keys = grad_keys + SCORE_SCALE * jnp.einsum(
            "grqk,qgrd->kgd", grad_scores, grouped, preferred_element_type=jnp.float32
        )
        grad_values = grad_values + jnp.einsum(
            "grqk,qgrd->kgd",
            probs.astype(jnp.bfloat16),
            grad_out,
            preferred_element_type=jnp.float32,
        )
        return (
            (grad_keys, grad_values),
            grad_query.reshape(length, heads_local * HDIM).astype(jnp.bfloat16),
        )

    empty_keys = jnp.zeros((group_len, kv_local, HDIM), jnp.float32)
    (grad_keys, grad_values), grad_query_blocks = lax.scan(
        backward_block, (empty_keys, empty_keys), back_args
    )
    grad_query_heads = grad_query_blocks.reshape(group_len, heads_local * HDIM)
    grad_key_heads = grad_keys.reshape(group_len, kv_local * HDIM).astype(jnp.bfloat16)
    grad_value_heads = grad_values.reshape(group_len, kv_local * HDIM).astype(jnp.bfloat16)
    grad_query_tok, grad_key_tok, grad_value_tok = (
        lax.all_to_all(grad_query_heads, "seq", split_axis=0, concat_axis=1, tiled=True),
        lax.all_to_all(grad_key_heads, "seq", split_axis=0, concat_axis=1, tiled=True),
        lax.all_to_all(grad_value_heads, "seq", split_axis=0, concat_axis=1, tiled=True),
    )
    grad_query_pre = (
        rotate(grad_query_tok.astype(jnp.float32).reshape(tok_count, QHEADS, HDIM), my_place, -1.0)
        .reshape(tok_count, QHEADS * HDIM)
        .astype(jnp.bfloat16)
    )
    grad_key_pre = (
        rotate(grad_key_tok.astype(jnp.float32).reshape(tok_count, KVHEADS, HDIM), my_place, -1.0)
        .reshape(tok_count, KVHEADS * HDIM)
        .astype(jnp.bfloat16)
    )
    grad_w_query = jnp.einsum(
        "td,te->de", normed, grad_query_pre, preferred_element_type=jnp.float32
    )
    grad_w_key = jnp.einsum("td,te->de", normed, grad_key_pre, preferred_element_type=jnp.float32)
    grad_w_value = jnp.einsum(
        "td,te->de", normed, grad_value_tok, preferred_element_type=jnp.float32
    )
    grad_normed = jnp.einsum(
        "te,de->td", grad_query_pre, query_full, preferred_element_type=jnp.float32
    )
    grad_normed = grad_normed + jnp.einsum(
        "te,de->td", grad_key_pre, key_full, preferred_element_type=jnp.float32
    )
    grad_normed = grad_normed + jnp.einsum(
        "te,de->td", grad_value_tok, value_full, preferred_element_type=jnp.float32
    )
    unused_first, first_pull = jax.vjp(rms_norm, inputs, gain_one)
    grad_inputs_norm, grad_gain_one = first_pull(grad_normed)
    grad_tokens = grad_middle + grad_inputs_norm
    summed = (
        lax.psum_scatter(grad_w_query, ("seq", "dp"), scatter_dimension=0, tiled=True),
        lax.psum_scatter(grad_w_key, ("seq", "dp"), scatter_dimension=0, tiled=True),
        lax.psum_scatter(grad_w_value, ("seq", "dp"), scatter_dimension=0, tiled=True),
        lax.psum_scatter(grad_w_output, ("seq", "dp"), scatter_dimension=0, tiled=True),
        lax.psum_scatter(grad_gain_one, ("seq", "dp"), scatter_dimension=0, tiled=True),
        lax.psum_scatter(grad_gain_two, ("seq", "dp"), scatter_dimension=0, tiled=True),
    )
    return (
        output,
        grad_tokens,
        summed[0],
        summed[1],
        summed[2],
        summed[3],
        summed[4],
        summed[5],
        grad_w_in,
        grad_w_out,
    )


BF16 = jnp.bfloat16
F32 = jnp.float32
LINE = 4
PAD = 128
VMEM_BYTES = 60 * 1024 * 1024


def in_planes(mesh):
    return mesh.shape["seq"] == 2 and mesh.shape["dp"] == 4 * LINE


def swap_seq(value):
    return lax.ppermute(value, "seq", [(0, 1), (1, 0)])


def swap_dp(value, mask):
    return lax.ppermute(value, "dp", [(i, i ^ mask) for i in range(4 * LINE)])


def swap_core(value):
    return swap_dp(value, 1)


def swap_y(value):
    return swap_dp(value, 2)


def line_up(value):
    return lax.ppermute(value, "dp", [(i, i + 4) for i in range(4 * LINE - 4)])


def line_down(value):
    return lax.ppermute(value, "dp", [(i, i - 4) for i in range(4, 4 * LINE)])


def after(value, *others):
    return lax.optimization_barrier((value,) + others)[0]


def line_scatter(take, place):
    up = down = None
    for step in range(LINE - 1):
        far = jnp.minimum(LINE - 1 - step + place, LINE - 1)
        near = jnp.maximum(step - LINE + 1 + place, 0)
        right, left = take(far), take(near)
        if up is not None:
            right = right + up.astype(F32)
            left = left + down.astype(F32)
        up = line_up(right.astype(BF16))
        down = line_down(left.astype(BF16))
    return take(place) + up.astype(F32) + down.astype(F32)


def near_pieces(own, own_x):
    return swap_seq(own_x), swap_y(own)


def far_pieces(near_x, near_y):
    half = near_x.shape[0] // 2
    return swap_y(near_x[:half]), swap_seq(near_y[half:])


def with_cores(*pieces):
    return pieces + tuple(swap_core(piece) for piece in pieces)


def over_cores(mine, others):
    return mine.astype(F32) + swap_core(others).astype(F32)


def far_links(far):
    half = far.shape[0] // 2
    return swap_y(far[:half]), swap_seq(far[half:])


def near_links(near, from_y, from_x):
    half = from_y.shape[0] // 2
    first = (near[:half] + from_y[half:].astype(F32)).astype(BF16)
    second = (near[half : 2 * half] + from_x[half:].astype(F32)).astype(BF16)
    return first, second


def own_sum(near, from_y, from_x, first, second):
    half = from_y.shape[0] // 2
    low = near[2 * half : 3 * half] + from_y[:half].astype(F32) + first.astype(F32)
    high = near[3 * half :] + from_x[:half].astype(F32) + second.astype(F32)
    return jnp.concatenate([low, high], axis=0)


def turned(values, cos, sin, direction):
    lanes = values.shape[1]
    place = lax.broadcasted_iota(jnp.int32, values.shape, 1) % HDIM
    swapped = jnp.where(
        place < HDIM // 2,
        pltpu.roll(values, lanes - HDIM // 2, 1),
        pltpu.roll(values, HDIM // 2, 1),
    )
    times = lanes // cos.shape[1]
    cos = jnp.concatenate([cos] * times, axis=1)
    sin = jnp.concatenate([sin] * times, axis=1)
    if direction > 0:
        return values * cos + swapped * sin
    return values * cos - swapped * sin


def qkv_kernel(x_ref, gain_ref, w_ref, cos_ref, sin_ref, h_ref, q_ref, k_ref, v_ref):
    value = x_ref[...].astype(F32)
    scale = lax.rsqrt(jnp.mean(value * value, axis=-1, keepdims=True) + EPSILON)
    normed = (value * scale * gain_ref[...]).astype(BF16)
    h_ref[...] = normed
    both = jnp.dot(normed, w_ref[...], preferred_element_type=F32)
    q_width, kv_heads = q_ref.shape[1], k_ref.shape[0]
    kv_width = kv_heads * HDIM
    spun = turned(both[:, : q_width + kv_width], cos_ref[...], sin_ref[...], 1)
    q_ref[...] = (spun[:, :q_width] * SCORE_SCALE).astype(BF16)
    for head in range(kv_heads):
        low = q_width + head * HDIM
        k_ref[head] = spun[:, low : low + HDIM].astype(BF16)
        low = low + kv_width
        v_ref[head] = both[:, low : low + HDIM].astype(BF16)


def project(x_sorted, gain, weights, cos, sin, q_width, kv_heads):
    rows, width = x_sorted.shape
    tile = 256
    columns = q_width + 2 * kv_heads * HDIM

    def row_block(lanes):
        return pl.BlockSpec((tile, lanes), lambda i: (i, 0))

    heads = pl.BlockSpec((kv_heads, tile, HDIM), lambda i: (0, i, 0))
    return pl.pallas_call(
        qkv_kernel,
        grid=(rows // tile,),
        in_specs=[
            row_block(width),
            pl.BlockSpec((1, width), lambda i: (0, 0)),
            pl.BlockSpec((width, columns), lambda i: (0, 0)),
            row_block(cos.shape[1]),
            row_block(cos.shape[1]),
        ],
        out_specs=[row_block(width), row_block(q_width), heads, heads],
        out_shape=[
            jax.ShapeDtypeStruct((rows, width), BF16),
            jax.ShapeDtypeStruct((rows, q_width), BF16),
            jax.ShapeDtypeStruct((kv_heads, rows, HDIM), BF16),
            jax.ShapeDtypeStruct((kv_heads, rows, HDIM), BF16),
        ],
        compiler_params=pltpu.CompilerParams(vmem_limit_bytes=VMEM_BYTES),
        cost_estimate=pl.CostEstimate(
            flops=rows * width * columns // 8,
            bytes_accessed=rows * width + width * columns,
            transcendentals=rows,
        ),
        name="project",
    )(x_sorted, gain, weights, cos, sin)


def token_grad_kernel(dq_ref, dk_ref, dv_ref, w_ref, own_ref, other_ref, mine_ref, sent_ref):
    q_width, kv_width = dq_ref.shape[1], dk_ref.shape[1]
    cuts = (0, q_width, q_width + kv_width, q_width + 2 * kv_width)
    grad = contract(dq_ref[...], w_ref[:, cuts[0] : cuts[1]], 1, 1)
    grad = grad + contract(dk_ref[...], w_ref[:, cuts[1] : cuts[2]], 1, 1)
    grad = (grad + contract(dv_ref[...], w_ref[:, cuts[2] : cuts[3]], 1, 1)).astype(BF16)
    for place_ref, out_ref in ((other_ref, sent_ref), (own_ref, mine_ref)):
        shape = (place_ref.shape[0], grad.shape[0])
        picked = lax.broadcasted_iota(jnp.int32, shape, 1) == place_ref[...]
        picked = jnp.where(picked, 1.0, 0.0).astype(BF16)
        out_ref[...] = jnp.dot(picked, grad, preferred_element_type=F32).astype(BF16)


def token_grad(grads, weights, own_places, other_places):
    rows, count = grads[0].shape[0], own_places.shape[0]
    width = weights.shape[0]
    columns = sum(grad.shape[1] for grad in grads)
    tile = width // 3

    def whole(array):
        return pl.BlockSpec(array.shape, lambda i: (0, 0))

    block = pl.BlockSpec((count, tile), lambda i: (0, i))
    return pl.pallas_call(
        token_grad_kernel,
        grid=(3,),
        in_specs=[whole(grad) for grad in grads]
        + [pl.BlockSpec((tile, columns), lambda i: (i, 0)), whole(own_places), whole(other_places)],
        out_specs=[block, block],
        out_shape=[jax.ShapeDtypeStruct((count, width), BF16)] * 2,
        compiler_params=pltpu.CompilerParams(vmem_limit_bytes=VMEM_BYTES),
        cost_estimate=pl.CostEstimate(
            flops=rows * width * columns // 8, bytes_accessed=rows * width, transcendentals=0
        ),
        name="token_grad",
    )(*grads, weights, own_places, other_places)


Q_TILE = 256


def windows(rows):
    longest = rows // 2
    for start in range(0, rows, Q_TILE):
        low = max(0, start - longest + 1) // Q_TILE * Q_TILE
        yield start, low, start + Q_TILE


def allowed_keys(start_ref, row, low, high):
    shape = (Q_TILE, high - low)
    rows = lax.broadcasted_iota(jnp.int32, shape, 0) + row
    keys = lax.broadcasted_iota(jnp.int32, shape, 1) + low
    return (keys <= rows) & (keys >= start_ref[row : row + Q_TILE, :])


def contract(left, right, left_dim, right_dim):
    return lax.dot_general(
        left, right, (((left_dim,), (right_dim,)), ((), ())), preferred_element_type=F32
    )


def masked_scores(query, keys, allowed):
    return jnp.where(allowed, contract(query, keys, 1, 1), -1e30)


def attend_kernel(base, q_ref, k_ref, v_ref, start_ref, o_ref, level_ref):
    pair = pl.program_id(0) + base
    ratio = QHEADS // KVHEADS
    for row, low, high in windows(q_ref.shape[0]):
        allowed = allowed_keys(start_ref, row, low, high)
        for side in range(2):
            head = (2 * pair + side) // ratio
            lanes = slice(side * HDIM, (side + 1) * HDIM)
            scores = masked_scores(
                q_ref[row : row + Q_TILE, lanes], k_ref[head, low:high, :], allowed
            )
            highest = jnp.max(scores, axis=-1, keepdims=True)
            expon = jnp.exp(scores - highest)
            total = jnp.sum(expon, axis=-1, keepdims=True)
            level_ref[0, row : row + Q_TILE, side : side + 1] = highest + jnp.log(total)
            probs = expon * (1.0 / total)
            mixed = contract(probs.astype(BF16), v_ref[head, low:high, :], 1, 0)
            o_ref[row : row + Q_TILE, lanes] = mixed.astype(BF16)


def attention_cost(rows, heads, products):
    area = sum(Q_TILE * (high - low) for _, low, high in windows(rows))
    return pl.CostEstimate(
        flops=products * heads * area * 16,
        bytes_accessed=8 * rows * heads * HDIM,
        transcendentals=heads * area,
    )


def attend(query, keys, values, starts, base, pairs):
    rows = query.shape[0]
    pair_block = pl.BlockSpec((rows, 2 * HDIM), lambda j: (0, j + base))
    whole = pl.BlockSpec(keys.shape, lambda j: (0, 0, 0))
    return pl.pallas_call(
        functools.partial(attend_kernel, base),
        grid=(pairs,),
        in_specs=[pair_block, whole, whole, pl.BlockSpec((rows, 1), lambda j: (0, 0))],
        out_specs=[
            pl.BlockSpec((rows, 2 * HDIM), lambda j: (0, j)),
            pl.BlockSpec((1, rows, 2), lambda j: (j, 0, 0)),
        ],
        out_shape=[
            jax.ShapeDtypeStruct((rows, pairs * 2 * HDIM), BF16),
            jax.ShapeDtypeStruct((pairs, rows, 2), F32),
        ],
        compiler_params=pltpu.CompilerParams(vmem_limit_bytes=VMEM_BYTES),
        cost_estimate=attention_cost(rows, 2 * pairs, 2),
        name="attend",
    )(query, keys, values, starts)


def attend_back_kernel(
    q_ref, k_ref, v_ref, d_ref, level_ref, start_ref, cos_ref, sin_ref,
    dq_ref, dk_ref, dv_ref, dk_sum, dv_sum,
):
    pair = pl.program_id(0)
    ratio = QHEADS // KVHEADS

    @pl.when(pair == 0)
    def _():
        dk_sum[...] = jnp.zeros_like(dk_sum)
        dv_sum[...] = jnp.zeros_like(dv_sum)

    for row, low, high in windows(q_ref.shape[0]):
        allowed = allowed_keys(start_ref, row, low, high)
        grads = []
        for side in range(2):
            head = (2 * pair + side) // ratio
            lanes = slice(side * HDIM, (side + 1) * HDIM)
            query = q_ref[row : row + Q_TILE, lanes]
            keys = k_ref[head, low:high, :]
            probs = jnp.exp(
                masked_scores(query, keys, allowed)
                - level_ref[0, row : row + Q_TILE, side : side + 1]
            )
            grad_out = d_ref[row : row + Q_TILE, lanes]
            grad_probs = contract(grad_out, v_ref[head, low:high, :], 1, 1)
            inner = jnp.sum(probs * grad_probs, axis=-1, keepdims=True)
            grad_scores = (probs * (grad_probs - inner)).astype(BF16)
            grads.append(contract(grad_scores, keys, 1, 0) * SCORE_SCALE)
            dk_sum[head, low:high, :] += contract(grad_scores, query, 0, 0)
            dv_sum[head, low:high, :] += contract(probs.astype(BF16), grad_out, 0, 0)
        grad_query = jnp.concatenate(grads, axis=1).astype(BF16).astype(F32)
        dq_ref[row : row + Q_TILE, :] = turned(
            grad_query,
            cos_ref[row : row + Q_TILE, :],
            sin_ref[row : row + Q_TILE, :],
            -1,
        ).astype(BF16)

    @pl.when(pair == pl.num_programs(0) - 1)
    def _():
        heads = range(dk_sum.shape[0])
        grad_keys = jnp.concatenate([dk_sum[head] for head in heads], axis=1)
        grad_keys = grad_keys.astype(BF16).astype(F32)
        dk_ref[...] = turned(grad_keys, cos_ref[...], sin_ref[...], -1).astype(BF16)
        dv_ref[...] = jnp.concatenate([dv_sum[head] for head in heads], axis=1).astype(BF16)


def attend_back(query, keys, values, grad_out, levels, starts, cos, sin):
    rows, lanes = query.shape
    pairs = lanes // (2 * HDIM)
    kv_heads = keys.shape[0]
    pair_block = pl.BlockSpec((rows, 2 * HDIM), lambda j: (0, j))
    whole = pl.BlockSpec(keys.shape, lambda j: (0, 0, 0))

    def fixed(lanes_of):
        return pl.BlockSpec((rows, lanes_of), lambda j: (0, 0))

    flat = kv_heads * HDIM
    return pl.pallas_call(
        attend_back_kernel,
        grid=(pairs,),
        in_specs=[
            pair_block, whole, whole, pair_block,
            pl.BlockSpec((1, rows, 2), lambda j: (j, 0, 0)), fixed(1), fixed(2 * HDIM), fixed(2 * HDIM),
        ],
        out_specs=[pair_block, fixed(flat), fixed(flat)],
        out_shape=[
            jax.ShapeDtypeStruct(query.shape, BF16),
            jax.ShapeDtypeStruct((rows, flat), BF16),
            jax.ShapeDtypeStruct((rows, flat), BF16),
        ],
        scratch_shapes=[pltpu.VMEM(keys.shape, F32), pltpu.VMEM(keys.shape, F32)],
        compiler_params=pltpu.CompilerParams(vmem_limit_bytes=VMEM_BYTES),
        cost_estimate=attention_cost(rows, 2 * pairs, 5),
        name="attend_back",
    )(query, keys, values, grad_out, levels, starts, cos, sin)


SLOTS = 2 * LINE - 1
SLOT_ORDER = (0, 3, 1, 2)
OWN, NEAR_X, NEAR_Y, FAR_Y, FAR_X = range(5)
FAR_TILES = (((NEAR_Y, 0), (FAR_Y, 0)), ((NEAR_X, 1), (FAR_X, 0)))
NEAR_TILES = (((NEAR_X, 0), (NEAR_Y, 1)), ((OWN, 0), (OWN, 1)))


def used_pieces(tiles):
    return sorted({piece for tile in tiles for piece, _ in tile})


def experts_kernel(tiles, half_rows, place_ref, *refs):
    used = used_pieces(tiles)
    sides = 2 * len(used)
    h_pieces, g_pieces, slots = refs[:sides], refs[sides : 2 * sides], refs[2 * sides : 2 * sides + SLOTS]
    select_ref = refs[2 * sides + SLOTS]
    (
        f_mine, f_other, d_mine, d_other, hid_a, hid_b, du_a, du_b, hcopy_ref, gcopy_ref,
        w_in, w_out, h_buf, g_buf, hidden, du_all, weight_sems, row_sems,
    ) = refs[-18:]
    width = h_buf.shape[2]
    half = slots[0].shape[1] // 3
    part = 2 * half
    step = pl.program_id(0)
    steps = 2 * len(tiles)

    def weight_copies(spot, slot):
        return (
            pltpu.make_async_copy(
                slots[slot].at[:, :part],
                w_in.at[:, spot * part : (spot + 1) * part],
                weight_sems.at[0, spot],
            ),
            pltpu.make_async_copy(
                slots[slot].at[:, part:],
                w_out.at[:, spot * half : (spot + 1) * half],
                weight_sems.at[1, spot],
            ),
        )

    def row_copies(number, buffer):
        side, tile = divmod(number, len(tiles))
        copies = []
        for spot, (piece, part_of) in enumerate(tiles[tile]):
            index = side * len(used) + used.index(piece)
            for kind, (pieces, held) in enumerate(((h_pieces, h_buf), (g_pieces, g_buf))):
                copies.append(
                    pltpu.make_async_copy(
                        pieces[index].at[pl.ds(part_of * half_rows, half_rows), :],
                        held.at[buffer, pl.ds(spot * half_rows, half_rows), :],
                        row_sems.at[buffer, 2 * kind + spot],
                    )
                )
        return copies

    def fetch(wanted, buffer):
        for number in range(steps):

            @pl.when(wanted == number)
            def _():
                for copy in row_copies(number, buffer):
                    copy.start()

    buffer = step % 2

    @pl.when(step == 0)
    def _():
        fetch(step, 0)
        for spot, expert in enumerate(SLOT_ORDER):
            for slot in range(expert, expert + LINE):

                @pl.when(slot == LINE - 1 + expert - place_ref[0])
                def _():
                    for copy in weight_copies(spot, slot):
                        copy.start()

        for spot in range(LINE):
            for copy in weight_copies(spot, LINE - 1):
                copy.wait()

    @pl.when(step + 1 < steps)
    def _():
        fetch(step + 1, 1 - buffer)

    for copy in row_copies(0, buffer):
        copy.wait()

    rows = h_buf[buffer]
    grads = g_buf[buffer, :, :width]
    hcopy_ref[...] = rows
    gcopy_ref[...] = grads
    gates = jnp.dot(g_buf[buffer, :, width:], select_ref[...], preferred_element_type=F32)
    for spot in range(LINE):
        units = slice(spot * half, (spot + 1) * half)
        both = jnp.dot(
            rows, w_in[:, spot * part : (spot + 1) * part], preferred_element_type=F32
        )
        back = jnp.dot(grads, w_out[:, units], preferred_element_type=F32)
        gate = gates[:, units]
        first, second = both[:, :half], both[:, half:]
        sigma = jax.nn.sigmoid(first)
        silu = first * sigma
        hidden[:, units] = (gate * (silu * second)).astype(BF16)
        back = back * (BRANCH_SCALE * gate)
        d_first = back * second * (sigma * (1.0 + first * (1.0 - sigma)))
        d_second = back * silu
        du_all[:, spot * part : spot * part + half] = d_first.astype(BF16)
        du_all[:, spot * part + half : (spot + 1) * part] = d_second.astype(BF16)
    hid_a[...] = hidden[:, : 2 * half]
    hid_b[...] = hidden[:, 2 * half :]
    du_a[...] = du_all[:, : 2 * part]
    du_b[...] = du_all[:, 2 * part :]
    ffn = contract(hidden[...], w_out[...], 1, 1).astype(BF16)
    back_rows = contract(du_all[...], w_in[...], 1, 1).astype(BF16)

    @pl.when(step < len(tiles))
    def _():
        f_mine[...] = ffn
        d_mine[...] = back_rows

    @pl.when(step >= len(tiles))
    def _():
        f_other[...] = ffn
        d_other[...] = back_rows


def run_experts(tiles, place, row_pieces, grad_pieces, slots, select, base, kept):
    used = used_pieces(tiles)
    sides = len(row_pieces) // 2
    wanted = used + [sides + piece for piece in used]
    rows = [row_pieces[piece] for piece in wanted]
    grads = [grad_pieces[piece] for piece in wanted]
    tile, width = row_pieces[OWN].shape
    wide = grad_pieces[OWN].shape[1]
    half = slots[0].shape[1] // 3
    part = 2 * half
    count = len(tiles)
    steps = 2 * count
    total = 8 * tile

    def late(lanes):
        return pl.BlockSpec((tile, lanes), lambda i, p: (i + base, 0))

    mine = pl.BlockSpec((tile, width), lambda i, p: (jnp.minimum(i, count - 1), 0))
    others = pl.BlockSpec((tile, width), lambda i, p: (jnp.maximum(i - count, 0), 0))
    anywhere = pl.BlockSpec(memory_space=pl.ANY)
    kept = list(kept)
    lead = 1 + 2 * len(wanted) + SLOTS + 1
    partial = jax.ShapeDtypeStruct((count * tile, width), BF16)
    lanes = [2 * half, 2 * half, 2 * part, 2 * part, width, width]
    return pl.pallas_call(
        functools.partial(experts_kernel, tiles, tile // 2),
        grid_spec=pltpu.PrefetchScalarGridSpec(
            num_scalar_prefetch=1,
            grid=(steps,),
            in_specs=[anywhere] * (2 * len(wanted) + SLOTS)
            + [pl.BlockSpec(select.shape, lambda i, p: (0, 0))]
            + [anywhere] * len(kept),
            out_specs=[mine, others, mine, others] + [late(n) for n in lanes],
            scratch_shapes=[
                pltpu.VMEM((width, LINE * part), BF16),
                pltpu.VMEM((width, LINE * half), BF16),
                pltpu.VMEM((2, tile, width), BF16),
                pltpu.VMEM((2, tile, wide), BF16),
                pltpu.VMEM((tile, LINE * half), BF16),
                pltpu.VMEM((tile, LINE * part), BF16),
                pltpu.SemaphoreType.DMA((2, LINE)),
                pltpu.SemaphoreType.DMA((2, 4)),
            ],
        ),
        out_shape=[partial] * 4 + [jax.ShapeDtypeStruct((total, n), BF16) for n in lanes],
        input_output_aliases={lead + i: 4 + i for i in range(len(kept))},
        compiler_params=pltpu.CompilerParams(vmem_limit_bytes=VMEM_BYTES),
        cost_estimate=pl.CostEstimate(
            flops=steps * tile * width * LINE * (part + half) // 4,
            bytes_accessed=2 * steps * tile * (6 * width + LINE * (part + half)),
            transcendentals=steps * tile * LINE * half,
        ),
        name="experts",
    )(place, *rows, *grads, *slots, select, *kept)


def qkv_grad_kernel(h_ref, dq_ref, dk_ref, dv_ref, gain_ref, o_ref):
    shard = o_ref.shape[-2]
    rows = h_ref[...]
    low = 0
    gains = jnp.broadcast_to(gain_ref[...], (PAD, gain_ref.shape[1])).T.astype(BF16)
    parts = [contract(rows, ref[...], 0, 0).astype(BF16) for ref in (dq_ref, dk_ref, dv_ref)]
    for part in parts + [gains]:
        for block in range(h_ref.shape[1] // shard):
            place = (block % 2, block // 2 % 2, 0, block // 4)
            o_ref[place + (slice(None), slice(low, low + part.shape[1]))] = part[
                block * shard : (block + 1) * shard
            ]
        low = low + part.shape[1]


def qkv_grad(normed, grads, gain_row, shard):
    rows, width = normed.shape
    columns = sum(grad.shape[1] for grad in grads)
    tile = width // 4
    planes = tile // (4 * shard)
    return pl.pallas_call(
        qkv_grad_kernel,
        grid=(4,),
        in_specs=[pl.BlockSpec((rows, tile), lambda i: (0, i))]
        + [pl.BlockSpec(grad.shape, lambda i: (0, 0)) for grad in grads]
        + [pl.BlockSpec((1, tile), lambda i: (0, i))],
        out_specs=pl.BlockSpec(
            (2, 2, 1, planes, shard, columns + PAD), lambda i: (0, 0, i // 2, i % 2, 0, 0)
        ),
        out_shape=jax.ShapeDtypeStruct((2, 2, 2, LINE, shard, columns + PAD), BF16),
        compiler_params=pltpu.CompilerParams(vmem_limit_bytes=VMEM_BYTES),
        cost_estimate=pl.CostEstimate(
            flops=rows * width * columns // 8,
            bytes_accessed=rows * width,
            transcendentals=0,
        ),
        name="qkv_grad",
    )(normed, *grads, gain_row)


def norm_back(value, gain, grad):
    scale = lax.rsqrt(jnp.mean(value * value, axis=-1, keepdims=True) + EPSILON)
    unit = value * scale
    grad_gain = jnp.sum(grad * unit, axis=0)
    scaled = grad * gain
    inner = jnp.mean(scaled * unit, axis=-1, keepdims=True)
    return scale * (scaled - unit * inner), grad_gain


def shards_plane(
    tokens,
    cotangent,
    positions,
    lengths,
    routes,
    logits,
    w_query,
    w_key,
    w_value,
    w_output,
    gain_attn,
    gain_ffn,
    w_in,
    w_out,
):
    seq = lax.axis_index("seq")
    data = lax.axis_index("dp")
    line, row_of, core = data // 4, (data // 2) % 2, data % 2
    tok_count, width = tokens.shape
    group_len = positions.shape[1]
    shard = w_query.shape[0]
    q_width = w_query.shape[1] // 2
    kv_width = w_key.shape[1] // 2
    kv_heads = kv_width // HDIM
    first_seq = seq == 0

    def ordered(mine, theirs, axis):
        low = jnp.where(first_seq, mine, theirs)
        high = jnp.where(first_seq, theirs, mine)
        return jnp.concatenate([low, high], axis=axis)

    def half_of(weights, which):
        half = weights.shape[1] // 2
        return lax.dynamic_slice_in_dim(weights, which * half, half, axis=1)

    def both_axes(value, pairs):
        return lax.ppermute(value, ("seq", "dp"), pairs)

    def device(s, d):
        return s * 4 * LINE + d

    straight, crossed = [], []
    for s in range(2):
        for d in range(4 * LINE):
            c = d % 2
            straight.append((device(s, d), device(c, d - c + s)))
            crossed.append((device(s, d), device(c, d - c + 1 - s)))
    crossed_back = [(there, here) for here, there in crossed]
    first_core = core == 0

    projections = (w_query, w_key, w_value)
    qkv_width = q_width + 2 * kv_width
    gain_columns = jnp.pad(jnp.stack([gain_attn, gain_ffn], axis=1), ((0, 0), (0, PAD - 2)))
    mine = jnp.concatenate([half_of(w, seq) for w in projections] + [gain_columns], axis=1)
    theirs = jnp.concatenate([half_of(w, 1 - seq) for w in projections] + [gain_columns], axis=1)
    theirs = swap_seq(theirs)
    pair = jnp.stack([jnp.where(first_seq, mine, theirs), jnp.where(first_seq, theirs, mine)])
    qkv_width = q_width + 2 * kv_width
    w_qkv = lax.all_gather(pair, "dp", axis=1, tiled=True).reshape(width, qkv_width + PAD)
    output_full = lax.all_gather(w_output, ("seq", "dp"), axis=0, tiled=True)

    in_own = w_in[0]
    half = in_own.shape[1] // 2
    sent = jnp.concatenate(
        [lax.dynamic_slice_in_dim(in_own, seq * half, half, axis=1), w_out[0].T], axis=1
    )
    same = both_axes(sent, straight)
    cross = both_axes(lax.dynamic_slice_in_dim(in_own, (1 - seq) * half, half, axis=1), crossed)
    own_part = jnp.concatenate(
        [
            jnp.where(first_core, same[:, :half], cross),
            jnp.where(first_core, cross, same[:, :half]),
            same[:, half:],
        ],
        axis=1,
    )
    other_tokens = swap_seq(after(tokens, own_part))
    up_one, down_one = line_up(own_part), line_down(own_part)
    cut = width // 2

    experts_all = 4 * LINE
    gates = jax.nn.softmax(logits, axis=-1)
    named = routes[:, :, None] == jnp.arange(experts_all, dtype=jnp.int32)[None, None, :]
    gate_table = jnp.sum(jnp.where(named, gates[:, :, None], 0.0), axis=1)
    gate_high = lax.reduce_precision(gate_table, 8, 7)
    grad_rows = jnp.concatenate(
        [
            cotangent,
            gate_high.astype(BF16),
            (gate_table - gate_high).astype(BF16),
            jnp.zeros((tok_count, PAD - 2 * experts_all), BF16),
        ],
        axis=1,
    )
    grad_near = near_pieces(grad_rows, after(grad_rows, other_tokens))
    lane = jnp.arange(PAD, dtype=jnp.int32)[:, None]
    hosted = jnp.repeat(
        jnp.array(SLOT_ORDER, jnp.int32) * 4 + 2 * row_of + seq, half, total_repeat_length=LINE * half
    )
    select = ((lane % experts_all == hosted[None, :]) & (lane < 2 * experts_all)).astype(BF16)

    places = positions[0]
    ends = jnp.cumsum(lengths[0])
    ranks = jnp.arange(group_len, dtype=jnp.int32)
    reached = ranks[:, None] >= ends[None, :]
    starts = jnp.max(jnp.where(reached, ends[None, :], 0), axis=1)
    local = (ranks - starts).astype(F32)
    freqs = jnp.power(THETA, -jnp.arange(HDIM // 2, dtype=F32) * 2.0 / HDIM)
    angles = local[:, None] * freqs[None, :]
    cos, sin = jnp.cos(angles), jnp.sin(angles)
    cos = jnp.concatenate([cos, cos, cos, cos], axis=1)
    sin = jnp.concatenate([-sin, sin, -sin, sin], axis=1)
    start_column = starts[:, None]
    own_places = lax.dynamic_slice_in_dim(places, seq * tok_count, tok_count)
    other_places = lax.dynamic_slice_in_dim(places, (1 - seq) * tok_count, tok_count)
    sort_own = (ranks[:, None] == own_places[None, :]).astype(BF16)
    sort_other = (ranks[:, None] == other_places[None, :]).astype(BF16)

    def to_order(own, other):
        return (
            contract(sort_own, own, 1, 0) + contract(sort_other, other, 1, 0)
        ).astype(BF16)

    def from_order(sort, values):
        return contract(sort, values, 0, 0).astype(BF16)

    x_sorted = to_order(tokens, other_tokens)
    gains = w_qkv[:, qkv_width : qkv_width + 2].astype(F32).T
    gain_one, gain_two = gains[0], gains[1]
    x_sorted, up_one, down_one = lax.optimization_barrier((x_sorted, up_one, down_one))
    up_two, down_two = line_up(up_one), line_down(down_one)
    normed, query, keys, values = project(
        x_sorted, gain_one[None, :], w_qkv, cos, sin, q_width, kv_heads
    )
    pairs = q_width // (2 * HDIM)
    first_pairs = (pairs + 1) // 2
    mixed_one, levels_one = attend(query, keys, values, start_column, 0, first_pairs)
    sent_one = swap_seq(from_order(sort_other, mixed_one))
    query_two, grad_near_x, grad_near_y = after((query, *grad_near), mixed_one)
    grad_near = (grad_near_x, grad_near_y)
    grad_far = far_pieces(*grad_near)
    mixed_two, levels_two = attend(
        query_two, keys, values, start_column, first_pairs, pairs - first_pairs
    )
    sent_two = swap_seq(from_order(sort_other, mixed_two))
    mixed_mine = [from_order(sort_own, mixed_one), from_order(sort_own, mixed_two)]
    mixed = ordered(
        jnp.concatenate(mixed_mine, axis=1), jnp.concatenate([sent_one, sent_two], axis=1), 1
    )
    mixed, up_two, down_two = lax.optimization_barrier((mixed, up_two, down_two))
    up_three, down_three = line_up(up_two), line_down(down_two)
    inputs = tokens.astype(F32)
    attn = jnp.dot(mixed, output_full, preferred_element_type=F32)
    middle = inputs + BRANCH_SCALE * attn
    normed_ffn = rms_norm(middle, gain_two).astype(BF16)

    normed_ffn = after(normed_ffn, *grad_far)
    row_near = near_pieces(normed_ffn, normed_ffn)
    row_far = far_pieces(*row_near)
    slots = [up_three, up_two, up_one, own_part, down_one, down_two, down_three]
    row_pieces = with_cores(normed_ffn, *row_near, *row_far)
    grad_pieces = with_cores(*after((grad_rows, *grad_near, *grad_far), row_near[0]))
    place = line.astype(jnp.int32)[None]
    far = run_experts(FAR_TILES, place, row_pieces, grad_pieces, slots, select, 0, ())
    far_back = over_cores(far[2], far[3]).astype(BF16)
    back_y, back_x = far_links(far_back)
    near = run_experts(
        NEAR_TILES, after(place, far_back), row_pieces, grad_pieces, slots, select, 4, far[4:]
    )
    hid_a, hid_b, du_a, du_b, all_rows, all_grads = near[4:]

    def weight_grads(rows, grads, grad_both, hidden):
        inner = contract(rows, grad_both, 0, 0)
        outer = contract(grads, hidden, 0, 0) * BRANCH_SCALE
        return [
            jnp.concatenate(
                [inner[:, 2 * half * i : 2 * half * (i + 1)], outer[:, half * i : half * (i + 1)]],
                axis=1,
            ).astype(BF16)
            for i in range(2)
        ]

    rows_early, grads_early, back_y, back_x = lax.optimization_barrier(
        (all_rows, all_grads, back_y, back_x)
    )
    outer_grads = weight_grads(rows_early, grads_early, du_a, hid_a)
    grads_of = dict(zip(SLOT_ORDER[:2], outer_grads))
    far_line = (line_up(outer_grads[1]), line_down(outer_grads[0]))
    near_back = over_cores(after(near[2], *outer_grads), near[3])
    first, second = near_links(near_back, back_y, back_x)
    rows_late, grads_late = after((all_rows, all_grads), first, second)
    inner_grads = weight_grads(rows_late, grads_late, du_b, hid_b)
    grads_of.update(zip(SLOT_ORDER[2:], inner_grads))
    first, second = swap_seq(first), swap_y(second)
    near_back = after(near_back, *inner_grads)
    grad_normed_ffn = own_sum(near_back, back_y, back_x, first, second)

    def line_partial(first, *rest, rows=slice(None)):
        value = grads_of[first][rows]
        for where, expert in enumerate(rest):
            value = jnp.where(line > where, grads_of[expert][rows], value)
        return value.astype(F32)

    def line_step(step, arrived, rows=slice(None)):
        up, down = arrived[0][rows], arrived[1][rows]
        last = LINE - 1
        right = line_partial(*range(last - step, LINE), rows=rows) + up.astype(F32)
        left = grads_of[step][rows]
        for where in range(step):
            left = jnp.where(line < last - where, grads_of[step - 1 - where][rows], left)
        left = left.astype(F32) + down.astype(F32)
        return right.astype(BF16), left.astype(BF16)

    grad_final = cotangent.astype(F32)
    grad_norm, grad_gain_two = norm_back(middle, gain_two, grad_normed_ffn)
    grad_middle = grad_final + grad_norm
    grad_attn = (BRANCH_SCALE * grad_middle).astype(BF16)
    grad_mixed = contract(grad_attn, output_full, 1, 1).astype(BF16)
    grad_w_output = contract(mixed, grad_attn, 0, 0)
    grad_other = swap_seq(half_of(grad_mixed, 1 - seq))
    far_f, far_f_other, near_f, near_f_other = after(
        (far[0], far[1], near[0], near[1]), grad_mixed
    )
    far_ffn = over_cores(far_f, far_f_other).astype(BF16)
    ffn_y, ffn_x = far_links(far_ffn)
    near_ffn = over_cores(near_f, near_f_other)
    right, left = line_step(1, far_line)
    grad_other = after(grad_other, right, left, far_ffn, grad_w_output)
    grad_sorted = to_order(half_of(grad_mixed, seq), grad_other)
    mid_line = (line_up(right), line_down(left))
    grad_query, grad_keys, grad_values = attend_back(
        query,
        keys,
        values,
        grad_sorted,
        jnp.concatenate([levels_one, levels_two], axis=0),
        start_column,
        cos,
        sin,
    )
    (grad_query, grad_keys, grad_values), mid_line, ffn_y, ffn_x = lax.optimization_barrier(
        ((grad_query, grad_keys, grad_values), mid_line, ffn_y, ffn_x)
    )
    right, left = line_step(2, mid_line, slice(0, cut))
    last_first = (line_up(right), line_down(left))
    first_ffn, second_ffn = near_links(near_ffn, ffn_y, ffn_x)
    first_ffn, second_ffn = swap_seq(first_ffn), swap_y(second_ffn)
    ffn = own_sum(near_ffn, ffn_y, ffn_x, first_ffn, second_ffn)
    output = (middle + BRANCH_SCALE * ffn).astype(BF16)
    grads_qkv = after((grad_query, grad_keys, grad_values), right, left)
    wide = qkv_grad(normed, grads_qkv, grad_gain_two[None, :], shard)


    def chosen(value, which, axis):
        return lax.dynamic_index_in_dim(value, which, axis=axis, keepdims=False)

    summed_output = lax.psum_scatter(
        grad_w_output.astype(BF16), ("seq", "dp"), scatter_dimension=0, tiled=True
    )
    kept = chosen(wide, core, 0).astype(F32)
    kept = kept + swap_core(chosen(wide, 1 - core, 0)).astype(F32)
    grads_late = after(grads_qkv, kept)
    grad_normed, sent_normed = token_grad(
        grads_late, w_qkv, own_places[:, None], other_places[:, None]
    )
    kept, sent_normed = lax.optimization_barrier((kept, sent_normed))
    mid_late, sent_normed = lax.optimization_barrier((mid_line, sent_normed))
    right_late, left_late = line_step(2, mid_late, slice(cut, width))
    right_late, left_late = after((right_late, left_late), last_first)
    last_late = (line_up(right_late), line_down(left_late))
    came_normed = swap_seq(sent_normed)
    next_kept = chosen(kept, row_of, 0)
    next_kept = next_kept + swap_y(chosen(kept, 1 - row_of, 0).astype(BF16)).astype(F32)
    next_kept, last_first, last_late, summed_output, came_normed = lax.optimization_barrier(
        (next_kept, last_first, last_late, summed_output, came_normed)
    )
    grad_normed = grad_normed.astype(F32) + came_normed.astype(F32)
    scale = lax.rsqrt(jnp.mean(inputs * inputs, axis=-1, keepdims=True) + EPSILON)
    unit = inputs * scale
    scaled = grad_normed * gain_one
    inner = jnp.mean(scaled * unit, axis=-1, keepdims=True)
    grad_tokens = grad_middle + scale * (scaled - unit * inner)
    own_grads = line_partial(*range(LINE))
    part_grads = jnp.concatenate(
        [
            own + up.astype(F32) + down.astype(F32)
            for own, (up, down) in ((own_grads[:cut], last_first), (own_grads[cut:], last_late))
        ],
        axis=0,
    ).astype(BF16)
    same_grads = jnp.where(first_core, part_grads[:, :half], part_grads[:, half : 2 * half])
    cross_grads = jnp.where(first_core, part_grads[:, half : 2 * half], part_grads[:, :half])
    same_grads = jnp.concatenate([same_grads, part_grads[:, 2 * half :]], axis=1)
    next_kept, same_grads, cross_grads = lax.optimization_barrier(
        (next_kept, same_grads, cross_grads)
    )
    same = both_axes(same_grads, straight)
    cross = both_axes(cross_grads, crossed_back)
    sent_lines = [
        swap_dp(chosen(next_kept, line ^ step, 1).astype(BF16), 4 * step) for step in range(1, LINE)
    ]
    summed = chosen(next_kept, line, 1) + sum(value.astype(F32) for value in sent_lines)
    summed, same, cross = lax.optimization_barrier((summed, same, cross))
    grad_w_in = ordered(same[:, :half], cross, 1)
    grad_w_out = same[:, half:].T
    kept_rows = chosen(summed, seq, 0)
    sent_rows = swap_seq(chosen(summed, 1 - seq, 0).astype(BF16)).astype(F32)
    cuts = (q_width, q_width + kv_width, qkv_width)
    pieces = [
        (a, b) for a, b in zip(jnp.split(kept_rows, cuts, axis=1), jnp.split(sent_rows, cuts, axis=1))
    ]
    grad_projections = [ordered(a, b, 1) for a, b in pieces[:3]]
    grad_gain_ffn = (pieces[3][0] + pieces[3][1])[:, 0]
    grad_gain_attn = sum(
        jnp.sum(grad * weight.astype(F32), axis=1)
        for grad, weight in zip(grad_projections, projections)
    ) / gain_attn.astype(F32)
    return (
        output,
        grad_tokens,
        grad_projections[0],
        grad_projections[1],
        grad_projections[2],
        summed_output.astype(F32),
        grad_gain_attn,
        grad_gain_ffn,
        grad_w_in.astype(F32)[None],
        grad_w_out.astype(F32)[None],
    )


def solution(mesh):
    placed = (
        P(("seq", "dp"), None),
        P(("seq", "dp"), None),
        P("dp", None),
        P("dp", None),
        P(("seq", "dp"), None),
        P(("seq", "dp"), None),
        P(("seq", "dp"), None),
        P(("seq", "dp"), None),
        P(("seq", "dp"), None),
        P(("seq", "dp"), None),
        P(("seq", "dp")),
        P(("seq", "dp")),
        P("dp", None, "seq"),
        P("dp", "seq", None),
    )
    return jax.shard_map(
        shards_plane if in_planes(mesh) else shards_general,
        mesh=mesh,
        in_specs=placed,
        out_specs=(
            P(("seq", "dp"), None),
            P(("seq", "dp"), None),
            P(("seq", "dp"), None),
            P(("seq", "dp"), None),
            P(("seq", "dp"), None),
            P(("seq", "dp"), None),
            P(("seq", "dp")),
            P(("seq", "dp")),
            P("dp", None, "seq"),
            P("dp", "seq", None),
        ),
        check_vma=False,
    )
```

```python
import functools

import jax
import jax.numpy as jnp
from jax import lax
from jax.experimental import pallas as pl
from jax.experimental.pallas import tpu as pltpu
from jax.sharding import PartitionSpec as P

QHEADS = 24
KVHEADS = 8
HDIM = 64
FF = 512
TOP = 8


EPSILON = 1e-06
BRANCH_SCALE = 0.22
SCORE_SCALE = 1.0 / 64.0
THETA = 10000.0


def rms_norm(value, gain):
    return value * lax.rsqrt(jnp.mean(value * value, axis=-1, keepdims=True) + EPSILON) * gain


def local_places(placing, seq_lengths):
    ends = jnp.cumsum(seq_lengths)
    segment = jnp.sum((placing[:, None] >= ends[None, :]).astype(jnp.int32), axis=1)
    starts = ends - seq_lengths
    member = segment[:, None] == jnp.arange(seq_lengths.shape[0], dtype=jnp.int32)[None, :]
    start_of = jnp.sum(jnp.where(member, starts[None, :], 0), axis=1)
    return (segment, placing - start_of)


def rotate(values, place, direction):
    half = values.shape[-1] // 2
    freqs = jnp.power(THETA, -jnp.arange(half, dtype=jnp.float32) * 2.0 / values.shape[-1])
    angles = place.astype(jnp.float32)[:, None] * freqs[None, :]
    cosine = jnp.cos(angles)[:, None, :]
    sine = direction * jnp.sin(angles)[:, None, :]
    first = values[..., :half]
    second = values[..., half:]
    return jnp.concatenate(
        [first * cosine - second * sine, second * cosine + first * sine], axis=-1
    )


def shards_general(
    tokens,
    cotangent,
    positions,
    lengths,
    routes,
    logits,
    w_query,
    w_key,
    w_value,
    w_output,
    gain_attn,
    gain_ffn,
    w_in,
    w_out,
):
    seq_count = lax.axis_size("seq")
    data_count = lax.axis_size("dp")
    tok_count = tokens.shape[0]
    group_len = positions.shape[1]
    local_experts = w_in.shape[0]
    experts_all = local_experts * data_count
    capacity = min(tok_count, 5 * tok_count * TOP // (4 * experts_all))
    heads_local = QHEADS // seq_count
    kv_local = KVHEADS // seq_count
    ratio = QHEADS // KVHEADS
    width = tokens.shape[1]
    query_full, key_full, value_full, output_full, gain_one, gain_two = (
        lax.all_gather(w_query, ("seq", "dp"), axis=0, tiled=True),
        lax.all_gather(w_key, ("seq", "dp"), axis=0, tiled=True),
        lax.all_gather(w_value, ("seq", "dp"), axis=0, tiled=True),
        lax.all_gather(w_output, ("seq", "dp"), axis=0, tiled=True),
        lax.all_gather(gain_attn, ("seq", "dp"), axis=0, tiled=True),
        lax.all_gather(gain_ffn, ("seq", "dp"), axis=0, tiled=True),
    )
    in_full, out_full = (
        lax.all_gather(w_in, "seq", axis=2, tiled=True),
        lax.all_gather(w_out, "seq", axis=1, tiled=True),
    )
    gain_one = gain_one.astype(jnp.float32)
    gain_two = gain_two.astype(jnp.float32)
    segment, place = local_places(positions[0], lengths[0])
    my_start = lax.axis_index("seq") * tok_count
    my_place = lax.dynamic_slice_in_dim(place, my_start, tok_count)
    inputs = tokens.astype(jnp.float32)
    normed = rms_norm(inputs, gain_one).astype(jnp.bfloat16)
    query_pre = jnp.dot(normed, query_full, preferred_element_type=jnp.float32)
    key_pre = jnp.dot(normed, key_full, preferred_element_type=jnp.float32)
    query_rot = (
        rotate(query_pre.reshape(tok_count, QHEADS, HDIM), my_place, 1.0)
        .reshape(tok_count, QHEADS * HDIM)
        .astype(jnp.bfloat16)
    )
    key_rot = (
        rotate(key_pre.reshape(tok_count, KVHEADS, HDIM), my_place, 1.0)
        .reshape(tok_count, KVHEADS * HDIM)
        .astype(jnp.bfloat16)
    )
    value_low = jnp.dot(normed, value_full, preferred_element_type=jnp.float32).astype(jnp.bfloat16)
    query_heads, key_heads, value_heads = (
        lax.all_to_all(query_rot, "seq", split_axis=1, concat_axis=0, tiled=True),
        lax.all_to_all(key_rot, "seq", split_axis=1, concat_axis=0, tiled=True),
        lax.all_to_all(value_low, "seq", split_axis=1, concat_axis=0, tiled=True),
    )
    keys_three = key_heads.reshape(group_len, kv_local, HDIM)
    values_three = value_heads.reshape(group_len, kv_local, HDIM)
    length = min(512, group_len)
    count = group_len // length

    def scores_of(query_block, seg_block, place_block):
        grouped = query_block.reshape(length, kv_local, ratio, HDIM)
        raw_scores = (
            jnp.einsum("qgrd,kgd->grqk", grouped, keys_three, preferred_element_type=jnp.float32)
            * SCORE_SCALE
        )
        allowed = (seg_block[:, None] == segment[None, :]) & (
            place[None, :] <= place_block[:, None]
        )
        return jnp.where(allowed[None, None], raw_scores, -1e30)

    def forward_block(pieces):
        query_block, seg_block, place_block = pieces
        scores = scores_of(query_block, seg_block, place_block)
        highest = jnp.max(scores, axis=-1, keepdims=True)
        expon = jnp.exp(scores - highest)
        totals = jnp.sum(expon, axis=-1, keepdims=True)
        probs = expon / totals
        mixed = jnp.einsum(
            "grqk,kgd->qgrd",
            probs.astype(jnp.bfloat16),
            values_three,
            preferred_element_type=jnp.float32,
        )
        return (
            mixed.reshape(length, heads_local * HDIM).astype(jnp.bfloat16),
            highest + jnp.log(totals),
            probs,
        )

    query_blocks = query_heads.reshape(count, length, heads_local * HDIM)
    seg_blocks = segment.reshape(count, length)
    place_blocks = place.reshape(count, length)
    block_args = (query_blocks, seg_blocks, place_blocks)

    def forward_light(pieces):
        mixed, lse_part, unused_probs = forward_block(pieces)
        return (mixed, lse_part)

    mixed_blocks, lse_blocks = lax.map(forward_light, block_args)
    mixed_heads = mixed_blocks.reshape(group_len, heads_local * HDIM)
    mixed_tokens = lax.all_to_all(mixed_heads, "seq", split_axis=0, concat_axis=1, tiled=True)
    attn = jnp.dot(mixed_tokens, output_full, preferred_element_type=jnp.float32)
    middle = inputs + BRANCH_SCALE * attn
    normed_ffn = rms_norm(middle, gain_two).astype(jnp.bfloat16)
    chosen = routes.reshape(-1)
    onehot = (chosen[:, None] == jnp.arange(experts_all, dtype=jnp.int32)[None, :]).astype(
        jnp.int32
    )
    ranking = jnp.sum(jnp.cumsum(onehot, axis=0) * onehot, axis=1) - 1
    target = chosen * capacity + ranking
    token_of = jnp.arange(tok_count * TOP, dtype=jnp.int32) // TOP
    gates = jax.nn.softmax(logits, axis=-1)
    source = jnp.full((experts_all * capacity,), tok_count, jnp.int32).at[target].set(token_of)
    slot_gate = jnp.zeros((experts_all * capacity,), jnp.float32).at[target].set(gates.reshape(-1))
    padded = jnp.concatenate([normed_ffn, jnp.zeros((1, width), jnp.bfloat16)], axis=0)
    outgoing = padded[source].reshape(data_count, local_experts * capacity, width)

    def expert_layout(arrived):
        return jnp.swapaxes(
            arrived.reshape(data_count, local_experts, capacity, width), 0, 1
        ).reshape(local_experts, data_count * capacity, width)

    def home_layout(values):
        return jnp.swapaxes(
            values.reshape(local_experts, data_count, capacity, width), 0, 1
        ).reshape(data_count, local_experts * capacity, width)

    def expert_forward(expert_rows):
        both = jnp.einsum("erd,edf->erf", expert_rows, in_full, preferred_element_type=jnp.float32)
        hidden = (jax.nn.silu(both[..., :FF]) * both[..., FF:]).astype(jnp.bfloat16)
        return (both, hidden)

    expert_rows = expert_layout(
        lax.all_to_all(outgoing, "dp", split_axis=0, concat_axis=0, tiled=True)
    )
    both, hidden = expert_forward(expert_rows)
    result = jnp.einsum(
        "erf,efd->erd", hidden, out_full, preferred_element_type=jnp.float32
    ).astype(jnp.bfloat16)
    returned = lax.all_to_all(
        home_layout(result), "dp", split_axis=0, concat_axis=0, tiled=True
    ).reshape(experts_all * capacity, width)
    picked = returned[target].reshape(tok_count, TOP, width).astype(jnp.float32)
    ffn = jnp.sum(picked * gates[:, :, None], axis=1)
    final = middle + BRANCH_SCALE * ffn
    output = final.astype(jnp.bfloat16)
    grad_final = cotangent.astype(jnp.float32)
    padded_grad = jnp.concatenate(
        [BRANCH_SCALE * grad_final, jnp.zeros((1, width), jnp.float32)], axis=0
    )
    grad_slots = (slot_gate[:, None] * padded_grad[source]).astype(jnp.bfloat16)
    grad_result = expert_layout(
        lax.all_to_all(
            grad_slots.reshape(data_count, local_experts * capacity, width),
            "dp",
            split_axis=0,
            concat_axis=0,
            tiled=True,
        )
    )
    rows_back = expert_layout(
        lax.all_to_all(outgoing, "dp", split_axis=0, concat_axis=0, tiled=True)
    )
    both_back, hidden_back = expert_forward(rows_back)
    grad_hidden = jnp.einsum(
        "erd,efd->erf", grad_result, out_full, preferred_element_type=jnp.float32
    )
    gate_part = both_back[..., :FF]
    up_part = both_back[..., FF:]
    sigma = jax.nn.sigmoid(gate_part)
    grad_gate = grad_hidden * up_part * sigma * (1.0 + gate_part * (1.0 - sigma))
    grad_up = grad_hidden * gate_part * sigma
    grad_both = jnp.concatenate([grad_gate, grad_up], axis=-1).astype(jnp.bfloat16)
    grad_out_local = jnp.einsum(
        "erf,erd->efd", hidden_back, grad_result, preferred_element_type=jnp.float32
    )
    grad_in_local = jnp.einsum(
        "erd,erf->edf", rows_back, grad_both, preferred_element_type=jnp.float32
    )
    grad_rows = jnp.einsum(
        "erf,edf->erd", grad_both, in_full, preferred_element_type=jnp.float32
    ).astype(jnp.bfloat16)
    grad_home = lax.all_to_all(
        home_layout(grad_rows), "dp", split_axis=0, concat_axis=0, tiled=True
    ).reshape(experts_all * capacity, width)
    grad_normed_ffn = jnp.sum(
        grad_home[target].reshape(tok_count, TOP, width).astype(jnp.float32), axis=1
    )
    grad_w_in, grad_w_out = (
        lax.psum_scatter(
            grad_in_local.astype(jnp.bfloat16), "seq", scatter_dimension=2, tiled=True
        ).astype(jnp.float32),
        lax.psum_scatter(
            grad_out_local.astype(jnp.bfloat16), "seq", scatter_dimension=1, tiled=True
        ).astype(jnp.float32),
    )
    unused_norm, norm_pull = jax.vjp(rms_norm, middle, gain_two)
    grad_middle_norm, grad_gain_two = norm_pull(grad_normed_ffn)
    grad_middle = grad_final + grad_middle_norm
    grad_attn = (BRANCH_SCALE * grad_middle).astype(jnp.bfloat16)
    grad_w_output = jnp.einsum(
        "te,td->ed", mixed_tokens, grad_attn, preferred_element_type=jnp.float32
    )
    grad_mixed = jnp.einsum(
        "td,ed->te", grad_attn, output_full, preferred_element_type=jnp.float32
    ).astype(jnp.bfloat16)
    grad_mixed_heads = lax.all_to_all(grad_mixed, "seq", split_axis=1, concat_axis=0, tiled=True)
    grad_blocks = grad_mixed_heads.reshape(count, length, heads_local * HDIM)
    back_args = (query_blocks, seg_blocks, place_blocks, lse_blocks, grad_blocks)

    def backward_block(carry, pieces):
        grad_keys, grad_values = carry
        query_block, seg_block, place_block, lse_block, grad_block = pieces[:5]
        probs = jnp.exp(scores_of(query_block, seg_block, place_block) - lse_block)
        grad_out = grad_block.reshape(length, kv_local, ratio, HDIM)
        grad_probs = jnp.einsum(
            "qgrd,kgd->grqk", grad_out, values_three, preferred_element_type=jnp.float32
        )
        grad_scores = (
            probs * (grad_probs - jnp.sum(probs * grad_probs, axis=-1, keepdims=True))
        ).astype(jnp.bfloat16)
        grad_query = SCORE_SCALE * jnp.einsum(
            "grqk,kgd->qgrd", grad_scores, keys_three, preferred_element_type=jnp.float32
        )
        grouped = query_block.reshape(length, kv_local, ratio, HDIM)
        grad_keys = grad_keys + SCORE_SCALE * jnp.einsum(
            "grqk,qgrd->kgd", grad_scores, grouped, preferred_element_type=jnp.float32
        )
        grad_values = grad_values + jnp.einsum(
            "grqk,qgrd->kgd",
            probs.astype(jnp.bfloat16),
            grad_out,
            preferred_element_type=jnp.float32,
        )
        return (
            (grad_keys, grad_values),
            grad_query.reshape(length, heads_local * HDIM).astype(jnp.bfloat16),
        )

    empty_keys = jnp.zeros((group_len, kv_local, HDIM), jnp.float32)
    (grad_keys, grad_values), grad_query_blocks = lax.scan(
        backward_block, (empty_keys, empty_keys), back_args
    )
    grad_query_heads = grad_query_blocks.reshape(group_len, heads_local * HDIM)
    grad_key_heads = grad_keys.reshape(group_len, kv_local * HDIM).astype(jnp.bfloat16)
    grad_value_heads = grad_values.reshape(group_len, kv_local * HDIM).astype(jnp.bfloat16)
    grad_query_tok, grad_key_tok, grad_value_tok = (
        lax.all_to_all(grad_query_heads, "seq", split_axis=0, concat_axis=1, tiled=True),
        lax.all_to_all(grad_key_heads, "seq", split_axis=0, concat_axis=1, tiled=True),
        lax.all_to_all(grad_value_heads, "seq", split_axis=0, concat_axis=1, tiled=True),
    )
    grad_query_pre = (
        rotate(grad_query_tok.astype(jnp.float32).reshape(tok_count, QHEADS, HDIM), my_place, -1.0)
        .reshape(tok_count, QHEADS * HDIM)
        .astype(jnp.bfloat16)
    )
    grad_key_pre = (
        rotate(grad_key_tok.astype(jnp.float32).reshape(tok_count, KVHEADS, HDIM), my_place, -1.0)
        .reshape(tok_count, KVHEADS * HDIM)
        .astype(jnp.bfloat16)
    )
    grad_w_query = jnp.einsum(
        "td,te->de", normed, grad_query_pre, preferred_element_type=jnp.float32
    )
    grad_w_key = jnp.einsum("td,te->de", normed, grad_key_pre, preferred_element_type=jnp.float32)
    grad_w_value = jnp.einsum(
        "td,te->de", normed, grad_value_tok, preferred_element_type=jnp.float32
    )
    grad_normed = jnp.einsum(
        "te,de->td", grad_query_pre, query_full, preferred_element_type=jnp.float32
    )
    grad_normed = grad_normed + jnp.einsum(
        "te,de->td", grad_key_pre, key_full, preferred_element_type=jnp.float32
    )
    grad_normed = grad_normed + jnp.einsum(
        "te,de->td", grad_value_tok, value_full, preferred_element_type=jnp.float32
    )
    unused_first, first_pull = jax.vjp(rms_norm, inputs, gain_one)
    grad_inputs_norm, grad_gain_one = first_pull(grad_normed)
    grad_tokens = grad_middle + grad_inputs_norm
    summed = (
        lax.psum_scatter(grad_w_query, ("seq", "dp"), scatter_dimension=0, tiled=True),
        lax.psum_scatter(grad_w_key, ("seq", "dp"), scatter_dimension=0, tiled=True),
        lax.psum_scatter(grad_w_value, ("seq", "dp"), scatter_dimension=0, tiled=True),
        lax.psum_scatter(grad_w_output, ("seq", "dp"), scatter_dimension=0, tiled=True),
        lax.psum_scatter(grad_gain_one, ("seq", "dp"), scatter_dimension=0, tiled=True),
        lax.psum_scatter(grad_gain_two, ("seq", "dp"), scatter_dimension=0, tiled=True),
    )
    return (
        output,
        grad_tokens,
        summed[0],
        summed[1],
        summed[2],
        summed[3],
        summed[4],
        summed[5],
        grad_w_in,
        grad_w_out,
    )


BF16 = jnp.bfloat16
F32 = jnp.float32
LINE = 4
PAD = 128
VMEM_BYTES = 60 * 1024 * 1024


def in_planes(mesh):
    return mesh.shape["seq"] == 2 and mesh.shape["dp"] == 4 * LINE


def swap_seq(value):
    return lax.ppermute(value, "seq", [(0, 1), (1, 0)])


def swap_dp(value, mask):
    return lax.ppermute(value, "dp", [(i, i ^ mask) for i in range(4 * LINE)])


def swap_core(value):
    return swap_dp(value, 1)


def swap_y(value):
    return swap_dp(value, 2)


def line_up(value):
    return lax.ppermute(value, "dp", [(i, i + 4) for i in range(4 * LINE - 4)])


def line_down(value):
    return lax.ppermute(value, "dp", [(i, i - 4) for i in range(4, 4 * LINE)])


def after(value, *others):
    return lax.optimization_barrier((value,) + others)[0]


def line_scatter(take, place):
    up = down = None
    for step in range(LINE - 1):
        far = jnp.minimum(LINE - 1 - step + place, LINE - 1)
        near = jnp.maximum(step - LINE + 1 + place, 0)
        right, left = take(far), take(near)
        if up is not None:
            right = right + up.astype(F32)
            left = left + down.astype(F32)
        up = line_up(right.astype(BF16))
        down = line_down(left.astype(BF16))
    return take(place) + up.astype(F32) + down.astype(F32)


def near_pieces(own, own_x):
    return swap_seq(own_x), swap_y(own)


def far_pieces(near_x, near_y):
    half = near_x.shape[0] // 2
    return swap_y(near_x[:half]), swap_seq(near_y[half:])


def with_cores(*pieces):
    return pieces + tuple(swap_core(piece) for piece in pieces)


def over_cores(mine, others):
    return mine.astype(F32) + swap_core(others).astype(F32)


def far_links(far):
    half = far.shape[0] // 2
    return swap_y(far[:half]), swap_seq(far[half:])


def near_links(near, from_y, from_x):
    half = from_y.shape[0] // 2
    first = (near[:half] + from_y[half:].astype(F32)).astype(BF16)
    second = (near[half : 2 * half] + from_x[half:].astype(F32)).astype(BF16)
    return first, second


def own_sum(near, from_y, from_x, first, second):
    half = from_y.shape[0] // 2
    low = near[2 * half : 3 * half] + from_y[:half].astype(F32) + first.astype(F32)
    high = near[3 * half :] + from_x[:half].astype(F32) + second.astype(F32)
    return jnp.concatenate([low, high], axis=0)


def turned(values, cos, sin, direction):
    lanes = values.shape[1]
    place = lax.broadcasted_iota(jnp.int32, values.shape, 1) % HDIM
    swapped = jnp.where(
        place < HDIM // 2,
        pltpu.roll(values, lanes - HDIM // 2, 1),
        pltpu.roll(values, HDIM // 2, 1),
    )
    times = lanes // cos.shape[1]
    cos = jnp.concatenate([cos] * times, axis=1)
    sin = jnp.concatenate([sin] * times, axis=1)
    if direction > 0:
        return values * cos + swapped * sin
    return values * cos - swapped * sin


def qkv_kernel(x_ref, gain_ref, w_ref, cos_ref, sin_ref, h_ref, q_ref, k_ref, v_ref):
    value = x_ref[...].astype(F32)
    scale = lax.rsqrt(jnp.mean(value * value, axis=-1, keepdims=True) + EPSILON)
    normed = (value * scale * gain_ref[...]).astype(BF16)
    h_ref[...] = normed
    both = jnp.dot(normed, w_ref[...], preferred_element_type=F32)
    q_width, kv_heads = q_ref.shape[1], k_ref.shape[0]
    kv_width = kv_heads * HDIM
    spun = turned(both[:, : q_width + kv_width], cos_ref[...], sin_ref[...], 1)
    q_ref[...] = (spun[:, :q_width] * SCORE_SCALE).astype(BF16)
    for head in range(kv_heads):
        low = q_width + head * HDIM
        k_ref[head] = spun[:, low : low + HDIM].astype(BF16)
        low = low + kv_width
        v_ref[head] = both[:, low : low + HDIM].astype(BF16)


def project(x_sorted, gain, weights, cos, sin, q_width, kv_heads):
    rows, width = x_sorted.shape
    tile = 256
    columns = q_width + 2 * kv_heads * HDIM

    def row_block(lanes):
        return pl.BlockSpec((tile, lanes), lambda i: (i, 0))

    heads = pl.BlockSpec((kv_heads, tile, HDIM), lambda i: (0, i, 0))
    return pl.pallas_call(
        qkv_kernel,
        grid=(rows // tile,),
        in_specs=[
            row_block(width),
            pl.BlockSpec((1, width), lambda i: (0, 0)),
            pl.BlockSpec((width, columns), lambda i: (0, 0)),
            row_block(cos.shape[1]),
            row_block(cos.shape[1]),
        ],
        out_specs=[row_block(width), row_block(q_width), heads, heads],
        out_shape=[
            jax.ShapeDtypeStruct((rows, width), BF16),
            jax.ShapeDtypeStruct((rows, q_width), BF16),
            jax.ShapeDtypeStruct((kv_heads, rows, HDIM), BF16),
            jax.ShapeDtypeStruct((kv_heads, rows, HDIM), BF16),
        ],
        compiler_params=pltpu.CompilerParams(vmem_limit_bytes=VMEM_BYTES),
        cost_estimate=pl.CostEstimate(
            flops=rows * width * columns // 8,
            bytes_accessed=rows * width + width * columns,
            transcendentals=rows,
        ),
        name="project",
    )(x_sorted, gain, weights, cos, sin)


def token_grad_kernel(dq_ref, dk_ref, dv_ref, w_ref, own_ref, other_ref, mine_ref, sent_ref):
    q_width, kv_width = dq_ref.shape[1], dk_ref.shape[1]
    cuts = (0, q_width, q_width + kv_width, q_width + 2 * kv_width)
    grad = contract(dq_ref[...], w_ref[:, cuts[0] : cuts[1]], 1, 1)
    grad = grad + contract(dk_ref[...], w_ref[:, cuts[1] : cuts[2]], 1, 1)
    grad = (grad + contract(dv_ref[...], w_ref[:, cuts[2] : cuts[3]], 1, 1)).astype(BF16)
    for place_ref, out_ref in ((other_ref, sent_ref), (own_ref, mine_ref)):
        shape = (place_ref.shape[0], grad.shape[0])
        picked = lax.broadcasted_iota(jnp.int32, shape, 1) == place_ref[...]
        picked = jnp.where(picked, 1.0, 0.0).astype(BF16)
        out_ref[...] = jnp.dot(picked, grad, preferred_element_type=F32).astype(BF16)


def token_grad(grads, weights, own_places, other_places):
    rows, count = grads[0].shape[0], own_places.shape[0]
    width = weights.shape[0]
    columns = sum(grad.shape[1] for grad in grads)
    tile = width // 3

    def whole(array):
        return pl.BlockSpec(array.shape, lambda i: (0, 0))

    block = pl.BlockSpec((count, tile), lambda i: (0, i))
    return pl.pallas_call(
        token_grad_kernel,
        grid=(3,),
        in_specs=[whole(grad) for grad in grads]
        + [pl.BlockSpec((tile, columns), lambda i: (i, 0)), whole(own_places), whole(other_places)],
        out_specs=[block, block],
        out_shape=[jax.ShapeDtypeStruct((count, width), BF16)] * 2,
        compiler_params=pltpu.CompilerParams(vmem_limit_bytes=VMEM_BYTES),
        cost_estimate=pl.CostEstimate(
            flops=rows * width * columns // 8, bytes_accessed=rows * width, transcendentals=0
        ),
        name="token_grad",
    )(*grads, weights, own_places, other_places)


Q_TILE = 256


def windows(rows):
    longest = rows // 2
    for start in range(0, rows, Q_TILE):
        low = max(0, start - longest + 1) // Q_TILE * Q_TILE
        yield start, low, start + Q_TILE


def allowed_keys(start_ref, row, low, high):
    shape = (Q_TILE, high - low)
    rows = lax.broadcasted_iota(jnp.int32, shape, 0) + row
    keys = lax.broadcasted_iota(jnp.int32, shape, 1) + low
    return (keys <= rows) & (keys >= start_ref[row : row + Q_TILE, :])


def contract(left, right, left_dim, right_dim):
    return lax.dot_general(
        left, right, (((left_dim,), (right_dim,)), ((), ())), preferred_element_type=F32
    )


def masked_scores(query, keys, allowed):
    return jnp.where(allowed, contract(query, keys, 1, 1), -1e30)


def attend_kernel(base, q_ref, k_ref, v_ref, start_ref, o_ref, level_ref):
    pair = pl.program_id(0) + base
    ratio = QHEADS // KVHEADS
    for row, low, high in windows(q_ref.shape[0]):
        allowed = allowed_keys(start_ref, row, low, high)
        for side in range(2):
            head = (2 * pair + side) // ratio
            lanes = slice(side * HDIM, (side + 1) * HDIM)
            scores = masked_scores(
                q_ref[row : row + Q_TILE, lanes], k_ref[head, low:high, :], allowed
            )
            highest = jnp.max(scores, axis=-1, keepdims=True)
            expon = jnp.exp(scores - highest)
            total = jnp.sum(expon, axis=-1, keepdims=True)
            level_ref[0, row : row + Q_TILE, side : side + 1] = highest + jnp.log(total)
            probs = expon * (1.0 / total)
            mixed = contract(probs.astype(BF16), v_ref[head, low:high, :], 1, 0)
            o_ref[row : row + Q_TILE, lanes] = mixed.astype(BF16)


def attention_cost(rows, heads, products):
    area = sum(Q_TILE * (high - low) for _, low, high in windows(rows))
    return pl.CostEstimate(
        flops=products * heads * area * 16,
        bytes_accessed=8 * rows * heads * HDIM,
        transcendentals=heads * area,
    )


def attend(query, keys, values, starts, base, pairs):
    rows = query.shape[0]
    pair_block = pl.BlockSpec((rows, 2 * HDIM), lambda j: (0, j + base))
    whole = pl.BlockSpec(keys.shape, lambda j: (0, 0, 0))
    return pl.pallas_call(
        functools.partial(attend_kernel, base),
        grid=(pairs,),
        in_specs=[pair_block, whole, whole, pl.BlockSpec((rows, 1), lambda j: (0, 0))],
        out_specs=[
            pl.BlockSpec((rows, 2 * HDIM), lambda j: (0, j)),
            pl.BlockSpec((1, rows, 2), lambda j: (j, 0, 0)),
        ],
        out_shape=[
            jax.ShapeDtypeStruct((rows, pairs * 2 * HDIM), BF16),
            jax.ShapeDtypeStruct((pairs, rows, 2), F32),
        ],
        compiler_params=pltpu.CompilerParams(vmem_limit_bytes=VMEM_BYTES),
        cost_estimate=attention_cost(rows, 2 * pairs, 2),
        name="attend",
    )(query, keys, values, starts)


def attend_back_kernel(
    q_ref, k_ref, v_ref, d_ref, level_ref, start_ref, cos_ref, sin_ref,
    dq_ref, dk_ref, dv_ref, dk_sum, dv_sum,
):
    pair = pl.program_id(0)
    ratio = QHEADS // KVHEADS

    @pl.when(pair == 0)
    def _():
        dk_sum[...] = jnp.zeros_like(dk_sum)
        dv_sum[...] = jnp.zeros_like(dv_sum)

    for row, low, high in windows(q_ref.shape[0]):
        allowed = allowed_keys(start_ref, row, low, high)
        grads = []
        for side in range(2):
            head = (2 * pair + side) // ratio
            lanes = slice(side * HDIM, (side + 1) * HDIM)
            query = q_ref[row : row + Q_TILE, lanes]
            keys = k_ref[head, low:high, :]
            probs = jnp.exp(
                masked_scores(query, keys, allowed)
                - level_ref[0, row : row + Q_TILE, side : side + 1]
            )
            grad_out = d_ref[row : row + Q_TILE, lanes]
            grad_probs = contract(grad_out, v_ref[head, low:high, :], 1, 1)
            inner = jnp.sum(probs * grad_probs, axis=-1, keepdims=True)
            grad_scores = (probs * (grad_probs - inner)).astype(BF16)
            grads.append(contract(grad_scores, keys, 1, 0) * SCORE_SCALE)
            dk_sum[head, low:high, :] += contract(grad_scores, query, 0, 0)
            dv_sum[head, low:high, :] += contract(probs.astype(BF16), grad_out, 0, 0)
        grad_query = jnp.concatenate(grads, axis=1).astype(BF16).astype(F32)
        dq_ref[row : row + Q_TILE, :] = turned(
            grad_query,
            cos_ref[row : row + Q_TILE, :],
            sin_ref[row : row + Q_TILE, :],
            -1,
        ).astype(BF16)

    @pl.when(pair == pl.num_programs(0) - 1)
    def _():
        heads = range(dk_sum.shape[0])
        grad_keys = jnp.concatenate([dk_sum[head] for head in heads], axis=1)
        grad_keys = grad_keys.astype(BF16).astype(F32)
        dk_ref[...] = turned(grad_keys, cos_ref[...], sin_ref[...], -1).astype(BF16)
        dv_ref[...] = jnp.concatenate([dv_sum[head] for head in heads], axis=1).astype(BF16)


def attend_back(query, keys, values, grad_out, levels, starts, cos, sin):
    rows, lanes = query.shape
    pairs = lanes // (2 * HDIM)
    kv_heads = keys.shape[0]
    pair_block = pl.BlockSpec((rows, 2 * HDIM), lambda j: (0, j))
    whole = pl.BlockSpec(keys.shape, lambda j: (0, 0, 0))

    def fixed(lanes_of):
        return pl.BlockSpec((rows, lanes_of), lambda j: (0, 0))

    flat = kv_heads * HDIM
    return pl.pallas_call(
        attend_back_kernel,
        grid=(pairs,),
        in_specs=[
            pair_block, whole, whole, pair_block,
            pl.BlockSpec((1, rows, 2), lambda j: (j, 0, 0)), fixed(1), fixed(2 * HDIM), fixed(2 * HDIM),
        ],
        out_specs=[pair_block, fixed(flat), fixed(flat)],
        out_shape=[
            jax.ShapeDtypeStruct(query.shape, BF16),
            jax.ShapeDtypeStruct((rows, flat), BF16),
            jax.ShapeDtypeStruct((rows, flat), BF16),
        ],
        scratch_shapes=[pltpu.VMEM(keys.shape, F32), pltpu.VMEM(keys.shape, F32)],
        compiler_params=pltpu.CompilerParams(vmem_limit_bytes=VMEM_BYTES),
        cost_estimate=attention_cost(rows, 2 * pairs, 5),
        name="attend_back",
    )(query, keys, values, grad_out, levels, starts, cos, sin)


SLOTS = 2 * LINE - 1
SLOT_ORDER = (0, 3, 1, 2)
OWN, NEAR_X, NEAR_Y, FAR_Y, FAR_X = range(5)
FAR_TILES = (((NEAR_Y, 0), (FAR_Y, 0)), ((NEAR_X, 1), (FAR_X, 0)))
NEAR_TILES = (((NEAR_X, 0), (NEAR_Y, 1)), ((OWN, 0), (OWN, 1)))


def used_pieces(tiles):
    return sorted({piece for tile in tiles for piece, _ in tile})


def experts_kernel(tiles, half_rows, place_ref, *refs):
    used = used_pieces(tiles)
    sides = 2 * len(used)
    h_pieces, g_pieces, slots = refs[:sides], refs[sides : 2 * sides], refs[2 * sides : 2 * sides + SLOTS]
    select_ref = refs[2 * sides + SLOTS]
    (
        f_mine, f_other, d_mine, d_other, hid_a, hid_b, du_a, du_b, hcopy_ref, gcopy_ref,
        w_in, w_out, h_buf, g_buf, hidden, du_all, weight_sems, row_sems,
    ) = refs[-18:]
    width = h_buf.shape[2]
    half = slots[0].shape[1] // 3
    part = 2 * half
    step = pl.program_id(0)
    steps = 2 * len(tiles)

    def weight_copies(spot, slot):
        return (
            pltpu.make_async_copy(
                slots[slot].at[:, :part],
                w_in.at[:, spot * part : (spot + 1) * part],
                weight_sems.at[0, spot],
            ),
            pltpu.make_async_copy(
                slots[slot].at[:, part:],
                w_out.at[:, spot * half : (spot + 1) * half],
                weight_sems.at[1, spot],
            ),
        )

    def row_copies(number, buffer):
        side, tile = divmod(number, len(tiles))
        copies = []
        for spot, (piece, part_of) in enumerate(tiles[tile]):
            index = side * len(used) + used.index(piece)
            for kind, (pieces, held) in enumerate(((h_pieces, h_buf), (g_pieces, g_buf))):
                copies.append(
                    pltpu.make_async_copy(
                        pieces[index].at[pl.ds(part_of * half_rows, half_rows), :],
                        held.at[buffer, pl.ds(spot * half_rows, half_rows), :],
                        row_sems.at[buffer, 2 * kind + spot],
                    )
                )
        return copies

    def fetch(wanted, buffer):
        for number in range(steps):

            @pl.when(wanted == number)
            def _():
                for copy in row_copies(number, buffer):
                    copy.start()

    buffer = step % 2

    @pl.when(step == 0)
    def _():
        fetch(step, 0)
        for spot, expert in enumerate(SLOT_ORDER):
            for slot in range(expert, expert + LINE):

                @pl.when(slot == LINE - 1 + expert - place_ref[0])
                def _():
                    for copy in weight_copies(spot, slot):
                        copy.start()

        for spot in range(LINE):
            for copy in weight_copies(spot, LINE - 1):
                copy.wait()

    @pl.when(step + 1 < steps)
    def _():
        fetch(step + 1, 1 - buffer)

    for copy in row_copies(0, buffer):
        copy.wait()

    rows = h_buf[buffer]
    grads = g_buf[buffer, :, :width]
    hcopy_ref[...] = rows
    gcopy_ref[...] = grads
    gates = jnp.dot(g_buf[buffer, :, width:], select_ref[...], preferred_element_type=F32)
    for spot in range(LINE):
        units = slice(spot * half, (spot + 1) * half)
        both = jnp.dot(
            rows, w_in[:, spot * part : (spot + 1) * part], preferred_element_type=F32
        )
        back = jnp.dot(grads, w_out[:, units], preferred_element_type=F32)
        gate = gates[:, units]
        first, second = both[:, :half], both[:, half:]
        sigma = jax.nn.sigmoid(first)
        silu = first * sigma
        hidden[:, units] = (gate * (silu * second)).astype(BF16)
        back = back * (BRANCH_SCALE * gate)
        d_first = back * second * (sigma * (1.0 + first * (1.0 - sigma)))
        d_second = back * silu
        du_all[:, spot * part : spot * part + half] = d_first.astype(BF16)
        du_all[:, spot * part + half : (spot + 1) * part] = d_second.astype(BF16)
    hid_a[...] = hidden[:, : 2 * half]
    hid_b[...] = hidden[:, 2 * half :]
    du_a[...] = du_all[:, : 2 * part]
    du_b[...] = du_all[:, 2 * part :]
    ffn = contract(hidden[...], w_out[...], 1, 1).astype(BF16)
    back_rows = contract(du_all[...], w_in[...], 1, 1).astype(BF16)

    @pl.when(step < len(tiles))
    def _():
        f_mine[...] = ffn
        d_mine[...] = back_rows

    @pl.when(step >= len(tiles))
    def _():
        f_other[...] = ffn
        d_other[...] = back_rows


def run_experts(tiles, place, row_pieces, grad_pieces, slots, select, base, kept):
    used = used_pieces(tiles)
    sides = len(row_pieces) // 2
    wanted = used + [sides + piece for piece in used]
    rows = [row_pieces[piece] for piece in wanted]
    grads = [grad_pieces[piece] for piece in wanted]
    tile, width = row_pieces[OWN].shape
    wide = grad_pieces[OWN].shape[1]
    half = slots[0].shape[1] // 3
    part = 2 * half
    count = len(tiles)
    steps = 2 * count
    total = 8 * tile

    def late(lanes):
        return pl.BlockSpec((tile, lanes), lambda i, p: (i + base, 0))

    mine = pl.BlockSpec((tile, width), lambda i, p: (jnp.minimum(i, count - 1), 0))
    others = pl.BlockSpec((tile, width), lambda i, p: (jnp.maximum(i - count, 0), 0))
    anywhere = pl.BlockSpec(memory_space=pl.ANY)
    kept = list(kept)
    lead = 1 + 2 * len(wanted) + SLOTS + 1
    partial = jax.ShapeDtypeStruct((count * tile, width), BF16)
    lanes = [2 * half, 2 * half, 2 * part, 2 * part, width, width]
    return pl.pallas_call(
        functools.partial(experts_kernel, tiles, tile // 2),
        grid_spec=pltpu.PrefetchScalarGridSpec(
            num_scalar_prefetch=1,
            grid=(steps,),
            in_specs=[anywhere] * (2 * len(wanted) + SLOTS)
            + [pl.BlockSpec(select.shape, lambda i, p: (0, 0))]
            + [anywhere] * len(kept),
            out_specs=[mine, others, mine, others] + [late(n) for n in lanes],
            scratch_shapes=[
                pltpu.VMEM((width, LINE * part), BF16),
                pltpu.VMEM((width, LINE * half), BF16),
                pltpu.VMEM((2, tile, width), BF16),
                pltpu.VMEM((2, tile, wide), BF16),
                pltpu.VMEM((tile, LINE * half), BF16),
                pltpu.VMEM((tile, LINE * part), BF16),
                pltpu.SemaphoreType.DMA((2, LINE)),
                pltpu.SemaphoreType.DMA((2, 4)),
            ],
        ),
        out_shape=[partial] * 4 + [jax.ShapeDtypeStruct((total, n), BF16) for n in lanes],
        input_output_aliases={lead + i: 4 + i for i in range(len(kept))},
        compiler_params=pltpu.CompilerParams(vmem_limit_bytes=VMEM_BYTES),
        cost_estimate=pl.CostEstimate(
            flops=steps * tile * width * LINE * (part + half) // 4,
            bytes_accessed=2 * steps * tile * (6 * width + LINE * (part + half)),
            transcendentals=steps * tile * LINE * half,
        ),
        name="experts",
    )(place, *rows, *grads, *slots, select, *kept)


def qkv_grad_kernel(h_ref, dq_ref, dk_ref, dv_ref, gain_ref, o_ref):
    shard = o_ref.shape[-2]
    rows = h_ref[...]
    low = 0
    gains = jnp.broadcast_to(gain_ref[...], (PAD, gain_ref.shape[1])).T.astype(BF16)
    parts = [contract(rows, ref[...], 0, 0).astype(BF16) for ref in (dq_ref, dk_ref, dv_ref)]
    for part in parts + [gains]:
        for block in range(h_ref.shape[1] // shard):
            place = (block % 2, block // 2 % 2, 0, block // 4)
            o_ref[place + (slice(None), slice(low, low + part.shape[1]))] = part[
                block * shard : (block + 1) * shard
            ]
        low = low + part.shape[1]


def qkv_grad(normed, grads, gain_row, shard):
    rows, width = normed.shape
    columns = sum(grad.shape[1] for grad in grads)
    tile = width // 4
    planes = tile // (4 * shard)
    return pl.pallas_call(
        qkv_grad_kernel,
        grid=(4,),
        in_specs=[pl.BlockSpec((rows, tile), lambda i: (0, i))]
        + [pl.BlockSpec(grad.shape, lambda i: (0, 0)) for grad in grads]
        + [pl.BlockSpec((1, tile), lambda i: (0, i))],
        out_specs=pl.BlockSpec(
            (2, 2, 1, planes, shard, columns + PAD), lambda i: (0, 0, i // 2, i % 2, 0, 0)
        ),
        out_shape=jax.ShapeDtypeStruct((2, 2, 2, LINE, shard, columns + PAD), BF16),
        compiler_params=pltpu.CompilerParams(vmem_limit_bytes=VMEM_BYTES),
        cost_estimate=pl.CostEstimate(
            flops=rows * width * columns // 8,
            bytes_accessed=rows * width,
            transcendentals=0,
        ),
        name="qkv_grad",
    )(normed, *grads, gain_row)


def norm_back(value, gain, grad):
    scale = lax.rsqrt(jnp.mean(value * value, axis=-1, keepdims=True) + EPSILON)
    unit = value * scale
    grad_gain = jnp.sum(grad * unit, axis=0)
    scaled = grad * gain
    inner = jnp.mean(scaled * unit, axis=-1, keepdims=True)
    return scale * (scaled - unit * inner), grad_gain


def shards_plane(
    tokens,
    cotangent,
    positions,
    lengths,
    routes,
    logits,
    w_query,
    w_key,
    w_value,
    w_output,
    gain_attn,
    gain_ffn,
    w_in,
    w_out,
):
    seq = lax.axis_index("seq")
    data = lax.axis_index("dp")
    line, row_of, core = data // 4, (data // 2) % 2, data % 2
    tok_count, width = tokens.shape
    group_len = positions.shape[1]
    shard = w_query.shape[0]
    q_width = w_query.shape[1] // 2
    kv_width = w_key.shape[1] // 2
    kv_heads = kv_width // HDIM
    first_seq = seq == 0

    def ordered(mine, theirs, axis):
        low = jnp.where(first_seq, mine, theirs)
        high = jnp.where(first_seq, theirs, mine)
        return jnp.concatenate([low, high], axis=axis)

    def half_of(weights, which):
        half = weights.shape[1] // 2
        return lax.dynamic_slice_in_dim(weights, which * half, half, axis=1)

    def both_axes(value, pairs):
        return lax.ppermute(value, ("seq", "dp"), pairs)

    def device(s, d):
        return s * 4 * LINE + d

    straight, crossed = [], []
    for s in range(2):
        for d in range(4 * LINE):
            c = d % 2
            straight.append((device(s, d), device(c, d - c + s)))
            crossed.append((device(s, d), device(c, d - c + 1 - s)))
    crossed_back = [(there, here) for here, there in crossed]
    first_core = core == 0

    projections = (w_query, w_key, w_value)
    qkv_width = q_width + 2 * kv_width
    gain_columns = jnp.pad(jnp.stack([gain_attn, gain_ffn], axis=1), ((0, 0), (0, PAD - 2)))
    mine = jnp.concatenate([half_of(w, seq) for w in projections] + [gain_columns], axis=1)
    theirs = jnp.concatenate([half_of(w, 1 - seq) for w in projections] + [gain_columns], axis=1)
    theirs = swap_seq(theirs)
    pair = jnp.stack([jnp.where(first_seq, mine, theirs), jnp.where(first_seq, theirs, mine)])
    qkv_width = q_width + 2 * kv_width
    w_qkv = lax.all_gather(pair, "dp", axis=1, tiled=True).reshape(width, qkv_width + PAD)
    output_full = lax.all_gather(w_output, ("seq", "dp"), axis=0, tiled=True)

    in_own = w_in[0]
    half = in_own.shape[1] // 2
    sent = jnp.concatenate(
        [lax.dynamic_slice_in_dim(in_own, seq * half, half, axis=1), w_out[0].T], axis=1
    )
    same = both_axes(sent, straight)
    cross = both_axes(lax.dynamic_slice_in_dim(in_own, (1 - seq) * half, half, axis=1), crossed)
    own_part = jnp.concatenate(
        [
            jnp.where(first_core, same[:, :half], cross),
            jnp.where(first_core, cross, same[:, :half]),
            same[:, half:],
        ],
        axis=1,
    )
    other_tokens = swap_seq(after(tokens, own_part))
    up_one, down_one = line_up(own_part), line_down(own_part)
    cut = width // 2

    experts_all = 4 * LINE
    gates = jax.nn.softmax(logits, axis=-1)
    named = routes[:, :, None] == jnp.arange(experts_all, dtype=jnp.int32)[None, None, :]
    gate_table = jnp.sum(jnp.where(named, gates[:, :, None], 0.0), axis=1)
    gate_high = lax.reduce_precision(gate_table, 8, 7)
    grad_rows = jnp.concatenate(
        [
            cotangent,
            gate_high.astype(BF16),
            (gate_table - gate_high).astype(BF16),
            jnp.zeros((tok_count, PAD - 2 * experts_all), BF16),
        ],
        axis=1,
    )
    grad_near = near_pieces(grad_rows, after(grad_rows, other_tokens))
    lane = jnp.arange(PAD, dtype=jnp.int32)[:, None]
    hosted = jnp.repeat(
        jnp.array(SLOT_ORDER, jnp.int32) * 4 + 2 * row_of + seq, half, total_repeat_length=LINE * half
    )
    select = ((lane % experts_all == hosted[None, :]) & (lane < 2 * experts_all)).astype(BF16)

    places = positions[0]
    ends = jnp.cumsum(lengths[0])
    ranks = jnp.arange(group_len, dtype=jnp.int32)
    reached = ranks[:, None] >= ends[None, :]
    starts = jnp.max(jnp.where(reached, ends[None, :], 0), axis=1)
    local = (ranks - starts).astype(F32)
    freqs = jnp.power(THETA, -jnp.arange(HDIM // 2, dtype=F32) * 2.0 / HDIM)
    angles = local[:, None] * freqs[None, :]
    cos, sin = jnp.cos(angles), jnp.sin(angles)
    cos = jnp.concatenate([cos, cos, cos, cos], axis=1)
    sin = jnp.concatenate([-sin, sin, -sin, sin], axis=1)
    start_column = starts[:, None]
    own_places = lax.dynamic_slice_in_dim(places, seq * tok_count, tok_count)
    other_places = lax.dynamic_slice_in_dim(places, (1 - seq) * tok_count, tok_count)
    sort_own = (ranks[:, None] == own_places[None, :]).astype(BF16)
    sort_other = (ranks[:, None] == other_places[None, :]).astype(BF16)

    def to_order(own, other):
        return (
            contract(sort_own, own, 1, 0) + contract(sort_other, other, 1, 0)
        ).astype(BF16)

    def from_order(sort, values):
        return contract(sort, values, 0, 0).astype(BF16)

    x_sorted = to_order(tokens, other_tokens)
    gains = w_qkv[:, qkv_width : qkv_width + 2].astype(F32).T
    gain_one, gain_two = gains[0], gains[1]
    x_sorted, up_one, down_one = lax.optimization_barrier((x_sorted, up_one, down_one))
    up_two, down_two = line_up(up_one), line_down(down_one)
    normed, query, keys, values = project(
        x_sorted, gain_one[None, :], w_qkv, cos, sin, q_width, kv_heads
    )
    pairs = q_width // (2 * HDIM)
    first_pairs = (pairs + 1) // 2
    mixed_one, levels_one = attend(query, keys, values, start_column, 0, first_pairs)
    sent_one = swap_seq(from_order(sort_other, mixed_one))
    query_two, grad_near_x, grad_near_y = after((query, *grad_near), mixed_one)
    grad_near = (grad_near_x, grad_near_y)
    grad_far = far_pieces(*grad_near)
    mixed_two, levels_two = attend(
        query_two, keys, values, start_column, first_pairs, pairs - first_pairs
    )
    sent_two = swap_seq(from_order(sort_other, mixed_two))
    mixed_mine = [from_order(sort_own, mixed_one), from_order(sort_own, mixed_two)]
    mixed = ordered(
        jnp.concatenate(mixed_mine, axis=1), jnp.concatenate([sent_one, sent_two], axis=1), 1
    )
    mixed, up_two, down_two = lax.optimization_barrier((mixed, up_two, down_two))
    up_three, down_three = line_up(up_two), line_down(down_two)
    inputs = tokens.astype(F32)
    attn = jnp.dot(mixed, output_full, preferred_element_type=F32)
    middle = inputs + BRANCH_SCALE * attn
    normed_ffn = rms_norm(middle, gain_two).astype(BF16)

    normed_ffn = after(normed_ffn, *grad_far)
    row_near = near_pieces(normed_ffn, normed_ffn)
    row_far = far_pieces(*row_near)
    slots = [up_three, up_two, up_one, own_part, down_one, down_two, down_three]
    row_pieces = with_cores(normed_ffn, *row_near, *row_far)
    grad_pieces = with_cores(*after((grad_rows, *grad_near, *grad_far), row_near[0]))
    place = line.astype(jnp.int32)[None]
    far = run_experts(FAR_TILES, place, row_pieces, grad_pieces, slots, select, 0, ())
    far_back = over_cores(far[2], far[3]).astype(BF16)
    back_y, back_x = far_links(far_back)
    near = run_experts(
        NEAR_TILES, after(place, far_back), row_pieces, grad_pieces, slots, select, 4, far[4:]
    )
    hid_a, hid_b, du_a, du_b, all_rows, all_grads = near[4:]

    def weight_grads(rows, grads, grad_both, hidden):
        inner = contract(rows, grad_both, 0, 0)
        outer = contract(grads, hidden, 0, 0) * BRANCH_SCALE
        return [
            jnp.concatenate(
                [inner[:, 2 * half * i : 2 * half * (i + 1)], outer[:, half * i : half * (i + 1)]],
                axis=1,
            ).astype(BF16)
            for i in range(2)
        ]

    rows_early, grads_early, back_y, back_x = lax.optimization_barrier(
        (all_rows, all_grads, back_y, back_x)
    )
    outer_grads = weight_grads(rows_early, grads_early, du_a, hid_a)
    grads_of = dict(zip(SLOT_ORDER[:2], outer_grads))
    far_line = (line_up(outer_grads[1]), line_down(outer_grads[0]))
    near_back = over_cores(after(near[2], *outer_grads), near[3])
    first, second = near_links(near_back, back_y, back_x)
    rows_late, grads_late = after((all_rows, all_grads), first, second)
    inner_grads = weight_grads(rows_late, grads_late, du_b, hid_b)
    grads_of.update(zip(SLOT_ORDER[2:], inner_grads))
    first, second = swap_seq(first), swap_y(second)
    near_back = after(near_back, *inner_grads)
    grad_normed_ffn = own_sum(near_back, back_y, back_x, first, second)

    def line_partial(first, *rest):
        value = grads_of[first]
        for where, expert in enumerate(rest):
            value = jnp.where(line > where, grads_of[expert], value)
        return value.astype(F32)

    def line_step(step, arrived):
        up, down = arrived
        last = LINE - 1
        right = line_partial(*range(last - step, LINE)) + up.astype(F32)
        left = grads_of[step]
        for where in range(step):
            left = jnp.where(line < last - where, grads_of[step - 1 - where], left)
        left = left.astype(F32) + down.astype(F32)
        return right.astype(BF16), left.astype(BF16)

    grad_final = cotangent.astype(F32)
    grad_norm, grad_gain_two = norm_back(middle, gain_two, grad_normed_ffn)
    grad_middle = grad_final + grad_norm
    grad_attn = (BRANCH_SCALE * grad_middle).astype(BF16)
    grad_mixed = contract(grad_attn, output_full, 1, 1).astype(BF16)
    grad_w_output = contract(mixed, grad_attn, 0, 0)
    grad_other = swap_seq(half_of(grad_mixed, 1 - seq))
    far_f, far_f_other, near_f, near_f_other = after(
        (far[0], far[1], near[0], near[1]), grad_mixed
    )
    far_ffn = over_cores(far_f, far_f_other).astype(BF16)
    ffn_y, ffn_x = far_links(after(far_ffn, grad_w_output))
    near_ffn = over_cores(near_f, near_f_other)
    right, left = line_step(1, far_line)
    grad_other = after(grad_other, right, left, far_ffn, grad_w_output)
    grad_sorted = to_order(half_of(grad_mixed, seq), grad_other)
    mid_line = (line_up(right), line_down(left))
    grad_query, grad_keys, grad_values = attend_back(
        query,
        keys,
        values,
        grad_sorted,
        jnp.concatenate([levels_one, levels_two], axis=0),
        start_column,
        cos,
        sin,
    )
    (grad_query, grad_keys, grad_values), mid_line, ffn_y, ffn_x = lax.optimization_barrier(
        ((grad_query, grad_keys, grad_values), mid_line, ffn_y, ffn_x)
    )
    right, left = line_step(2, mid_line)
    last_first = (line_up(right[:cut]), line_down(left[:cut]))
    first_ffn, second_ffn = near_links(near_ffn, ffn_y, ffn_x)
    first_ffn, second_ffn = swap_seq(first_ffn), swap_y(second_ffn)
    ffn = own_sum(near_ffn, ffn_y, ffn_x, first_ffn, second_ffn)
    output = (middle + BRANCH_SCALE * ffn).astype(BF16)
    grads_qkv = after((grad_query, grad_keys, grad_values), right, left)
    wide = qkv_grad(normed, grads_qkv, grad_gain_two[None, :], shard)


    def chosen(value, which, axis):
        return lax.dynamic_index_in_dim(value, which, axis=axis, keepdims=False)

    summed_output = lax.psum_scatter(
        grad_w_output.astype(BF16), ("seq", "dp"), scatter_dimension=0, tiled=True
    )
    kept = chosen(wide, core, 0).astype(F32)
    kept = kept + swap_core(chosen(wide, 1 - core, 0)).astype(F32)
    grads_late = after(grads_qkv, kept)
    grad_normed, sent_normed = token_grad(
        grads_late, w_qkv, own_places[:, None], other_places[:, None]
    )
    kept, sent_normed = lax.optimization_barrier((kept, sent_normed))
    right_late, left_late = after((right[cut:], left[cut:]), last_first, sent_normed)
    last_late = (line_up(right_late), line_down(left_late))
    grad_normed = grad_normed.astype(F32) + swap_seq(sent_normed).astype(F32)
    scale = lax.rsqrt(jnp.mean(inputs * inputs, axis=-1, keepdims=True) + EPSILON)
    unit = inputs * scale
    scaled = grad_normed * gain_one
    inner = jnp.mean(scaled * unit, axis=-1, keepdims=True)
    grad_tokens = grad_middle + scale * (scaled - unit * inner)
    next_kept = chosen(kept, row_of, 0)
    next_kept = next_kept + swap_y(chosen(kept, 1 - row_of, 0).astype(BF16)).astype(F32)
    next_kept, last_first, last_late, summed_output = lax.optimization_barrier(
        (next_kept, last_first, last_late, summed_output)
    )
    own_grads = line_partial(*range(LINE))
    part_grads = jnp.concatenate(
        [
            own + up.astype(F32) + down.astype(F32)
            for own, (up, down) in ((own_grads[:cut], last_first), (own_grads[cut:], last_late))
        ],
        axis=0,
    ).astype(BF16)
    same_grads = jnp.where(first_core, part_grads[:, :half], part_grads[:, half : 2 * half])
    cross_grads = jnp.where(first_core, part_grads[:, half : 2 * half], part_grads[:, :half])
    same_grads = jnp.concatenate([same_grads, part_grads[:, 2 * half :]], axis=1)
    next_kept, same_grads, cross_grads = lax.optimization_barrier(
        (next_kept, same_grads, cross_grads)
    )
    same = both_axes(same_grads, straight)
    cross = both_axes(cross_grads, crossed_back)
    sent_lines = [
        swap_dp(chosen(next_kept, line ^ step, 1).astype(BF16), 4 * step) for step in range(1, LINE)
    ]
    summed = chosen(next_kept, line, 1) + sum(value.astype(F32) for value in sent_lines)
    summed, same, cross = lax.optimization_barrier((summed, same, cross))
    grad_w_in = ordered(same[:, :half], cross, 1)
    grad_w_out = same[:, half:].T
    kept_rows = chosen(summed, seq, 0)
    sent_rows = swap_seq(chosen(summed, 1 - seq, 0).astype(BF16)).astype(F32)
    cuts = (q_width, q_width + kv_width, qkv_width)
    pieces = [
        (a, b) for a, b in zip(jnp.split(kept_rows, cuts, axis=1), jnp.split(sent_rows, cuts, axis=1))
    ]
    grad_projections = [ordered(a, b, 1) for a, b in pieces[:3]]
    grad_gain_ffn = (pieces[3][0] + pieces[3][1])[:, 0]
    grad_gain_attn = sum(
        jnp.sum(grad * weight.astype(F32), axis=1)
        for grad, weight in zip(grad_projections, projections)
    ) / gain_attn.astype(F32)
    return (
        output,
        grad_tokens,
        grad_projections[0],
        grad_projections[1],
        grad_projections[2],
        summed_output.astype(F32),
        grad_gain_attn,
        grad_gain_ffn,
        grad_w_in.astype(F32)[None],
        grad_w_out.astype(F32)[None],
    )


def solution(mesh):
    placed = (
        P(("seq", "dp"), None),
        P(("seq", "dp"), None),
        P("dp", None),
        P("dp", None),
        P(("seq", "dp"), None),
        P(("seq", "dp"), None),
        P(("seq", "dp"), None),
        P(("seq", "dp"), None),
        P(("seq", "dp"), None),
        P(("seq", "dp"), None),
        P(("seq", "dp")),
        P(("seq", "dp")),
        P("dp", None, "seq"),
        P("dp", "seq", None),
    )
    return jax.shard_map(
        shards_plane if in_planes(mesh) else shards_general,
        mesh=mesh,
        in_specs=placed,
        out_specs=(
            P(("seq", "dp"), None),
            P(("seq", "dp"), None),
            P(("seq", "dp"), None),
            P(("seq", "dp"), None),
            P(("seq", "dp"), None),
            P(("seq", "dp"), None),
            P(("seq", "dp")),
            P(("seq", "dp")),
            P("dp", None, "seq"),
            P("dp", "seq", None),
        ),
        check_vma=False,
    )
```

```python
import functools

import jax
import jax.numpy as jnp
from jax import lax
from jax.experimental import pallas as pl
from jax.experimental.pallas import tpu as pltpu
from jax.sharding import PartitionSpec as P

QHEADS = 24
KVHEADS = 8
HDIM = 64
FF = 512
TOP = 8


EPSILON = 1e-06
BRANCH_SCALE = 0.22
SCORE_SCALE = 1.0 / 64.0
THETA = 10000.0


def rms_norm(value, gain):
    return value * lax.rsqrt(jnp.mean(value * value, axis=-1, keepdims=True) + EPSILON) * gain


def local_places(placing, seq_lengths):
    ends = jnp.cumsum(seq_lengths)
    segment = jnp.sum((placing[:, None] >= ends[None, :]).astype(jnp.int32), axis=1)
    starts = ends - seq_lengths
    member = segment[:, None] == jnp.arange(seq_lengths.shape[0], dtype=jnp.int32)[None, :]
    start_of = jnp.sum(jnp.where(member, starts[None, :], 0), axis=1)
    return (segment, placing - start_of)


def rotate(values, place, direction):
    half = values.shape[-1] // 2
    freqs = jnp.power(THETA, -jnp.arange(half, dtype=jnp.float32) * 2.0 / values.shape[-1])
    angles = place.astype(jnp.float32)[:, None] * freqs[None, :]
    cosine = jnp.cos(angles)[:, None, :]
    sine = direction * jnp.sin(angles)[:, None, :]
    first = values[..., :half]
    second = values[..., half:]
    return jnp.concatenate(
        [first * cosine - second * sine, second * cosine + first * sine], axis=-1
    )


def shards_general(
    tokens,
    cotangent,
    positions,
    lengths,
    routes,
    logits,
    w_query,
    w_key,
    w_value,
    w_output,
    gain_attn,
    gain_ffn,
    w_in,
    w_out,
):
    seq_count = lax.axis_size("seq")
    data_count = lax.axis_size("dp")
    tok_count = tokens.shape[0]
    group_len = positions.shape[1]
    local_experts = w_in.shape[0]
    experts_all = local_experts * data_count
    capacity = min(tok_count, 5 * tok_count * TOP // (4 * experts_all))
    heads_local = QHEADS // seq_count
    kv_local = KVHEADS // seq_count
    ratio = QHEADS // KVHEADS
    width = tokens.shape[1]
    query_full, key_full, value_full, output_full, gain_one, gain_two = (
        lax.all_gather(w_query, ("seq", "dp"), axis=0, tiled=True),
        lax.all_gather(w_key, ("seq", "dp"), axis=0, tiled=True),
        lax.all_gather(w_value, ("seq", "dp"), axis=0, tiled=True),
        lax.all_gather(w_output, ("seq", "dp"), axis=0, tiled=True),
        lax.all_gather(gain_attn, ("seq", "dp"), axis=0, tiled=True),
        lax.all_gather(gain_ffn, ("seq", "dp"), axis=0, tiled=True),
    )
    in_full, out_full = (
        lax.all_gather(w_in, "seq", axis=2, tiled=True),
        lax.all_gather(w_out, "seq", axis=1, tiled=True),
    )
    gain_one = gain_one.astype(jnp.float32)
    gain_two = gain_two.astype(jnp.float32)
    segment, place = local_places(positions[0], lengths[0])
    my_start = lax.axis_index("seq") * tok_count
    my_place = lax.dynamic_slice_in_dim(place, my_start, tok_count)
    inputs = tokens.astype(jnp.float32)
    normed = rms_norm(inputs, gain_one).astype(jnp.bfloat16)
    query_pre = jnp.dot(normed, query_full, preferred_element_type=jnp.float32)
    key_pre = jnp.dot(normed, key_full, preferred_element_type=jnp.float32)
    query_rot = (
        rotate(query_pre.reshape(tok_count, QHEADS, HDIM), my_place, 1.0)
        .reshape(tok_count, QHEADS * HDIM)
        .astype(jnp.bfloat16)
    )
    key_rot = (
        rotate(key_pre.reshape(tok_count, KVHEADS, HDIM), my_place, 1.0)
        .reshape(tok_count, KVHEADS * HDIM)
        .astype(jnp.bfloat16)
    )
    value_low = jnp.dot(normed, value_full, preferred_element_type=jnp.float32).astype(jnp.bfloat16)
    query_heads, key_heads, value_heads = (
        lax.all_to_all(query_rot, "seq", split_axis=1, concat_axis=0, tiled=True),
        lax.all_to_all(key_rot, "seq", split_axis=1, concat_axis=0, tiled=True),
        lax.all_to_all(value_low, "seq", split_axis=1, concat_axis=0, tiled=True),
    )
    keys_three = key_heads.reshape(group_len, kv_local, HDIM)
    values_three = value_heads.reshape(group_len, kv_local, HDIM)
    length = min(512, group_len)
    count = group_len // length

    def scores_of(query_block, seg_block, place_block):
        grouped = query_block.reshape(length, kv_local, ratio, HDIM)
        raw_scores = (
            jnp.einsum("qgrd,kgd->grqk", grouped, keys_three, preferred_element_type=jnp.float32)
            * SCORE_SCALE
        )
        allowed = (seg_block[:, None] == segment[None, :]) & (
            place[None, :] <= place_block[:, None]
        )
        return jnp.where(allowed[None, None], raw_scores, -1e30)

    def forward_block(pieces):
        query_block, seg_block, place_block = pieces
        scores = scores_of(query_block, seg_block, place_block)
        highest = jnp.max(scores, axis=-1, keepdims=True)
        expon = jnp.exp(scores - highest)
        totals = jnp.sum(expon, axis=-1, keepdims=True)
        probs = expon / totals
        mixed = jnp.einsum(
            "grqk,kgd->qgrd",
            probs.astype(jnp.bfloat16),
            values_three,
            preferred_element_type=jnp.float32,
        )
        return (
            mixed.reshape(length, heads_local * HDIM).astype(jnp.bfloat16),
            highest + jnp.log(totals),
            probs,
        )

    query_blocks = query_heads.reshape(count, length, heads_local * HDIM)
    seg_blocks = segment.reshape(count, length)
    place_blocks = place.reshape(count, length)
    block_args = (query_blocks, seg_blocks, place_blocks)

    def forward_light(pieces):
        mixed, lse_part, unused_probs = forward_block(pieces)
        return (mixed, lse_part)

    mixed_blocks, lse_blocks = lax.map(forward_light, block_args)
    mixed_heads = mixed_blocks.reshape(group_len, heads_local * HDIM)
    mixed_tokens = lax.all_to_all(mixed_heads, "seq", split_axis=0, concat_axis=1, tiled=True)
    attn = jnp.dot(mixed_tokens, output_full, preferred_element_type=jnp.float32)
    middle = inputs + BRANCH_SCALE * attn
    normed_ffn = rms_norm(middle, gain_two).astype(jnp.bfloat16)
    chosen = routes.reshape(-1)
    onehot = (chosen[:, None] == jnp.arange(experts_all, dtype=jnp.int32)[None, :]).astype(
        jnp.int32
    )
    ranking = jnp.sum(jnp.cumsum(onehot, axis=0) * onehot, axis=1) - 1
    target = chosen * capacity + ranking
    token_of = jnp.arange(tok_count * TOP, dtype=jnp.int32) // TOP
    gates = jax.nn.softmax(logits, axis=-1)
    source = jnp.full((experts_all * capacity,), tok_count, jnp.int32).at[target].set(token_of)
    slot_gate = jnp.zeros((experts_all * capacity,), jnp.float32).at[target].set(gates.reshape(-1))
    padded = jnp.concatenate([normed_ffn, jnp.zeros((1, width), jnp.bfloat16)], axis=0)
    outgoing = padded[source].reshape(data_count, local_experts * capacity, width)

    def expert_layout(arrived):
        return jnp.swapaxes(
            arrived.reshape(data_count, local_experts, capacity, width), 0, 1
        ).reshape(local_experts, data_count * capacity, width)

    def home_layout(values):
        return jnp.swapaxes(
            values.reshape(local_experts, data_count, capacity, width), 0, 1
        ).reshape(data_count, local_experts * capacity, width)

    def expert_forward(expert_rows):
        both = jnp.einsum("erd,edf->erf", expert_rows, in_full, preferred_element_type=jnp.float32)
        hidden = (jax.nn.silu(both[..., :FF]) * both[..., FF:]).astype(jnp.bfloat16)
        return (both, hidden)

    expert_rows = expert_layout(
        lax.all_to_all(outgoing, "dp", split_axis=0, concat_axis=0, tiled=True)
    )
    both, hidden = expert_forward(expert_rows)
    result = jnp.einsum(
        "erf,efd->erd", hidden, out_full, preferred_element_type=jnp.float32
    ).astype(jnp.bfloat16)
    returned = lax.all_to_all(
        home_layout(result), "dp", split_axis=0, concat_axis=0, tiled=True
    ).reshape(experts_all * capacity, width)
    picked = returned[target].reshape(tok_count, TOP, width).astype(jnp.float32)
    ffn = jnp.sum(picked * gates[:, :, None], axis=1)
    final = middle + BRANCH_SCALE * ffn
    output = final.astype(jnp.bfloat16)
    grad_final = cotangent.astype(jnp.float32)
    padded_grad = jnp.concatenate(
        [BRANCH_SCALE * grad_final, jnp.zeros((1, width), jnp.float32)], axis=0
    )
    grad_slots = (slot_gate[:, None] * padded_grad[source]).astype(jnp.bfloat16)
    grad_result = expert_layout(
        lax.all_to_all(
            grad_slots.reshape(data_count, local_experts * capacity, width),
            "dp",
            split_axis=0,
            concat_axis=0,
            tiled=True,
        )
    )
    rows_back = expert_layout(
        lax.all_to_all(outgoing, "dp", split_axis=0, concat_axis=0, tiled=True)
    )
    both_back, hidden_back = expert_forward(rows_back)
    grad_hidden = jnp.einsum(
        "erd,efd->erf", grad_result, out_full, preferred_element_type=jnp.float32
    )
    gate_part = both_back[..., :FF]
    up_part = both_back[..., FF:]
    sigma = jax.nn.sigmoid(gate_part)
    grad_gate = grad_hidden * up_part * sigma * (1.0 + gate_part * (1.0 - sigma))
    grad_up = grad_hidden * gate_part * sigma
    grad_both = jnp.concatenate([grad_gate, grad_up], axis=-1).astype(jnp.bfloat16)
    grad_out_local = jnp.einsum(
        "erf,erd->efd", hidden_back, grad_result, preferred_element_type=jnp.float32
    )
    grad_in_local = jnp.einsum(
        "erd,erf->edf", rows_back, grad_both, preferred_element_type=jnp.float32
    )
    grad_rows = jnp.einsum(
        "erf,edf->erd", grad_both, in_full, preferred_element_type=jnp.float32
    ).astype(jnp.bfloat16)
    grad_home = lax.all_to_all(
        home_layout(grad_rows), "dp", split_axis=0, concat_axis=0, tiled=True
    ).reshape(experts_all * capacity, width)
    grad_normed_ffn = jnp.sum(
        grad_home[target].reshape(tok_count, TOP, width).astype(jnp.float32), axis=1
    )
    grad_w_in, grad_w_out = (
        lax.psum_scatter(
            grad_in_local.astype(jnp.bfloat16), "seq", scatter_dimension=2, tiled=True
        ).astype(jnp.float32),
        lax.psum_scatter(
            grad_out_local.astype(jnp.bfloat16), "seq", scatter_dimension=1, tiled=True
        ).astype(jnp.float32),
    )
    unused_norm, norm_pull = jax.vjp(rms_norm, middle, gain_two)
    grad_middle_norm, grad_gain_two = norm_pull(grad_normed_ffn)
    grad_middle = grad_final + grad_middle_norm
    grad_attn = (BRANCH_SCALE * grad_middle).astype(jnp.bfloat16)
    grad_w_output = jnp.einsum(
        "te,td->ed", mixed_tokens, grad_attn, preferred_element_type=jnp.float32
    )
    grad_mixed = jnp.einsum(
        "td,ed->te", grad_attn, output_full, preferred_element_type=jnp.float32
    ).astype(jnp.bfloat16)
    grad_mixed_heads = lax.all_to_all(grad_mixed, "seq", split_axis=1, concat_axis=0, tiled=True)
    grad_blocks = grad_mixed_heads.reshape(count, length, heads_local * HDIM)
    back_args = (query_blocks, seg_blocks, place_blocks, lse_blocks, grad_blocks)

    def backward_block(carry, pieces):
        grad_keys, grad_values = carry
        query_block, seg_block, place_block, lse_block, grad_block = pieces[:5]
        probs = jnp.exp(scores_of(query_block, seg_block, place_block) - lse_block)
        grad_out = grad_block.reshape(length, kv_local, ratio, HDIM)
        grad_probs = jnp.einsum(
            "qgrd,kgd->grqk", grad_out, values_three, preferred_element_type=jnp.float32
        )
        grad_scores = (
            probs * (grad_probs - jnp.sum(probs * grad_probs, axis=-1, keepdims=True))
        ).astype(jnp.bfloat16)
        grad_query = SCORE_SCALE * jnp.einsum(
            "grqk,kgd->qgrd", grad_scores, keys_three, preferred_element_type=jnp.float32
        )
        grouped = query_block.reshape(length, kv_local, ratio, HDIM)
        grad_keys = grad_keys + SCORE_SCALE * jnp.einsum(
            "grqk,qgrd->kgd", grad_scores, grouped, preferred_element_type=jnp.float32
        )
        grad_values = grad_values + jnp.einsum(
            "grqk,qgrd->kgd",
            probs.astype(jnp.bfloat16),
            grad_out,
            preferred_element_type=jnp.float32,
        )
        return (
            (grad_keys, grad_values),
            grad_query.reshape(length, heads_local * HDIM).astype(jnp.bfloat16),
        )

    empty_keys = jnp.zeros((group_len, kv_local, HDIM), jnp.float32)
    (grad_keys, grad_values), grad_query_blocks = lax.scan(
        backward_block, (empty_keys, empty_keys), back_args
    )
    grad_query_heads = grad_query_blocks.reshape(group_len, heads_local * HDIM)
    grad_key_heads = grad_keys.reshape(group_len, kv_local * HDIM).astype(jnp.bfloat16)
    grad_value_heads = grad_values.reshape(group_len, kv_local * HDIM).astype(jnp.bfloat16)
    grad_query_tok, grad_key_tok, grad_value_tok = (
        lax.all_to_all(grad_query_heads, "seq", split_axis=0, concat_axis=1, tiled=True),
        lax.all_to_all(grad_key_heads, "seq", split_axis=0, concat_axis=1, tiled=True),
        lax.all_to_all(grad_value_heads, "seq", split_axis=0, concat_axis=1, tiled=True),
    )
    grad_query_pre = (
        rotate(grad_query_tok.astype(jnp.float32).reshape(tok_count, QHEADS, HDIM), my_place, -1.0)
        .reshape(tok_count, QHEADS * HDIM)
        .astype(jnp.bfloat16)
    )
    grad_key_pre = (
        rotate(grad_key_tok.astype(jnp.float32).reshape(tok_count, KVHEADS, HDIM), my_place, -1.0)
        .reshape(tok_count, KVHEADS * HDIM)
        .astype(jnp.bfloat16)
    )
    grad_w_query = jnp.einsum(
        "td,te->de", normed, grad_query_pre, preferred_element_type=jnp.float32
    )
    grad_w_key = jnp.einsum("td,te->de", normed, grad_key_pre, preferred_element_type=jnp.float32)
    grad_w_value = jnp.einsum(
        "td,te->de", normed, grad_value_tok, preferred_element_type=jnp.float32
    )
    grad_normed = jnp.einsum(
        "te,de->td", grad_query_pre, query_full, preferred_element_type=jnp.float32
    )
    grad_normed = grad_normed + jnp.einsum(
        "te,de->td", grad_key_pre, key_full, preferred_element_type=jnp.float32
    )
    grad_normed = grad_normed + jnp.einsum(
        "te,de->td", grad_value_tok, value_full, preferred_element_type=jnp.float32
    )
    unused_first, first_pull = jax.vjp(rms_norm, inputs, gain_one)
    grad_inputs_norm, grad_gain_one = first_pull(grad_normed)
    grad_tokens = grad_middle + grad_inputs_norm
    summed = (
        lax.psum_scatter(grad_w_query, ("seq", "dp"), scatter_dimension=0, tiled=True),
        lax.psum_scatter(grad_w_key, ("seq", "dp"), scatter_dimension=0, tiled=True),
        lax.psum_scatter(grad_w_value, ("seq", "dp"), scatter_dimension=0, tiled=True),
        lax.psum_scatter(grad_w_output, ("seq", "dp"), scatter_dimension=0, tiled=True),
        lax.psum_scatter(grad_gain_one, ("seq", "dp"), scatter_dimension=0, tiled=True),
        lax.psum_scatter(grad_gain_two, ("seq", "dp"), scatter_dimension=0, tiled=True),
    )
    return (
        output,
        grad_tokens,
        summed[0],
        summed[1],
        summed[2],
        summed[3],
        summed[4],
        summed[5],
        grad_w_in,
        grad_w_out,
    )


BF16 = jnp.bfloat16
F32 = jnp.float32
LINE = 4
PAD = 128
VMEM_BYTES = 60 * 1024 * 1024


def in_planes(mesh):
    return mesh.shape["seq"] == 2 and mesh.shape["dp"] == 4 * LINE


def swap_seq(value):
    return lax.ppermute(value, "seq", [(0, 1), (1, 0)])


def swap_dp(value, mask):
    return lax.ppermute(value, "dp", [(i, i ^ mask) for i in range(4 * LINE)])


def swap_core(value):
    return swap_dp(value, 1)


def swap_y(value):
    return swap_dp(value, 2)


def line_up(value):
    return lax.ppermute(value, "dp", [(i, i + 4) for i in range(4 * LINE - 4)])


def line_down(value):
    return lax.ppermute(value, "dp", [(i, i - 4) for i in range(4, 4 * LINE)])


def after(value, *others):
    return lax.optimization_barrier((value,) + others)[0]


def line_scatter(take, place):
    up = down = None
    for step in range(LINE - 1):
        far = jnp.minimum(LINE - 1 - step + place, LINE - 1)
        near = jnp.maximum(step - LINE + 1 + place, 0)
        right, left = take(far), take(near)
        if up is not None:
            right = right + up.astype(F32)
            left = left + down.astype(F32)
        up = line_up(right.astype(BF16))
        down = line_down(left.astype(BF16))
    return take(place) + up.astype(F32) + down.astype(F32)


def near_pieces(own, own_x):
    return swap_seq(own_x), swap_y(own)


def far_pieces(near_x, near_y):
    half = near_x.shape[0] // 2
    return swap_y(near_x[:half]), swap_seq(near_y[half:])


def with_cores(*pieces):
    return pieces + tuple(swap_core(piece) for piece in pieces)


def over_cores(mine, others):
    return mine.astype(F32) + swap_core(others).astype(F32)


def far_links(far):
    half = far.shape[0] // 2
    return swap_y(far[:half]), swap_seq(far[half:])


def near_links(near, from_y, from_x):
    half = from_y.shape[0] // 2
    first = (near[:half] + from_y[half:].astype(F32)).astype(BF16)
    second = (near[half : 2 * half] + from_x[half:].astype(F32)).astype(BF16)
    return first, second


def own_sum(near, from_y, from_x, first, second):
    half = from_y.shape[0] // 2
    low = near[2 * half : 3 * half] + from_y[:half].astype(F32) + first.astype(F32)
    high = near[3 * half :] + from_x[:half].astype(F32) + second.astype(F32)
    return jnp.concatenate([low, high], axis=0)


def turned(values, cos, sin, direction):
    lanes = values.shape[1]
    place = lax.broadcasted_iota(jnp.int32, values.shape, 1) % HDIM
    swapped = jnp.where(
        place < HDIM // 2,
        pltpu.roll(values, lanes - HDIM // 2, 1),
        pltpu.roll(values, HDIM // 2, 1),
    )
    times = lanes // cos.shape[1]
    cos = jnp.concatenate([cos] * times, axis=1)
    sin = jnp.concatenate([sin] * times, axis=1)
    if direction > 0:
        return values * cos + swapped * sin
    return values * cos - swapped * sin


def qkv_kernel(x_ref, gain_ref, w_ref, cos_ref, sin_ref, h_ref, q_ref, k_ref, v_ref):
    value = x_ref[...].astype(F32)
    scale = lax.rsqrt(jnp.mean(value * value, axis=-1, keepdims=True) + EPSILON)
    normed = (value * scale * gain_ref[...]).astype(BF16)
    h_ref[...] = normed
    both = jnp.dot(normed, w_ref[...], preferred_element_type=F32)
    q_width, kv_heads = q_ref.shape[1], k_ref.shape[0]
    kv_width = kv_heads * HDIM
    spun = turned(both[:, : q_width + kv_width], cos_ref[...], sin_ref[...], 1)
    q_ref[...] = (spun[:, :q_width] * SCORE_SCALE).astype(BF16)
    for head in range(kv_heads):
        low = q_width + head * HDIM
        k_ref[head] = spun[:, low : low + HDIM].astype(BF16)
        low = low + kv_width
        v_ref[head] = both[:, low : low + HDIM].astype(BF16)


def project(x_sorted, gain, weights, cos, sin, q_width, kv_heads):
    rows, width = x_sorted.shape
    tile = 256
    columns = q_width + 2 * kv_heads * HDIM

    def row_block(lanes):
        return pl.BlockSpec((tile, lanes), lambda i: (i, 0))

    heads = pl.BlockSpec((kv_heads, tile, HDIM), lambda i: (0, i, 0))
    return pl.pallas_call(
        qkv_kernel,
        grid=(rows // tile,),
        in_specs=[
            row_block(width),
            pl.BlockSpec((1, width), lambda i: (0, 0)),
            pl.BlockSpec((width, columns), lambda i: (0, 0)),
            row_block(cos.shape[1]),
            row_block(cos.shape[1]),
        ],
        out_specs=[row_block(width), row_block(q_width), heads, heads],
        out_shape=[
            jax.ShapeDtypeStruct((rows, width), BF16),
            jax.ShapeDtypeStruct((rows, q_width), BF16),
            jax.ShapeDtypeStruct((kv_heads, rows, HDIM), BF16),
            jax.ShapeDtypeStruct((kv_heads, rows, HDIM), BF16),
        ],
        compiler_params=pltpu.CompilerParams(vmem_limit_bytes=VMEM_BYTES),
        cost_estimate=pl.CostEstimate(
            flops=rows * width * columns // 8,
            bytes_accessed=rows * width + width * columns,
            transcendentals=rows,
        ),
        name="project",
    )(x_sorted, gain, weights, cos, sin)


def token_grad_kernel(dq_ref, dk_ref, dv_ref, w_ref, own_ref, other_ref, mine_ref, sent_ref):
    q_width, kv_width = dq_ref.shape[1], dk_ref.shape[1]
    cuts = (0, q_width, q_width + kv_width, q_width + 2 * kv_width)
    grad = contract(dq_ref[...], w_ref[:, cuts[0] : cuts[1]], 1, 1)
    grad = grad + contract(dk_ref[...], w_ref[:, cuts[1] : cuts[2]], 1, 1)
    grad = (grad + contract(dv_ref[...], w_ref[:, cuts[2] : cuts[3]], 1, 1)).astype(BF16)
    for place_ref, out_ref in ((other_ref, sent_ref), (own_ref, mine_ref)):
        shape = (place_ref.shape[0], grad.shape[0])
        picked = lax.broadcasted_iota(jnp.int32, shape, 1) == place_ref[...]
        picked = jnp.where(picked, 1.0, 0.0).astype(BF16)
        out_ref[...] = jnp.dot(picked, grad, preferred_element_type=F32).astype(BF16)


def token_grad(grads, weights, own_places, other_places):
    rows, count = grads[0].shape[0], own_places.shape[0]
    width = weights.shape[0]
    columns = sum(grad.shape[1] for grad in grads)
    tile = width // 3

    def whole(array):
        return pl.BlockSpec(array.shape, lambda i: (0, 0))

    block = pl.BlockSpec((count, tile), lambda i: (0, i))
    return pl.pallas_call(
        token_grad_kernel,
        grid=(3,),
        in_specs=[whole(grad) for grad in grads]
        + [pl.BlockSpec((tile, columns), lambda i: (i, 0)), whole(own_places), whole(other_places)],
        out_specs=[block, block],
        out_shape=[jax.ShapeDtypeStruct((count, width), BF16)] * 2,
        compiler_params=pltpu.CompilerParams(vmem_limit_bytes=VMEM_BYTES),
        cost_estimate=pl.CostEstimate(
            flops=rows * width * columns // 8, bytes_accessed=rows * width, transcendentals=0
        ),
        name="token_grad",
    )(*grads, weights, own_places, other_places)


Q_TILE = 256


def windows(rows):
    longest = rows // 2
    for start in range(0, rows, Q_TILE):
        low = max(0, start - longest + 1) // Q_TILE * Q_TILE
        yield start, low, start + Q_TILE


def allowed_keys(start_ref, row, low, high):
    shape = (Q_TILE, high - low)
    rows = lax.broadcasted_iota(jnp.int32, shape, 0) + row
    keys = lax.broadcasted_iota(jnp.int32, shape, 1) + low
    return (keys <= rows) & (keys >= start_ref[row : row + Q_TILE, :])


def contract(left, right, left_dim, right_dim):
    return lax.dot_general(
        left, right, (((left_dim,), (right_dim,)), ((), ())), preferred_element_type=F32
    )


def masked_scores(query, keys, allowed):
    return jnp.where(allowed, contract(query, keys, 1, 1), -1e30)


def attend_kernel(base, q_ref, k_ref, v_ref, start_ref, o_ref, level_ref):
    pair = pl.program_id(0) + base
    ratio = QHEADS // KVHEADS
    for row, low, high in windows(q_ref.shape[0]):
        allowed = allowed_keys(start_ref, row, low, high)
        for side in range(2):
            head = (2 * pair + side) // ratio
            lanes = slice(side * HDIM, (side + 1) * HDIM)
            scores = masked_scores(
                q_ref[row : row + Q_TILE, lanes], k_ref[head, low:high, :], allowed
            )
            highest = jnp.max(scores, axis=-1, keepdims=True)
            expon = jnp.exp(scores - highest)
            total = jnp.sum(expon, axis=-1, keepdims=True)
            level_ref[0, row : row + Q_TILE, side : side + 1] = highest + jnp.log(total)
            probs = expon * (1.0 / total)
            mixed = contract(probs.astype(BF16), v_ref[head, low:high, :], 1, 0)
            o_ref[row : row + Q_TILE, lanes] = mixed.astype(BF16)


def attention_cost(rows, heads, products):
    area = sum(Q_TILE * (high - low) for _, low, high in windows(rows))
    return pl.CostEstimate(
        flops=products * heads * area * 16,
        bytes_accessed=8 * rows * heads * HDIM,
        transcendentals=heads * area,
    )


def attend(query, keys, values, starts, base, pairs):
    rows = query.shape[0]
    pair_block = pl.BlockSpec((rows, 2 * HDIM), lambda j: (0, j + base))
    whole = pl.BlockSpec(keys.shape, lambda j: (0, 0, 0))
    return pl.pallas_call(
        functools.partial(attend_kernel, base),
        grid=(pairs,),
        in_specs=[pair_block, whole, whole, pl.BlockSpec((rows, 1), lambda j: (0, 0))],
        out_specs=[
            pl.BlockSpec((rows, 2 * HDIM), lambda j: (0, j)),
            pl.BlockSpec((1, rows, 2), lambda j: (j, 0, 0)),
        ],
        out_shape=[
            jax.ShapeDtypeStruct((rows, pairs * 2 * HDIM), BF16),
            jax.ShapeDtypeStruct((pairs, rows, 2), F32),
        ],
        compiler_params=pltpu.CompilerParams(vmem_limit_bytes=VMEM_BYTES),
        cost_estimate=attention_cost(rows, 2 * pairs, 2),
        name="attend",
    )(query, keys, values, starts)


def attend_back_kernel(
    q_ref, k_ref, v_ref, d_ref, level_ref, start_ref, cos_ref, sin_ref,
    dq_ref, dk_ref, dv_ref, dk_sum, dv_sum,
):
    pair = pl.program_id(0)
    ratio = QHEADS // KVHEADS

    @pl.when(pair == 0)
    def _():
        dk_sum[...] = jnp.zeros_like(dk_sum)
        dv_sum[...] = jnp.zeros_like(dv_sum)

    for row, low, high in windows(q_ref.shape[0]):
        allowed = allowed_keys(start_ref, row, low, high)
        grads = []
        for side in range(2):
            head = (2 * pair + side) // ratio
            lanes = slice(side * HDIM, (side + 1) * HDIM)
            query = q_ref[row : row + Q_TILE, lanes]
            keys = k_ref[head, low:high, :]
            probs = jnp.exp(
                masked_scores(query, keys, allowed)
                - level_ref[0, row : row + Q_TILE, side : side + 1]
            )
            grad_out = d_ref[row : row + Q_TILE, lanes]
            grad_probs = contract(grad_out, v_ref[head, low:high, :], 1, 1)
            inner = jnp.sum(probs * grad_probs, axis=-1, keepdims=True)
            grad_scores = (probs * (grad_probs - inner)).astype(BF16)
            grads.append(contract(grad_scores, keys, 1, 0) * SCORE_SCALE)
            dk_sum[head, low:high, :] += contract(grad_scores, query, 0, 0)
            dv_sum[head, low:high, :] += contract(probs.astype(BF16), grad_out, 0, 0)
        grad_query = jnp.concatenate(grads, axis=1).astype(BF16).astype(F32)
        dq_ref[row : row + Q_TILE, :] = turned(
            grad_query,
            cos_ref[row : row + Q_TILE, :],
            sin_ref[row : row + Q_TILE, :],
            -1,
        ).astype(BF16)

    @pl.when(pair == pl.num_programs(0) - 1)
    def _():
        heads = range(dk_sum.shape[0])
        grad_keys = jnp.concatenate([dk_sum[head] for head in heads], axis=1)
        grad_keys = grad_keys.astype(BF16).astype(F32)
        dk_ref[...] = turned(grad_keys, cos_ref[...], sin_ref[...], -1).astype(BF16)
        dv_ref[...] = jnp.concatenate([dv_sum[head] for head in heads], axis=1).astype(BF16)


def attend_back(query, keys, values, grad_out, levels, starts, cos, sin):
    rows, lanes = query.shape
    pairs = lanes // (2 * HDIM)
    kv_heads = keys.shape[0]
    pair_block = pl.BlockSpec((rows, 2 * HDIM), lambda j: (0, j))
    whole = pl.BlockSpec(keys.shape, lambda j: (0, 0, 0))

    def fixed(lanes_of):
        return pl.BlockSpec((rows, lanes_of), lambda j: (0, 0))

    flat = kv_heads * HDIM
    return pl.pallas_call(
        attend_back_kernel,
        grid=(pairs,),
        in_specs=[
            pair_block, whole, whole, pair_block,
            pl.BlockSpec((1, rows, 2), lambda j: (j, 0, 0)), fixed(1), fixed(2 * HDIM), fixed(2 * HDIM),
        ],
        out_specs=[pair_block, fixed(flat), fixed(flat)],
        out_shape=[
            jax.ShapeDtypeStruct(query.shape, BF16),
            jax.ShapeDtypeStruct((rows, flat), BF16),
            jax.ShapeDtypeStruct((rows, flat), BF16),
        ],
        scratch_shapes=[pltpu.VMEM(keys.shape, F32), pltpu.VMEM(keys.shape, F32)],
        compiler_params=pltpu.CompilerParams(vmem_limit_bytes=VMEM_BYTES),
        cost_estimate=attention_cost(rows, 2 * pairs, 5),
        name="attend_back",
    )(query, keys, values, grad_out, levels, starts, cos, sin)


SLOTS = 2 * LINE - 1
SLOT_ORDER = (0, 3, 1, 2)
OWN, NEAR_X, NEAR_Y, FAR_Y, FAR_X = range(5)
FAR_TILES = (((NEAR_Y, 0), (FAR_Y, 0)), ((NEAR_X, 1), (FAR_X, 0)))
NEAR_TILES = (((NEAR_X, 0), (NEAR_Y, 1)), ((OWN, 0), (OWN, 1)))


def used_pieces(tiles):
    return sorted({piece for tile in tiles for piece, _ in tile})


def experts_kernel(tiles, half_rows, place_ref, *refs):
    used = used_pieces(tiles)
    sides = 2 * len(used)
    h_pieces, g_pieces, slots = refs[:sides], refs[sides : 2 * sides], refs[2 * sides : 2 * sides + SLOTS]
    select_ref = refs[2 * sides + SLOTS]
    (
        f_mine, f_other, d_mine, d_other, hid_a, hid_b, du_a, du_b, hcopy_ref, gcopy_ref,
        w_in, w_out, h_buf, g_buf, hidden, du_all, weight_sems, row_sems,
    ) = refs[-18:]
    width = h_buf.shape[2]
    half = slots[0].shape[1] // 3
    part = 2 * half
    step = pl.program_id(0)
    steps = 2 * len(tiles)

    def weight_copies(spot, slot):
        return (
            pltpu.make_async_copy(
                slots[slot].at[:, :part],
                w_in.at[:, spot * part : (spot + 1) * part],
                weight_sems.at[0, spot],
            ),
            pltpu.make_async_copy(
                slots[slot].at[:, part:],
                w_out.at[:, spot * half : (spot + 1) * half],
                weight_sems.at[1, spot],
            ),
        )

    def row_copies(number, buffer):
        side, tile = divmod(number, len(tiles))
        copies = []
        for spot, (piece, part_of) in enumerate(tiles[tile]):
            index = side * len(used) + used.index(piece)
            for kind, (pieces, held) in enumerate(((h_pieces, h_buf), (g_pieces, g_buf))):
                copies.append(
                    pltpu.make_async_copy(
                        pieces[index].at[pl.ds(part_of * half_rows, half_rows), :],
                        held.at[buffer, pl.ds(spot * half_rows, half_rows), :],
                        row_sems.at[buffer, 2 * kind + spot],
                    )
                )
        return copies

    def fetch(wanted, buffer):
        for number in range(steps):

            @pl.when(wanted == number)
            def _():
                for copy in row_copies(number, buffer):
                    copy.start()

    buffer = step % 2

    @pl.when(step == 0)
    def _():
        fetch(step, 0)
        for spot, expert in enumerate(SLOT_ORDER):
            for slot in range(expert, expert + LINE):

                @pl.when(slot == LINE - 1 + expert - place_ref[0])
                def _():
                    for copy in weight_copies(spot, slot):
                        copy.start()

        for spot in range(LINE):
            for copy in weight_copies(spot, LINE - 1):
                copy.wait()

    @pl.when(step + 1 < steps)
    def _():
        fetch(step + 1, 1 - buffer)

    for copy in row_copies(0, buffer):
        copy.wait()

    rows = h_buf[buffer]
    grads = g_buf[buffer, :, :width]
    hcopy_ref[...] = rows
    gcopy_ref[...] = grads
    gates = jnp.dot(g_buf[buffer, :, width:], select_ref[...], preferred_element_type=F32)
    for spot in range(LINE):
        units = slice(spot * half, (spot + 1) * half)
        both = jnp.dot(
            rows, w_in[:, spot * part : (spot + 1) * part], preferred_element_type=F32
        )
        back = jnp.dot(grads, w_out[:, units], preferred_element_type=F32)
        gate = gates[:, units]
        first, second = both[:, :half], both[:, half:]
        sigma = jax.nn.sigmoid(first)
        silu = first * sigma
        hidden[:, units] = (gate * (silu * second)).astype(BF16)
        back = back * (BRANCH_SCALE * gate)
        d_first = back * second * (sigma * (1.0 + first * (1.0 - sigma)))
        d_second = back * silu
        du_all[:, spot * part : spot * part + half] = d_first.astype(BF16)
        du_all[:, spot * part + half : (spot + 1) * part] = d_second.astype(BF16)
    hid_a[...] = hidden[:, : 2 * half]
    hid_b[...] = hidden[:, 2 * half :]
    du_a[...] = du_all[:, : 2 * part]
    du_b[...] = du_all[:, 2 * part :]
    ffn = contract(hidden[...], w_out[...], 1, 1).astype(BF16)
    back_rows = contract(du_all[...], w_in[...], 1, 1).astype(BF16)

    @pl.when(step < len(tiles))
    def _():
        f_mine[...] = ffn
        d_mine[...] = back_rows

    @pl.when(step >= len(tiles))
    def _():
        f_other[...] = ffn
        d_other[...] = back_rows


def run_experts(tiles, place, row_pieces, grad_pieces, slots, select, base, kept):
    used = used_pieces(tiles)
    sides = len(row_pieces) // 2
    wanted = used + [sides + piece for piece in used]
    rows = [row_pieces[piece] for piece in wanted]
    grads = [grad_pieces[piece] for piece in wanted]
    tile, width = row_pieces[OWN].shape
    wide = grad_pieces[OWN].shape[1]
    half = slots[0].shape[1] // 3
    part = 2 * half
    count = len(tiles)
    steps = 2 * count
    total = 8 * tile

    def late(lanes):
        return pl.BlockSpec((tile, lanes), lambda i, p: (i + base, 0))

    mine = pl.BlockSpec((tile, width), lambda i, p: (jnp.minimum(i, count - 1), 0))
    others = pl.BlockSpec((tile, width), lambda i, p: (jnp.maximum(i - count, 0), 0))
    anywhere = pl.BlockSpec(memory_space=pl.ANY)
    kept = list(kept)
    lead = 1 + 2 * len(wanted) + SLOTS + 1
    partial = jax.ShapeDtypeStruct((count * tile, width), BF16)
    lanes = [2 * half, 2 * half, 2 * part, 2 * part, width, width]
    return pl.pallas_call(
        functools.partial(experts_kernel, tiles, tile // 2),
        grid_spec=pltpu.PrefetchScalarGridSpec(
            num_scalar_prefetch=1,
            grid=(steps,),
            in_specs=[anywhere] * (2 * len(wanted) + SLOTS)
            + [pl.BlockSpec(select.shape, lambda i, p: (0, 0))]
            + [anywhere] * len(kept),
            out_specs=[mine, others, mine, others] + [late(n) for n in lanes],
            scratch_shapes=[
                pltpu.VMEM((width, LINE * part), BF16),
                pltpu.VMEM((width, LINE * half), BF16),
                pltpu.VMEM((2, tile, width), BF16),
                pltpu.VMEM((2, tile, wide), BF16),
                pltpu.VMEM((tile, LINE * half), BF16),
                pltpu.VMEM((tile, LINE * part), BF16),
                pltpu.SemaphoreType.DMA((2, LINE)),
                pltpu.SemaphoreType.DMA((2, 4)),
            ],
        ),
        out_shape=[partial] * 4 + [jax.ShapeDtypeStruct((total, n), BF16) for n in lanes],
        input_output_aliases={lead + i: 4 + i for i in range(len(kept))},
        compiler_params=pltpu.CompilerParams(vmem_limit_bytes=VMEM_BYTES),
        cost_estimate=pl.CostEstimate(
            flops=steps * tile * width * LINE * (part + half) // 4,
            bytes_accessed=2 * steps * tile * (6 * width + LINE * (part + half)),
            transcendentals=steps * tile * LINE * half,
        ),
        name="experts",
    )(place, *rows, *grads, *slots, select, *kept)


def qkv_grad_kernel(h_ref, dq_ref, dk_ref, dv_ref, gain_ref, o_ref):
    shard = o_ref.shape[-2]
    rows = h_ref[...]
    low = 0
    gains = jnp.broadcast_to(gain_ref[...], (PAD, gain_ref.shape[1])).T.astype(BF16)
    parts = [contract(rows, ref[...], 0, 0).astype(BF16) for ref in (dq_ref, dk_ref, dv_ref)]
    for part in parts + [gains]:
        for block in range(h_ref.shape[1] // shard):
            place = (block % 2, block // 2 % 2, 0, block // 4)
            o_ref[place + (slice(None), slice(low, low + part.shape[1]))] = part[
                block * shard : (block + 1) * shard
            ]
        low = low + part.shape[1]


def qkv_grad(normed, grads, gain_row, shard):
    rows, width = normed.shape
    columns = sum(grad.shape[1] for grad in grads)
    tile = width // 4
    planes = tile // (4 * shard)
    return pl.pallas_call(
        qkv_grad_kernel,
        grid=(4,),
        in_specs=[pl.BlockSpec((rows, tile), lambda i: (0, i))]
        + [pl.BlockSpec(grad.shape, lambda i: (0, 0)) for grad in grads]
        + [pl.BlockSpec((1, tile), lambda i: (0, i))],
        out_specs=pl.BlockSpec(
            (2, 2, 1, planes, shard, columns + PAD), lambda i: (0, 0, i // 2, i % 2, 0, 0)
        ),
        out_shape=jax.ShapeDtypeStruct((2, 2, 2, LINE, shard, columns + PAD), BF16),
        compiler_params=pltpu.CompilerParams(vmem_limit_bytes=VMEM_BYTES),
        cost_estimate=pl.CostEstimate(
            flops=rows * width * columns // 8,
            bytes_accessed=rows * width,
            transcendentals=0,
        ),
        name="qkv_grad",
    )(normed, *grads, gain_row)


def norm_back(value, gain, grad):
    scale = lax.rsqrt(jnp.mean(value * value, axis=-1, keepdims=True) + EPSILON)
    unit = value * scale
    grad_gain = jnp.sum(grad * unit, axis=0)
    scaled = grad * gain
    inner = jnp.mean(scaled * unit, axis=-1, keepdims=True)
    return scale * (scaled - unit * inner), grad_gain


def shards_plane(
    tokens,
    cotangent,
    positions,
    lengths,
    routes,
    logits,
    w_query,
    w_key,
    w_value,
    w_output,
    gain_attn,
    gain_ffn,
    w_in,
    w_out,
):
    seq = lax.axis_index("seq")
    data = lax.axis_index("dp")
    line, row_of, core = data // 4, (data // 2) % 2, data % 2
    tok_count, width = tokens.shape
    group_len = positions.shape[1]
    shard = w_query.shape[0]
    q_width = w_query.shape[1] // 2
    kv_width = w_key.shape[1] // 2
    kv_heads = kv_width // HDIM
    first_seq = seq == 0

    def ordered(mine, theirs, axis):
        low = jnp.where(first_seq, mine, theirs)
        high = jnp.where(first_seq, theirs, mine)
        return jnp.concatenate([low, high], axis=axis)

    def half_of(weights, which):
        half = weights.shape[1] // 2
        return lax.dynamic_slice_in_dim(weights, which * half, half, axis=1)

    def both_axes(value, pairs):
        return lax.ppermute(value, ("seq", "dp"), pairs)

    def device(s, d):
        return s * 4 * LINE + d

    straight, crossed = [], []
    for s in range(2):
        for d in range(4 * LINE):
            c = d % 2
            straight.append((device(s, d), device(c, d - c + s)))
            crossed.append((device(s, d), device(c, d - c + 1 - s)))
    crossed_back = [(there, here) for here, there in crossed]
    first_core = core == 0

    projections = (w_query, w_key, w_value)
    qkv_width = q_width + 2 * kv_width
    gain_columns = jnp.pad(jnp.stack([gain_attn, gain_ffn], axis=1), ((0, 0), (0, PAD - 2)))
    mine = jnp.concatenate([half_of(w, seq) for w in projections] + [gain_columns], axis=1)
    theirs = jnp.concatenate([half_of(w, 1 - seq) for w in projections] + [gain_columns], axis=1)
    theirs = swap_seq(theirs)
    pair = jnp.stack([jnp.where(first_seq, mine, theirs), jnp.where(first_seq, theirs, mine)])
    qkv_width = q_width + 2 * kv_width
    w_qkv = lax.all_gather(pair, "dp", axis=1, tiled=True).reshape(width, qkv_width + PAD)
    output_full = lax.all_gather(w_output, ("seq", "dp"), axis=0, tiled=True)

    in_own = w_in[0]
    half = in_own.shape[1] // 2
    sent = jnp.concatenate(
        [lax.dynamic_slice_in_dim(in_own, seq * half, half, axis=1), w_out[0].T], axis=1
    )
    same = both_axes(sent, straight)
    cross = both_axes(lax.dynamic_slice_in_dim(in_own, (1 - seq) * half, half, axis=1), crossed)
    own_part = jnp.concatenate(
        [
            jnp.where(first_core, same[:, :half], cross),
            jnp.where(first_core, cross, same[:, :half]),
            same[:, half:],
        ],
        axis=1,
    )
    other_tokens = swap_seq(after(tokens, own_part))
    up_one, down_one = line_up(own_part), line_down(own_part)
    cut = width // 2

    experts_all = 4 * LINE
    gates = jax.nn.softmax(logits, axis=-1)
    named = routes[:, :, None] == jnp.arange(experts_all, dtype=jnp.int32)[None, None, :]
    gate_table = jnp.sum(jnp.where(named, gates[:, :, None], 0.0), axis=1)
    gate_high = lax.reduce_precision(gate_table, 8, 7)
    grad_rows = jnp.concatenate(
        [
            cotangent,
            gate_high.astype(BF16),
            (gate_table - gate_high).astype(BF16),
            jnp.zeros((tok_count, PAD - 2 * experts_all), BF16),
        ],
        axis=1,
    )
    grad_near = near_pieces(grad_rows, after(grad_rows, other_tokens))
    lane = jnp.arange(PAD, dtype=jnp.int32)[:, None]
    hosted = jnp.repeat(
        jnp.array(SLOT_ORDER, jnp.int32) * 4 + 2 * row_of + seq, half, total_repeat_length=LINE * half
    )
    select = ((lane % experts_all == hosted[None, :]) & (lane < 2 * experts_all)).astype(BF16)

    places = positions[0]
    ends = jnp.cumsum(lengths[0])
    ranks = jnp.arange(group_len, dtype=jnp.int32)
    reached = ranks[:, None] >= ends[None, :]
    starts = jnp.max(jnp.where(reached, ends[None, :], 0), axis=1)
    local = (ranks - starts).astype(F32)
    freqs = jnp.power(THETA, -jnp.arange(HDIM // 2, dtype=F32) * 2.0 / HDIM)
    angles = local[:, None] * freqs[None, :]
    cos, sin = jnp.cos(angles), jnp.sin(angles)
    cos = jnp.concatenate([cos, cos, cos, cos], axis=1)
    sin = jnp.concatenate([-sin, sin, -sin, sin], axis=1)
    start_column = starts[:, None]
    own_places = lax.dynamic_slice_in_dim(places, seq * tok_count, tok_count)
    other_places = lax.dynamic_slice_in_dim(places, (1 - seq) * tok_count, tok_count)
    sort_own = (ranks[:, None] == own_places[None, :]).astype(BF16)
    sort_other = (ranks[:, None] == other_places[None, :]).astype(BF16)

    def to_order(own, other):
        return (
            contract(sort_own, own, 1, 0) + contract(sort_other, other, 1, 0)
        ).astype(BF16)

    def from_order(sort, values):
        return contract(sort, values, 0, 0).astype(BF16)

    x_sorted = to_order(tokens, other_tokens)
    gains = w_qkv[:, qkv_width : qkv_width + 2].astype(F32).T
    gain_one, gain_two = gains[0], gains[1]
    x_sorted, up_one, down_one = lax.optimization_barrier((x_sorted, up_one, down_one))
    up_two, down_two = line_up(up_one), line_down(down_one)
    normed, query, keys, values = project(
        x_sorted, gain_one[None, :], w_qkv, cos, sin, q_width, kv_heads
    )
    pairs = q_width // (2 * HDIM)
    first_pairs = (pairs + 1) // 2
    mixed_one, levels_one = attend(query, keys, values, start_column, 0, first_pairs)
    sent_one = swap_seq(from_order(sort_other, mixed_one))
    query_two, grad_near_x, grad_near_y = after((query, *grad_near), mixed_one)
    grad_near = (grad_near_x, grad_near_y)
    grad_far = far_pieces(*grad_near)
    mixed_two, levels_two = attend(
        query_two, keys, values, start_column, first_pairs, pairs - first_pairs
    )
    sent_two = swap_seq(from_order(sort_other, mixed_two))
    mixed_mine = [from_order(sort_own, mixed_one), from_order(sort_own, mixed_two)]
    mixed = ordered(
        jnp.concatenate(mixed_mine, axis=1), jnp.concatenate([sent_one, sent_two], axis=1), 1
    )
    mixed, up_two, down_two = lax.optimization_barrier((mixed, up_two, down_two))
    up_three, down_three = line_up(up_two), line_down(down_two)
    inputs = tokens.astype(F32)
    attn = jnp.dot(mixed, output_full, preferred_element_type=F32)
    middle = inputs + BRANCH_SCALE * attn
    normed_ffn = rms_norm(middle, gain_two).astype(BF16)

    normed_ffn = after(normed_ffn, *grad_far)
    row_near = near_pieces(normed_ffn, normed_ffn)
    row_far = far_pieces(*row_near)
    slots = [up_three, up_two, up_one, own_part, down_one, down_two, down_three]
    row_pieces = with_cores(normed_ffn, *row_near, *row_far)
    grad_pieces = with_cores(*after((grad_rows, *grad_near, *grad_far), row_near[0]))
    place = line.astype(jnp.int32)[None]
    far = run_experts(FAR_TILES, place, row_pieces, grad_pieces, slots, select, 0, ())
    far_back = over_cores(far[2], far[3]).astype(BF16)
    back_y, back_x = far_links(far_back)
    near = run_experts(
        NEAR_TILES, after(place, far_back), row_pieces, grad_pieces, slots, select, 4, far[4:]
    )
    hid_a, hid_b, du_a, du_b, all_rows, all_grads = near[4:]

    def weight_grads(rows, grads, grad_both, hidden):
        inner = contract(rows, grad_both, 0, 0)
        outer = contract(grads, hidden, 0, 0) * BRANCH_SCALE
        return [
            jnp.concatenate(
                [inner[:, 2 * half * i : 2 * half * (i + 1)], outer[:, half * i : half * (i + 1)]],
                axis=1,
            ).astype(BF16)
            for i in range(2)
        ]

    rows_early, grads_early, back_y, back_x = lax.optimization_barrier(
        (all_rows, all_grads, back_y, back_x)
    )
    outer_grads = weight_grads(rows_early, grads_early, du_a, hid_a)
    grads_of = dict(zip(SLOT_ORDER[:2], outer_grads))
    far_line = (line_up(outer_grads[1]), line_down(outer_grads[0]))
    near_back = over_cores(after(near[2], *outer_grads), near[3])
    first, second = near_links(near_back, back_y, back_x)
    rows_late, grads_late = after((all_rows, all_grads), first, second)
    inner_grads = weight_grads(rows_late, grads_late, du_b, hid_b)
    grads_of.update(zip(SLOT_ORDER[2:], inner_grads))
    first, second = swap_seq(first), swap_y(second)
    near_back = after(near_back, *inner_grads)
    grad_normed_ffn = own_sum(near_back, back_y, back_x, first, second)

    def line_partial(first, *rest):
        value = grads_of[first]
        for where, expert in enumerate(rest):
            value = jnp.where(line > where, grads_of[expert], value)
        return value.astype(F32)

    def line_step(step, arrived):
        up, down = arrived
        last = LINE - 1
        right = line_partial(*range(last - step, LINE)) + up.astype(F32)
        left = grads_of[step]
        for where in range(step):
            left = jnp.where(line < last - where, grads_of[step - 1 - where], left)
        left = left.astype(F32) + down.astype(F32)
        return right.astype(BF16), left.astype(BF16)

    grad_final = cotangent.astype(F32)
    grad_norm, grad_gain_two = norm_back(middle, gain_two, grad_normed_ffn)
    grad_middle = grad_final + grad_norm
    grad_attn = (BRANCH_SCALE * grad_middle).astype(BF16)
    grad_mixed = contract(grad_attn, output_full, 1, 1).astype(BF16)
    grad_w_output = contract(mixed, grad_attn, 0, 0)
    grad_other = swap_seq(half_of(grad_mixed, 1 - seq))
    far_f, far_f_other, near_f, near_f_other = after(
        (far[0], far[1], near[0], near[1]), grad_mixed
    )
    far_ffn = over_cores(far_f, far_f_other).astype(BF16)
    ffn_y, ffn_x = far_links(after(far_ffn, grad_w_output))
    near_ffn = over_cores(near_f, near_f_other)
    right, left = line_step(1, far_line)
    grad_other = after(grad_other, right, left, far_ffn, grad_w_output)
    grad_sorted = to_order(half_of(grad_mixed, seq), grad_other)
    mid_line = (line_up(right), line_down(left))
    grad_query, grad_keys, grad_values = attend_back(
        query,
        keys,
        values,
        grad_sorted,
        jnp.concatenate([levels_one, levels_two], axis=0),
        start_column,
        cos,
        sin,
    )
    (grad_query, grad_keys, grad_values), mid_line, ffn_y, ffn_x = lax.optimization_barrier(
        ((grad_query, grad_keys, grad_values), mid_line, ffn_y, ffn_x)
    )
    right, left = line_step(2, mid_line)
    last_first = (line_up(right[:cut]), line_down(left[:cut]))
    first_ffn, second_ffn = near_links(near_ffn, ffn_y, ffn_x)
    first_ffn, second_ffn = swap_seq(first_ffn), swap_y(second_ffn)
    grads_qkv = after((grad_query, grad_keys, grad_values), right, left)
    wide = qkv_grad(normed, grads_qkv, grad_gain_two[None, :], shard)


    def chosen(value, which, axis):
        return lax.dynamic_index_in_dim(value, which, axis=axis, keepdims=False)

    summed_output = lax.psum_scatter(
        grad_w_output.astype(BF16), ("seq", "dp"), scatter_dimension=0, tiled=True
    )
    kept = chosen(wide, core, 0).astype(F32)
    kept = kept + swap_core(chosen(wide, 1 - core, 0)).astype(F32)
    grads_late = after(grads_qkv, kept)
    grad_normed, sent_normed = token_grad(
        grads_late, w_qkv, own_places[:, None], other_places[:, None]
    )
    kept, sent_normed = lax.optimization_barrier((kept, sent_normed))
    first_ffn, second_ffn = after((first_ffn, second_ffn), sent_normed)
    ffn = own_sum(near_ffn, ffn_y, ffn_x, first_ffn, second_ffn)
    output = (middle + BRANCH_SCALE * ffn).astype(BF16)
    right_late, left_late = after((right[cut:], left[cut:]), last_first, sent_normed)
    last_late = (line_up(right_late), line_down(left_late))
    grad_normed = grad_normed.astype(F32) + swap_seq(sent_normed).astype(F32)
    scale = lax.rsqrt(jnp.mean(inputs * inputs, axis=-1, keepdims=True) + EPSILON)
    unit = inputs * scale
    scaled = grad_normed * gain_one
    inner = jnp.mean(scaled * unit, axis=-1, keepdims=True)
    grad_tokens = grad_middle + scale * (scaled - unit * inner)
    next_kept = chosen(kept, row_of, 0)
    next_kept = next_kept + swap_y(chosen(kept, 1 - row_of, 0).astype(BF16)).astype(F32)
    next_kept, last_first, last_late, summed_output = lax.optimization_barrier(
        (next_kept, last_first, last_late, summed_output)
    )
    own_grads = line_partial(*range(LINE))
    part_grads = jnp.concatenate(
        [
            own + up.astype(F32) + down.astype(F32)
            for own, (up, down) in ((own_grads[:cut], last_first), (own_grads[cut:], last_late))
        ],
        axis=0,
    ).astype(BF16)
    same_grads = jnp.where(first_core, part_grads[:, :half], part_grads[:, half : 2 * half])
    cross_grads = jnp.where(first_core, part_grads[:, half : 2 * half], part_grads[:, :half])
    same_grads = jnp.concatenate([same_grads, part_grads[:, 2 * half :]], axis=1)
    next_kept, same_grads, cross_grads = lax.optimization_barrier(
        (next_kept, same_grads, cross_grads)
    )
    same = both_axes(same_grads, straight)
    cross = both_axes(cross_grads, crossed_back)
    sent_lines = [
        swap_dp(chosen(next_kept, line ^ step, 1).astype(BF16), 4 * step) for step in range(1, LINE)
    ]
    summed = chosen(next_kept, line, 1) + sum(value.astype(F32) for value in sent_lines)
    summed, same, cross = lax.optimization_barrier((summed, same, cross))
    grad_w_in = ordered(same[:, :half], cross, 1)
    grad_w_out = same[:, half:].T
    kept_rows = chosen(summed, seq, 0)
    sent_rows = swap_seq(chosen(summed, 1 - seq, 0).astype(BF16)).astype(F32)
    cuts = (q_width, q_width + kv_width, qkv_width)
    pieces = [
        (a, b) for a, b in zip(jnp.split(kept_rows, cuts, axis=1), jnp.split(sent_rows, cuts, axis=1))
    ]
    grad_projections = [ordered(a, b, 1) for a, b in pieces[:3]]
    grad_gain_ffn = (pieces[3][0] + pieces[3][1])[:, 0]
    grad_gain_attn = sum(
        jnp.sum(grad * weight.astype(F32), axis=1)
        for grad, weight in zip(grad_projections, projections)
    ) / gain_attn.astype(F32)
    return (
        output,
        grad_tokens,
        grad_projections[0],
        grad_projections[1],
        grad_projections[2],
        summed_output.astype(F32),
        grad_gain_attn,
        grad_gain_ffn,
        grad_w_in.astype(F32)[None],
        grad_w_out.astype(F32)[None],
    )


def solution(mesh):
    placed = (
        P(("seq", "dp"), None),
        P(("seq", "dp"), None),
        P("dp", None),
        P("dp", None),
        P(("seq", "dp"), None),
        P(("seq", "dp"), None),
        P(("seq", "dp"), None),
        P(("seq", "dp"), None),
        P(("seq", "dp"), None),
        P(("seq", "dp"), None),
        P(("seq", "dp")),
        P(("seq", "dp")),
        P("dp", None, "seq"),
        P("dp", "seq", None),
    )
    return jax.shard_map(
        shards_plane if in_planes(mesh) else shards_general,
        mesh=mesh,
        in_specs=placed,
        out_specs=(
            P(("seq", "dp"), None),
            P(("seq", "dp"), None),
            P(("seq", "dp"), None),
            P(("seq", "dp"), None),
            P(("seq", "dp"), None),
            P(("seq", "dp"), None),
            P(("seq", "dp")),
            P(("seq", "dp")),
            P("dp", None, "seq"),
            P("dp", "seq", None),
        ),
        check_vma=False,
    )
```
